32 devices in a mesh: dp: 4 (over y, x), mp: 8 (over z, core).
Axes of the slice: x: 2, y: 2, z: 4, core: 2. Of those that a mesh axis runs over, the one named last changes fastest.
Arguments:
- tokens: bfloat16 [16384, 768], P(('dp', 'mp')), may hold values from -6 to 6
- segment_ids: int32 [32, 512], P('dp'), may hold values from 0 to 15, never falling along the last dimension, each value on 1 to 256 neighbouring positions
- gain_one: float32 [768], replicated, may hold values from 0.5 to 1.5
- gain_two: float32 [768], replicated, may hold values from 0.5 to 1.5
- value_weight: bfloat16 [768, 768], P('dp', 'mp'), may hold values from -0.21875 to 0.21875
- mixgate_weight: bfloat16 [768, 768], P('dp', 'mp'), may hold values from -0.21875 to 0.21875
- condition_weight: bfloat16 [768, 48], P('dp', 'mp'), may hold values from -5 to 5
- filter_base: bfloat16 [48, 1024], P('mp', 'dp'), may hold values from -0.8984375 to 0.8984375
- filter_shift: bfloat16 [48, 1024], P('mp', 'dp'), may hold values from -0.8984375 to 0.8984375
- mixout_weight: bfloat16 [768, 768], P('mp', 'dp'), may hold values from -0.21875 to 0.21875
- gate_weight: bfloat16 [768, 3072], P('dp', 'mp'), may hold values from -0.21875 to 0.21875
- up_weight: bfloat16 [768, 3072], P('dp', 'mp'), may hold values from -0.21875 to 0.21875
- down_weight: bfloat16 [3072, 768], P('mp', 'dp'), may hold values from -0.109375 to 0.109375
- output_grad: bfloat16 [16384, 768], P(('dp', 'mp')), may hold values from -6 to 6
Outputs:
- output: bfloat16 [16384, 768], P(('dp', 'mp'))
- input_grad: bfloat16 [16384, 768], P(('dp', 'mp'))
- gain_one_grad: float32 [768], replicated
- gain_two_grad: float32 [768], replicated
- value_grad: float32 [768, 768], P('dp', 'mp')
- mixgate_grad: float32 [768, 768], P('dp', 'mp')
- condition_grad: float32 [768, 48], P('dp', 'mp')
- filter_base_grad: float32 [48, 1024], P('mp', 'dp')
- filter_shift_grad: float32 [48, 1024], P('mp', 'dp')
- mixout_grad: float32 [768, 768], P('mp', 'dp')
- gate_grad: float32 [768, 3072], P('dp', 'mp')
- up_grad: float32 [768, 3072], P('dp', 'mp')
- down_grad: float32 [3072, 768], P('mp', 'dp')
The draws below stay inside these ranges and needn't reach their ends.
Inputs may be any that keep to these rules, and one draw needn't show every extreme that they name: `segment_ids`: in each row the ids start at 0, never fall and rise by one at each new sentence, up to 15; a sentence has 1 to 256 tokens.
All inputs are finite; a program needn't handle non-finite values.
Results may differ from the reference program's by a relative error of at most 0.024.
Values may be sent and summed in bfloat16 or wider, within the bound.
No kernel may reach another device: no remote copies, remote signals or barrier semaphores. Data moves between devices by JAX's collectives and lax.ppermute only.
A program may use at most 192 MiB of HBM per device.

```python
import math
import jax
import jax.numpy as jnp
import numpy as np
from jax import lax

D = 768
FF = 3072
GROUP_CH = 16
L = 512
G = 48
ROWS_ALL = 32
TOKENS = 16384


def steps_of(rng, extent, split, low, top_value):
    loudness, own = 1.0, jax.random.fold_in(rng, 6)
    for dim, blocks in split:
        heights = jnp.exp(jax.random.uniform(jax.random.fold_in(own, dim), (blocks,), jnp.float32, low / len(split), top_value / len(split)))
        loudness = loudness * jnp.repeat(heights, extent[dim] // blocks).reshape([-1 if axis == dim else 1 for axis in range(len(extent))])
    return loudness


def profile(count, total, limit, slope):
    portions = [(1 << 20) // math.isqrt(standing ** slope) + 1 for standing in range(2, count + 1)]
    rest, counts = total - limit - (count - 1), [1] * (count - 1)
    while rest > 0:
        candidates = [i for i in range(count - 1) if counts[i] < limit]
        mass, left = sum([portions[i] for i in candidates]), rest
        for i in candidates:
            extra = min(limit - counts[i], max(1, left * portions[i] // mass), rest)
            counts[i] = counts[i] + extra
            rest = rest - extra
    return np.array([limit] + counts)


def uneven_parts(stream_key, number_of, total, reach, skew):
    if number_of == 2:
        one = jax.random.randint(stream_key, (), max(1, total - reach), min(reach, total - 1) + 1)
        return jnp.stack([one, total - one])
    sizes = jnp.asarray(profile(number_of, total, reach, skew), jnp.int32)
    pairs = (number_of - 1) // 2
    source_of, sink = sizes[1:1 + 2 * pairs:2], sizes[2:2 + 2 * pairs:2]
    room = jnp.minimum(source_of - 1, reach - sink)
    moved = jax.random.randint(jax.random.fold_in(stream_key, 1), (pairs,), 0, 1 << 20) % (room + 1)
    sizes = sizes.at[1:1 + 2 * pairs:2].set(source_of - moved).at[2:2 + 2 * pairs:2].set(sink + moved)
    return sizes[jax.random.permutation(jax.random.fold_in(stream_key, 2), number_of)]


def bell_draw(stream_key, dims, scale, bound, split=(), held_as=jnp.bfloat16):
    drawn = jax.random.normal(stream_key, dims, jnp.float32) * scale
    if len(split) > 0:
        drawn = steps_of(stream_key, dims, split, -0.22, 0.18) * drawn
    return jnp.clip(drawn, min=-bound, max=bound).astype(held_as)


def setup_inputs(seed: int = 0) -> dict:
    streams_of = jax.random.split(jax.random.key(seed), 15)
    return {
        "tokens": bell_draw(streams_of[0], (TOKENS, D), 1.0, 6.0, ((0, 32),)),
        "segment_ids": jax.vmap(lambda own: jnp.searchsorted(jnp.cumsum(uneven_parts(own, L // 32, L, L // 2, 1)), jnp.arange(L), side="right"))(jax.random.split(streams_of[1], ROWS_ALL)).reshape((ROWS_ALL, L)).astype(jnp.int32),
        "gain_one": jnp.clip(1.0 + 0.1 * jax.random.normal(streams_of[2], (D,), jnp.float32), 0.5, 1.5),
        "gain_two": jnp.clip(1.0 + 0.1 * jax.random.normal(streams_of[3], (D,), jnp.float32), 0.5, 1.5),
        "value_weight": bell_draw(streams_of[4], (D, D), D ** -0.5, 0.21875, ((0, 4), (1, 8))),
        "mixgate_weight": bell_draw(streams_of[5], (D, D), D ** -0.5, 0.21875, ((0, 4), (1, 8))),
        "condition_weight": bell_draw(streams_of[6], (D, G), 1.0, 5.0, ((0, 4), (1, 8))),
        "filter_base": bell_draw(streams_of[7], (G, 2 * L), 0.15, 0.8984375, ((0, 8), (1, 4))),
        "filter_shift": bell_draw(streams_of[8], (G, 2 * L), 0.15, 0.8984375, ((0, 8), (1, 4))),
        "mixout_weight": bell_draw(streams_of[9], (D, D), D ** -0.5, 0.21875, ((0, 8), (1, 4))),
        "gate_weight": bell_draw(streams_of[10], (D, FF), D ** -0.5, 0.21875, ((0, 4), (1, 8))),
        "up_weight": bell_draw(streams_of[11], (D, FF), D ** -0.5, 0.21875, ((0, 4), (1, 8))),
        "down_weight": bell_draw(streams_of[12], (FF, D), FF ** -0.5, 0.109375, ((0, 8), (1, 4))),
        "output_grad": bell_draw(streams_of[13], (TOKENS, D), 1.0, 6.0, ((0, 32),)),
    }


@jax.custom_vjp
def low(v):
    return lax.optimization_barrier(v.astype(jnp.bfloat16)).astype(jnp.float32)

@jax.custom_vjp
def low_back(v):
    return v

def low_keep(v):
    return (low(v), None)

def low_pass(kept, grad):
    return (grad,)

def back_keep(v):
    return (v, None)

def back_low(kept, grad):
    return (low(grad),)
low.defvjp(low_keep, low_pass)
low_back.defvjp(back_keep, back_low)
epsilon = 1e-05
highest = lax.Precision.HIGHEST

def matmul(left, right):
    return jnp.dot(left, right, precision=highest, preferred_element_type=jnp.float32)

def normalize(token_rows, scale_gain):
    centre = lax.optimization_barrier(jnp.mean(token_rows, axis=-1, keepdims=True))
    centred = token_rows - centre
    spread = lax.optimization_barrier(jnp.mean(centred * centred, axis=-1, keepdims=True))
    return centred * lax.rsqrt(spread + epsilon) * scale_gain

def banded(kernel):
    width = kernel.shape[-1] // 2
    lags = jnp.arange(width)[:, None] - jnp.arange(width)[None, :] + width
    return jnp.take(kernel, lags, axis=-1)

def convolve_row(values_row, segment_row, cond_row, filter_base, filter_shift):
    kernel = filter_base + cond_row[:, None] * filter_shift
    same_doc = (segment_row[:, None] == segment_row[None, :]).astype(jnp.float32)
    band_matrix = low(banded(kernel) * same_doc[None])
    groups = kernel.shape[0]
    split_values = values_row.reshape(L, groups, GROUP_CH)
    mixed_row = jnp.einsum('gij,jgc->igc', band_matrix, split_values, precision=highest)
    return mixed_row.reshape(L, D)

def layer_block(input_float, segment_block, gain_one, gain_two, value_weight, mixgate_weight, condition_weight, filter_base, filter_shift, mixout_weight, gate_weight, up_weight, down_weight):
    row_total = segment_block.shape[0]
    normed_one = low(normalize(input_float, gain_one))
    values = low_back(low(matmul(normed_one, value_weight)))
    gates = low_back(matmul(normed_one, mixgate_weight))
    summary = lax.optimization_barrier(jnp.mean(normed_one.reshape(row_total, L, D), axis=1))
    cond = jnp.tanh(matmul(summary, condition_weight))

    def one_row(member):
        return convolve_row(member[0], member[1], member[2], filter_base, filter_shift)
    conv = lax.map(jax.checkpoint(one_row), (values.reshape(row_total, L, D), segment_block, cond))
    conv = low_back(conv.reshape(row_total * L, D))
    mixed = low(conv * gates)
    branch = low_back(matmul(mixed, mixout_weight))
    middle = input_float + branch
    normed_two = low(normalize(middle, gain_two))
    gate_pre = low_back(matmul(normed_two, gate_weight))
    up_pre = low_back(matmul(normed_two, up_weight))
    hidden = low(jax.nn.silu(gate_pre) * up_pre)
    feed = low_back(matmul(hidden, down_weight))
    return middle + feed

def reference(tokens, segment_ids, gain_one, gain_two, value_weight, mixgate_weight, condition_weight, filter_base, filter_shift, mixout_weight, gate_weight, up_weight, down_weight, output_grad):
    rows_block = 8 if ROWS_ALL % 8 == 0 else 1
    blocks = ROWS_ALL // rows_block

    def forward(input_float, *weights):
        inputs = input_float.reshape(blocks, rows_block * L, D)
        segments = segment_ids.reshape(blocks, rows_block, L)
        block_fn = jax.checkpoint(layer_block)

        def scan_step(carry, member):
            return (carry, block_fn(member[0], member[1], *weights))
        _, results = lax.scan(scan_step, jnp.zeros((), jnp.float32), (inputs, segments))
        return results.reshape(TOKENS, D)
    weights = [gain_one.astype(jnp.float32), gain_two.astype(jnp.float32)]
    for weight in (value_weight, mixgate_weight, condition_weight, filter_base, filter_shift, mixout_weight, gate_weight, up_weight, down_weight):
        weights.append(weight.astype(jnp.float32))
    result, pull = jax.vjp(forward, tokens.astype(jnp.float32), *weights)
    grads = pull(output_grad.astype(jnp.float32))
    return (result.astype(jnp.bfloat16), grads[0].astype(jnp.bfloat16), grads[1], grads[2], grads[3], grads[4], grads[5], grads[6], grads[7], grads[8], grads[9], grads[10], grads[11])
```

```python
import functools

import jax
import jax.numpy as jnp
from jax import lax
from jax.experimental import pallas as pl
from jax.experimental.pallas import tpu as pltpu
from jax.sharding import PartitionSpec as P

epsilon = 1e-05
highest = lax.Precision.HIGHEST
BF = jnp.bfloat16
F32 = jnp.float32
BLOCK = 128
SENTENCE = 256


def build_band(taps_row, mask_ref, band_ref, length, reach):
    blocks = length // BLOCK
    low = length - (reach + 1) * BLOCK
    width = (2 * reach + 2) * BLOCK
    spread = jnp.broadcast_to(taps_row[:, low : low + width], (BLOCK, width))
    shifted = pltpu.roll(spread, 0, 1, stride=1, stride_axis=0).astype(BF)
    for i in range(blocks):
        first, last = max(0, i - reach), min(blocks, i + reach + 1)
        rows = slice(i * BLOCK, (i + 1) * BLOCK)
        columns = slice(first * BLOCK, last * BLOCK)
        offset = (first - i + reach + 1) * BLOCK
        band_ref[rows, columns] = (
            shifted[:, offset : offset + (last - first) * BLOCK] * mask_ref[rows, columns]
        )


def conv_forward_kernel(
    unroll, channels, reach, column_ref, row_ref, cond_ref, base_ref, shift_ref, values_ref,
    conv_ref, mask_ref, taps_ref, band_ref,
):
    length = row_ref.shape[1]
    filters = base_ref.shape[0]
    mask_ref[...] = (column_ref[...] == row_ref[...]).astype(BF)
    taps_ref[...] = base_ref[...].astype(F32) + cond_ref[...] * shift_ref[...].astype(F32)
    band_ref[...] = jnp.zeros_like(band_ref)

    def some(step, carry):
        for u in range(unroll):
            f = step * unroll + u
            build_band(taps_ref[pl.ds(f, 1), :], mask_ref, band_ref.at[u], length, reach)
            rows = pl.ds(pl.multiple_of(f * channels, channels), channels)
            conv_ref[rows, :] = jnp.dot(
                values_ref[rows, :], band_ref[u], preferred_element_type=F32
            )
        return carry

    lax.fori_loop(0, filters // unroll, some, 0)


def conv_forward(segments, cond, base, shift, values, unroll=8):
    filters, length = base.shape[0], segments.shape[0]
    channels = values.shape[0] // filters
    unroll = next(u for u in range(unroll, 0, -1) if filters % u == 0)
    vmem = pl.BlockSpec(memory_space=pltpu.VMEM)
    flops = 2 * values.shape[0] * length * length
    return pl.pallas_call(
        functools.partial(conv_forward_kernel, unroll, channels, SENTENCE // BLOCK),
        out_shape=jax.ShapeDtypeStruct(values.shape, F32),
        in_specs=[vmem] * 6,
        out_specs=vmem,
        scratch_shapes=[
            pltpu.VMEM((length, length), BF),
            pltpu.VMEM(base.shape, F32),
            pltpu.VMEM((unroll, length, length), BF),
        ],
        compiler_params=pltpu.CompilerParams(vmem_limit_bytes=40 << 20),
        cost_estimate=pl.CostEstimate(
            flops=flops * 16, bytes_accessed=values.size * 6, transcendentals=0
        ),
        name="conv_forward",
    )(segments[:, None], segments[None, :], cond[:, None], base, shift, values)


def conv_backward_kernel(
    unroll, channels, reach, column_ref, turned_ref, row_ref, cond_ref, base_ref, shift_ref,
    values_ref, grad_ref, grad_values_ref, grad_taps_ref, mask_ref, mask_turned_ref, taps_ref,
    band_ref, grad_turned_ref,
):
    length = row_ref.shape[1]
    filters = base_ref.shape[0]
    blocks = length // BLOCK
    mask_ref[...] = (column_ref[...] == row_ref[...]).astype(BF)
    mask_turned_ref[...] = (turned_ref[...] == row_ref[...]).astype(F32)
    taps_ref[...] = base_ref[...].astype(F32) + cond_ref[...] * shift_ref[...].astype(F32)
    band_ref[...] = jnp.zeros_like(band_ref)
    turn = (
        lax.broadcasted_iota(jnp.int32, (length, length), 0)
        + lax.broadcasted_iota(jnp.int32, (length, length), 1)
        == length - 1
    ).astype(BF)
    grad_turned_ref[...] = jnp.dot(grad_ref[...], turn, preferred_element_type=F32)

    def some(step, carry):
        for u in range(unroll):
            f = step * unroll + u
            build_band(taps_ref[pl.ds(f, 1), :], mask_ref, band_ref.at[u], length, reach)
            rows = pl.ds(pl.multiple_of(f * channels, channels), channels)
            grad_values_ref[rows, :] = jnp.dot(
                grad_ref[rows, :], band_ref[u], preferred_element_type=F32
            ).astype(BF)
            turned = grad_turned_ref[rows, :].T.astype(BF)
            product = jnp.dot(turned, values_ref[rows, :], preferred_element_type=F32)
            parts = [jnp.zeros((BLOCK, BLOCK), F32)] + [None] * (2 * reach + 1)
            for i in range(blocks):
                back = blocks - 1 - i
                for j in range(max(0, back - reach), min(blocks, back + reach + 1)):
                    here = (
                        slice(i * BLOCK, (i + 1) * BLOCK),
                        slice(j * BLOCK, (j + 1) * BLOCK),
                    )
                    block = product[here] * mask_turned_ref[here]
                    d = j - back + reach + 1
                    parts[d] = block if parts[d] is None else parts[d] + block
            aligned = pltpu.roll(jnp.concatenate(parts, axis=1), 0, 1, stride=1, stride_axis=0)
            grad_taps_ref[pl.ds(f, 1), :] = jnp.sum(aligned, axis=0, keepdims=True)
        return carry

    lax.fori_loop(0, filters // unroll, some, 0)


def conv_backward(segments, cond, base_turned, shift_turned, values, grad, unroll=4):
    filters, length = base_turned.shape[0], segments.shape[0]
    channels = values.shape[0] // filters
    reach = SENTENCE // BLOCK
    width = (2 * reach + 2) * BLOCK
    unroll = next(u for u in range(unroll, 0, -1) if filters % u == 0)
    vmem = pl.BlockSpec(memory_space=pltpu.VMEM)
    flops = 2 * values.shape[0] * length * length
    grad_values, grad_taps = pl.pallas_call(
        functools.partial(conv_backward_kernel, unroll, channels, reach),
        out_shape=(
            jax.ShapeDtypeStruct(values.shape, BF),
            jax.ShapeDtypeStruct((filters, width), F32),
        ),
        in_specs=[vmem] * 8,
        out_specs=(vmem, vmem),
        scratch_shapes=[
            pltpu.VMEM((length, length), BF),
            pltpu.VMEM((length, length), F32),
            pltpu.VMEM(base_turned.shape, F32),
            pltpu.VMEM((unroll, length, length), BF),
            pltpu.VMEM(values.shape, F32),
        ],
        compiler_params=pltpu.CompilerParams(vmem_limit_bytes=48 << 20),
        cost_estimate=pl.CostEstimate(
            flops=flops * 32, bytes_accessed=values.size * 6, transcendentals=0
        ),
        name="conv_backward",
    )(
        segments[:, None],
        segments[::-1][:, None],
        segments[None, :],
        cond[:, None],
        base_turned,
        shift_turned,
        values,
        grad,
    )
    lags = jnp.roll(grad_taps, -(BLOCK - 1), axis=1)[:, ::-1]
    start = length + (reach + 1) * BLOCK - (width - 1)
    full = jnp.pad(lags, ((0, 0), (start, 2 * length - start - width + 1)))
    return grad_values, full[:, : 2 * length]


def swap(value, axis, mask):
    return lax.ppermute(value, axis, [(i, i ^ mask) for i in range(lax.axis_size(axis))])


def bits_of(count):
    return [1 << b for b in range(count.bit_length() - 1)]


def gather_dp(block):
    bits = bits_of(lax.axis_size("dp"))
    half = block.shape[1] // 2
    found = []
    for part, order in ((block[:, :half], bits), (block[:, half:], bits[::-1])):
        held, masks = part[None], [0]
        for bit in order:
            held = jnp.concatenate([held, swap(held, "dp", bit)], axis=0)
            masks = masks + [m | bit for m in masks]
        found.append({m: held[i] for i, m in enumerate(masks)})
    return [jnp.concatenate([f[m] for f in found], axis=1) for m in range(lax.axis_size("dp"))]


def natural(pieces, me):
    held = jnp.stack(pieces)
    return jnp.concatenate(
        [lax.dynamic_index_in_dim(held, j ^ me, 0, keepdims=False) for j in range(len(pieces))],
        axis=1,
    )


def scatter_dp(pieces):
    bits = bits_of(lax.axis_size("dp"))
    half = pieces[0].shape[1] // 2
    done = []
    for part, order in ((slice(None, half), bits[::-1]), (slice(half, None), bits)):
        held = {m: p[:, part] for m, p in enumerate(pieces)}
        for bit in order:
            stay = [m for m in held if not m & bit]
            got = swap(jnp.stack([held[m | bit] for m in stay]), "dp", bit)
            held = {m: held[m] + got[i] for i, m in enumerate(stay)}
        done.append(held[0])
    return jnp.concatenate(done, axis=1)


def everywhere(value):
    for bit in bits_of(lax.axis_size("mp")):
        value = value + swap(value, "mp", bit)
    for bit in bits_of(lax.axis_size("dp")):
        value = value + swap(value, "dp", bit)
    return value


def statistics(value):
    centred = value - jnp.mean(value, axis=-1, keepdims=True)
    scale = lax.rsqrt(jnp.mean(centred * centred, axis=-1, keepdims=True) + epsilon)
    return centred * scale, scale


def normalize_back(normal, scale, gain, grad):
    scaled = grad * gain
    return scale * (
        scaled
        - jnp.mean(scaled, axis=-1, keepdims=True)
        - normal * jnp.mean(scaled * normal, axis=-1, keepdims=True)
    )


def mm(left, right, dims):
    return lax.dot_general(left, right, (dims, ((), ())), preferred_element_type=F32)


def body(
    tokens, segment_ids, gain_one, gain_two, value_weight, mixgate_weight, condition_weight,
    filter_base, filter_shift, mixout_weight, gate_weight, up_weight, down_weight, output_grad,
):
    dp_size, mp_size = lax.axis_size("dp"), lax.axis_size("mp")
    dp, mp = lax.axis_index("dp"), lax.axis_index("mp")
    core = mp & 1
    chips = mp_size // 2
    local, width = tokens.shape
    length = segment_ids.shape[1]
    whole_rows = local % length == 0
    total = 2 * local
    rows = total // length

    def pair(own, other):
        if whole_rows:
            return jnp.concatenate([own, other], axis=0)
        first = core == 0
        return jnp.concatenate([jnp.where(first, own, other), jnp.where(first, other, own)], axis=0)

    def mine(value):
        return value[:local] if whole_rows else lax.dynamic_slice_in_dim(value, core * local, local)

    def others(value):
        if whole_rows:
            return value[local:]
        return lax.dynamic_slice_in_dim(value, (1 - core) * local, local)

    def pair_sum(value):
        got = swap(value, "mp", 1)
        if whole_rows:
            got = jnp.concatenate([got[local:], got[:local]], axis=0)
        return value.astype(F32) + got.astype(F32)

    def pair_scatter(value):
        return mine(value) + swap(others(value).astype(BF), "mp", 1).astype(F32)

    block_c = value_weight.shape[1]
    block_g = condition_weight.shape[1]
    block_f = gate_weight.shape[1]
    taps = filter_base.shape[1]
    mixer_pack = jnp.stack([value_weight, mixgate_weight, mixout_weight.T])
    filter_pack = jnp.stack([filter_base.T, filter_shift.T])
    ffn_pack = jnp.stack([gate_weight, up_weight, down_weight.T])

    tokens_all = pair(tokens, swap(tokens, "mp", 1))
    grad_all = pair(output_grad, swap(output_grad, "mp", 1))
    if whole_rows:
        per = local // length
        seg_rows = jnp.concatenate(
            [
                lax.dynamic_slice_in_dim(segment_ids, mp * per, per),
                lax.dynamic_slice_in_dim(segment_ids, (mp ^ 1) * per, per),
            ]
        )
    else:
        seg_rows = lax.dynamic_slice_in_dim(segment_ids, (mp // 2) * rows, rows)

    def gather(block):
        found = [block] + [swap(block, "mp", 2 * k) for k in range(1, chips)]
        return [natural(gather_dp(b), dp) for b in found]

    mixer = jnp.concatenate(gather(mixer_pack), axis=2)
    small = jnp.concatenate(gather(jnp.pad(condition_weight, ((0, 0), (0, 0)))[None]), axis=2)[0]
    filters = jnp.concatenate(gather(filter_pack), axis=2)
    ffn = gather(ffn_pack)
    value_full, mixgate_full, mixout_full = mixer
    base, shift = jnp.swapaxes(filters, 1, 2)
    base_turned = jnp.roll(base[:, ::-1], 1, axis=1)
    shift_turned = jnp.roll(shift[:, ::-1], 1, axis=1)

    xf = tokens_all.astype(F32)
    normal_one, scale_one = statistics(xf)
    normed_one = (normal_one * gain_one).astype(BF)
    values = mm(value_full, normed_one, ((0,), (1,))).astype(BF)
    gates = mm(mixgate_full, normed_one, ((0,), (1,)))
    summary = jnp.mean(normed_one.astype(F32).reshape(rows, length, width), axis=1)
    condition = small.astype(F32)
    cond = jnp.tanh(jnp.dot(summary, condition, precision=highest))
    cuts = [slice(r * length, (r + 1) * length) for r in range(rows)]
    conv = jnp.concatenate(
        [conv_forward(seg_rows[r], cond[r], base, shift, values[:, cuts[r]]) for r in range(rows)],
        axis=1,
    )
    mixed = (conv * gates).astype(BF)
    branch = pair_sum(mm(mixed, mixout_full, ((0,), (1,))).astype(BF))
    middle = xf + branch
    normal_two, scale_two = statistics(middle)
    normed_two = (normal_two * gain_two).astype(BF)

    feed = jnp.zeros((total, width), F32)
    grad_two = jnp.zeros((total, width), F32)
    ffn_grads = []
    for k in range(chips):
        gate_full, up_full, down_full = ffn[k]
        gate_pre = mm(normed_two, gate_full, ((1,), (0,)))
        up_pre = mm(normed_two, up_full, ((1,), (0,)))
        grad_hidden = mm(grad_all, down_full, ((1,), (0,)))
        sigmoid = jax.nn.sigmoid(gate_pre)
        silu = gate_pre * sigmoid
        hidden = (silu * up_pre).astype(BF)
        grad_gate = (grad_hidden * up_pre * (sigmoid + silu * (1.0 - sigmoid))).astype(BF)
        grad_up = (grad_hidden * silu).astype(BF)
        feed = feed + mm(hidden, down_full, ((1,), (1,)))
        grad_two = (
            grad_two + mm(grad_gate, gate_full, ((1,), (1,))) + mm(grad_up, up_full, ((1,), (1,)))
        )
        ffn_grads.append(
            jnp.stack(
                [
                    mm(normed_two, grad_gate, ((0,), (0,))).astype(BF),
                    mm(normed_two, grad_up, ((0,), (0,))).astype(BF),
                    mm(grad_all, hidden, ((0,), (0,))).astype(BF),
                ]
            )
        )

    def scatter(grads):
        sums = None
        for k, grad in enumerate(grads):
            size = grad.shape[1] // dp_size
            pieces = [
                lax.dynamic_slice_in_dim(grad, (dp ^ m) * size, size, axis=1)
                for m in range(dp_size)
            ]
            part = scatter_dp(pieces)
            part = part if k == 0 else swap(part, "mp", 2 * k)
            sums = part.astype(F32) if sums is None else sums + part.astype(F32)
        return sums

    gate_sum, up_sum, down_sum = scatter(ffn_grads)
    output = (mine(middle) + pair_scatter(feed)).astype(BF)

    grad_normed_two = pair_sum(grad_two.astype(BF))
    gain_two_part = jnp.sum(mine(grad_normed_two * normal_two), axis=0)
    grad_middle = grad_all.astype(F32) + normalize_back(
        normal_two, scale_two, gain_two, grad_normed_two
    )
    grad_branch = grad_middle.astype(BF)

    mixout_grad = mm(grad_branch, mixed, ((0,), (1,)))
    grad_mixed = mm(mixout_full, grad_branch, ((0,), (1,)))
    grad_conv = (grad_mixed * gates).astype(BF)
    grad_gates = (grad_mixed * conv).astype(BF)
    backs = [
        conv_backward(
            seg_rows[r], cond[r], base_turned, shift_turned, values[:, cuts[r]],
            grad_conv[:, cuts[r]],
        )
        for r in range(rows)
    ]
    grad_values = jnp.concatenate([b[0] for b in backs], axis=1)
    grad_taps = jnp.stack([b[1] for b in backs])
    base_grad = jnp.sum(grad_taps, axis=0)
    shift_grad = jnp.sum(grad_taps * cond[:, :, None], axis=0)
    grad_cond = jnp.sum(grad_taps * shift.astype(F32)[None], axis=2) * (1.0 - cond * cond)
    condition_grad = mm(summary, grad_cond, ((0,), (0,)))
    grad_summary = jnp.dot(grad_cond, condition.T, precision=highest) / length
    value_grad = mm(normed_one, grad_values, ((0,), (1,)))
    mixgate_grad = mm(normed_one, grad_gates, ((0,), (1,)))
    grad_one = mm(grad_values, value_full, ((0,), (1,))) + mm(
        grad_gates, mixgate_full, ((0,), (1,))
    )
    grad_one = (grad_one.reshape(rows, length, width) + grad_summary[:, None, :]).reshape(
        total, width
    )
    grad_normed_one = pair_scatter(grad_one)
    input_grad = (
        mine(grad_middle)
        + normalize_back(mine(normal_one), mine(scale_one), gain_one, grad_normed_one)
    ).astype(BF)
    gain_one_part = jnp.sum(grad_normed_one * mine(normal_one), axis=0)
    gain_one_grad, gain_two_grad = everywhere(jnp.stack([gain_one_part, gain_two_part]))

    def split(grad, size):
        return [grad[..., k * size : (k + 1) * size].astype(BF) for k in range(chips)]

    value_sum, mixgate_sum, mixout_sum = scatter(
        split(jnp.stack([value_grad, mixgate_grad, mixout_grad]), block_c)
    )
    condition_sum = scatter(split(condition_grad[None], block_g))[0]
    base_sum, shift_sum = scatter(
        split(jnp.swapaxes(jnp.stack([base_grad, shift_grad]), 1, 2), block_g)
    )
    return (
        output, input_grad, gain_one_grad, gain_two_grad, value_sum, mixgate_sum, condition_sum,
        base_sum.T, shift_sum.T, mixout_sum.T, gate_sum, up_sum, down_sum.T,
    )


def solution(mesh):
    sides = P(("dp", "mp"), None)
    columns, rows = P("dp", "mp"), P("mp", "dp")
    in_specs = (
        sides, P("dp", None), P(), P(), columns, columns, columns, rows, rows, rows, columns,
        columns, rows, sides,
    )
    out_specs = (
        sides, sides, P(), P(), columns, columns, columns, rows, rows, rows, columns, columns, rows,
    )
    return jax.shard_map(body, mesh=mesh, in_specs=in_specs, out_specs=out_specs, check_vma=False)
```

```python
import functools

import jax
import jax.numpy as jnp
from jax import lax
from jax.experimental import pallas as pl
from jax.experimental.pallas import tpu as pltpu
from jax.sharding import PartitionSpec as P

epsilon = 1e-05
highest = lax.Precision.HIGHEST
BF = jnp.bfloat16
F32 = jnp.float32
BLOCK = 128
SENTENCE = 256


def build_band(taps_row, mask_ref, band_ref, length, reach):
    blocks = length // BLOCK
    low = length - (reach + 1) * BLOCK
    width = (2 * reach + 2) * BLOCK
    spread = jnp.broadcast_to(taps_row[:, low : low + width], (BLOCK, width))
    shifted = pltpu.roll(spread, 0, 1, stride=1, stride_axis=0).astype(BF)
    for i in range(blocks):
        first, last = max(0, i - reach), min(blocks, i + reach + 1)
        rows = slice(i * BLOCK, (i + 1) * BLOCK)
        columns = slice(first * BLOCK, last * BLOCK)
        offset = (first - i + reach + 1) * BLOCK
        band_ref[rows, columns] = (
            shifted[:, offset : offset + (last - first) * BLOCK] * mask_ref[rows, columns]
        )


def conv_forward_kernel(
    unroll, channels, reach, column_ref, row_ref, cond_ref, base_ref, shift_ref, values_ref,
    conv_ref, mask_ref, taps_ref, band_ref,
):
    length = row_ref.shape[1]
    filters = base_ref.shape[0]
    mask_ref[...] = (column_ref[...] == row_ref[...]).astype(BF)
    taps_ref[...] = base_ref[...].astype(F32) + cond_ref[...] * shift_ref[...].astype(F32)
    band_ref[...] = jnp.zeros_like(band_ref)

    def some(step, carry):
        for u in range(unroll):
            f = step * unroll + u
            build_band(taps_ref[pl.ds(f, 1), :], mask_ref, band_ref.at[u], length, reach)
            rows = pl.ds(pl.multiple_of(f * channels, channels), channels)
            conv_ref[rows, :] = jnp.dot(
                values_ref[rows, :], band_ref[u], preferred_element_type=F32
            )
        return carry

    lax.fori_loop(0, filters // unroll, some, 0)


def conv_forward(segments, cond, base, shift, values, unroll=8):
    filters, length = base.shape[0], segments.shape[0]
    channels = values.shape[0] // filters
    unroll = next(u for u in range(unroll, 0, -1) if filters % u == 0)
    vmem = pl.BlockSpec(memory_space=pltpu.VMEM)
    flops = 2 * values.shape[0] * length * length
    return pl.pallas_call(
        functools.partial(conv_forward_kernel, unroll, channels, SENTENCE // BLOCK),
        out_shape=jax.ShapeDtypeStruct(values.shape, F32),
        in_specs=[vmem] * 6,
        out_specs=vmem,
        scratch_shapes=[
            pltpu.VMEM((length, length), BF),
            pltpu.VMEM(base.shape, F32),
            pltpu.VMEM((unroll, length, length), BF),
        ],
        compiler_params=pltpu.CompilerParams(vmem_limit_bytes=40 << 20),
        cost_estimate=pl.CostEstimate(
            flops=flops * 16, bytes_accessed=values.size * 6, transcendentals=0
        ),
        name="conv_forward",
    )(segments[:, None], segments[None, :], cond[:, None], base, shift, values)


def conv_backward_kernel(
    unroll, channels, reach, column_ref, turned_ref, row_ref, cond_ref, base_ref, shift_ref,
    values_ref, grad_ref, grad_values_ref, grad_taps_ref, mask_ref, mask_turned_ref, taps_ref,
    band_ref, grad_turned_ref,
):
    length = row_ref.shape[1]
    filters = base_ref.shape[0]
    blocks = length // BLOCK
    mask_ref[...] = (column_ref[...] == row_ref[...]).astype(BF)
    mask_turned_ref[...] = (turned_ref[...] == row_ref[...]).astype(F32)
    taps_ref[...] = base_ref[...].astype(F32) + cond_ref[...] * shift_ref[...].astype(F32)
    band_ref[...] = jnp.zeros_like(band_ref)
    turn = (
        lax.broadcasted_iota(jnp.int32, (length, length), 0)
        + lax.broadcasted_iota(jnp.int32, (length, length), 1)
        == length - 1
    ).astype(BF)
    grad_turned_ref[...] = jnp.dot(grad_ref[...], turn, preferred_element_type=F32)

    def some(step, carry):
        for u in range(unroll):
            f = step * unroll + u
            build_band(taps_ref[pl.ds(f, 1), :], mask_ref, band_ref.at[u], length, reach)
            rows = pl.ds(pl.multiple_of(f * channels, channels), channels)
            grad_values_ref[rows, :] = jnp.dot(
                grad_ref[rows, :], band_ref[u], preferred_element_type=F32
            ).astype(BF)
            turned = grad_turned_ref[rows, :].T.astype(BF)
            product = jnp.dot(turned, values_ref[rows, :], preferred_element_type=F32)
            parts = [jnp.zeros((BLOCK, BLOCK), F32)] + [None] * (2 * reach + 1)
            for i in range(blocks):
                back = blocks - 1 - i
                for j in range(max(0, back - reach), min(blocks, back + reach + 1)):
                    here = (
                        slice(i * BLOCK, (i + 1) * BLOCK),
                        slice(j * BLOCK, (j + 1) * BLOCK),
                    )
                    block = product[here] * mask_turned_ref[here]
                    d = j - back + reach + 1
                    parts[d] = block if parts[d] is None else parts[d] + block
            aligned = pltpu.roll(jnp.concatenate(parts, axis=1), 0, 1, stride=1, stride_axis=0)
            grad_taps_ref[pl.ds(f, 1), :] = jnp.sum(aligned, axis=0, keepdims=True)
        return carry

    lax.fori_loop(0, filters // unroll, some, 0)


def conv_backward(segments, cond, base_turned, shift_turned, values, grad, unroll=4):
    filters, length = base_turned.shape[0], segments.shape[0]
    channels = values.shape[0] // filters
    reach = SENTENCE // BLOCK
    width = (2 * reach + 2) * BLOCK
    unroll = next(u for u in range(unroll, 0, -1) if filters % u == 0)
    vmem = pl.BlockSpec(memory_space=pltpu.VMEM)
    flops = 2 * values.shape[0] * length * length
    grad_values, grad_taps = pl.pallas_call(
        functools.partial(conv_backward_kernel, unroll, channels, reach),
        out_shape=(
            jax.ShapeDtypeStruct(values.shape, BF),
            jax.ShapeDtypeStruct((filters, width), F32),
        ),
        in_specs=[vmem] * 8,
        out_specs=(vmem, vmem),
        scratch_shapes=[
            pltpu.VMEM((length, length), BF),
            pltpu.VMEM((length, length), F32),
            pltpu.VMEM(base_turned.shape, F32),
            pltpu.VMEM((unroll, length, length), BF),
            pltpu.VMEM(values.shape, F32),
        ],
        compiler_params=pltpu.CompilerParams(vmem_limit_bytes=48 << 20),
        cost_estimate=pl.CostEstimate(
            flops=flops * 32, bytes_accessed=values.size * 6, transcendentals=0
        ),
        name="conv_backward",
    )(
        segments[:, None],
        segments[::-1][:, None],
        segments[None, :],
        cond[:, None],
        base_turned,
        shift_turned,
        values,
        grad,
    )
    lags = jnp.roll(grad_taps, -(BLOCK - 1), axis=1)[:, ::-1]
    start = length + (reach + 1) * BLOCK - (width - 1)
    full = jnp.pad(lags, ((0, 0), (start, 2 * length - start - width + 1)))
    return grad_values, full[:, : 2 * length]


def swap(value, axis, mask):
    return lax.ppermute(value, axis, [(i, i ^ mask) for i in range(lax.axis_size(axis))])


def bits_of(count):
    return [1 << b for b in range(count.bit_length() - 1)]


def gather_dp(block):
    bits = bits_of(lax.axis_size("dp"))
    half = block.shape[1] // 2
    found = []
    for part, order in ((block[:, :half], bits), (block[:, half:], bits[::-1])):
        held, masks = part[None], [0]
        for bit in order:
            held = jnp.concatenate([held, swap(held, "dp", bit)], axis=0)
            masks = masks + [m | bit for m in masks]
        found.append({m: held[i] for i, m in enumerate(masks)})
    return [jnp.concatenate([f[m] for f in found], axis=1) for m in range(lax.axis_size("dp"))]


def natural(pieces, me):
    held = jnp.stack(pieces)
    return jnp.concatenate(
        [lax.dynamic_index_in_dim(held, j ^ me, 0, keepdims=False) for j in range(len(pieces))],
        axis=1,
    )


def scatter_dp(pieces):
    bits = bits_of(lax.axis_size("dp"))
    half = pieces[0].shape[1] // 2
    done = []
    for part, order in ((slice(None, half), bits[::-1]), (slice(half, None), bits)):
        held = {m: p[:, part] for m, p in enumerate(pieces)}
        for bit in order:
            stay = [m for m in held if not m & bit]
            got = swap(jnp.stack([held[m | bit] for m in stay]), "dp", bit)
            held = {m: held[m] + got[i] for i, m in enumerate(stay)}
        done.append(held[0])
    return jnp.concatenate(done, axis=1)


def everywhere(value):
    for bit in bits_of(lax.axis_size("mp")):
        value = value + swap(value, "mp", bit)
    for bit in bits_of(lax.axis_size("dp")):
        value = value + swap(value, "dp", bit)
    return value


def statistics(value):
    centred = value - jnp.mean(value, axis=-1, keepdims=True)
    scale = lax.rsqrt(jnp.mean(centred * centred, axis=-1, keepdims=True) + epsilon)
    return centred * scale, scale


def normalize_back(normal, scale, gain, grad):
    scaled = grad * gain
    return scale * (
        scaled
        - jnp.mean(scaled, axis=-1, keepdims=True)
        - normal * jnp.mean(scaled * normal, axis=-1, keepdims=True)
    )


def mm(left, right, dims):
    return lax.dot_general(left, right, (dims, ((), ())), preferred_element_type=F32)


def body(
    tokens, segment_ids, gain_one, gain_two, value_weight, mixgate_weight, condition_weight,
    filter_base, filter_shift, mixout_weight, gate_weight, up_weight, down_weight, output_grad,
):
    dp_size, mp_size = lax.axis_size("dp"), lax.axis_size("mp")
    dp, mp = lax.axis_index("dp"), lax.axis_index("mp")
    core = mp & 1
    chips = mp_size // 2
    local, width = tokens.shape
    length = segment_ids.shape[1]
    whole_rows = local % length == 0
    total = 2 * local
    rows = total // length

    def pair(own, other):
        if whole_rows:
            return jnp.concatenate([own, other], axis=0)
        first = core == 0
        return jnp.concatenate([jnp.where(first, own, other), jnp.where(first, other, own)], axis=0)

    def mine(value):
        return value[:local] if whole_rows else lax.dynamic_slice_in_dim(value, core * local, local)

    def others(value):
        if whole_rows:
            return value[local:]
        return lax.dynamic_slice_in_dim(value, (1 - core) * local, local)

    def pair_sum(value):
        got = swap(value, "mp", 1)
        if whole_rows:
            got = jnp.concatenate([got[local:], got[:local]], axis=0)
        return value.astype(F32) + got.astype(F32)

    def pair_scatter(value):
        return mine(value) + swap(others(value).astype(BF), "mp", 1).astype(F32)

    block_c = value_weight.shape[1]
    block_g = condition_weight.shape[1]
    block_f = gate_weight.shape[1]
    taps = filter_base.shape[1]
    mixer_pack = jnp.stack([value_weight, mixgate_weight, mixout_weight.T])
    filter_pack = jnp.stack([filter_base.T, filter_shift.T])
    ffn_pack = jnp.stack([gate_weight, up_weight, down_weight.T])

    tokens_all = pair(tokens, swap(tokens, "mp", 1))
    grad_all = pair(output_grad, swap(output_grad, "mp", 1))
    if whole_rows:
        per = local // length
        seg_rows = jnp.concatenate(
            [
                lax.dynamic_slice_in_dim(segment_ids, mp * per, per),
                lax.dynamic_slice_in_dim(segment_ids, (mp ^ 1) * per, per),
            ]
        )
    else:
        seg_rows = lax.dynamic_slice_in_dim(segment_ids, (mp // 2) * rows, rows)

    def gather(block):
        found = [block] + [swap(block, "mp", 2 * k) for k in range(1, chips)]
        return [natural(gather_dp(b), dp) for b in found]

    mixer = jnp.concatenate(gather(mixer_pack), axis=2)
    small = jnp.concatenate(gather(jnp.pad(condition_weight, ((0, 0), (0, 0)))[None]), axis=2)[0]
    filters = jnp.concatenate(gather(filter_pack), axis=2)
    ffn = gather(ffn_pack)
    value_full, mixgate_full, mixout_full = mixer
    base, shift = jnp.swapaxes(filters, 1, 2)
    base_turned = jnp.roll(base[:, ::-1], 1, axis=1)
    shift_turned = jnp.roll(shift[:, ::-1], 1, axis=1)

    xf = tokens_all.astype(F32)
    normal_one, scale_one = statistics(xf)
    normed_one = (normal_one * gain_one).astype(BF)
    values = mm(value_full, normed_one, ((0,), (1,))).astype(BF)
    gates = mm(mixgate_full, normed_one, ((0,), (1,)))
    summary = jnp.mean(normed_one.astype(F32).reshape(rows, length, width), axis=1)
    condition = small.astype(F32)
    cond = jnp.tanh(jnp.dot(summary, condition, precision=highest))
    cuts = [slice(r * length, (r + 1) * length) for r in range(rows)]
    conv = jnp.concatenate(
        [conv_forward(seg_rows[r], cond[r], base, shift, values[:, cuts[r]]) for r in range(rows)],
        axis=1,
    )
    mixed = (conv * gates).astype(BF)
    branch = pair_sum(mm(mixed, mixout_full, ((0,), (1,))).astype(BF))
    middle = xf + branch
    normal_two, scale_two = statistics(middle)
    normed_two = (normal_two * gain_two).astype(BF)

    feed = jnp.zeros((total, width), F32)
    grad_two = jnp.zeros((total, width), F32)
    ffn_grads = []
    for k in range(chips):
        gate_full, up_full, down_full = ffn[k]
        gate_pre = mm(normed_two, gate_full, ((1,), (0,)))
        up_pre = mm(normed_two, up_full, ((1,), (0,)))
        grad_hidden = mm(grad_all, down_full, ((1,), (0,)))
        sigmoid = jax.nn.sigmoid(gate_pre)
        silu = gate_pre * sigmoid
        hidden = (silu * up_pre).astype(BF)
        grad_gate = (grad_hidden * up_pre * (sigmoid + silu * (1.0 - sigmoid))).astype(BF)
        grad_up = (grad_hidden * silu).astype(BF)
        feed = feed + mm(hidden, down_full, ((1,), (1,)))
        grad_two = (
            grad_two + mm(grad_gate, gate_full, ((1,), (1,))) + mm(grad_up, up_full, ((1,), (1,)))
        )
        ffn_grads.append(
            jnp.stack(
                [
                    mm(normed_two, grad_gate, ((0,), (0,))).astype(BF),
                    mm(normed_two, grad_up, ((0,), (0,))).astype(BF),
                    mm(grad_all, hidden, ((0,), (0,))).astype(BF),
                ]
            )
        )

    def scatter(grads):
        sums = None
        for k, grad in enumerate(grads):
            size = grad.shape[1] // dp_size
            pieces = [
                lax.dynamic_slice_in_dim(grad, (dp ^ m) * size, size, axis=1)
                for m in range(dp_size)
            ]
            part = scatter_dp(pieces)
            part = part if k == 0 else swap(part, "mp", 2 * k)
            sums = part.astype(F32) if sums is None else sums + part.astype(F32)
        return sums

    gate_sum, up_sum, down_sum = scatter(ffn_grads)
    output = (mine(middle) + pair_scatter(feed)).astype(BF)

    grad_normed_two = pair_sum(grad_two.astype(BF))
    gain_two_part = jnp.sum(mine(grad_normed_two * normal_two), axis=0)
    grad_middle = grad_all.astype(F32) + normalize_back(
        normal_two, scale_two, gain_two, grad_normed_two
    )
    grad_branch = grad_middle.astype(BF)

    mixout_grad = mm(grad_branch, mixed, ((0,), (1,)))
    grad_mixed = mm(mixout_full, grad_branch, ((0,), (1,)))
    grad_conv = (grad_mixed * gates).astype(BF)
    grad_gates = (grad_mixed * conv).astype(BF)
    backs = [
        conv_backward(
            seg_rows[r], cond[r], base_turned, shift_turned, values[:, cuts[r]],
            grad_conv[:, cuts[r]],
        )
        for r in range(rows)
    ]
    grad_values = jnp.concatenate([b[0] for b in backs], axis=1)
    grad_taps = jnp.stack([b[1] for b in backs])
    base_grad = jnp.sum(grad_taps, axis=0)
    shift_grad = jnp.sum(grad_taps * cond[:, :, None], axis=0)
    grad_cond = jnp.sum(grad_taps * shift.astype(F32)[None], axis=2) * (1.0 - cond * cond)
    condition_grad = mm(summary, grad_cond, ((0,), (0,)))
    grad_summary = jnp.dot(grad_cond, condition.T, precision=highest) / length
    value_grad = mm(normed_one, grad_values, ((0,), (1,)))
    mixgate_grad = mm(normed_one, grad_gates, ((0,), (1,)))
    grad_one = mm(grad_values, value_full, ((0,), (1,))) + mm(
        grad_gates, mixgate_full, ((0,), (1,))
    )
    grad_one = (grad_one.reshape(rows, length, width) + grad_summary[:, None, :]).reshape(
        total, width
    )
    grad_normed_one = pair_scatter(grad_one)
    input_grad = (
        mine(grad_middle)
        + normalize_back(mine(normal_one), mine(scale_one), gain_one, grad_normed_one)
    ).astype(BF)
    gain_one_part = jnp.sum(grad_normed_one * mine(normal_one), axis=0)
    gain_one_grad, gain_two_grad = everywhere(jnp.stack([gain_one_part, gain_two_part]))

    def split(grad, size):
        return [grad[..., k * size : (k + 1) * size].astype(BF) for k in range(chips)]

    value_sum, mixgate_sum, mixout_sum = scatter(
        split(jnp.stack([value_grad, mixgate_grad, mixout_grad]), block_c)
    )
    condition_sum = scatter(split(condition_grad[None], block_g))[0]
    base_sum, shift_sum = scatter(
        split(jnp.swapaxes(jnp.stack([base_grad, shift_grad]), 1, 2), block_g)
    )
    return (
        output, input_grad, gain_one_grad, gain_two_grad, value_sum, mixgate_sum, condition_sum,
        base_sum.T, shift_sum.T, mixout_sum.T, gate_sum, up_sum, down_sum.T,
    )


def hold(count):
    return [pl.BlockSpec(memory_space=pltpu.VMEM)] * count


def shaped(*shape, dtype=BF):
    return jax.ShapeDtypeStruct(shape, dtype)


def kernel_call(body, name, outs, scratch, args, flops, transcendentals=0, scalars=0, limit=56):
    bytes_accessed = sum(a.size * a.dtype.itemsize for a in args)
    bytes_accessed += sum(o.size * o.dtype.itemsize for o in outs)
    smem = [pl.BlockSpec(memory_space=pltpu.SMEM)] * scalars
    return pl.pallas_call(
        body,
        out_shape=tuple(outs),
        in_specs=smem + hold(len(args) - scalars),
        out_specs=tuple(hold(len(outs))),
        scratch_shapes=scratch,
        compiler_params=pltpu.CompilerParams(vmem_limit_bytes=limit << 20),
        cost_estimate=pl.CostEstimate(
            flops=int(flops), bytes_accessed=int(bytes_accessed), transcendentals=transcendentals
        ),
        name=name,
    )(*args)


def nn(left, right):
    return lax.dot_general(left, right, (((1,), (0,)), ((), ())), preferred_element_type=F32)


def nt(left, right):
    return lax.dot_general(left, right, (((1,), (1,)), ((), ())), preferred_element_type=F32)


def turned_over(value):
    return value.astype(F32).T


def pack_kernel(
    value_ref, mixgate_ref, condition_ref, base_ref, shift_ref, mixout_ref, gate_ref, up_ref,
    down_ref, mixer_ref, ffn_ref,
):
    depth, block_c = value_ref.shape
    block_g = condition_ref.shape[1]
    span = base_ref.shape[1] // 128
    spare = jnp.zeros((depth, 128 - block_c), F32)
    first = jnp.concatenate(
        [
            value_ref[...].astype(F32),
            condition_ref[...].astype(F32),
            jnp.zeros((depth, 128 - block_c - block_g), F32),
        ],
        axis=1,
    ).astype(BF)
    second = jnp.concatenate([mixgate_ref[...].astype(F32), spare], axis=1).astype(BF)
    third = jnp.concatenate([turned_over(mixout_ref[...]), spare], axis=1).astype(BF)
    half = mixer_ref.shape[1]
    mixer_ref[0, :depth, :] = first
    mixer_ref[0, depth:, :] = second[: half - depth]
    left = 2 * depth - half
    mixer_ref[1, :left, :] = second[half - depth :]
    mixer_ref[1, left : left + depth, :] = third
    mixer_ref[1, left + depth :, :] = jnp.zeros((half - left - depth, 128), BF)
    for n, ref in enumerate((base_ref, shift_ref)):
        piece = jnp.concatenate([ref[:, h * 128 : (h + 1) * 128] for h in range(span)], axis=0)
        start = left + depth + 16 * n
        mixer_ref[1, start : start + span * block_g, :] = piece
    part = ffn_ref.shape[2]
    down = turned_over(down_ref[...]).astype(BF)
    for h in range(2):
        cut = slice(h * part, (h + 1) * part)
        ffn_ref[h, 0] = gate_ref[cut, :]
        ffn_ref[h, 1] = up_ref[cut, :]
        ffn_ref[h, 2] = down[cut, :]


def norm_rows(value, gain):
    centred = value - jnp.mean(value, axis=-1, keepdims=True)
    scale = lax.rsqrt(jnp.mean(centred * centred, axis=-1, keepdims=True) + epsilon)
    normal = centred * scale
    return normal, scale, normal * gain


def mixer_forward_kernel(
    sizes, dp_ref, column_ref, row_ref, own_ref, other_ref, gain_ref, p0_ref, p1_ref, p2_ref,
    p3a_ref, p3b_ref, branch_ref, normed_ref, values_ref, gates_ref, conv_ref, weights_ref,
    condition_ref, taps_ref, shift_out_ref, cond_ref, summary_ref, whole_ref, base_ref,
    mask_ref, band_ref, mixed_ref,
):
    depth, block_c, block_g, chips, span, unroll, channels, reach, half = sizes
    local, width = own_ref.shape
    rows, length = row_ref.shape[0], row_ref.shape[2]
    per = local // length
    dp = dp_ref[0]
    pieces = ((p0_ref, None), (p1_ref, None), (p2_ref, None), (p3a_ref, p3b_ref))
    left = 2 * depth - half
    side = chips * block_c

    for k in range(chips):
        for m, (first, second) in enumerate(pieces):
            low = first.at[0, k] if second is None else first.at[k]
            high = first.at[1, k] if second is None else second.at[k]
            j = dp ^ m
            at = pl.multiple_of(j * depth, depth)
            whole_ref[0, pl.ds(at, depth), :] = low[:depth, :]
            whole_ref[1, pl.ds(at, half - depth), :] = low[depth:, :]
            whole_ref[1, pl.ds(pl.multiple_of(at + half - depth, 64), left), :] = high[:left, :]
            whole_ref[2, pl.ds(at, depth), :] = high[left : left + depth, :]
            for n, ref in enumerate((base_ref, shift_out_ref)):
                start = left + depth + 16 * n
                piece = high[start : start + 16, :].astype(F32)
                for h in range(span):
                    lane = pl.multiple_of((j * span + h) * 128, 128)
                    ref[k * block_g : (k + 1) * block_g, pl.ds(lane, 128)] = piece[
                        h * block_g : (h + 1) * block_g
                    ]
        for s in range(3):
            turned = turned_over(whole_ref[s])
            weights_ref[s * side + k * block_c : s * side + (k + 1) * block_c, :] = turned[
                :block_c
            ].astype(BF)
            if s == 0:
                condition_ref[k * block_g : (k + 1) * block_g, :] = turned[
                    block_c : block_c + block_g
                ]

    for h, ref in enumerate((own_ref, other_ref)):
        for q in range(per):
            r = h * per + q
            _, _, normed = norm_rows(
                ref[q * length : (q + 1) * length, :].astype(F32), gain_ref[...]
            )
            normed = normed.astype(BF)
            normed_ref[r * length : (r + 1) * length, :] = normed
            summary = jnp.mean(normed.astype(F32), axis=0, keepdims=True)
            summary_ref[r : r + 1, :] = summary
            cond = jnp.tanh(jnp.sum(condition_ref[...] * summary, axis=1, keepdims=True))
            cond_ref[r] = jnp.broadcast_to(cond, cond_ref.shape[1:])
            taps_ref[r] = base_ref[...] + cond * shift_out_ref[...]
            lanes = slice(r * length, (r + 1) * length)
            values_ref[:, lanes] = nt(weights_ref[:side, :], normed).astype(BF)
            gates_ref[:, lanes] = nt(weights_ref[side : 2 * side, :], normed).astype(BF)

    band_ref[...] = jnp.zeros_like(band_ref)
    filters = chips * block_g
    for r in range(rows):
        lanes = slice(r * length, (r + 1) * length)
        mask_ref[...] = (column_ref[lanes, :] == row_ref[r]).astype(BF)

        def some(step, carry, r=r, lanes=lanes):
            for u in range(unroll):
                f = step * unroll + u
                build_band(taps_ref[r, pl.ds(f, 1), :], mask_ref, band_ref.at[u], length, reach)
                at = pl.ds(pl.multiple_of(f * channels, channels), channels)
                conv = nn(values_ref[at, lanes], band_ref[u])
                conv_ref[at, lanes] = conv.astype(BF)
                mixed_ref[at, :] = conv * gates_ref[at, lanes].astype(F32)
            return carry

        lax.fori_loop(0, filters // unroll, some, 0)
        branch_ref[lanes, :] = nn(mixed_ref[...].T.astype(BF), weights_ref[2 * side :, :]).astype(BF)


def norm_two_kernel(
    own_ref, other_ref, branch_ref, got_ref, grad_own_ref, grad_other_ref, gain_ref, normed_ref,
    normed_turned_ref, grad_turned_ref,
):
    local = own_ref.shape[0]
    for h, (ref, grad_ref) in enumerate(((own_ref, grad_own_ref), (other_ref, grad_other_ref))):
        here, there = slice(h * local, (h + 1) * local), slice((1 - h) * local, (2 - h) * local)
        middle = (
            ref[...].astype(F32) + branch_ref[here, :].astype(F32) + got_ref[there, :].astype(F32)
        )
        _, _, normed = norm_rows(middle, gain_ref[...])
        normed = normed.astype(BF)
        normed_ref[here, :] = normed
        normed_turned_ref[:, here] = turned_over(normed).astype(BF)
        grad_turned_ref[:, here] = turned_over(grad_ref[...]).astype(BF)


def ffn_kernel(
    first, dp_ref, normed_ref, normed_turned_ref, grad_own_ref, grad_other_ref, grad_turned_ref,
    p0_ref, p1_ref, p2_ref, p3a_ref, p3b_ref, *refs,
):
    if first:
        before = (None, None, None)
    else:
        before, refs = refs[:3], refs[3:]
    feed_own_ref, feed_other_ref, back_ref, g0_ref, g1a_ref, g1b_ref, g2a_ref, g2b_ref = refs[:8]
    g3a_ref, g3b_ref, weight_ref, hidden_ref, gate_ref, up_ref, grads_ref = refs[8:15]
    feed_sum_ref, back_sum_ref = refs[15:]
    total = normed_ref.shape[0]
    local = grad_own_ref.shape[0]
    count, _, part, _ = g1a_ref.shape
    dp = dp_ref[0]
    step = min(256, local)
    pieces = ((p0_ref, None), (p1_ref, None), (p2_ref, None), (p3a_ref, p3b_ref))
    outs = ((g0_ref.at[0], g0_ref.at[1]), (g1a_ref, g1b_ref), (g2a_ref, g2b_ref), (g3a_ref, g3b_ref))
    for k in range(count):
        for m, (one, two) in enumerate(pieces):
            for h in range(2):
                source = one.at[h, k] if two is None else (one, two)[h].at[k]
                at = pl.multiple_of((dp ^ m) * (2 * part) + h * part, part)
                for s in range(3):
                    weight_ref[s, pl.ds(at, part), :] = source[s]
        for t in range(total // step):
            here = slice(t * step, (t + 1) * step)
            grad_ref = grad_own_ref if t * step < local else grad_other_ref
            there = slice(t * step % local, t * step % local + step)
            gate_pre = nn(normed_ref[here, :], weight_ref[0])
            up_pre = nn(normed_ref[here, :], weight_ref[1])
            grad_hidden = nn(grad_ref[there, :], weight_ref[2])
            sigmoid = 1.0 / (1.0 + jnp.exp(-gate_pre))
            silu = gate_pre * sigmoid
            hidden = (silu * up_pre).astype(BF)
            grad_gate = (grad_hidden * up_pre * (sigmoid + silu * (1.0 - sigmoid))).astype(BF)
            grad_up = (grad_hidden * silu).astype(BF)
            hidden_ref[here, :] = hidden
            gate_ref[here, :] = grad_gate
            up_ref[here, :] = grad_up
            feed = nt(hidden, weight_ref[2])
            back = nt(grad_gate, weight_ref[0]) + nt(grad_up, weight_ref[1])
            feed_out = feed_own_ref if t * step < local else feed_other_ref
            if k == 0 and not first:
                feed_in = before[0] if t * step < local else before[1]
                feed = feed + feed_in[there, :].astype(F32)
                back = back + before[2][here, :].astype(F32)
            if k > 0:
                feed = feed + feed_sum_ref[here, :]
                back = back + back_sum_ref[here, :]
            if k == count - 1:
                feed_out[there, :] = feed.astype(BF)
                back_ref[here, :] = back.astype(BF)
            else:
                feed_sum_ref[here, :] = feed
                back_sum_ref[here, :] = back
        grads_ref[0] = nn(normed_turned_ref[...], gate_ref[...]).astype(BF)
        grads_ref[1] = nn(normed_turned_ref[...], up_ref[...]).astype(BF)
        grads_ref[2] = nn(grad_turned_ref[...], hidden_ref[...]).astype(BF)
        for m, pair in enumerate(outs):
            for h in range(2):
                at = pl.multiple_of((dp ^ m) * (2 * part) + h * part, part)
                for s in range(3):
                    pair[h][k, s] = grads_ref[s, pl.ds(at, part), :]


def mixout_back_kernel(
    own_ref, other_ref, branch_ref, got_ref, back_ref, back_got_ref, grad_own_ref, grad_other_ref,
    gain_ref, weights_ref, gates_ref, conv_ref, middle_ref, mixout_ref, grad_conv_ref,
    grad_gates_ref, gain_grad_ref, rounded_ref,
):
    local = own_ref.shape[0]
    side = weights_ref.shape[0]
    for h, (ref, grad_ref) in enumerate(((own_ref, grad_own_ref), (other_ref, grad_other_ref))):
        here, there = slice(h * local, (h + 1) * local), slice((1 - h) * local, (2 - h) * local)
        middle = (
            ref[...].astype(F32) + branch_ref[here, :].astype(F32) + got_ref[there, :].astype(F32)
        )
        normal, scale, _ = norm_rows(middle, gain_ref[...])
        grad = back_ref[here, :].astype(F32) + back_got_ref[there, :].astype(F32)
        grad_middle = grad_ref[...].astype(F32) + normalize_back(
            normal, scale, gain_ref[...], grad
        )
        if h == 0:
            gain_grad_ref[...] = jnp.sum(grad * normal, axis=0, keepdims=True)
            middle_ref[...] = grad_middle
        rounded = grad_middle.astype(BF)
        rounded_ref[here, :] = rounded
        grad_mixed = nt(weights_ref[...], rounded)
        gates, conv = gates_ref[:, here].astype(F32), conv_ref[:, here].astype(F32)
        grad_conv_ref[:, here] = (grad_mixed * gates).astype(BF)
        grad_gates_ref[:, here] = (grad_mixed * conv).astype(BF)
    mixed = (gates_ref[...].astype(F32) * conv_ref[...].astype(F32)).astype(BF)
    mixout_ref[...] = nn(mixed, rounded_ref[...]).astype(BF)


def conv_back_kernel(
    unroll, channels, reach, column_ref, turned_ref, row_ref, taps_ref, values_ref, grad_ref,
    grad_values_ref, grad_taps_ref, mask_ref, mask_turned_ref, band_ref, grad_turned_ref,
):
    length = row_ref.shape[1]
    filters = taps_ref.shape[0]
    blocks = length // BLOCK
    mask_ref[...] = (column_ref[...] == row_ref[...]).astype(BF)
    mask_turned_ref[...] = (turned_ref[...] == row_ref[...]).astype(F32)
    band_ref[...] = jnp.zeros_like(band_ref)
    turn = (
        lax.broadcasted_iota(jnp.int32, (length, length), 0)
        + lax.broadcasted_iota(jnp.int32, (length, length), 1)
        == length - 1
    ).astype(BF)
    grad_turned_ref[...] = nn(grad_ref[...], turn)

    def some(step, carry):
        for u in range(unroll):
            f = step * unroll + u
            build_band(taps_ref[pl.ds(f, 1), :], mask_ref, band_ref.at[u], length, reach)
            rows = pl.ds(pl.multiple_of(f * channels, channels), channels)
            grad_values_ref[rows, :] = nt(grad_ref[rows, :], band_ref[u]).astype(BF)
            turned = grad_turned_ref[rows, :].T.astype(BF)
            product = nn(turned, values_ref[rows, :])
            parts = [jnp.zeros((BLOCK, BLOCK), F32)] + [None] * (2 * reach + 1)
            for i in range(blocks):
                back = blocks - 1 - i
                for j in range(max(0, back - reach), min(blocks, back + reach + 1)):
                    here = (
                        slice(i * BLOCK, (i + 1) * BLOCK),
                        slice(j * BLOCK, (j + 1) * BLOCK),
                    )
                    block = product[here] * mask_turned_ref[here]
                    d = j - back + reach + 1
                    parts[d] = block if parts[d] is None else parts[d] + block
            aligned = pltpu.roll(jnp.concatenate(parts, axis=1), 0, 1, stride=1, stride_axis=0)
            grad_taps_ref[pl.ds(f, 1), :] = jnp.sum(aligned, axis=0, keepdims=True)
        return carry

    lax.fori_loop(0, filters // unroll, some, 0)


def mixer_back_kernel(
    sizes, rows, dp_ref, normed_ref, gates_ref, mixout_ref, weights_ref, condition_ref, shift_ref,
    cond_ref, summary_ref, *refs,
):
    depth, block_c, block_g, chips, span, unroll, channels, reach, half = sizes
    values_refs, taps_refs, refs = refs[:rows], refs[rows : 2 * rows], refs[2 * rows :]
    back_ref, g0_ref, g1a_ref, g1b_ref, g2a_ref, g2b_ref, g3a_ref, g3b_ref = refs[:8]
    whole_ref, filter_ref = refs[8:]
    length = values_refs[0].shape[1]
    side = chips * block_c
    filters = chips * block_g
    width = taps_refs[0].shape[1]
    taps = shift_ref.shape[1]
    left = 2 * depth - half
    dp = dp_ref[0]
    lane = lax.broadcasted_iota(jnp.int32, (width, taps), 0)
    tap = lax.broadcasted_iota(jnp.int32, (width, taps), 1)
    reachable = (tap > taps // 2 - (reach + 1) * BLOCK) & (tap < taps // 2 + (reach + 1) * BLOCK)
    spot = taps - 1 - tap
    spot = jnp.where(spot >= width, spot - width, spot)
    place = ((lane == spot) & reachable).astype(BF)
    shift_there = nt(shift_ref[...].astype(BF), place)
    base_grad = shift_grad = condition_grad = None
    value_grad = gate_grad = None
    for r in range(rows):
        lanes = slice(r * length, (r + 1) * length)
        grad_taps = taps_refs[r][...]
        cond = cond_ref[r, :, :1]
        summary = summary_ref[r : r + 1, :]
        grad_cond = jnp.sum(grad_taps * shift_there, axis=1, keepdims=True) * (1.0 - cond * cond)
        grad_summary = jnp.sum(grad_cond * condition_ref[...], axis=0, keepdims=True) / length
        one, two, three = grad_taps, cond * grad_taps, grad_cond * summary
        values, gates = values_refs[r][...], gates_ref[:, lanes]
        normed = normed_ref[lanes, :]
        four, five = nn(values, normed), nn(gates, normed)
        if r == 0:
            base_grad, shift_grad, condition_grad = one, two, three
            value_grad, gate_grad = four, five
        else:
            base_grad, shift_grad = base_grad + one, shift_grad + two
            condition_grad = condition_grad + three
            value_grad, gate_grad = value_grad + four, gate_grad + five
        back = nn(turned_over(values).astype(BF), weights_ref[:side, :])
        back = back + nn(turned_over(gates).astype(BF), weights_ref[side : 2 * side, :])
        back_ref[lanes, :] = (back + grad_summary).astype(BF)
    filter_ref[0] = nn(base_grad.astype(BF), place)
    filter_ref[1] = nn(shift_grad.astype(BF), place)
    outs = ((g0_ref.at[0], g0_ref.at[1]), (g1a_ref, g1b_ref), (g2a_ref, g2b_ref), (g3a_ref, g3b_ref))
    spare = jnp.zeros((128 - block_c, value_grad.shape[1]), F32)
    for k in range(chips):
        cut = slice(k * block_c, (k + 1) * block_c)
        own = slice(k * block_g, (k + 1) * block_g)
        first = jnp.concatenate(
            [value_grad[cut], condition_grad[own], spare[: 128 - block_c - block_g]], axis=0
        )
        whole_ref[0] = first.T.astype(BF)
        whole_ref[1] = jnp.concatenate([gate_grad[cut], spare], axis=0).T.astype(BF)
        whole_ref[2] = jnp.concatenate([mixout_ref[cut, :].astype(F32), spare], axis=0).T.astype(BF)
        for m, (low, high) in enumerate(outs):
            j = dp ^ m
            at = pl.multiple_of(j * depth, depth)
            low[k, :depth, :] = whole_ref[0, pl.ds(at, depth), :]
            low[k, depth:, :] = whole_ref[1, pl.ds(at, half - depth), :]
            high[k, :left, :] = whole_ref[1, pl.ds(pl.multiple_of(at + half - depth, 64), left), :]
            high[k, left : left + depth, :] = whole_ref[2, pl.ds(at, depth), :]
            for n in range(2):
                start = left + depth + 16 * n
                parts = [
                    filter_ref[n, own, pl.ds(pl.multiple_of((j * span + h) * 128, 128), 128)]
                    for h in range(span)
                ] + [jnp.zeros((16 - span * block_g, 128), F32)]
                high[k, start : start + 16, :] = jnp.concatenate(parts, axis=0).astype(BF)
            end = left + depth + 32
            high[k, end:, :] = jnp.zeros((half - end, 128), BF)


def norm_one_back_kernel(
    own_ref, back_ref, got_ref, middle_ref, gain_ref, grad_ref, gain_grad_ref
):
    local = own_ref.shape[0]
    normal, scale, _ = norm_rows(own_ref[...].astype(F32), gain_ref[...])
    grad = back_ref[:local, :].astype(F32) + got_ref[...].astype(F32)
    grad_ref[...] = (
        middle_ref[...] + normalize_back(normal, scale, gain_ref[...], grad)
    ).astype(BF)
    gain_grad_ref[...] = jnp.sum(grad * normal, axis=0, keepdims=True)


def square_gather(column):
    along_x, along_y = swap(column, "dp", 1), swap(column, "dp", 2)
    return column, along_x, along_y, swap(along_x[0], "dp", 2), swap(along_y[1], "dp", 1)


def add(left, right):
    return (left.astype(F32) + right.astype(F32)).astype(BF)


def square_scatter(g0, g1a, g1b, g2a, g2b, g3a, g3b):
    e1, e2 = swap(g3a, "dp", 2), swap(g3b, "dp", 1)
    f1b, f2a = swap(g1b, "dp", 1), swap(g2a, "dp", 2)
    f1a, f2b = swap(add(g1a, e1), "dp", 1), swap(add(g2b, e2), "dp", 2)

    def three(one, two, other):
        return (one.astype(F32) + two.astype(F32) + other.astype(F32)).astype(BF)

    return jnp.stack([three(g0[0], f1a, f2a), three(g0[1], f1b, f2b)])


def fast_body(
    tokens, segment_ids, gain_one, gain_two, value_weight, mixgate_weight, condition_weight,
    filter_base, filter_shift, mixout_weight, gate_weight, up_weight, down_weight, output_grad,
):
    dp, mp = lax.axis_index("dp"), lax.axis_index("mp")
    chips = lax.axis_size("mp") // 2
    local, width = tokens.shape
    length = segment_ids.shape[1]
    per = local // length
    rows, total = 2 * per, 2 * local
    depth, block_c = value_weight.shape
    block_g, taps = filter_base.shape
    block_f = gate_weight.shape[1]
    channels = block_c // block_g
    reach = SENTENCE // BLOCK
    side, filters = chips * block_c, chips * block_g
    half = 5 * depth // 3
    part = depth // 2
    sizes = (depth, block_c, block_g, chips, taps // 128, 4, channels, reach, half)
    dp_one = dp[None].astype(jnp.int32)
    gain_first, gain_second = gain_one[None, :], gain_two[None, :]

    mixer_pack, ffn_pack = kernel_call(
        pack_kernel, "pack_weights",
        [shaped(2, half, 128), shaped(2, 3, part, block_f)], [],
        (
            value_weight, mixgate_weight, condition_weight, filter_base, filter_shift,
            mixout_weight, gate_weight, up_weight, down_weight,
        ),
        1e6,
    )
    other = swap(tokens, "mp", 1)
    other_grad = swap(output_grad, "mp", 1)
    seg_rows = jnp.concatenate(
        [
            lax.dynamic_slice_in_dim(segment_ids, mp * per, per),
            lax.dynamic_slice_in_dim(segment_ids, (mp ^ 1) * per, per),
        ]
    )
    seg_column = seg_rows.reshape(total, 1)
    seg_turned = seg_rows[:, ::-1].reshape(total, 1)

    mixer_line = [mixer_pack] + [swap(mixer_pack, "mp", 2 * k) for k in range(1, chips)]
    mixer_column = jnp.stack(mixer_line, axis=1)
    ffn_first = square_gather(ffn_pack[:, None])
    mixer = square_gather(mixer_column)
    ffn_pack, mixer_column = lax.optimization_barrier((ffn_pack, mixer_column))
    ffn_line = [swap(ffn_pack, "mp", 2 * k) for k in range(1, chips)]
    columns = [ffn_line[0][:, None], jnp.stack(ffn_line[1:], axis=1)]
    columns[0], d1, d2 = lax.optimization_barrier((columns[0], mixer[3], mixer[4]))
    mixer = mixer[:3] + (d1, d2)
    ffn_second = square_gather(columns[0])
    columns[1], d1, d2 = lax.optimization_barrier((columns[1], ffn_second[3], ffn_second[4]))
    ffn_second = ffn_second[:3] + (d1, d2)
    ffn_third = square_gather(columns[1])

    (
        branch, normed_one, values, gates, conv, weights, condition, row_taps, shift, cond, summary,
    ) = kernel_call(
        functools.partial(mixer_forward_kernel, sizes), "mixer_forward",
        [
            shaped(total, width), shaped(total, width), shaped(side, total), shaped(side, total),
            shaped(side, total), shaped(3 * side, width), shaped(filters, width, dtype=F32),
            shaped(rows, filters, 2 * length, dtype=F32), shaped(filters, 2 * length, dtype=F32),
            shaped(rows, filters, 128, dtype=F32), shaped(rows, width, dtype=F32),
        ],
        [
            pltpu.VMEM((3, width, 128), BF), pltpu.VMEM((filters, 2 * length), F32),
            pltpu.VMEM((length, length), BF), pltpu.VMEM((sizes[5], length, length), BF),
            pltpu.VMEM((side, length), F32),
        ],
        (dp_one, seg_column, seg_rows[:, None, :], tokens, other, gain_first) + mixer,
        14e9, scalars=1,
    )
    branch_got = swap(branch, "mp", 1)
    normed_two, normed_turned, grad_turned = kernel_call(
        norm_two_kernel, "norm_two",
        [shaped(total, width), shaped(width, total), shaped(width, total)], [],
        (tokens, other, branch, branch_got, output_grad, other_grad, gain_second),
        1e9,
    )

    carried = ()
    ffn_grads = []
    for index, group in enumerate((ffn_first, ffn_second, ffn_third)):
        count = group[0].shape[1]
        quarter = shaped(count, 3, part, block_f)
        results = kernel_call(
            functools.partial(ffn_kernel, index == 0), "ffn",
            [shaped(local, width), shaped(local, width), shaped(total, width)]
            + [shaped(2, count, 3, part, block_f)] + [quarter] * 6,
            [
                pltpu.VMEM((3, width, block_f), BF), pltpu.VMEM((total, block_f), BF),
                pltpu.VMEM((total, block_f), BF), pltpu.VMEM((total, block_f), BF),
                pltpu.VMEM((3, width, block_f), BF),
                pltpu.VMEM((total, width) if count > 1 else (8, 128), F32),
                pltpu.VMEM((total, width) if count > 1 else (8, 128), F32),
            ],
            (dp_one, normed_two, normed_turned, output_grad, other_grad, grad_turned)
            + group + carried,
            18 * total * width * block_f * count, scalars=1,
        )
        carried = tuple(results[:3])
        ffn_grads.append(results[3:])
    feed, feed_other, back = carried

    ffn_sums = [square_scatter(*g) for g in ffn_grads]
    by_chip = [ffn_sums[0][:, 0], ffn_sums[1][:, 0], ffn_sums[2][:, 0], ffn_sums[2][:, 1]]
    ffn_sum = by_chip[0].astype(F32)
    for k in range(1, chips):
        ffn_sum = ffn_sum + swap(by_chip[k], "mp", 2 * k).astype(F32)
    gate_sum, up_sum, down_sum = jnp.concatenate([ffn_sum[0], ffn_sum[1]], axis=1)

    back_got = swap(back, "mp", 1)
    feed_got = swap(feed_other, "mp", 1)
    output = (
        tokens.astype(F32) + branch[:local].astype(F32) + branch_got[local:].astype(F32)
        + feed.astype(F32) + feed_got.astype(F32)
    ).astype(BF)
    grad_middle, mixout_grad, grad_conv, grad_gates, gain_two_part = kernel_call(
        mixout_back_kernel, "mixout_back",
        [
            shaped(local, width, dtype=F32), shaped(side, width), shaped(side, total),
            shaped(side, total), shaped(1, width, dtype=F32),
        ],
        [pltpu.VMEM((total, width), BF)],
        (
            tokens, other, branch, branch_got, back, back_got, output_grad, other_grad, gain_second,
            weights[2 * side :], gates, conv,
        ),
        4 * total * width * side,
    )
    backs = []
    for r in range(rows):
        lanes = slice(r * length, (r + 1) * length)
        backs.append(
            kernel_call(
                functools.partial(conv_back_kernel, 4, channels, reach), "conv_back",
                [shaped(side, length), shaped(filters, (2 * reach + 2) * BLOCK, dtype=F32)],
                [
                    pltpu.VMEM((length, length), BF), pltpu.VMEM((length, length), F32),
                    pltpu.VMEM((4, length, length), BF), pltpu.VMEM((side, length), F32),
                ],
                (
                    seg_column[lanes], seg_turned[lanes], seg_rows[r : r + 1], row_taps[r],
                    values[:, lanes], grad_conv[:, lanes],
                ),
                8e9,
            )
        )
    eighth = shaped(chips, half, 128)
    results = kernel_call(
        functools.partial(mixer_back_kernel, sizes, rows), "mixer_back",
        [shaped(total, width), shaped(2, chips, half, 128)] + [eighth] * 6,
        [pltpu.VMEM((3, width, 128), BF), pltpu.VMEM((2, filters, 2 * length), F32)],
        (
            dp_one, normed_one, grad_gates, mixout_grad, weights, condition, shift, cond, summary,
        ) + tuple(b[0] for b in backs) + tuple(b[1] for b in backs),
        8 * total * width * side, scalars=1,
    )
    grad_one, mixer_grads = results[0], results[1:]
    mixer_part = square_scatter(*mixer_grads)
    mixer_sum = mixer_part[:, 0].astype(F32)
    for k in range(1, chips):
        mixer_sum = mixer_sum + swap(mixer_part[:, k], "mp", 2 * k).astype(F32)
    mixer_sum = mixer_sum.reshape(2 * half, 128)

    got_one = swap(grad_one[local:], "mp", 1)
    input_grad, gain_one_part = kernel_call(
        norm_one_back_kernel, "norm_one_back",
        [shaped(local, width), shaped(1, width, dtype=F32)], [],
        (tokens, grad_one, got_one, grad_middle, gain_first),
        1e9,
    )
    gain_one_grad, gain_two_grad = everywhere(
        jnp.concatenate([gain_one_part, gain_two_part])
    )
    span = taps // 128

    def filter_out(start):
        piece = mixer_sum[start : start + span * block_g].reshape(span, block_g, 128)
        return jnp.swapaxes(piece, 0, 1).reshape(block_g, taps)

    return (
        output, input_grad, gain_one_grad, gain_two_grad,
        mixer_sum[:depth, :block_c],
        mixer_sum[depth : 2 * depth, :block_c],
        mixer_sum[:depth, block_c : block_c + block_g],
        filter_out(3 * depth), filter_out(3 * depth + 16),
        mixer_sum[2 * depth : 3 * depth, :block_c].T,
        gate_sum, up_sum, down_sum.T,
    )


def choose(tokens, segment_ids, gain_one, gain_two, value_weight, mixgate_weight, condition_weight,
           filter_base, filter_shift, mixout_weight, gate_weight, up_weight, down_weight,
           output_grad):
    depth, block_c = value_weight.shape
    block_g, taps = filter_base.shape
    fits = (
        lax.axis_size("dp") == 4
        and lax.axis_size("mp") == 8
        and tokens.shape[0] % segment_ids.shape[1] == 0
        and depth == 192
        and block_c % 16 == 0
        and block_c + block_g <= 128
        and taps % 128 == 0
        and taps // 128 * block_g <= 16
        and gate_weight.shape[1] % 128 == 0
    )
    return (fast_body if fits else body)(
        tokens, segment_ids, gain_one, gain_two, value_weight, mixgate_weight, condition_weight,
        filter_base, filter_shift, mixout_weight, gate_weight, up_weight, down_weight, output_grad,
    )


def solution(mesh):
    sides = P(("dp", "mp"), None)
    columns, rows = P("dp", "mp"), P("mp", "dp")
    in_specs = (
        sides, P("dp", None), P(), P(), columns, columns, columns, rows, rows, rows, columns,
        columns, rows, sides,
    )
    out_specs = (
        sides, sides, P(), P(), columns, columns, columns, rows, rows, rows, columns, columns, rows,
    )
    return jax.shard_map(choose, mesh=mesh, in_specs=in_specs, out_specs=out_specs, check_vma=False)
```

```python
import functools

import jax
import jax.numpy as jnp
from jax import lax
from jax.experimental import pallas as pl
from jax.experimental.pallas import tpu as pltpu
from jax.sharding import PartitionSpec as P

epsilon = 1e-05
highest = lax.Precision.HIGHEST
BF = jnp.bfloat16
F32 = jnp.float32
BLOCK = 128
SENTENCE = 256


def build_band(taps_row, mask_ref, band_ref, length, reach):
    blocks = length // BLOCK
    low = length - (reach + 1) * BLOCK
    width = (2 * reach + 2) * BLOCK
    spread = jnp.broadcast_to(taps_row[:, low : low + width], (BLOCK, width))
    shifted = pltpu.roll(spread, 0, 1, stride=1, stride_axis=0).astype(BF)
    for i in range(blocks):
        first, last = max(0, i - reach), min(blocks, i + reach + 1)
        rows = slice(i * BLOCK, (i + 1) * BLOCK)
        columns = slice(first * BLOCK, last * BLOCK)
        offset = (first - i + reach + 1) * BLOCK
        band_ref[rows, columns] = (
            shifted[:, offset : offset + (last - first) * BLOCK] * mask_ref[rows, columns]
        )


def conv_forward_kernel(
    unroll, channels, reach, column_ref, row_ref, cond_ref, base_ref, shift_ref, values_ref,
    conv_ref, mask_ref, taps_ref, band_ref,
):
    length = row_ref.shape[1]
    filters = base_ref.shape[0]
    mask_ref[...] = (column_ref[...] == row_ref[...]).astype(BF)
    taps_ref[...] = base_ref[...].astype(F32) + cond_ref[...] * shift_ref[...].astype(F32)
    band_ref[...] = jnp.zeros_like(band_ref)

    def some(step, carry):
        for u in range(unroll):
            f = step * unroll + u
            build_band(taps_ref[pl.ds(f, 1), :], mask_ref, band_ref.at[u], length, reach)
            rows = pl.ds(pl.multiple_of(f * channels, channels), channels)
            conv_ref[rows, :] = jnp.dot(
                values_ref[rows, :], band_ref[u], preferred_element_type=F32
            )
        return carry

    lax.fori_loop(0, filters // unroll, some, 0)


def conv_forward(segments, cond, base, shift, values, unroll=8):
    filters, length = base.shape[0], segments.shape[0]
    channels = values.shape[0] // filters
    unroll = next(u for u in range(unroll, 0, -1) if filters % u == 0)
    vmem = pl.BlockSpec(memory_space=pltpu.VMEM)
    flops = 2 * values.shape[0] * length * length
    return pl.pallas_call(
        functools.partial(conv_forward_kernel, unroll, channels, SENTENCE // BLOCK),
        out_shape=jax.ShapeDtypeStruct(values.shape, F32),
        in_specs=[vmem] * 6,
        out_specs=vmem,
        scratch_shapes=[
            pltpu.VMEM((length, length), BF),
            pltpu.VMEM(base.shape, F32),
            pltpu.VMEM((unroll, length, length), BF),
        ],
        compiler_params=pltpu.CompilerParams(vmem_limit_bytes=40 << 20),
        cost_estimate=pl.CostEstimate(
            flops=flops * 16, bytes_accessed=values.size * 6, transcendentals=0
        ),
        name="conv_forward",
    )(segments[:, None], segments[None, :], cond[:, None], base, shift, values)


def conv_backward_kernel(
    unroll, channels, reach, column_ref, turned_ref, row_ref, cond_ref, base_ref, shift_ref,
    values_ref, grad_ref, grad_values_ref, grad_taps_ref, mask_ref, mask_turned_ref, taps_ref,
    band_ref, grad_turned_ref,
):
    length = row_ref.shape[1]
    filters = base_ref.shape[0]
    blocks = length // BLOCK
    mask_ref[...] = (column_ref[...] == row_ref[...]).astype(BF)
    mask_turned_ref[...] = (turned_ref[...] == row_ref[...]).astype(F32)
    taps_ref[...] = base_ref[...].astype(F32) + cond_ref[...] * shift_ref[...].astype(F32)
    band_ref[...] = jnp.zeros_like(band_ref)
    turn = (
        lax.broadcasted_iota(jnp.int32, (length, length), 0)
        + lax.broadcasted_iota(jnp.int32, (length, length), 1)
        == length - 1
    ).astype(BF)
    grad_turned_ref[...] = jnp.dot(grad_ref[...], turn, preferred_element_type=F32)

    def some(step, carry):
        for u in range(unroll):
            f = step * unroll + u
            build_band(taps_ref[pl.ds(f, 1), :], mask_ref, band_ref.at[u], length, reach)
            rows = pl.ds(pl.multiple_of(f * channels, channels), channels)
            grad_values_ref[rows, :] = jnp.dot(
                grad_ref[rows, :], band_ref[u], preferred_element_type=F32
            ).astype(BF)
            turned = grad_turned_ref[rows, :].T.astype(BF)
            product = jnp.dot(turned, values_ref[rows, :], preferred_element_type=F32)
            parts = [jnp.zeros((BLOCK, BLOCK), F32)] + [None] * (2 * reach + 1)
            for i in range(blocks):
                back = blocks - 1 - i
                for j in range(max(0, back - reach), min(blocks, back + reach + 1)):
                    here = (
                        slice(i * BLOCK, (i + 1) * BLOCK),
                        slice(j * BLOCK, (j + 1) * BLOCK),
                    )
                    block = product[here] * mask_turned_ref[here]
                    d = j - back + reach + 1
                    parts[d] = block if parts[d] is None else parts[d] + block
            aligned = pltpu.roll(jnp.concatenate(parts, axis=1), 0, 1, stride=1, stride_axis=0)
            grad_taps_ref[pl.ds(f, 1), :] = jnp.sum(aligned, axis=0, keepdims=True)
        return carry

    lax.fori_loop(0, filters // unroll, some, 0)


def conv_backward(segments, cond, base_turned, shift_turned, values, grad, unroll=4):
    filters, length = base_turned.shape[0], segments.shape[0]
    channels = values.shape[0] // filters
    reach = SENTENCE // BLOCK
    width = (2 * reach + 2) * BLOCK
    unroll = next(u for u in range(unroll, 0, -1) if filters % u == 0)
    vmem = pl.BlockSpec(memory_space=pltpu.VMEM)
    flops = 2 * values.shape[0] * length * length
    grad_values, grad_taps = pl.pallas_call(
        functools.partial(conv_backward_kernel, unroll, channels, reach),
        out_shape=(
            jax.ShapeDtypeStruct(values.shape, BF),
            jax.ShapeDtypeStruct((filters, width), F32),
        ),
        in_specs=[vmem] * 8,
        out_specs=(vmem, vmem),
        scratch_shapes=[
            pltpu.VMEM((length, length), BF),
            pltpu.VMEM((length, length), F32),
            pltpu.VMEM(base_turned.shape, F32),
            pltpu.VMEM((unroll, length, length), BF),
            pltpu.VMEM(values.shape, F32),
        ],
        compiler_params=pltpu.CompilerParams(vmem_limit_bytes=48 << 20),
        cost_estimate=pl.CostEstimate(
            flops=flops * 32, bytes_accessed=values.size * 6, transcendentals=0
        ),
        name="conv_backward",
    )(
        segments[:, None],
        segments[::-1][:, None],
        segments[None, :],
        cond[:, None],
        base_turned,
        shift_turned,
        values,
        grad,
    )
    lags = jnp.roll(grad_taps, -(BLOCK - 1), axis=1)[:, ::-1]
    start = length + (reach + 1) * BLOCK - (width - 1)
    full = jnp.pad(lags, ((0, 0), (start, 2 * length - start - width + 1)))
    return grad_values, full[:, : 2 * length]


def swap(value, axis, mask):
    return lax.ppermute(value, axis, [(i, i ^ mask) for i in range(lax.axis_size(axis))])


def bits_of(count):
    return [1 << b for b in range(count.bit_length() - 1)]


def gather_dp(block):
    bits = bits_of(lax.axis_size("dp"))
    half = block.shape[1] // 2
    found = []
    for part, order in ((block[:, :half], bits), (block[:, half:], bits[::-1])):
        held, masks = part[None], [0]
        for bit in order:
            held = jnp.concatenate([held, swap(held, "dp", bit)], axis=0)
            masks = masks + [m | bit for m in masks]
        found.append({m: held[i] for i, m in enumerate(masks)})
    return [jnp.concatenate([f[m] for f in found], axis=1) for m in range(lax.axis_size("dp"))]


def natural(pieces, me):
    held = jnp.stack(pieces)
    return jnp.concatenate(
        [lax.dynamic_index_in_dim(held, j ^ me, 0, keepdims=False) for j in range(len(pieces))],
        axis=1,
    )


def scatter_dp(pieces):
    bits = bits_of(lax.axis_size("dp"))
    half = pieces[0].shape[1] // 2
    done = []
    for part, order in ((slice(None, half), bits[::-1]), (slice(half, None), bits)):
        held = {m: p[:, part] for m, p in enumerate(pieces)}
        for bit in order:
            stay = [m for m in held if not m & bit]
            got = swap(jnp.stack([held[m | bit] for m in stay]), "dp", bit)
            held = {m: held[m] + got[i] for i, m in enumerate(stay)}
        done.append(held[0])
    return jnp.concatenate(done, axis=1)


def everywhere(value):
    for bit in bits_of(lax.axis_size("mp")):
        value = value + swap(value, "mp", bit)
    for bit in bits_of(lax.axis_size("dp")):
        value = value + swap(value, "dp", bit)
    return value


def statistics(value):
    centred = value - jnp.mean(value, axis=-1, keepdims=True)
    scale = lax.rsqrt(jnp.mean(centred * centred, axis=-1, keepdims=True) + epsilon)
    return centred * scale, scale


def normalize_back(normal, scale, gain, grad):
    scaled = grad * gain
    return scale * (
        scaled
        - jnp.mean(scaled, axis=-1, keepdims=True)
        - normal * jnp.mean(scaled * normal, axis=-1, keepdims=True)
    )


def mm(left, right, dims):
    return lax.dot_general(left, right, (dims, ((), ())), preferred_element_type=F32)


def body(
    tokens, segment_ids, gain_one, gain_two, value_weight, mixgate_weight, condition_weight,
    filter_base, filter_shift, mixout_weight, gate_weight, up_weight, down_weight, output_grad,
):
    dp_size, mp_size = lax.axis_size("dp"), lax.axis_size("mp")
    dp, mp = lax.axis_index("dp"), lax.axis_index("mp")
    core = mp & 1
    chips = mp_size // 2
    local, width = tokens.shape
    length = segment_ids.shape[1]
    whole_rows = local % length == 0
    total = 2 * local
    rows = total // length

    def pair(own, other):
        if whole_rows:
            return jnp.concatenate([own, other], axis=0)
        first = core == 0
        return jnp.concatenate([jnp.where(first, own, other), jnp.where(first, other, own)], axis=0)

    def mine(value):
        return value[:local] if whole_rows else lax.dynamic_slice_in_dim(value, core * local, local)

    def others(value):
        if whole_rows:
            return value[local:]
        return lax.dynamic_slice_in_dim(value, (1 - core) * local, local)

    def pair_sum(value):
        got = swap(value, "mp", 1)
        if whole_rows:
            got = jnp.concatenate([got[local:], got[:local]], axis=0)
        return value.astype(F32) + got.astype(F32)

    def pair_scatter(value):
        return mine(value) + swap(others(value).astype(BF), "mp", 1).astype(F32)

    block_c = value_weight.shape[1]
    block_g = condition_weight.shape[1]
    block_f = gate_weight.shape[1]
    taps = filter_base.shape[1]
    mixer_pack = jnp.stack([value_weight, mixgate_weight, mixout_weight.T])
    filter_pack = jnp.stack([filter_base.T, filter_shift.T])
    ffn_pack = jnp.stack([gate_weight, up_weight, down_weight.T])

    tokens_all = pair(tokens, swap(tokens, "mp", 1))
    grad_all = pair(output_grad, swap(output_grad, "mp", 1))
    if whole_rows:
        per = local // length
        seg_rows = jnp.concatenate(
            [
                lax.dynamic_slice_in_dim(segment_ids, mp * per, per),
                lax.dynamic_slice_in_dim(segment_ids, (mp ^ 1) * per, per),
            ]
        )
    else:
        seg_rows = lax.dynamic_slice_in_dim(segment_ids, (mp // 2) * rows, rows)

    def gather(block):
        found = [block] + [swap(block, "mp", 2 * k) for k in range(1, chips)]
        return [natural(gather_dp(b), dp) for b in found]

    mixer = jnp.concatenate(gather(mixer_pack), axis=2)
    small = jnp.concatenate(gather(jnp.pad(condition_weight, ((0, 0), (0, 0)))[None]), axis=2)[0]
    filters = jnp.concatenate(gather(filter_pack), axis=2)
    ffn = gather(ffn_pack)
    value_full, mixgate_full, mixout_full = mixer
    base, shift = jnp.swapaxes(filters, 1, 2)
    base_turned = jnp.roll(base[:, ::-1], 1, axis=1)
    shift_turned = jnp.roll(shift[:, ::-1], 1, axis=1)

    xf = tokens_all.astype(F32)
    normal_one, scale_one = statistics(xf)
    normed_one = (normal_one * gain_one).astype(BF)
    values = mm(value_full, normed_one, ((0,), (1,))).astype(BF)
    gates = mm(mixgate_full, normed_one, ((0,), (1,)))
    summary = jnp.mean(normed_one.astype(F32).reshape(rows, length, width), axis=1)
    condition = small.astype(F32)
    cond = jnp.tanh(jnp.dot(summary, condition, precision=highest))
    cuts = [slice(r * length, (r + 1) * length) for r in range(rows)]
    conv = jnp.concatenate(
        [conv_forward(seg_rows[r], cond[r], base, shift, values[:, cuts[r]]) for r in range(rows)],
        axis=1,
    )
    mixed = (conv * gates).astype(BF)
    branch = pair_sum(mm(mixed, mixout_full, ((0,), (1,))).astype(BF))
    middle = xf + branch
    normal_two, scale_two = statistics(middle)
    normed_two = (normal_two * gain_two).astype(BF)

    feed = jnp.zeros((total, width), F32)
    grad_two = jnp.zeros((total, width), F32)
    ffn_grads = []
    for k in range(chips):
        gate_full, up_full, down_full = ffn[k]
        gate_pre = mm(normed_two, gate_full, ((1,), (0,)))
        up_pre = mm(normed_two, up_full, ((1,), (0,)))
        grad_hidden = mm(grad_all, down_full, ((1,), (0,)))
        sigmoid = jax.nn.sigmoid(gate_pre)
        silu = gate_pre * sigmoid
        hidden = (silu * up_pre).astype(BF)
        grad_gate = (grad_hidden * up_pre * (sigmoid + silu * (1.0 - sigmoid))).astype(BF)
        grad_up = (grad_hidden * silu).astype(BF)
        feed = feed + mm(hidden, down_full, ((1,), (1,)))
        grad_two = (
            grad_two + mm(grad_gate, gate_full, ((1,), (1,))) + mm(grad_up, up_full, ((1,), (1,)))
        )
        ffn_grads.append(
            jnp.stack(
                [
                    mm(normed_two, grad_gate, ((0,), (0,))).astype(BF),
                    mm(normed_two, grad_up, ((0,), (0,))).astype(BF),
                    mm(grad_all, hidden, ((0,), (0,))).astype(BF),
                ]
            )
        )

    def scatter(grads):
        sums = None
        for k, grad in enumerate(grads):
            size = grad.shape[1] // dp_size
            pieces = [
                lax.dynamic_slice_in_dim(grad, (dp ^ m) * size, size, axis=1)
                for m in range(dp_size)
            ]
            part = scatter_dp(pieces)
            part = part if k == 0 else swap(part, "mp", 2 * k)
            sums = part.astype(F32) if sums is None else sums + part.astype(F32)
        return sums

    gate_sum, up_sum, down_sum = scatter(ffn_grads)
    output = (mine(middle) + pair_scatter(feed)).astype(BF)

    grad_normed_two = pair_sum(grad_two.astype(BF))
    gain_two_part = jnp.sum(mine(grad_normed_two * normal_two), axis=0)
    grad_middle = grad_all.astype(F32) + normalize_back(
        normal_two, scale_two, gain_two, grad_normed_two
    )
    grad_branch = grad_middle.astype(BF)

    mixout_grad = mm(grad_branch, mixed, ((0,), (1,)))
    grad_mixed = mm(mixout_full, grad_branch, ((0,), (1,)))
    grad_conv = (grad_mixed * gates).astype(BF)
    grad_gates = (grad_mixed * conv).astype(BF)
    backs = [
        conv_backward(
            seg_rows[r], cond[r], base_turned, shift_turned, values[:, cuts[r]],
            grad_conv[:, cuts[r]],
        )
        for r in range(rows)
    ]
    grad_values = jnp.concatenate([b[0] for b in backs], axis=1)
    grad_taps = jnp.stack([b[1] for b in backs])
    base_grad = jnp.sum(grad_taps, axis=0)
    shift_grad = jnp.sum(grad_taps * cond[:, :, None], axis=0)
    grad_cond = jnp.sum(grad_taps * shift.astype(F32)[None], axis=2) * (1.0 - cond * cond)
    condition_grad = mm(summary, grad_cond, ((0,), (0,)))
    grad_summary = jnp.dot(grad_cond, condition.T, precision=highest) / length
    value_grad = mm(normed_one, grad_values, ((0,), (1,)))
    mixgate_grad = mm(normed_one, grad_gates, ((0,), (1,)))
    grad_one = mm(grad_values, value_full, ((0,), (1,))) + mm(
        grad_gates, mixgate_full, ((0,), (1,))
    )
    grad_one = (grad_one.reshape(rows, length, width) + grad_summary[:, None, :]).reshape(
        total, width
    )
    grad_normed_one = pair_scatter(grad_one)
    input_grad = (
        mine(grad_middle)
        + normalize_back(mine(normal_one), mine(scale_one), gain_one, grad_normed_one)
    ).astype(BF)
    gain_one_part = jnp.sum(grad_normed_one * mine(normal_one), axis=0)
    gain_one_grad, gain_two_grad = everywhere(jnp.stack([gain_one_part, gain_two_part]))

    def split(grad, size):
        return [grad[..., k * size : (k + 1) * size].astype(BF) for k in range(chips)]

    value_sum, mixgate_sum, mixout_sum = scatter(
        split(jnp.stack([value_grad, mixgate_grad, mixout_grad]), block_c)
    )
    condition_sum = scatter(split(condition_grad[None], block_g))[0]
    base_sum, shift_sum = scatter(
        split(jnp.swapaxes(jnp.stack([base_grad, shift_grad]), 1, 2), block_g)
    )
    return (
        output, input_grad, gain_one_grad, gain_two_grad, value_sum, mixgate_sum, condition_sum,
        base_sum.T, shift_sum.T, mixout_sum.T, gate_sum, up_sum, down_sum.T,
    )


def hold(count):
    return [pl.BlockSpec(memory_space=pltpu.VMEM)] * count


def shaped(*shape, dtype=BF):
    return jax.ShapeDtypeStruct(shape, dtype)


def kernel_call(body, name, outs, scratch, args, flops, transcendentals=0, scalars=0, limit=56):
    bytes_accessed = sum(a.size * a.dtype.itemsize for a in args)
    bytes_accessed += sum(o.size * o.dtype.itemsize for o in outs)
    smem = [pl.BlockSpec(memory_space=pltpu.SMEM)] * scalars
    return pl.pallas_call(
        body,
        out_shape=tuple(outs),
        in_specs=smem + hold(len(args) - scalars),
        out_specs=tuple(hold(len(outs))),
        scratch_shapes=scratch,
        compiler_params=pltpu.CompilerParams(vmem_limit_bytes=limit << 20),
        cost_estimate=pl.CostEstimate(
            flops=int(flops), bytes_accessed=int(bytes_accessed), transcendentals=transcendentals
        ),
        name=name,
    )(*args)


def nn(left, right):
    return lax.dot_general(left, right, (((1,), (0,)), ((), ())), preferred_element_type=F32)


def nt(left, right):
    return lax.dot_general(left, right, (((1,), (1,)), ((), ())), preferred_element_type=F32)


def turned_over(value):
    return value.astype(F32).T


def fold(value):
    rows = value.shape[0] // 2
    return jnp.concatenate([value[:rows], value[rows:]], axis=1)


def pack_kernel(
    value_ref, mixgate_ref, condition_ref, base_ref, shift_ref, mixout_ref, gate_ref, up_ref,
    down_ref, mixer_ref, ffn_ref,
):
    depth, block_c = value_ref.shape
    block_g = condition_ref.shape[1]
    span = base_ref.shape[1] // 128
    spare = 128 - block_c
    mixgate = mixgate_ref[...].astype(F32)
    mixout = turned_over(mixout_ref[...])
    first = jnp.concatenate([value_ref[...].astype(F32), mixgate[:, :spare]], axis=1)
    second = jnp.concatenate([mixgate[:, spare:], mixout[:, : 2 * spare]], axis=1)
    empty = jnp.zeros((depth, spare - block_g), F32)
    third = jnp.concatenate(
        [mixout[:, 2 * spare :], condition_ref[...].astype(F32), empty], axis=1
    )
    half = mixer_ref.shape[1]
    cut = half - depth
    mixer_ref[0, :depth, :] = first.astype(BF)
    mixer_ref[0, depth:, :] = second[:cut].astype(BF)
    mixer_ref[1, : depth - cut, :] = second[cut:].astype(BF)
    start = depth - cut + depth // 2
    mixer_ref[1, depth - cut : start, :] = fold(third).astype(BF)
    blank = jnp.zeros((16 - span * block_g, 128), F32)
    for ref in (base_ref, shift_ref):
        pieces = [ref[:, h * 128 : (h + 1) * 128].astype(F32) for h in range(span)] + [blank]
        mixer_ref[1, start : start + 16, :] = jnp.concatenate(pieces, axis=0).astype(BF)
        start += 16
    part = ffn_ref.shape[2]
    down = turned_over(down_ref[...]).astype(BF)
    for h in range(2):
        cut = slice(h * part, (h + 1) * part)
        ffn_ref[h, 0] = gate_ref[cut, :]
        ffn_ref[h, 1] = up_ref[cut, :]
        ffn_ref[h, 2] = down[cut, :]


def norm_rows(value, gain):
    centred = value - jnp.mean(value, axis=-1, keepdims=True)
    scale = lax.rsqrt(jnp.mean(centred * centred, axis=-1, keepdims=True) + epsilon)
    normal = centred * scale
    return normal, scale, normal * gain


def mixer_forward_kernel(
    sizes, dp_ref, column_ref, row_ref, own_ref, other_ref, gain_ref, p0_ref, p1_ref, p2_ref,
    p3a_ref, p3b_ref, branch_ref, values_0, values_1, gates_0, gates_1, conv_0, conv_1,
    weights_ref, mixout_ref, condition_ref, taps_0, taps_1, shift_out_ref, cond_ref, summary_ref,
    one_ref, two_ref, three_ref, base_ref, mask_ref, band_ref, mixed_ref,
):
    depth, block_c, block_g, chips, span, unroll, channels, reach, half = sizes
    length = own_ref.shape[0]
    values_refs, gates_refs = (values_0, values_1), (gates_0, gates_1)
    conv_refs, taps_refs = (conv_0, conv_1), (taps_0, taps_1)
    dp = dp_ref[0]
    pieces = ((p0_ref, None), (p1_ref, None), (p2_ref, None), (p3a_ref, p3b_ref))
    side = chips * block_c
    spare, cut = 128 - block_c, half - depth
    filters = chips * block_g

    for k in range(chips):
        for m, (first, second) in enumerate(pieces):
            low = first.at[0, k] if second is None else first.at[k]
            high = first.at[1, k] if second is None else second.at[k]
            j = dp ^ m
            at = pl.multiple_of(j * depth, depth)
            one_ref[pl.ds(at, depth), :] = low[:depth, :]
            two_ref[pl.ds(at, cut), :] = low[depth:, :]
            two_ref[pl.ds(pl.multiple_of(at + cut, cut), depth - cut), :] = high[: depth - cut, :]
            start = depth - cut + depth // 2
            folded = high[depth - cut : start, :]
            three_ref[pl.ds(at, depth // 2), :] = folded
            three_ref[pl.ds(pl.multiple_of(at + depth // 2, depth // 2), depth // 2), :] = (
                jnp.concatenate([folded[:, 64:], folded[:, :64]], axis=1)
            )
            for ref in (base_ref, shift_out_ref):
                piece = high[start : start + 16, :].astype(F32)
                start += 16
                for h in range(span):
                    lane = pl.multiple_of((j * span + h) * 128, 128)
                    ref[k * block_g : (k + 1) * block_g, pl.ds(lane, 128)] = piece[
                        h * block_g : (h + 1) * block_g
                    ]
        here, there = k * block_c, side + k * block_c
        turned = turned_over(one_ref[...]).astype(BF)
        weights_ref[here : here + block_c, :] = turned[:block_c]
        weights_ref[there : there + spare, :] = turned[block_c:]
        turned = turned_over(two_ref[...]).astype(BF)
        weights_ref[there + spare : there + block_c, :] = turned[: block_c - spare]
        mixout_ref[here : here + 2 * spare, :] = turned[block_c - spare :]
        turned = turned_over(three_ref[...]).astype(BF)
        mixout_ref[here + 2 * spare : here + block_c, :] = turned[:spare]
        condition_ref[k * block_g : (k + 1) * block_g, :] = turned[spare : 2 * spare].astype(F32)[
            :block_g
        ]

    band_ref[...] = jnp.zeros_like(band_ref)
    for r, ref in enumerate((own_ref, other_ref)):
        _, _, normed = norm_rows(ref[...].astype(F32), gain_ref[...])
        normed = normed.astype(BF)
        summary = jnp.mean(normed.astype(F32), axis=0, keepdims=True)
        summary_ref[r : r + 1, :] = summary
        cond = jnp.tanh(jnp.sum(condition_ref[...] * summary, axis=1, keepdims=True))
        cond_ref[r] = jnp.broadcast_to(cond, cond_ref.shape[1:])
        taps_refs[r][...] = base_ref[...] + cond * shift_out_ref[...]
        values_refs[r][...] = nt(weights_ref[:side, :], normed).astype(BF)
        gates_refs[r][...] = nt(weights_ref[side:, :], normed).astype(BF)
        mask_ref[...] = (
            column_ref[r * length : (r + 1) * length, :] == row_ref[r : r + 1, :]
        ).astype(BF)

        def some(step, carry, r=r):
            for u in range(unroll):
                f = step * unroll + u
                build_band(taps_refs[r][pl.ds(f, 1), :], mask_ref, band_ref.at[u], length, reach)
                at = pl.ds(pl.multiple_of(f * channels, channels), channels)
                conv = nn(values_refs[r][at, :], band_ref[u])
                conv_refs[r][at, :] = conv.astype(BF)
                mixed_ref[at, :] = (conv * gates_refs[r][at, :].astype(F32)).astype(BF)
            return carry

        lax.fori_loop(0, filters // unroll, some, 0)
        branch_ref[r * length : (r + 1) * length, :] = nn(
            mixed_ref[...].T, mixout_ref[...]
        ).astype(BF)


def norm_two_kernel(
    own_ref, other_ref, branch_ref, got_ref, grad_own_ref, grad_other_ref, gain_ref, normed_ref,
    normed_turned_ref, grad_turned_ref,
):
    local = own_ref.shape[0]
    for h, (ref, grad_ref) in enumerate(((own_ref, grad_own_ref), (other_ref, grad_other_ref))):
        here, there = slice(h * local, (h + 1) * local), slice((1 - h) * local, (2 - h) * local)
        middle = (
            ref[...].astype(F32) + branch_ref[here, :].astype(F32) + got_ref[there, :].astype(F32)
        )
        _, _, normed = norm_rows(middle, gain_ref[...])
        normed = normed.astype(BF)
        normed_ref[here, :] = normed
        normed_turned_ref[:, here] = normed.T
        grad_turned_ref[:, here] = grad_ref[...].T


def ffn_kernel(
    first, dp_ref, normed_ref, normed_turned_ref, grad_own_ref, grad_other_ref, grad_turned_ref,
    p0_ref, p1_ref, p2_ref, p3a_ref, p3b_ref, *refs,
):
    if first:
        before = (None, None, None)
    else:
        before, refs = refs[:3], refs[3:]
    feed_own_ref, feed_other_ref, back_ref, g0a_ref, g0b_ref, g1a_ref, g2b_ref = refs[:7]
    gx_ref, gy_ref = refs[7:9]
    two_ref, down_ref, hidden_ref, act_ref, two_grad_ref, down_grad_ref = refs[9:15]
    feed_sum_ref, back_sum_ref = refs[15:]
    total = normed_ref.shape[0]
    local = grad_own_ref.shape[0]
    count, _, part, block = g0a_ref.shape
    dp = dp_ref[0]
    step = min(256, local)
    pieces = ((p0_ref, None), (p1_ref, None), (p2_ref, None), (p3a_ref, p3b_ref))
    outs = (
        (g0a_ref, g0b_ref), (g1a_ref, gx_ref.at[0]), (gy_ref.at[0], g2b_ref),
        (gy_ref.at[1], gx_ref.at[1]),
    )
    for k in range(count):
        for m, (one, two) in enumerate(pieces):
            for h in range(2):
                source = one.at[h, k] if two is None else (one, two)[h].at[k]
                at = pl.multiple_of((dp ^ m) * (2 * part) + h * part, part)
                two_ref[pl.ds(at, part), :block] = source[0]
                two_ref[pl.ds(at, part), block:] = source[1]
                down_ref[pl.ds(at, part), :] = source[2]
        for t in range(total // step):
            here = slice(t * step, (t + 1) * step)
            grad_ref = grad_own_ref if t * step < local else grad_other_ref
            there = slice(t * step % local, t * step % local + step)
            both = nn(normed_ref[here, :], two_ref[...])
            gate_pre, up_pre = both[:, :block], both[:, block:]
            grad_hidden = nn(grad_ref[there, :], down_ref[...])
            sigmoid = 1.0 / (1.0 + jnp.exp(-gate_pre))
            silu = gate_pre * sigmoid
            hidden = (silu * up_pre).astype(BF)
            hidden_ref[here, :] = hidden
            act_ref[here, :block] = (
                grad_hidden * up_pre * (sigmoid + silu * (1.0 - sigmoid))
            ).astype(BF)
            act_ref[here, block:] = (grad_hidden * silu).astype(BF)
            feed = nt(hidden, down_ref[...])
            back = nt(act_ref[here, :], two_ref[...])
            feed_out = feed_own_ref if t * step < local else feed_other_ref
            if k == 0 and not first:
                feed_in = before[0] if t * step < local else before[1]
                feed = feed + feed_in[there, :].astype(F32)
                back = back + before[2][here, :].astype(F32)
            if k > 0:
                feed = feed + feed_sum_ref[here, :]
                back = back + back_sum_ref[here, :]
            if k == count - 1:
                feed_out[there, :] = feed.astype(BF)
                back_ref[here, :] = back.astype(BF)
            else:
                feed_sum_ref[here, :] = feed
                back_sum_ref[here, :] = back
        two_grad_ref[...] = nn(normed_turned_ref[...], act_ref[...]).astype(BF)
        down_grad_ref[...] = nn(grad_turned_ref[...], hidden_ref[...]).astype(BF)
        for m, pair in enumerate(outs):
            for h in range(2):
                at = pl.multiple_of((dp ^ m) * (2 * part) + h * part, part)
                pair[h][k, 0] = two_grad_ref[pl.ds(at, part), :block]
                pair[h][k, 1] = two_grad_ref[pl.ds(at, part), block:]
                pair[h][k, 2] = down_grad_ref[pl.ds(at, part), :]


def ffn_call(first, count, *args):
    total, width = args[1].shape
    local = args[3].shape[0]
    _, _, _, part, block_f = args[6].shape
    sums = pltpu.VMEM((total, width) if count > 1 else (8, 128), F32)
    return kernel_call(
        functools.partial(ffn_kernel, first), "feed_forward",
        [shaped(local, width), shaped(local, width), shaped(total, width)]
        + [shaped(count, 3, part, block_f)] * 4 + [shaped(2, count, 3, part, block_f)] * 2,
        [
            pltpu.VMEM((width, 2 * block_f), BF), pltpu.VMEM((width, block_f), BF),
            pltpu.VMEM((total, block_f), BF), pltpu.VMEM((total, 2 * block_f), BF),
            pltpu.VMEM((width, 2 * block_f), BF), pltpu.VMEM((width, block_f), BF), sums, sums,
        ],
        args,
        18 * total * width * block_f * count, scalars=1,
    )


def mixout_back_kernel(
    own_ref, other_ref, branch_ref, got_ref, back_ref, back_got_ref, grad_own_ref, grad_other_ref,
    gain_ref, weights_ref, gates_0, gates_1, conv_0, conv_1, middle_ref, mixout_ref, grad_conv_0,
    grad_conv_1, grad_gates_0, grad_gates_1, gain_grad_ref,
):
    local = own_ref.shape[0]
    mixout = None
    for h, (ref, grad_ref, gates_ref, conv_ref, grad_conv_ref, grad_gates_ref) in enumerate(
        (
            (own_ref, grad_own_ref, gates_0, conv_0, grad_conv_0, grad_gates_0),
            (other_ref, grad_other_ref, gates_1, conv_1, grad_conv_1, grad_gates_1),
        )
    ):
        here, there = slice(h * local, (h + 1) * local), slice((1 - h) * local, (2 - h) * local)
        middle = (
            ref[...].astype(F32) + branch_ref[here, :].astype(F32) + got_ref[there, :].astype(F32)
        )
        normal, scale, _ = norm_rows(middle, gain_ref[...])
        grad = back_ref[here, :].astype(F32) + back_got_ref[there, :].astype(F32)
        grad_middle = grad_ref[...].astype(F32) + normalize_back(
            normal, scale, gain_ref[...], grad
        )
        if h == 0:
            gain_grad_ref[...] = jnp.sum(grad * normal, axis=0, keepdims=True)
            middle_ref[...] = grad_middle
        rounded = grad_middle.astype(BF)
        grad_mixed = nt(weights_ref[...], rounded)
        gates, conv = gates_ref[...].astype(F32), conv_ref[...].astype(F32)
        grad_conv_ref[...] = (grad_mixed * gates).astype(BF)
        grad_gates_ref[...] = (grad_mixed * conv).astype(BF)
        part = nn((gates * conv).astype(BF), rounded)
        mixout = part if h == 0 else mixout + part
    mixout_ref[...] = mixout.astype(BF)


def conv_back_kernel(
    unroll, channels, reach, column_ref, turned_ref, row_ref, taps_ref, values_ref, grad_ref,
    grad_values_ref, grad_taps_ref, mask_ref, mask_turned_ref, band_ref, grad_turned_ref,
):
    length = row_ref.shape[1]
    filters = taps_ref.shape[0]
    blocks = length // BLOCK
    mask_ref[...] = (column_ref[...] == row_ref[...]).astype(BF)
    mask_turned_ref[...] = (turned_ref[...] == row_ref[...]).astype(F32)
    band_ref[...] = jnp.zeros_like(band_ref)
    turn = (
        lax.broadcasted_iota(jnp.int32, (length, length), 0)
        + lax.broadcasted_iota(jnp.int32, (length, length), 1)
        == length - 1
    ).astype(BF)
    grad_turned_ref[...] = nn(grad_ref[...], turn)

    def some(step, carry):
        for u in range(unroll):
            f = step * unroll + u
            build_band(taps_ref[pl.ds(f, 1), :], mask_ref, band_ref.at[u], length, reach)
            rows = pl.ds(pl.multiple_of(f * channels, channels), channels)
            grad_values_ref[rows, :] = nt(grad_ref[rows, :], band_ref[u]).astype(BF)
            turned = grad_turned_ref[rows, :].T.astype(BF)
            product = nn(turned, values_ref[rows, :])
            parts = [jnp.zeros((BLOCK, BLOCK), F32)] + [None] * (2 * reach + 1)
            for i in range(blocks):
                back = blocks - 1 - i
                for j in range(max(0, back - reach), min(blocks, back + reach + 1)):
                    here = (
                        slice(i * BLOCK, (i + 1) * BLOCK),
                        slice(j * BLOCK, (j + 1) * BLOCK),
                    )
                    block = product[here] * mask_turned_ref[here]
                    d = j - back + reach + 1
                    parts[d] = block if parts[d] is None else parts[d] + block
            aligned = pltpu.roll(jnp.concatenate(parts, axis=1), 0, 1, stride=1, stride_axis=0)
            grad_taps_ref[pl.ds(f, 1), :] = jnp.sum(aligned, axis=0, keepdims=True)
        return carry

    lax.fori_loop(0, filters // unroll, some, 0)


def mixer_back_kernel(
    sizes, dp_ref, own_ref, other_ref, gain_ref, gain_two_ref, gates_0, gates_1, mixout_ref,
    weights_ref, condition_ref, shift_ref, cond_ref, summary_ref, values_0, values_1, taps_0,
    taps_1, back_own_ref, back_other_ref, g0a_ref, g0b_ref, g1a_ref, g2b_ref, gx_ref, gy_ref,
    one_ref, two_ref, three_ref, filter_ref,
):
    depth, block_c, block_g, chips, span, unroll, channels, reach, half = sizes
    length = own_ref.shape[0]
    side = chips * block_c
    filters = chips * block_g
    width = taps_0.shape[1]
    taps = shift_ref.shape[1]
    spare, cut = 128 - block_c, half - depth
    dp = dp_ref[0]
    lane = lax.broadcasted_iota(jnp.int32, (width, taps), 0)
    tap = lax.broadcasted_iota(jnp.int32, (width, taps), 1)
    reachable = (tap > taps // 2 - (reach + 1) * BLOCK) & (tap < taps // 2 + (reach + 1) * BLOCK)
    spot = taps - 1 - tap
    spot = jnp.where(spot >= width, spot - width, spot)
    place = ((lane == spot) & reachable).astype(BF)
    shift_there = nt(shift_ref[...].astype(BF), place)
    base_grad = shift_grad = condition_grad = value_grad = gate_grad = gain_grad = None
    for r, (ref, values_ref, gates_ref, taps_ref, back_ref) in enumerate(
        (
            (own_ref, values_0, gates_0, taps_0, back_own_ref),
            (other_ref, values_1, gates_1, taps_1, back_other_ref),
        )
    ):
        normal, _, normed = norm_rows(ref[...].astype(F32), gain_ref[...])
        normed = normed.astype(BF)
        grad_taps = taps_ref[...]
        cond = cond_ref[r, :, :1]
        summary = summary_ref[r : r + 1, :]
        grad_cond = jnp.sum(grad_taps * shift_there, axis=1, keepdims=True) * (1.0 - cond * cond)
        grad_summary = jnp.sum(grad_cond * condition_ref[...], axis=0, keepdims=True) / length
        values, gates = values_ref[...], gates_ref[...]
        back = nn(values.T, weights_ref[:side, :]) + nn(gates.T, weights_ref[side:, :])
        back = back + grad_summary
        back_ref[...] = back.astype(BF)
        parts = (
            grad_taps, cond * grad_taps, grad_cond * summary, nn(values, normed),
            nn(gates, normed), jnp.sum(back * normal, axis=0, keepdims=True),
        )
        if r > 0:
            parts = tuple(
                p + q
                for p, q in zip(
                    (base_grad, shift_grad, condition_grad, value_grad, gate_grad, gain_grad), parts
                )
            )
        base_grad, shift_grad, condition_grad, value_grad, gate_grad, gain_grad = parts
    filter_ref[0] = nn(base_grad.astype(BF), place)
    filter_ref[1] = nn(shift_grad.astype(BF), place)
    gain_rows = jnp.concatenate(
        [
            vector[:, h * 128 : (h + 1) * 128]
            for vector in (gain_grad, gain_two_ref[...])
            for h in range(vector.shape[1] // 128)
        ],
        axis=0,
    )
    gain_rows = jnp.concatenate(
        [gain_rows, jnp.zeros((16 - gain_rows.shape[0], 128), F32)], axis=0
    ).astype(BF)
    outs = (
        (g0a_ref, g0b_ref), (g1a_ref, gx_ref.at[0]), (gy_ref.at[0], g2b_ref),
        (gy_ref.at[1], gx_ref.at[1]),
    )
    empty = jnp.zeros((128 - spare - block_g, value_grad.shape[1]), F32)
    blank = jnp.zeros((16 - span * block_g, 128), F32)
    for k in range(chips):
        at = k * block_c
        own = slice(k * block_g, (k + 1) * block_g)
        mixout = mixout_ref[at : at + block_c, :].astype(F32)
        value, gate = value_grad[at : at + block_c], gate_grad[at : at + block_c]
        one_ref[...] = jnp.concatenate([value, gate[:spare]], axis=0).T.astype(BF)
        two_ref[...] = jnp.concatenate([gate[spare:], mixout[: 2 * spare]], axis=0).T.astype(BF)
        third = jnp.concatenate(
            [mixout[2 * spare :], condition_grad[own], empty], axis=0
        ).T
        for j in range(third.shape[0] // depth):
            three_ref[j * (depth // 2) : (j + 1) * (depth // 2), :] = fold(
                third[j * depth : (j + 1) * depth, :64]
            ).astype(BF)
        for m, (low, high) in enumerate(outs):
            j = dp ^ m
            at = pl.multiple_of(j * depth, depth)
            low[k, :depth, :] = one_ref[pl.ds(at, depth), :]
            low[k, depth:, :] = two_ref[pl.ds(at, cut), :]
            high[k, : depth - cut, :] = two_ref[
                pl.ds(pl.multiple_of(at + cut, cut), depth - cut), :
            ]
            start = depth - cut + depth // 2
            high[k, depth - cut : start, :] = three_ref[
                pl.ds(pl.multiple_of(j * (depth // 2), depth // 2), depth // 2), :
            ]
            for n in range(2):
                parts = [
                    filter_ref[n, own, pl.ds(pl.multiple_of((j * span + h) * 128, 128), 128)]
                    for h in range(span)
                ] + [blank]
                high[k, start : start + 16, :] = jnp.concatenate(parts, axis=0).astype(BF)
                start += 16
            high[k, start:, :] = gain_rows


def unpack_kernel(
    half, span, p0_ref, p1_ref, p2_ref, p3_ref, value_ref, mixgate_ref, condition_ref, base_ref,
    shift_ref, mixout_ref, gains_ref,
):
    depth, block_c = value_ref.shape
    block_g = condition_ref.shape[1]
    spare, cut = 128 - block_c, half - depth
    total = p0_ref[...].astype(F32) + p1_ref[...].astype(F32)
    total = total + p2_ref[...].astype(F32) + p3_ref[...].astype(F32)
    first, second = total[:depth], total[depth : 2 * depth]
    start = 2 * depth + depth // 2
    folded = total[2 * depth : start]
    third = jnp.concatenate([folded[:, :64], folded[:, 64:]], axis=0)
    value_ref[...] = first[:, :block_c]
    mixgate_ref[...] = jnp.concatenate([first[:, block_c:], second[:, : block_c - spare]], axis=1)
    mixout_ref[...] = jnp.concatenate(
        [second[:, block_c - spare :], third[:, :spare]], axis=1
    ).T
    condition_ref[...] = third[:, spare : spare + block_g]
    for ref in (base_ref, shift_ref):
        for h in range(span):
            ref[:, h * 128 : (h + 1) * 128] = total[start + h * block_g : start + (h + 1) * block_g]
        start += 16
    rows = gains_ref.shape[1] // 128
    for g in range(2):
        for h in range(rows):
            at = start + g * rows + h
            gains_ref[g : g + 1, h * 128 : (h + 1) * 128] = total[at : at + 1]


def norm_one_back_kernel(
    own_ref, back_ref, got_ref, middle_ref, gain_ref, grad_ref
):
    normal, scale, _ = norm_rows(own_ref[...].astype(F32), gain_ref[...])
    grad = back_ref[...].astype(F32) + got_ref[...].astype(F32)
    grad_ref[...] = (
        middle_ref[...] + normalize_back(normal, scale, gain_ref[...], grad)
    ).astype(BF)


def stage(*values):
    return lax.optimization_barrier(values)


def sides(column):
    return swap(column, "dp", 1), swap(column, "dp", 2)


def corners(along_x, along_y):
    return swap(along_x[0], "dp", 2), swap(along_y[1], "dp", 1)


def added(*terms):
    return sum(t.astype(F32) for t in terms).astype(BF)


class Scatter:
    def __init__(self, pieces):
        self.g0a, self.g0b, self.g1a, self.g2b, self.gx, self.gy = pieces

    def start(self):
        self.ex, self.ey = swap(self.gx, "dp", 1), swap(self.gy, "dp", 2)

    def middle(self):
        self.f1a = swap(added(self.g1a, self.ey[1]), "dp", 1)
        self.f2b = swap(added(self.g2b, self.ex[1]), "dp", 2)

    def end(self):
        f1a, f2b = self.f1a, self.f2b
        return [
            jnp.concatenate(
                [added(self.g0a[k], f1a[k], self.ey[0, k]), added(self.g0b[k], self.ex[0, k], f2b[k])],
                axis=-2,
            )
            for k in range(self.g0a.shape[0])
        ]


def fast_body(
    tokens, segment_ids, gain_one, gain_two, value_weight, mixgate_weight, condition_weight,
    filter_base, filter_shift, mixout_weight, gate_weight, up_weight, down_weight, output_grad,
):
    dp, mp = lax.axis_index("dp"), lax.axis_index("mp")
    chips = lax.axis_size("mp") // 2
    length, width = tokens.shape
    rows, total = 2, 2 * length
    depth, block_c = value_weight.shape
    block_g, taps = filter_base.shape
    block_f = gate_weight.shape[1]
    channels = block_c // block_g
    reach = SENTENCE // BLOCK
    side, filters = chips * block_c, chips * block_g
    half = 4 * depth // 3
    part = depth // 2
    span = taps // 128
    sizes = (depth, block_c, block_g, chips, span, 4, channels, reach, half)

    other, other_grad = swap(tokens, "mp", 1), swap(output_grad, "mp", 1)
    mixer_pack, ffn_pack = kernel_call(
        pack_kernel, "pack_weights",
        [shaped(2, half, 128), shaped(2, 3, part, block_f)], [],
        (
            value_weight, mixgate_weight, condition_weight, filter_base, filter_shift,
            mixout_weight, gate_weight, up_weight, down_weight,
        ),
        1e6,
    )
    mixer_pack, ffn_pack, other, other_grad = stage(mixer_pack, ffn_pack, other, other_grad)

    mixer_line = [mixer_pack] + [swap(mixer_pack, "mp", 2 * k) for k in range(1, chips)]
    dp_one = dp[None].astype(jnp.int32)
    gains = (gain_one[None, :], gain_two[None, :])
    row_ids = [lax.dynamic_slice_in_dim(segment_ids, mp ^ r, 1) for r in range(rows)]
    columns = [ids.reshape(length, 1) for ids in row_ids]
    turned = [ids[:, ::-1].reshape(length, 1) for ids in row_ids]
    two_rows, two_columns = jnp.concatenate(row_ids), jnp.concatenate(columns)
    mixer_line, ffn_pack, small = stage(
        mixer_line, ffn_pack, (dp_one, gains, row_ids, columns, turned, two_rows, two_columns)
    )
    dp_one, (gain_first, gain_second), row_ids, columns, turned, two_rows, two_columns = small
    mixer_column = jnp.stack(mixer_line, axis=1)
    mixer_sides = sides(mixer_column)
    opposite = swap(ffn_pack, "mp", 2 * (chips - 1))
    mixer_sides, ffn_pack = stage(mixer_sides, ffn_pack)
    mixer_corners = corners(*mixer_sides)
    mixer_corners, opposite, ffn_pack = stage(mixer_corners, opposite, ffn_pack)
    ffn_columns = [jnp.stack([ffn_pack, opposite], axis=1)]
    ffn_sides = [sides(ffn_columns[0])]
    nearer = [swap(ffn_pack, "mp", 2 * k) for k in range(1, chips - 1)]
    (
        branch, values_0, values_1, gates_0, gates_1, conv_0, conv_1, weights, mixout, condition,
        taps_0, taps_1, shift, cond, summary,
    ) = kernel_call(
        functools.partial(mixer_forward_kernel, sizes), "mixer_forward",
        [shaped(total, width)] + [shaped(side, length)] * 6
        + [
            shaped(2 * side, width), shaped(side, width), shaped(filters, width, dtype=F32),
            shaped(filters, 2 * length, dtype=F32), shaped(filters, 2 * length, dtype=F32),
            shaped(filters, 2 * length, dtype=F32), shaped(rows, filters, 128, dtype=F32),
            shaped(rows, width, dtype=F32),
        ],
        [
            pltpu.VMEM((width, 128), BF), pltpu.VMEM((width, 128), BF),
            pltpu.VMEM((width, 128), BF), pltpu.VMEM((filters, 2 * length), F32),
            pltpu.VMEM((length, length), BF), pltpu.VMEM((sizes[5], length, length), BF),
            pltpu.VMEM((side, length), BF),
        ],
        (dp_one, two_columns, two_rows, tokens, other, gain_first, mixer_column)
        + tuple(mixer_sides) + tuple(mixer_corners),
        14e9, scalars=1,
    )
    branch, ffn_sides[0], nearer = stage(branch, ffn_sides[0], nearer)
    values, gates, conv = (values_0, values_1), (gates_0, gates_1), (conv_0, conv_1)
    branch_got = swap(branch, "mp", 1)
    ffn_corners = [corners(*ffn_sides[0])]
    normed_two, normed_turned, grad_turned = kernel_call(
        norm_two_kernel, "norm_two",
        [shaped(total, width), shaped(width, total), shaped(width, total)], [],
        (tokens, other, branch, branch_got, output_grad, other_grad, gain_second),
        1e9,
    )
    normed_two, normed_turned, grad_turned, ffn_corners[0] = stage(
        normed_two, normed_turned, grad_turned, ffn_corners[0]
    )
    ffn_columns.append(jnp.stack(nearer, axis=1))
    ffn_sides.append(sides(ffn_columns[1]))

    def feed_forward(n, *carried):
        group = (ffn_columns[n],) + tuple(ffn_sides[n]) + tuple(ffn_corners[n])
        fixed = (dp_one, normed_two, normed_turned, output_grad, other_grad, grad_turned)
        return ffn_call(n == 0, group[0].shape[1], *fixed, *group, *carried)

    first = feed_forward(0)
    first, ffn_sides[1] = stage(first, ffn_sides[1])
    ffn_corners.append(corners(*ffn_sides[1]))
    ffn_corners[1], first = stage(ffn_corners[1], first)
    scatters = [Scatter(first[3:])]
    scatters[0].start()
    second = feed_forward(1, *first[:3])
    second, scatters[0].ex, scatters[0].ey = stage(second, scatters[0].ex, scatters[0].ey)
    feed, feed_other, back = second[:3]
    back_got = swap(back, "mp", 1)
    scatters.append(Scatter(second[3:]))
    scatters[0].middle()
    scatters[1].start()
    grad_middle, mixout_grad, grad_conv_0, grad_conv_1, grad_gates_0, grad_gates_1, gain_two_part = (
        kernel_call(
            mixout_back_kernel, "mixout_back",
            [shaped(length, width, dtype=F32), shaped(side, width)]
            + [shaped(side, length)] * 4 + [shaped(1, width, dtype=F32)],
            [],
            (
                tokens, other, branch, branch_got, back, back_got, output_grad, other_grad,
                gain_second, mixout,
            ) + gates + conv,
            4 * total * width * side,
        )
    )
    grad_conv_0, grad_conv_1, scatters[0].f1a, scatters[0].f2b = stage(
        grad_conv_0, grad_conv_1, scatters[0].f1a, scatters[0].f2b
    )
    feed_got = swap(feed_other, "mp", 1)
    sums = scatters[0].end()
    ffn_terms = [sums[0], swap(sums[1], "mp", 2 * (chips - 1))]

    def conv_back(r, row_taps, grad_conv):
        return kernel_call(
            functools.partial(conv_back_kernel, 4, channels, reach), "conv_back",
            [shaped(side, length), shaped(filters, (2 * reach + 2) * BLOCK, dtype=F32)],
            [
                pltpu.VMEM((length, length), BF), pltpu.VMEM((length, length), F32),
                pltpu.VMEM((4, length, length), BF), pltpu.VMEM((side, length), F32),
            ],
            (columns[r], turned[r], row_ids[r], row_taps, values[r], grad_conv),
            8e9,
        )

    grad_values_0, grad_taps_0 = conv_back(0, taps_0, grad_conv_0)
    grad_taps_0, grad_conv_1, scatters[1].ex, scatters[1].ey = stage(
        grad_taps_0, grad_conv_1, scatters[1].ex, scatters[1].ey
    )
    scatters[1].middle()
    grad_values_1, grad_taps_1 = conv_back(1, taps_1, grad_conv_1)
    grad_values_1, grad_taps_1, scatters[1].f1a, scatters[1].f2b, ffn_terms = stage(
        grad_values_1, grad_taps_1, scatters[1].f1a, scatters[1].f2b, ffn_terms
    )
    sums = scatters[1].end()
    ffn_terms += [swap(sums[k - 1], "mp", 2 * k) for k in range(1, chips - 1)]
    results = kernel_call(
        functools.partial(mixer_back_kernel, sizes), "mixer_back",
        [shaped(length, width), shaped(length, width)]
        + [
            shaped(chips, half, 128), shaped(chips, half + 16, 128), shaped(chips, half, 128),
            shaped(chips, half + 16, 128), shaped(2, chips, half + 16, 128),
            shaped(2, chips, half, 128),
        ],
        [
            pltpu.VMEM((width, 128), BF), pltpu.VMEM((width, 128), BF),
            pltpu.VMEM((width, 128), BF), pltpu.VMEM((2, filters, 2 * length), F32),
        ],
        (
            dp_one, tokens, other, gain_first, gain_two_part, grad_gates_0, grad_gates_1,
            mixout_grad, weights, condition, shift, cond, summary, grad_values_0, grad_values_1,
            grad_taps_0, grad_taps_1,
        ),
        8 * total * width * side, scalars=1,
    )
    back_own, back_other, mixer_grads = results[0], results[1], Scatter(results[2:])
    mixer_grads.start()
    got_one = swap(back_other, "mp", 1)
    mixer_grads.ex, mixer_grads.ey, got_one, back_own = stage(
        mixer_grads.ex, mixer_grads.ey, got_one, back_own
    )
    mixer_grads.middle()
    input_grad = kernel_call(
        norm_one_back_kernel, "norm_one_back",
        [shaped(length, width)], [],
        (tokens, back_own, got_one, grad_middle, gain_first),
        1e9,
    )[0]
    input_grad, mixer_grads.f1a, mixer_grads.f2b, ffn_terms, feed_got = stage(
        input_grad, mixer_grads.f1a, mixer_grads.f2b, ffn_terms, feed_got
    )
    mixer_terms = mixer_grads.end()
    mixer_terms = [mixer_terms[0]] + [swap(mixer_terms[k], "mp", 2 * k) for k in range(1, chips)]
    gate_sum, up_sum, down_sum = sum(t.astype(F32) for t in ffn_terms)
    output = (
        tokens.astype(F32) + branch[:length].astype(F32) + branch_got[length:].astype(F32)
        + feed.astype(F32) + feed_got.astype(F32)
    ).astype(BF)
    value_sum, mixgate_sum, condition_sum, base_sum, shift_sum, mixout_sum, gain_sums = kernel_call(
        functools.partial(unpack_kernel, half, span), "unpack",
        [
            shaped(depth, block_c, dtype=F32), shaped(depth, block_c, dtype=F32),
            shaped(depth, block_g, dtype=F32), shaped(block_g, taps, dtype=F32),
            shaped(block_g, taps, dtype=F32), shaped(block_c, depth, dtype=F32),
            shaped(2, width, dtype=F32),
        ],
        [], tuple(mixer_terms), 1e6,
    )
    gain_sums = gain_sums + swap(gain_sums, "mp", 1)
    return (
        output, input_grad, gain_sums[0], gain_sums[1], value_sum, mixgate_sum, condition_sum,
        base_sum, shift_sum, mixout_sum, gate_sum, up_sum, down_sum.T,
    )


def choose(tokens, segment_ids, gain_one, gain_two, value_weight, mixgate_weight, condition_weight,
           filter_base, filter_shift, mixout_weight, gate_weight, up_weight, down_weight,
           output_grad):
    fits = (
        lax.axis_size("dp") == 4
        and lax.axis_size("mp") == 8
        and tokens.shape[0] == segment_ids.shape[1] == 512
        and value_weight.shape == (192, 96)
        and filter_base.shape == (6, 256)
        and gate_weight.shape == (192, 384)
    )
    return (fast_body if fits else body)(
        tokens, segment_ids, gain_one, gain_two, value_weight, mixgate_weight, condition_weight,
        filter_base, filter_shift, mixout_weight, gate_weight, up_weight, down_weight, output_grad,
    )


def solution(mesh):
    sides = P(("dp", "mp"), None)
    columns, rows = P("dp", "mp"), P("mp", "dp")
    in_specs = (
        sides, P("dp", None), P(), P(), columns, columns, columns, rows, rows, rows, columns,
        columns, rows, sides,
    )
    out_specs = (
        sides, sides, P(), P(), columns, columns, columns, rows, rows, rows, columns, columns, rows,
    )
    return jax.shard_map(choose, mesh=mesh, in_specs=in_specs, out_specs=out_specs, check_vma=False)
```

```python
import functools

import jax
import jax.numpy as jnp
from jax import lax
from jax.experimental import pallas as pl
from jax.experimental.pallas import tpu as pltpu
from jax.sharding import PartitionSpec as P

epsilon = 1e-05
highest = lax.Precision.HIGHEST
BF = jnp.bfloat16
F32 = jnp.float32
BLOCK = 128
SENTENCE = 256


def build_band(taps_row, mask_ref, band_ref, length, reach):
    blocks = length // BLOCK
    low = length - (reach + 1) * BLOCK
    width = (2 * reach + 2) * BLOCK
    spread = jnp.broadcast_to(taps_row[:, low : low + width], (BLOCK, width))
    shifted = pltpu.roll(spread, 0, 1, stride=1, stride_axis=0).astype(BF)
    for i in range(blocks):
        first, last = max(0, i - reach), min(blocks, i + reach + 1)
        rows = slice(i * BLOCK, (i + 1) * BLOCK)
        columns = slice(first * BLOCK, last * BLOCK)
        offset = (first - i + reach + 1) * BLOCK
        band_ref[rows, columns] = (
            shifted[:, offset : offset + (last - first) * BLOCK] * mask_ref[rows, columns]
        )


def conv_forward_kernel(
    unroll, channels, reach, column_ref, row_ref, cond_ref, base_ref, shift_ref, values_ref,
    conv_ref, mask_ref, taps_ref, band_ref,
):
    length = row_ref.shape[1]
    filters = base_ref.shape[0]
    mask_ref[...] = (column_ref[...] == row_ref[...]).astype(BF)
    taps_ref[...] = base_ref[...].astype(F32) + cond_ref[...] * shift_ref[...].astype(F32)
    band_ref[...] = jnp.zeros_like(band_ref)

    def some(step, carry):
        for u in range(unroll):
            f = step * unroll + u
            build_band(taps_ref[pl.ds(f, 1), :], mask_ref, band_ref.at[u], length, reach)
            rows = pl.ds(pl.multiple_of(f * channels, channels), channels)
            conv_ref[rows, :] = jnp.dot(
                values_ref[rows, :], band_ref[u], preferred_element_type=F32
            )
        return carry

    lax.fori_loop(0, filters // unroll, some, 0)


def conv_forward(segments, cond, base, shift, values, unroll=8):
    filters, length = base.shape[0], segments.shape[0]
    channels = values.shape[0] // filters
    unroll = next(u for u in range(unroll, 0, -1) if filters % u == 0)
    vmem = pl.BlockSpec(memory_space=pltpu.VMEM)
    flops = 2 * values.shape[0] * length * length
    return pl.pallas_call(
        functools.partial(conv_forward_kernel, unroll, channels, SENTENCE // BLOCK),
        out_shape=jax.ShapeDtypeStruct(values.shape, F32),
        in_specs=[vmem] * 6,
        out_specs=vmem,
        scratch_shapes=[
            pltpu.VMEM((length, length), BF),
            pltpu.VMEM(base.shape, F32),
            pltpu.VMEM((unroll, length, length), BF),
        ],
        compiler_params=pltpu.CompilerParams(vmem_limit_bytes=40 << 20),
        cost_estimate=pl.CostEstimate(
            flops=flops * 16, bytes_accessed=values.size * 6, transcendentals=0
        ),
        name="conv_forward",
    )(segments[:, None], segments[None, :], cond[:, None], base, shift, values)


def conv_backward_kernel(
    unroll, channels, reach, column_ref, turned_ref, row_ref, cond_ref, base_ref, shift_ref,
    values_ref, grad_ref, grad_values_ref, grad_taps_ref, mask_ref, mask_turned_ref, taps_ref,
    band_ref, grad_turned_ref,
):
    length = row_ref.shape[1]
    filters = base_ref.shape[0]
    blocks = length // BLOCK
    mask_ref[...] = (column_ref[...] == row_ref[...]).astype(BF)
    mask_turned_ref[...] = (turned_ref[...] == row_ref[...]).astype(F32)
    taps_ref[...] = base_ref[...].astype(F32) + cond_ref[...] * shift_ref[...].astype(F32)
    band_ref[...] = jnp.zeros_like(band_ref)
    turn = (
        lax.broadcasted_iota(jnp.int32, (length, length), 0)
        + lax.broadcasted_iota(jnp.int32, (length, length), 1)
        == length - 1
    ).astype(BF)
    grad_turned_ref[...] = jnp.dot(grad_ref[...], turn, preferred_element_type=F32)

    def some(step, carry):
        for u in range(unroll):
            f = step * unroll + u
            build_band(taps_ref[pl.ds(f, 1), :], mask_ref, band_ref.at[u], length, reach)
            rows = pl.ds(pl.multiple_of(f * channels, channels), channels)
            grad_values_ref[rows, :] = jnp.dot(
                grad_ref[rows, :], band_ref[u], preferred_element_type=F32
            ).astype(BF)
            turned = grad_turned_ref[rows, :].T.astype(BF)
            product = jnp.dot(turned, values_ref[rows, :], preferred_element_type=F32)
            parts = [jnp.zeros((BLOCK, BLOCK), F32)] + [None] * (2 * reach + 1)
            for i in range(blocks):
                back = blocks - 1 - i
                for j in range(max(0, back - reach), min(blocks, back + reach + 1)):
                    here = (
                        slice(i * BLOCK, (i + 1) * BLOCK),
                        slice(j * BLOCK, (j + 1) * BLOCK),
                    )
                    block = product[here] * mask_turned_ref[here]
                    d = j - back + reach + 1
                    parts[d] = block if parts[d] is None else parts[d] + block
            aligned = pltpu.roll(jnp.concatenate(parts, axis=1), 0, 1, stride=1, stride_axis=0)
            grad_taps_ref[pl.ds(f, 1), :] = jnp.sum(aligned, axis=0, keepdims=True)
        return carry

    lax.fori_loop(0, filters // unroll, some, 0)


def conv_backward(segments, cond, base_turned, shift_turned, values, grad, unroll=4):
    filters, length = base_turned.shape[0], segments.shape[0]
    channels = values.shape[0] // filters
    reach = SENTENCE // BLOCK
    width = (2 * reach + 2) * BLOCK
    unroll = next(u for u in range(unroll, 0, -1) if filters % u == 0)
    vmem = pl.BlockSpec(memory_space=pltpu.VMEM)
    flops = 2 * values.shape[0] * length * length
    grad_values, grad_taps = pl.pallas_call(
        functools.partial(conv_backward_kernel, unroll, channels, reach),
        out_shape=(
            jax.ShapeDtypeStruct(values.shape, BF),
            jax.ShapeDtypeStruct((filters, width), F32),
        ),
        in_specs=[vmem] * 8,
        out_specs=(vmem, vmem),
        scratch_shapes=[
            pltpu.VMEM((length, length), BF),
            pltpu.VMEM((length, length), F32),
            pltpu.VMEM(base_turned.shape, F32),
            pltpu.VMEM((unroll, length, length), BF),
            pltpu.VMEM(values.shape, F32),
        ],
        compiler_params=pltpu.CompilerParams(vmem_limit_bytes=48 << 20),
        cost_estimate=pl.CostEstimate(
            flops=flops * 32, bytes_accessed=values.size * 6, transcendentals=0
        ),
        name="conv_backward",
    )(
        segments[:, None],
        segments[::-1][:, None],
        segments[None, :],
        cond[:, None],
        base_turned,
        shift_turned,
        values,
        grad,
    )
    lags = jnp.roll(grad_taps, -(BLOCK - 1), axis=1)[:, ::-1]
    start = length + (reach + 1) * BLOCK - (width - 1)
    full = jnp.pad(lags, ((0, 0), (start, 2 * length - start - width + 1)))
    return grad_values, full[:, : 2 * length]


def swap(value, axis, mask):
    return lax.ppermute(value, axis, [(i, i ^ mask) for i in range(lax.axis_size(axis))])


def bits_of(count):
    return [1 << b for b in range(count.bit_length() - 1)]


def gather_dp(block):
    bits = bits_of(lax.axis_size("dp"))
    half = block.shape[1] // 2
    found = []
    for part, order in ((block[:, :half], bits), (block[:, half:], bits[::-1])):
        held, masks = part[None], [0]
        for bit in order:
            held = jnp.concatenate([held, swap(held, "dp", bit)], axis=0)
            masks = masks + [m | bit for m in masks]
        found.append({m: held[i] for i, m in enumerate(masks)})
    return [jnp.concatenate([f[m] for f in found], axis=1) for m in range(lax.axis_size("dp"))]


def natural(pieces, me):
    held = jnp.stack(pieces)
    return jnp.concatenate(
        [lax.dynamic_index_in_dim(held, j ^ me, 0, keepdims=False) for j in range(len(pieces))],
        axis=1,
    )


def scatter_dp(pieces):
    bits = bits_of(lax.axis_size("dp"))
    half = pieces[0].shape[1] // 2
    done = []
    for part, order in ((slice(None, half), bits[::-1]), (slice(half, None), bits)):
        held = {m: p[:, part] for m, p in enumerate(pieces)}
        for bit in order:
            stay = [m for m in held if not m & bit]
            got = swap(jnp.stack([held[m | bit] for m in stay]), "dp", bit)
            held = {m: held[m] + got[i] for i, m in enumerate(stay)}
        done.append(held[0])
    return jnp.concatenate(done, axis=1)


def everywhere(value):
    for bit in bits_of(lax.axis_size("mp")):
        value = value + swap(value, "mp", bit)
    for bit in bits_of(lax.axis_size("dp")):
        value = value + swap(value, "dp", bit)
    return value


def statistics(value):
    centred = value - jnp.mean(value, axis=-1, keepdims=True)
    scale = lax.rsqrt(jnp.mean(centred * centred, axis=-1, keepdims=True) + epsilon)
    return centred * scale, scale


def normalize_back(normal, scale, gain, grad):
    scaled = grad * gain
    return scale * (
        scaled
        - jnp.mean(scaled, axis=-1, keepdims=True)
        - normal * jnp.mean(scaled * normal, axis=-1, keepdims=True)
    )


def mm(left, right, dims):
    return lax.dot_general(left, right, (dims, ((), ())), preferred_element_type=F32)


def body(
    tokens, segment_ids, gain_one, gain_two, value_weight, mixgate_weight, condition_weight,
    filter_base, filter_shift, mixout_weight, gate_weight, up_weight, down_weight, output_grad,
):
    dp_size, mp_size = lax.axis_size("dp"), lax.axis_size("mp")
    dp, mp = lax.axis_index("dp"), lax.axis_index("mp")
    core = mp & 1
    chips = mp_size // 2
    local, width = tokens.shape
    length = segment_ids.shape[1]
    whole_rows = local % length == 0
    total = 2 * local
    rows = total // length

    def pair(own, other):
        if whole_rows:
            return jnp.concatenate([own, other], axis=0)
        first = core == 0
        return jnp.concatenate([jnp.where(first, own, other), jnp.where(first, other, own)], axis=0)

    def mine(value):
        return value[:local] if whole_rows else lax.dynamic_slice_in_dim(value, core * local, local)

    def others(value):
        if whole_rows:
            return value[local:]
        return lax.dynamic_slice_in_dim(value, (1 - core) * local, local)

    def pair_sum(value):
        got = swap(value, "mp", 1)
        if whole_rows:
            got = jnp.concatenate([got[local:], got[:local]], axis=0)
        return value.astype(F32) + got.astype(F32)

    def pair_scatter(value):
        return mine(value) + swap(others(value).astype(BF), "mp", 1).astype(F32)

    block_c = value_weight.shape[1]
    block_g = condition_weight.shape[1]
    block_f = gate_weight.shape[1]
    taps = filter_base.shape[1]
    mixer_pack = jnp.stack([value_weight, mixgate_weight, mixout_weight.T])
    filter_pack = jnp.stack([filter_base.T, filter_shift.T])
    ffn_pack = jnp.stack([gate_weight, up_weight, down_weight.T])

    tokens_all = pair(tokens, swap(tokens, "mp", 1))
    grad_all = pair(output_grad, swap(output_grad, "mp", 1))
    if whole_rows:
        per = local // length
        seg_rows = jnp.concatenate(
            [
                lax.dynamic_slice_in_dim(segment_ids, mp * per, per),
                lax.dynamic_slice_in_dim(segment_ids, (mp ^ 1) * per, per),
            ]
        )
    else:
        seg_rows = lax.dynamic_slice_in_dim(segment_ids, (mp // 2) * rows, rows)

    def gather(block):
        found = [block] + [swap(block, "mp", 2 * k) for k in range(1, chips)]
        return [natural(gather_dp(b), dp) for b in found]

    mixer = jnp.concatenate(gather(mixer_pack), axis=2)
    small = jnp.concatenate(gather(jnp.pad(condition_weight, ((0, 0), (0, 0)))[None]), axis=2)[0]
    filters = jnp.concatenate(gather(filter_pack), axis=2)
    ffn = gather(ffn_pack)
    value_full, mixgate_full, mixout_full = mixer
    base, shift = jnp.swapaxes(filters, 1, 2)
    base_turned = jnp.roll(base[:, ::-1], 1, axis=1)
    shift_turned = jnp.roll(shift[:, ::-1], 1, axis=1)

    xf = tokens_all.astype(F32)
    normal_one, scale_one = statistics(xf)
    normed_one = (normal_one * gain_one).astype(BF)
    values = mm(value_full, normed_one, ((0,), (1,))).astype(BF)
    gates = mm(mixgate_full, normed_one, ((0,), (1,)))
    summary = jnp.mean(normed_one.astype(F32).reshape(rows, length, width), axis=1)
    condition = small.astype(F32)
    cond = jnp.tanh(jnp.dot(summary, condition, precision=highest))
    cuts = [slice(r * length, (r + 1) * length) for r in range(rows)]
    conv = jnp.concatenate(
        [conv_forward(seg_rows[r], cond[r], base, shift, values[:, cuts[r]]) for r in range(rows)],
        axis=1,
    )
    mixed = (conv * gates).astype(BF)
    branch = pair_sum(mm(mixed, mixout_full, ((0,), (1,))).astype(BF))
    middle = xf + branch
    normal_two, scale_two = statistics(middle)
    normed_two = (normal_two * gain_two).astype(BF)

    feed = jnp.zeros((total, width), F32)
    grad_two = jnp.zeros((total, width), F32)
    ffn_grads = []
    for k in range(chips):
        gate_full, up_full, down_full = ffn[k]
        gate_pre = mm(normed_two, gate_full, ((1,), (0,)))
        up_pre = mm(normed_two, up_full, ((1,), (0,)))
        grad_hidden = mm(grad_all, down_full, ((1,), (0,)))
        sigmoid = jax.nn.sigmoid(gate_pre)
        silu = gate_pre * sigmoid
        hidden = (silu * up_pre).astype(BF)
        grad_gate = (grad_hidden * up_pre * (sigmoid + silu * (1.0 - sigmoid))).astype(BF)
        grad_up = (grad_hidden * silu).astype(BF)
        feed = feed + mm(hidden, down_full, ((1,), (1,)))
        grad_two = (
            grad_two + mm(grad_gate, gate_full, ((1,), (1,))) + mm(grad_up, up_full, ((1,), (1,)))
        )
        ffn_grads.append(
            jnp.stack(
                [
                    mm(normed_two, grad_gate, ((0,), (0,))).astype(BF),
                    mm(normed_two, grad_up, ((0,), (0,))).astype(BF),
                    mm(grad_all, hidden, ((0,), (0,))).astype(BF),
                ]
            )
        )

    def scatter(grads):
        sums = None
        for k, grad in enumerate(grads):
            size = grad.shape[1] // dp_size
            pieces = [
                lax.dynamic_slice_in_dim(grad, (dp ^ m) * size, size, axis=1)
                for m in range(dp_size)
            ]
            part = scatter_dp(pieces)
            part = part if k == 0 else swap(part, "mp", 2 * k)
            sums = part.astype(F32) if sums is None else sums + part.astype(F32)
        return sums

    gate_sum, up_sum, down_sum = scatter(ffn_grads)
    output = (mine(middle) + pair_scatter(feed)).astype(BF)

    grad_normed_two = pair_sum(grad_two.astype(BF))
    gain_two_part = jnp.sum(mine(grad_normed_two * normal_two), axis=0)
    grad_middle = grad_all.astype(F32) + normalize_back(
        normal_two, scale_two, gain_two, grad_normed_two
    )
    grad_branch = grad_middle.astype(BF)

    mixout_grad = mm(grad_branch, mixed, ((0,), (1,)))
    grad_mixed = mm(mixout_full, grad_branch, ((0,), (1,)))
    grad_conv = (grad_mixed * gates).astype(BF)
    grad_gates = (grad_mixed * conv).astype(BF)
    backs = [
        conv_backward(
            seg_rows[r], cond[r], base_turned, shift_turned, values[:, cuts[r]],
            grad_conv[:, cuts[r]],
        )
        for r in range(rows)
    ]
    grad_values = jnp.concatenate([b[0] for b in backs], axis=1)
    grad_taps = jnp.stack([b[1] for b in backs])
    base_grad = jnp.sum(grad_taps, axis=0)
    shift_grad = jnp.sum(grad_taps * cond[:, :, None], axis=0)
    grad_cond = jnp.sum(grad_taps * shift.astype(F32)[None], axis=2) * (1.0 - cond * cond)
    condition_grad = mm(summary, grad_cond, ((0,), (0,)))
    grad_summary = jnp.dot(grad_cond, condition.T, precision=highest) / length
    value_grad = mm(normed_one, grad_values, ((0,), (1,)))
    mixgate_grad = mm(normed_one, grad_gates, ((0,), (1,)))
    grad_one = mm(grad_values, value_full, ((0,), (1,))) + mm(
        grad_gates, mixgate_full, ((0,), (1,))
    )
    grad_one = (grad_one.reshape(rows, length, width) + grad_summary[:, None, :]).reshape(
        total, width
    )
    grad_normed_one = pair_scatter(grad_one)
    input_grad = (
        mine(grad_middle)
        + normalize_back(mine(normal_one), mine(scale_one), gain_one, grad_normed_one)
    ).astype(BF)
    gain_one_part = jnp.sum(grad_normed_one * mine(normal_one), axis=0)
    gain_one_grad, gain_two_grad = everywhere(jnp.stack([gain_one_part, gain_two_part]))

    def split(grad, size):
        return [grad[..., k * size : (k + 1) * size].astype(BF) for k in range(chips)]

    value_sum, mixgate_sum, mixout_sum = scatter(
        split(jnp.stack([value_grad, mixgate_grad, mixout_grad]), block_c)
    )
    condition_sum = scatter(split(condition_grad[None], block_g))[0]
    base_sum, shift_sum = scatter(
        split(jnp.swapaxes(jnp.stack([base_grad, shift_grad]), 1, 2), block_g)
    )
    return (
        output, input_grad, gain_one_grad, gain_two_grad, value_sum, mixgate_sum, condition_sum,
        base_sum.T, shift_sum.T, mixout_sum.T, gate_sum, up_sum, down_sum.T,
    )


def hold(count):
    return [pl.BlockSpec(memory_space=pltpu.VMEM)] * count


def shaped(*shape, dtype=BF):
    return jax.ShapeDtypeStruct(shape, dtype)


def kernel_call(body, name, outs, scratch, args, flops, transcendentals=0, scalars=0, limit=16):
    held = sum(a.size * a.dtype.itemsize for a in tuple(args) + tuple(outs))
    smem = [pl.BlockSpec(memory_space=pltpu.SMEM)] * scalars
    return pl.pallas_call(
        body,
        out_shape=tuple(outs),
        in_specs=smem + hold(len(args) - scalars),
        out_specs=tuple(hold(len(outs))),
        scratch_shapes=scratch,
        compiler_params=pltpu.CompilerParams(vmem_limit_bytes=limit << 20),
        cost_estimate=pl.CostEstimate(
            flops=int(flops), bytes_accessed=int(held), transcendentals=transcendentals
        ),
        name=name,
    )(*args)


def nn(left, right):
    return lax.dot_general(left, right, (((1,), (0,)), ((), ())), preferred_element_type=F32)


def nt(left, right):
    return lax.dot_general(left, right, (((1,), (1,)), ((), ())), preferred_element_type=F32)


def turned_over(value):
    return value.astype(F32).T


def fold(value):
    rows = value.shape[0] // 2
    return jnp.concatenate([value[:rows], value[rows:]], axis=1)


def pack_kernel(
    value_ref, mixgate_ref, condition_ref, base_ref, shift_ref, mixout_ref, gate_ref, up_ref,
    down_ref, mixer_ref, ffn_ref,
):
    depth, block_c = value_ref.shape
    block_g = condition_ref.shape[0]
    span = base_ref.shape[1] // 128
    spare = 128 - block_c
    mixgate = mixgate_ref[...].astype(F32)
    mixout = turned_over(mixout_ref[...])
    first = jnp.concatenate([value_ref[...].astype(F32), mixgate[:, :spare]], axis=1)
    second = jnp.concatenate([mixgate[:, spare:], mixout[:, : 2 * spare]], axis=1)
    condition = jnp.concatenate(
        [condition_ref[...].astype(F32), jnp.zeros((spare - block_g, depth), F32)], axis=0
    )
    third = jnp.concatenate([mixout[:, 2 * spare :], condition.T], axis=1)
    half = mixer_ref.shape[1]
    cut = half - depth
    mixer_ref[0, :depth, :] = first.astype(BF)
    mixer_ref[0, depth:, :] = second[:cut].astype(BF)
    mixer_ref[1, : depth - cut, :] = second[cut:].astype(BF)
    start = depth - cut + depth // 2
    mixer_ref[1, depth - cut : start, :] = fold(third).astype(BF)
    blank = jnp.zeros((16 - span * block_g, 128), F32)
    for ref in (base_ref, shift_ref):
        pieces = [ref[:, h * 128 : (h + 1) * 128].astype(F32) for h in range(span)] + [blank]
        mixer_ref[1, start : start + 16, :] = jnp.concatenate(pieces, axis=0).astype(BF)
        start += 16
    part = ffn_ref.shape[2]
    for h in range(2):
        cut = slice(h * part, (h + 1) * part)
        ffn_ref[h, 0] = gate_ref[cut, :]
        ffn_ref[h, 1] = up_ref[cut, :]
        ffn_ref[h, 2] = down_ref[cut, :]


def norm_rows(value, gain):
    centred = value - jnp.mean(value, axis=-1, keepdims=True)
    scale = lax.rsqrt(jnp.mean(centred * centred, axis=-1, keepdims=True) + epsilon)
    normal = centred * scale
    return normal, scale, normal * gain


def column_of(row):
    return jnp.broadcast_to(row.astype(F32), (8, row.shape[1])).T[:, :1]


def mixer_forward_kernel(
    sizes, dp_ref, row_ref, own_ref, other_ref, gain_ref, p0_ref, p1_ref, p2_ref,
    p3a_ref, p3b_ref, branch_ref, values_0, values_1, gates_0, gates_1, conv_0, conv_1,
    weights_ref, mixout_ref, condition_ref, taps_0, taps_1, shift_out_ref, cond_ref, summary_ref,
    one_ref, two_ref, three_ref, base_ref, mask_ref, band_ref, mixed_ref,
):
    depth, block_c, block_g, chips, span, unroll, channels, reach, half = sizes
    length = own_ref.shape[0]
    values_refs, gates_refs = (values_0, values_1), (gates_0, gates_1)
    conv_refs, taps_refs = (conv_0, conv_1), (taps_0, taps_1)
    dp = dp_ref[0]
    pieces = ((p0_ref, None), (p1_ref, None), (p2_ref, None), (p3a_ref, p3b_ref))
    side = chips * block_c
    spare, cut = 128 - block_c, half - depth
    filters = chips * block_g

    for k in range(chips):
        for m, (first, second) in enumerate(pieces):
            low = first.at[0, k] if second is None else first.at[k]
            high = first.at[1, k] if second is None else second.at[k]
            j = dp ^ m
            at = pl.multiple_of(j * depth, depth)
            one_ref[pl.ds(at, depth), :] = low[:depth, :]
            two_ref[pl.ds(at, cut), :] = low[depth:, :]
            two_ref[pl.ds(pl.multiple_of(at + cut, cut), depth - cut), :] = high[: depth - cut, :]
            start = depth - cut + depth // 2
            folded = high[depth - cut : start, :]
            three_ref[pl.ds(at, depth // 2), :] = folded
            three_ref[pl.ds(pl.multiple_of(at + depth // 2, depth // 2), depth // 2), :] = (
                jnp.concatenate([folded[:, 64:], folded[:, :64]], axis=1)
            )
            for ref in (base_ref, shift_out_ref):
                piece = high[start : start + 16, :].astype(F32)
                start += 16
                for h in range(span):
                    lane = pl.multiple_of((j * span + h) * 128, 128)
                    ref[k * block_g : (k + 1) * block_g, pl.ds(lane, 128)] = piece[
                        h * block_g : (h + 1) * block_g
                    ]
        here, there = k * block_c, side + k * block_c
        turned = turned_over(one_ref[...]).astype(BF)
        weights_ref[here : here + block_c, :] = turned[:block_c]
        weights_ref[there : there + spare, :] = turned[block_c:]
        turned = turned_over(two_ref[...]).astype(BF)
        weights_ref[there + spare : there + block_c, :] = turned[: block_c - spare]
        mixout_ref[here : here + 2 * spare, :] = turned[block_c - spare :]
        turned = turned_over(three_ref[...]).astype(BF)
        mixout_ref[here + 2 * spare : here + block_c, :] = turned[:spare]
        condition_ref[k * block_g : (k + 1) * block_g, :] = turned[spare : 2 * spare].astype(F32)[
            :block_g
        ]

    band_ref[...] = jnp.zeros_like(band_ref)
    for r, ref in enumerate((own_ref, other_ref)):
        _, _, normed = norm_rows(ref[...].astype(F32), gain_ref[...])
        normed = normed.astype(BF)
        summary = jnp.mean(normed.astype(F32), axis=0, keepdims=True)
        summary_ref[r : r + 1, :] = summary
        cond = jnp.tanh(jnp.sum(condition_ref[...] * summary, axis=1, keepdims=True))
        cond_ref[r] = jnp.broadcast_to(cond, cond_ref.shape[1:])
        taps_refs[r][...] = base_ref[...] + cond * shift_out_ref[...]
        values_refs[r][...] = nt(weights_ref[:side, :], normed).astype(BF)
        gates_refs[r][...] = nt(weights_ref[side:, :], normed).astype(BF)
        ids = row_ref[r : r + 1, :]
        mask_ref[...] = (column_of(ids) == ids.astype(F32)).astype(BF)

        def some(step, carry, r=r):
            for u in range(unroll):
                f = step * unroll + u
                build_band(taps_refs[r][pl.ds(f, 1), :], mask_ref, band_ref.at[u], length, reach)
                at = pl.ds(pl.multiple_of(f * channels, channels), channels)
                conv = nn(values_refs[r][at, :], band_ref[u])
                conv_refs[r][at, :] = conv.astype(BF)
                mixed_ref[at, :] = (conv * gates_refs[r][at, :].astype(F32)).astype(BF)
            return carry

        lax.fori_loop(0, filters // unroll, some, 0)
        branch_ref[r * length : (r + 1) * length, :] = nn(
            mixed_ref[...].T, mixout_ref[...]
        ).astype(BF)


def norm_two_kernel(
    own_ref, other_ref, branch_ref, got_ref, gain_ref, normed_ref, normed_turned_ref,
):
    local = own_ref.shape[0]
    for h, ref in enumerate((own_ref, other_ref)):
        here, there = slice(h * local, (h + 1) * local), slice((1 - h) * local, (2 - h) * local)
        middle = (
            ref[...].astype(F32) + branch_ref[here, :].astype(F32) + got_ref[there, :].astype(F32)
        )
        _, _, normed = norm_rows(middle, gain_ref[...])
        normed = normed.astype(BF)
        normed_ref[here, :] = normed
        normed_turned_ref[:, here] = normed.T


def turn_kernel(own_ref, other_ref, turned_ref):
    local = own_ref.shape[0]
    turned_ref[:, :local] = own_ref[...].T
    turned_ref[:, local:] = other_ref[...].T


def ffn_kernel(
    carried, kept, last, dp_ref, normed_ref, normed_turned_ref, grad_own_ref, grad_other_ref,
    grad_turned_ref, p0_ref, p1_ref, p2_ref, p3a_ref, p3b_ref, *refs,
):
    before, refs = refs[: 3 * carried], refs[3 * carried :]
    kept_refs, refs = refs[: 6 * kept], refs[6 * kept :]
    feed_own_ref, feed_other_ref, back_ref, g0a, g0b, g1a, g2b, gx, gy = refs[:9]
    two_ref, down_ref, hidden_ref, act_ref, two_grad_ref, down_grad_ref = refs[9:]
    local = grad_own_ref.shape[0]
    _, _, part, block = g0a.shape
    dp = dp_ref[0]
    pieces = ((p0_ref, None), (p1_ref, None), (p2_ref, None), (p3a_ref, p3b_ref))
    outs = ((g0a, g0b), (g1a, gx.at[0]), (gy.at[0], g2b), (gy.at[1], gx.at[1]))
    for m, (one, two) in enumerate(pieces):
        for h in range(2):
            source = one.at[h, 0] if two is None else (one, two)[h].at[0]
            at = pl.ds(pl.multiple_of((dp ^ m) * (2 * part) + h * part, part), part)
            two_ref[at, :block] = source[0]
            two_ref[at, block:] = source[1]
            down_ref[at, :] = source[2]
    for t, (grad_ref, feed_ref) in enumerate(
        ((grad_own_ref, feed_own_ref), (grad_other_ref, feed_other_ref))
    ):
        here = slice(t * local, (t + 1) * local)
        both = nn(normed_ref[here, :], two_ref[...])
        gate_pre, up_pre = both[:, :block], both[:, block:]
        grad_hidden = nn(grad_ref[...], down_ref[...])
        sigmoid = 1.0 / (1.0 + jnp.exp(-gate_pre))
        silu = gate_pre * sigmoid
        hidden = (silu * up_pre).astype(BF)
        hidden_ref[here, :] = hidden
        act_ref[here, :block] = (
            grad_hidden * up_pre * (sigmoid + silu * (1.0 - sigmoid))
        ).astype(BF)
        act_ref[here, block:] = (grad_hidden * silu).astype(BF)
        feed = nt(hidden, down_ref[...])
        back = nt(act_ref[here, :], two_ref[...])
        if carried:
            feed = feed + before[t][...]
            back = back + before[2][here, :]
        feed_ref[...] = feed.astype(feed_ref.dtype)
        back_ref[here, :] = back.astype(back_ref.dtype)
    two_grad_ref[...] = nn(normed_turned_ref[...], act_ref[...]).astype(BF)
    down_grad_ref[...] = nn(grad_turned_ref[...], hidden_ref[...]).astype(BF)
    if kept:
        for source, target in zip(kept_refs[:4], (g0a, g0b, g1a, g2b)):
            target[0] = source[0]
        for source, target in zip(kept_refs[4:], (gx, gy)):
            target[:, 0] = source[:, 0]
    for m, pair in enumerate(outs):
        for h in range(2):
            at = pl.ds(pl.multiple_of((dp ^ m) * (2 * part) + h * part, part), part)
            pair[h][int(kept), 0] = two_grad_ref[at, :block]
            pair[h][int(kept), 1] = two_grad_ref[at, block:]
            pair[h][int(kept), 2] = down_grad_ref[at, :]


def ffn_call(fixed, group, before=(), kept=(), last=False):
    total, width = fixed[1].shape
    local = fixed[3].shape[0]
    _, _, _, part, block = group[0].shape
    count, kind = 1 + bool(kept), BF if last else F32
    outs = [
        shaped(local, width, dtype=kind), shaped(local, width, dtype=kind),
        shaped(total, width, dtype=kind),
    ]
    outs += [shaped(count, 3, part, block)] * 4 + [shaped(2, count, 3, part, block)] * 2
    return kernel_call(
        functools.partial(ffn_kernel, bool(before), bool(kept), last), "feed_forward", outs,
        [
            pltpu.VMEM((width, 2 * block), BF), pltpu.VMEM((width, block), BF),
            pltpu.VMEM((total, block), BF), pltpu.VMEM((total, 2 * block), BF),
            pltpu.VMEM((width, 2 * block), BF), pltpu.VMEM((width, block), BF),
        ],
        fixed + tuple(group) + tuple(before) + tuple(kept),
        18 * total * width * block, transcendentals=total * block, scalars=1,
    )


def mixout_back_kernel(
    own_ref, other_ref, branch_ref, got_ref, back_ref, back_got_ref, grad_own_ref, grad_other_ref,
    gain_ref, weights_ref, gates_0, gates_1, conv_0, conv_1, middle_ref, mixout_ref, grad_conv_0,
    grad_conv_1, grad_gates_0, grad_gates_1, gain_grad_ref,
):
    local = own_ref.shape[0]
    mixout = None
    for h, (ref, grad_ref, gates_ref, conv_ref, grad_conv_ref, grad_gates_ref) in enumerate(
        (
            (own_ref, grad_own_ref, gates_0, conv_0, grad_conv_0, grad_gates_0),
            (other_ref, grad_other_ref, gates_1, conv_1, grad_conv_1, grad_gates_1),
        )
    ):
        here, there = slice(h * local, (h + 1) * local), slice((1 - h) * local, (2 - h) * local)
        middle = (
            ref[...].astype(F32) + branch_ref[here, :].astype(F32) + got_ref[there, :].astype(F32)
        )
        normal, scale, _ = norm_rows(middle, gain_ref[...])
        grad = back_ref[here, :].astype(F32) + back_got_ref[there, :].astype(F32)
        grad_middle = grad_ref[...].astype(F32) + normalize_back(
            normal, scale, gain_ref[...], grad
        )
        if h == 0:
            gain_grad_ref[...] = jnp.sum(grad * normal, axis=0, keepdims=True)
            middle_ref[...] = grad_middle
        rounded = grad_middle.astype(BF)
        grad_mixed = nt(weights_ref[...], rounded)
        gates, conv = gates_ref[...].astype(F32), conv_ref[...].astype(F32)
        grad_conv_ref[...] = (grad_mixed * gates).astype(BF)
        grad_gates_ref[...] = (grad_mixed * conv).astype(BF)
        part = nn((gates * conv).astype(BF), rounded)
        mixout = part if h == 0 else mixout + part
    mixout_ref[...] = mixout.astype(BF)


def conv_back_kernel(
    unroll, channels, reach, r, row_ref, taps_ref, values_ref, grad_ref, grad_values_ref,
    grad_taps_ref, mask_ref, mask_turned_ref, band_ref, grad_turned_ref,
):
    length = row_ref.shape[1]
    filters = taps_ref.shape[0]
    blocks = length // BLOCK
    ids = row_ref[r : r + 1, :]
    mask_ref[...] = (column_of(ids) == ids.astype(F32)).astype(BF)
    band_ref[...] = jnp.zeros_like(band_ref)
    turn = (
        lax.broadcasted_iota(jnp.int32, (length, length), 0)
        + lax.broadcasted_iota(jnp.int32, (length, length), 1)
        == length - 1
    ).astype(BF)
    grad_turned_ref[...] = nn(grad_ref[...], turn)
    mask_turned_ref[...] = nn(turn, mask_ref[...])

    def some(step, carry):
        for u in range(unroll):
            f = step * unroll + u
            build_band(taps_ref[pl.ds(f, 1), :], mask_ref, band_ref.at[u], length, reach)
            rows = pl.ds(pl.multiple_of(f * channels, channels), channels)
            grad_values_ref[rows, :] = nt(grad_ref[rows, :], band_ref[u]).astype(BF)
            turned = grad_turned_ref[rows, :].T.astype(BF)
            product = nn(turned, values_ref[rows, :])
            parts = [jnp.zeros((BLOCK, BLOCK), F32)] + [None] * (2 * reach + 1)
            for i in range(blocks):
                back = blocks - 1 - i
                for j in range(max(0, back - reach), min(blocks, back + reach + 1)):
                    here = (
                        slice(i * BLOCK, (i + 1) * BLOCK),
                        slice(j * BLOCK, (j + 1) * BLOCK),
                    )
                    block = product[here] * mask_turned_ref[here]
                    d = j - back + reach + 1
                    parts[d] = block if parts[d] is None else parts[d] + block
            aligned = pltpu.roll(jnp.concatenate(parts, axis=1), 0, 1, stride=1, stride_axis=0)
            grad_taps_ref[pl.ds(f, 1), :] = jnp.sum(aligned, axis=0, keepdims=True)
        return carry

    lax.fori_loop(0, filters // unroll, some, 0)


def mixer_back_kernel(
    sizes, dp_ref, own_ref, other_ref, gain_ref, gain_two_ref, gates_0, gates_1, mixout_ref,
    weights_ref, condition_ref, shift_ref, cond_ref, summary_ref, values_0, values_1, taps_0,
    taps_1, back_own_ref, back_other_ref, g0a_ref, g0b_ref, g1a_ref, g2b_ref, gx_ref, gy_ref,
    one_ref, two_ref, three_ref, filter_ref,
):
    depth, block_c, block_g, chips, span, unroll, channels, reach, half = sizes
    length = own_ref.shape[0]
    side = chips * block_c
    filters = chips * block_g
    width = taps_0.shape[1]
    taps = shift_ref.shape[1]
    spare, cut = 128 - block_c, half - depth
    dp = dp_ref[0]
    lane = lax.broadcasted_iota(jnp.int32, (width, taps), 0)
    tap = lax.broadcasted_iota(jnp.int32, (width, taps), 1)
    reachable = (tap > taps // 2 - (reach + 1) * BLOCK) & (tap < taps // 2 + (reach + 1) * BLOCK)
    spot = taps - 1 - tap
    spot = jnp.where(spot >= width, spot - width, spot)
    place = ((lane == spot) & reachable).astype(BF)
    shift_there = nt(shift_ref[...].astype(BF), place)
    base_grad = shift_grad = condition_grad = value_grad = gate_grad = gain_grad = None
    for r, (ref, values_ref, gates_ref, taps_ref, back_ref) in enumerate(
        (
            (own_ref, values_0, gates_0, taps_0, back_own_ref),
            (other_ref, values_1, gates_1, taps_1, back_other_ref),
        )
    ):
        normal, _, normed = norm_rows(ref[...].astype(F32), gain_ref[...])
        normed = normed.astype(BF)
        grad_taps = taps_ref[...]
        cond = cond_ref[r, :, :1]
        summary = summary_ref[r : r + 1, :]
        grad_cond = jnp.sum(grad_taps * shift_there, axis=1, keepdims=True) * (1.0 - cond * cond)
        grad_summary = jnp.sum(grad_cond * condition_ref[...], axis=0, keepdims=True) / length
        values, gates = values_ref[...], gates_ref[...]
        back = nn(values.T, weights_ref[:side, :]) + nn(gates.T, weights_ref[side:, :])
        back = back + grad_summary
        back_ref[...] = back.astype(BF)
        parts = (
            grad_taps, cond * grad_taps, grad_cond * summary, nn(values, normed),
            nn(gates, normed), jnp.sum(back * normal, axis=0, keepdims=True),
        )
        if r > 0:
            parts = tuple(
                p + q
                for p, q in zip(
                    (base_grad, shift_grad, condition_grad, value_grad, gate_grad, gain_grad), parts
                )
            )
        base_grad, shift_grad, condition_grad, value_grad, gate_grad, gain_grad = parts
    filter_ref[0] = nn(base_grad.astype(BF), place)
    filter_ref[1] = nn(shift_grad.astype(BF), place)
    gain_rows = jnp.concatenate(
        [
            vector[:, h * 128 : (h + 1) * 128]
            for vector in (gain_grad, gain_two_ref[...])
            for h in range(vector.shape[1] // 128)
        ],
        axis=0,
    )
    gain_rows = jnp.concatenate(
        [gain_rows, jnp.zeros((16 - gain_rows.shape[0], 128), F32)], axis=0
    ).astype(BF)
    outs = (
        (g0a_ref, g0b_ref), (g1a_ref, gx_ref.at[0]), (gy_ref.at[0], g2b_ref),
        (gy_ref.at[1], gx_ref.at[1]),
    )
    empty = jnp.zeros((128 - spare - block_g, value_grad.shape[1]), F32)
    blank = jnp.zeros((16 - span * block_g, 128), F32)
    for k in range(chips):
        at = k * block_c
        own = slice(k * block_g, (k + 1) * block_g)
        mixout = mixout_ref[at : at + block_c, :].astype(F32)
        value, gate = value_grad[at : at + block_c], gate_grad[at : at + block_c]
        one_ref[...] = jnp.concatenate([value, gate[:spare]], axis=0).T.astype(BF)
        two_ref[...] = jnp.concatenate([gate[spare:], mixout[: 2 * spare]], axis=0).T.astype(BF)
        third = jnp.concatenate(
            [mixout[2 * spare :], condition_grad[own], empty], axis=0
        ).T
        for j in range(third.shape[0] // depth):
            three_ref[j * (depth // 2) : (j + 1) * (depth // 2), :] = fold(
                third[j * depth : (j + 1) * depth, :64]
            ).astype(BF)
        for m, (low, high) in enumerate(outs):
            j = dp ^ m
            at = pl.multiple_of(j * depth, depth)
            low[k, :depth, :] = one_ref[pl.ds(at, depth), :]
            low[k, depth:, :] = two_ref[pl.ds(at, cut), :]
            high[k, : depth - cut, :] = two_ref[
                pl.ds(pl.multiple_of(at + cut, cut), depth - cut), :
            ]
            start = depth - cut + depth // 2
            high[k, depth - cut : start, :] = three_ref[
                pl.ds(pl.multiple_of(j * (depth // 2), depth // 2), depth // 2), :
            ]
            for n in range(2):
                parts = [
                    filter_ref[n, own, pl.ds(pl.multiple_of((j * span + h) * 128, 128), 128)]
                    for h in range(span)
                ] + [blank]
                high[k, start : start + 16, :] = jnp.concatenate(parts, axis=0).astype(BF)
                start += 16
            high[k, start:, :] = gain_rows


def unpack_kernel(
    half, span, p0_ref, p1_ref, p2_ref, p3_ref, value_ref, mixgate_ref, condition_ref, base_ref,
    shift_ref, mixout_ref, gains_ref,
):
    depth, block_c = value_ref.shape
    block_g = condition_ref.shape[0]
    spare, cut = 128 - block_c, half - depth
    total = p0_ref[...].astype(F32) + p1_ref[...].astype(F32)
    total = total + p2_ref[...].astype(F32) + p3_ref[...].astype(F32)
    first, second = total[:depth], total[depth : 2 * depth]
    start = 2 * depth + depth // 2
    folded = total[2 * depth : start]
    third = jnp.concatenate([folded[:, :64], folded[:, 64:]], axis=0)
    value_ref[...] = first[:, :block_c]
    mixgate_ref[...] = jnp.concatenate([first[:, block_c:], second[:, : block_c - spare]], axis=1)
    mixout_ref[...] = jnp.concatenate(
        [second[:, block_c - spare :], third[:, :spare]], axis=1
    ).T
    condition_ref[...] = third[:, spare:].T[:block_g]
    for ref in (base_ref, shift_ref):
        for h in range(span):
            ref[:, h * 128 : (h + 1) * 128] = total[start + h * block_g : start + (h + 1) * block_g]
        start += 16
    rows = gains_ref.shape[1] // 128
    for g in range(2):
        for h in range(rows):
            at = start + g * rows + h
            gains_ref[g : g + 1, h * 128 : (h + 1) * 128] = total[at : at + 1]


def norm_one_back_kernel(
    own_ref, back_ref, got_ref, middle_ref, gain_ref, grad_ref
):
    normal, scale, _ = norm_rows(own_ref[...].astype(F32), gain_ref[...])
    grad = back_ref[...].astype(F32) + got_ref[...].astype(F32)
    grad_ref[...] = (
        middle_ref[...] + normalize_back(normal, scale, gain_ref[...], grad)
    ).astype(BF)


def stage(*values):
    return lax.optimization_barrier(values)


def sides(column):
    return swap(column, "dp", 1), swap(column, "dp", 2)


def corners(along_x, along_y):
    return swap(along_x[0], "dp", 2), swap(along_y[1], "dp", 1)


def added(*terms):
    return sum(t.astype(F32) for t in terms).astype(BF)


class Scatter:
    def __init__(self, pieces):
        self.g0a, self.g0b, self.g1a, self.g2b, self.gx, self.gy = pieces

    def start(self):
        self.ex, self.ey = swap(self.gx, "dp", 1), swap(self.gy, "dp", 2)

    def middle(self):
        self.f1a = swap(added(self.g1a, self.ey[1]), "dp", 1)
        self.f2b = swap(added(self.g2b, self.ex[1]), "dp", 2)

    def end(self):
        f1a, f2b = self.f1a, self.f2b
        return [
            jnp.concatenate(
                [added(self.g0a[k], f1a[k], self.ey[0, k]), added(self.g0b[k], self.ex[0, k], f2b[k])],
                axis=-2,
            )
            for k in range(self.g0a.shape[0])
        ]


def fast_body(
    tokens, segment_ids, gain_one, gain_two, value_weight, mixgate_weight, condition_weight,
    filter_base, filter_shift, mixout_weight, gate_weight, up_weight, down_weight, output_grad,
):
    dp, mp = lax.axis_index("dp"), lax.axis_index("mp")
    chips = lax.axis_size("mp") // 2
    length, width = tokens.shape
    rows, total = 2, 2 * length
    depth, block_c = value_weight.shape
    block_g, taps = filter_base.shape
    block_f = gate_weight.shape[1]
    channels = block_c // block_g
    reach = SENTENCE // BLOCK
    side, filters = chips * block_c, chips * block_g
    half = 4 * depth // 3
    part = depth // 2
    span = taps // 128
    sizes = (depth, block_c, block_g, chips, span, 4, channels, reach, half)

    other, other_grad = swap(tokens, "mp", 1), swap(output_grad, "mp", 1)
    mixer_pack, ffn_pack = kernel_call(
        pack_kernel, "pack_weights",
        [shaped(2, half, 128), shaped(2, 3, part, block_f)], [],
        (
            value_weight, mixgate_weight, condition_weight.T, filter_base, filter_shift,
            mixout_weight, gate_weight, up_weight, down_weight.T,
        ),
        1e6, limit=60,
    )
    mixer_pack, ffn_pack, other, other_grad = stage(mixer_pack, ffn_pack, other, other_grad)

    mixer_line = [mixer_pack] + [swap(mixer_pack, "mp", 2 * k) for k in range(1, chips)]
    dp_one = dp[None].astype(jnp.int32)
    gains = (gain_one[None, :], gain_two[None, :])
    row_ids = [lax.dynamic_slice_in_dim(segment_ids, mp ^ r, 1) for r in range(rows)]
    two_rows = jnp.concatenate(row_ids)
    (grad_turned,) = kernel_call(
        turn_kernel, "turn_gradient", [shaped(width, total)], [], (output_grad, other_grad), 1e6
    )
    own_column = ffn_pack[:, None]
    mixer_line, own_sides, small, ffn_pack, grad_turned = stage(
        mixer_line, sides(own_column), (dp_one, gains, two_rows), ffn_pack, grad_turned
    )
    dp_one, (gain_first, gain_second), two_rows = small
    mixer_column = jnp.stack(mixer_line, axis=1)
    mixer_sides = sides(mixer_column)
    second_pack = swap(ffn_pack, "mp", 4)
    mixer_sides, ffn_pack, own_sides = stage(mixer_sides, ffn_pack, own_sides)
    mixer_corners = corners(*mixer_sides)
    mixer_corners, second_pack, ffn_pack, own_sides = stage(
        mixer_corners, second_pack, ffn_pack, own_sides
    )
    second_column = second_pack[:, None]
    second_sides = sides(second_column)
    own_corners = corners(*own_sides)
    near = swap(jnp.stack([ffn_pack, second_pack], axis=1), "mp", 2)
    (
        branch, values_0, values_1, gates_0, gates_1, conv_0, conv_1, weights, mixout, condition,
        taps_0, taps_1, shift, cond, summary,
    ) = kernel_call(
        functools.partial(mixer_forward_kernel, sizes), "mixer_forward",
        [shaped(total, width)] + [shaped(side, length)] * 6
        + [
            shaped(2 * side, width), shaped(side, width), shaped(filters, width, dtype=F32),
            shaped(filters, 2 * length, dtype=F32), shaped(filters, 2 * length, dtype=F32),
            shaped(filters, 2 * length, dtype=F32), shaped(rows, filters, 128, dtype=F32),
            shaped(rows, width, dtype=F32),
        ],
        [
            pltpu.VMEM((width, 128), BF), pltpu.VMEM((width, 128), BF),
            pltpu.VMEM((width, 128), BF), pltpu.VMEM((filters, 2 * length), F32),
            pltpu.VMEM((length, length), BF), pltpu.VMEM((sizes[5], length, length), BF),
            pltpu.VMEM((side, length), BF),
        ],
        (dp_one, two_rows, tokens, other, gain_first, mixer_column)
        + tuple(mixer_sides) + tuple(mixer_corners),
        14e9, scalars=1,
    )
    branch, second_sides, own_corners, near = stage(branch, second_sides, own_corners, near)
    values, gates, conv = (values_0, values_1), (gates_0, gates_1), (conv_0, conv_1)
    branch_got = swap(branch, "mp", 1)
    first_column, third_column = near[:, :1], near[:, 1:]
    second_corners = corners(*second_sides)
    third_sides = sides(third_column)
    normed_two, normed_turned = kernel_call(
        norm_two_kernel, "norm_two", [shaped(total, width), shaped(width, total)], [],
        (tokens, other, branch, branch_got, gain_second),
        1e9,
    )
    fixed = (dp_one, normed_two, normed_turned, output_grad, other_grad, grad_turned)
    own = ffn_call(fixed, (own_column, *own_sides, *own_corners))
    own, second_corners, third_sides = stage(own, second_corners, third_sides)
    third_corners = corners(*third_sides)
    first_sides = sides(first_column)
    far = ffn_call(fixed, (second_column, *second_sides, *second_corners), own[:3])
    far, third_corners, first_sides = stage(far, third_corners, first_sides)
    first_corners = corners(*first_sides)
    far = ffn_call(fixed, (third_column, *third_sides, *third_corners), far[:3], far[3:])
    far, first_corners = stage(far, first_corners)
    scatters = [Scatter(far[3:])]
    scatters[0].start()
    second = ffn_call(
        fixed, (first_column, *first_sides, *first_corners), far[:3], own[3:], last=True
    )
    second, scatters[0].ex, scatters[0].ey = stage(second, scatters[0].ex, scatters[0].ey)
    feed, feed_other, back = second[:3]
    back_got = swap(back, "mp", 1)
    scatters.append(Scatter(second[3:]))
    scatters[0].middle()
    scatters[1].start()
    grad_middle, mixout_grad, grad_conv_0, grad_conv_1, grad_gates_0, grad_gates_1, gain_two_part = (
        kernel_call(
            mixout_back_kernel, "mixout_back",
            [shaped(length, width, dtype=F32), shaped(side, width)]
            + [shaped(side, length)] * 4 + [shaped(1, width, dtype=F32)],
            [],
            (
                tokens, other, branch, branch_got, back, back_got, output_grad, other_grad,
                gain_second, mixout,
            ) + gates + conv,
            4 * total * width * side,
        )
    )
    grad_conv_0, grad_conv_1, scatters[0].f1a, scatters[0].f2b = stage(
        grad_conv_0, grad_conv_1, scatters[0].f1a, scatters[0].f2b
    )
    feed_got = swap(feed_other, "mp", 1)
    sums = scatters[0].end()
    third_got = swap(sums[1], "mp", 2)
    second_sum = sums[0]

    def conv_back(r, row_taps, grad_conv):
        return kernel_call(
            functools.partial(conv_back_kernel, 4, channels, reach, r), "conv_back",
            [shaped(side, length), shaped(filters, (2 * reach + 2) * BLOCK, dtype=F32)],
            [
                pltpu.VMEM((length, length), BF), pltpu.VMEM((length, length), F32),
                pltpu.VMEM((4, length, length), BF), pltpu.VMEM((side, length), F32),
            ],
            (two_rows, row_taps, values[r], grad_conv),
            8e9,
        )

    grad_values_0, grad_taps_0 = conv_back(0, taps_0, grad_conv_0)
    grad_taps_0, grad_conv_1, scatters[1].ex, scatters[1].ey, third_got = stage(
        grad_taps_0, grad_conv_1, scatters[1].ex, scatters[1].ey, third_got
    )
    ffn_terms = [swap(added(second_sum, third_got), "mp", 4)]
    scatters[1].middle()
    grad_values_1, grad_taps_1 = conv_back(1, taps_1, grad_conv_1)
    grad_values_1, grad_taps_1, scatters[1].f1a, scatters[1].f2b = stage(
        grad_values_1, grad_taps_1, scatters[1].f1a, scatters[1].f2b
    )
    sums = scatters[1].end()
    ffn_terms += [sums[0], swap(sums[1], "mp", 2)]
    results = kernel_call(
        functools.partial(mixer_back_kernel, sizes), "mixer_back",
        [shaped(length, width), shaped(length, width)]
        + [
            shaped(chips, half, 128), shaped(chips, half + 16, 128), shaped(chips, half, 128),
            shaped(chips, half + 16, 128), shaped(2, chips, half + 16, 128),
            shaped(2, chips, half, 128),
        ],
        [
            pltpu.VMEM((width, 128), BF), pltpu.VMEM((width, 128), BF),
            pltpu.VMEM((width, 128), BF), pltpu.VMEM((2, filters, 2 * length), F32),
        ],
        (
            dp_one, tokens, other, gain_first, gain_two_part, grad_gates_0, grad_gates_1,
            mixout_grad, weights, condition, shift, cond, summary, grad_values_0, grad_values_1,
            grad_taps_0, grad_taps_1,
        ),
        8 * total * width * side, scalars=1,
    )
    back_own, back_other, mixer_grads = results[0], results[1], Scatter(results[2:])
    mixer_grads.start()
    got_one = swap(back_other, "mp", 1)
    mixer_grads.ex, mixer_grads.ey, got_one, back_own, ffn_terms = stage(
        mixer_grads.ex, mixer_grads.ey, got_one, back_own, ffn_terms
    )
    mixer_grads.middle()
    input_grad = kernel_call(
        norm_one_back_kernel, "norm_one_back",
        [shaped(length, width)], [],
        (tokens, back_own, got_one, grad_middle, gain_first),
        1e9,
    )[0]
    input_grad, mixer_grads.f1a, mixer_grads.f2b, ffn_terms, feed_got = stage(
        input_grad, mixer_grads.f1a, mixer_grads.f2b, ffn_terms, feed_got
    )
    mixer_terms = mixer_grads.end()
    mixer_terms = [mixer_terms[0]] + [swap(mixer_terms[k], "mp", 2 * k) for k in range(1, chips)]
    gate_sum, up_sum, down_sum = sum(t.astype(F32) for t in ffn_terms)
    output = (
        tokens.astype(F32) + branch[:length].astype(F32) + branch_got[length:].astype(F32)
        + feed.astype(F32) + feed_got.astype(F32)
    ).astype(BF)
    value_sum, mixgate_sum, condition_sum, base_sum, shift_sum, mixout_sum, gain_sums = kernel_call(
        functools.partial(unpack_kernel, half, span), "unpack",
        [
            shaped(depth, block_c, dtype=F32), shaped(depth, block_c, dtype=F32),
            shaped(block_g, depth, dtype=F32), shaped(block_g, taps, dtype=F32),
            shaped(block_g, taps, dtype=F32), shaped(block_c, depth, dtype=F32),
            shaped(2, width, dtype=F32),
        ],
        [], tuple(mixer_terms), 1e6,
    )
    gain_sums = gain_sums + swap(gain_sums, "mp", 1)
    return (
        output, input_grad, gain_sums[0], gain_sums[1], value_sum, mixgate_sum, condition_sum.T,
        base_sum, shift_sum, mixout_sum, gate_sum, up_sum, down_sum.T,
    )


def choose(tokens, segment_ids, gain_one, gain_two, value_weight, mixgate_weight, condition_weight,
           filter_base, filter_shift, mixout_weight, gate_weight, up_weight, down_weight,
           output_grad):
    fits = (
        lax.axis_size("dp") == 4
        and lax.axis_size("mp") == 8
        and tokens.shape[0] == segment_ids.shape[1] == 512
        and value_weight.shape == (192, 96)
        and filter_base.shape == (6, 256)
        and gate_weight.shape == (192, 384)
    )
    return (fast_body if fits else body)(
        tokens, segment_ids, gain_one, gain_two, value_weight, mixgate_weight, condition_weight,
        filter_base, filter_shift, mixout_weight, gate_weight, up_weight, down_weight, output_grad,
    )


def solution(mesh):
    sides = P(("dp", "mp"), None)
    columns, rows = P("dp", "mp"), P("mp", "dp")
    in_specs = (
        sides, P("dp", None), P(), P(), columns, columns, columns, rows, rows, rows, columns,
        columns, rows, sides,
    )
    out_specs = (
        sides, sides, P(), P(), columns, columns, columns, rows, rows, rows, columns, columns, rows,
    )
    return jax.shard_map(choose, mesh=mesh, in_specs=in_specs, out_specs=out_specs, check_vma=False)
```

```python
import functools

import jax
import jax.numpy as jnp
from jax import lax
from jax.experimental import pallas as pl
from jax.experimental.pallas import tpu as pltpu
from jax.sharding import PartitionSpec as P

epsilon = 1e-05
highest = lax.Precision.HIGHEST
BF = jnp.bfloat16
F32 = jnp.float32
BLOCK = 128
SENTENCE = 256


def build_band(taps_row, mask_ref, band_ref, length, reach):
    blocks = length // BLOCK
    low = length - (reach + 1) * BLOCK
    width = (2 * reach + 2) * BLOCK
    spread = jnp.broadcast_to(taps_row[:, low : low + width], (BLOCK, width))
    shifted = pltpu.roll(spread, 0, 1, stride=1, stride_axis=0).astype(BF)
    for i in range(blocks):
        first, last = max(0, i - reach), min(blocks, i + reach + 1)
        rows = slice(i * BLOCK, (i + 1) * BLOCK)
        columns = slice(first * BLOCK, last * BLOCK)
        offset = (first - i + reach + 1) * BLOCK
        band_ref[rows, columns] = (
            shifted[:, offset : offset + (last - first) * BLOCK] * mask_ref[rows, columns]
        )


def conv_forward_kernel(
    unroll, channels, reach, column_ref, row_ref, cond_ref, base_ref, shift_ref, values_ref,
    conv_ref, mask_ref, taps_ref, band_ref,
):
    length = row_ref.shape[1]
    filters = base_ref.shape[0]
    mask_ref[...] = (column_ref[...] == row_ref[...]).astype(BF)
    taps_ref[...] = base_ref[...].astype(F32) + cond_ref[...] * shift_ref[...].astype(F32)
    band_ref[...] = jnp.zeros_like(band_ref)

    def some(step, carry):
        for u in range(unroll):
            f = step * unroll + u
            build_band(taps_ref[pl.ds(f, 1), :], mask_ref, band_ref.at[u], length, reach)
            rows = pl.ds(pl.multiple_of(f * channels, channels), channels)
            conv_ref[rows, :] = jnp.dot(
                values_ref[rows, :], band_ref[u], preferred_element_type=F32
            )
        return carry

    lax.fori_loop(0, filters // unroll, some, 0)


def conv_forward(segments, cond, base, shift, values, unroll=8):
    filters, length = base.shape[0], segments.shape[0]
    channels = values.shape[0] // filters
    unroll = next(u for u in range(unroll, 0, -1) if filters % u == 0)
    vmem = pl.BlockSpec(memory_space=pltpu.VMEM)
    flops = 2 * values.shape[0] * length * length
    return pl.pallas_call(
        functools.partial(conv_forward_kernel, unroll, channels, SENTENCE // BLOCK),
        out_shape=jax.ShapeDtypeStruct(values.shape, F32),
        in_specs=[vmem] * 6,
        out_specs=vmem,
        scratch_shapes=[
            pltpu.VMEM((length, length), BF),
            pltpu.VMEM(base.shape, F32),
            pltpu.VMEM((unroll, length, length), BF),
        ],
        compiler_params=pltpu.CompilerParams(vmem_limit_bytes=40 << 20),
        cost_estimate=pl.CostEstimate(
            flops=flops * 16, bytes_accessed=values.size * 6, transcendentals=0
        ),
        name="conv_forward",
    )(segments[:, None], segments[None, :], cond[:, None], base, shift, values)


def conv_backward_kernel(
    unroll, channels, reach, column_ref, turned_ref, row_ref, cond_ref, base_ref, shift_ref,
    values_ref, grad_ref, grad_values_ref, grad_taps_ref, mask_ref, mask_turned_ref, taps_ref,
    band_ref, grad_turned_ref,
):
    length = row_ref.shape[1]
    filters = base_ref.shape[0]
    blocks = length // BLOCK
    mask_ref[...] = (column_ref[...] == row_ref[...]).astype(BF)
    mask_turned_ref[...] = (turned_ref[...] == row_ref[...]).astype(F32)
    taps_ref[...] = base_ref[...].astype(F32) + cond_ref[...] * shift_ref[...].astype(F32)
    band_ref[...] = jnp.zeros_like(band_ref)
    turn = (
        lax.broadcasted_iota(jnp.int32, (length, length), 0)
        + lax.broadcasted_iota(jnp.int32, (length, length), 1)
        == length - 1
    ).astype(BF)
    grad_turned_ref[...] = jnp.dot(grad_ref[...], turn, preferred_element_type=F32)

    def some(step, carry):
        for u in range(unroll):
            f = step * unroll + u
            build_band(taps_ref[pl.ds(f, 1), :], mask_ref, band_ref.at[u], length, reach)
            rows = pl.ds(pl.multiple_of(f * channels, channels), channels)
            grad_values_ref[rows, :] = jnp.dot(
                grad_ref[rows, :], band_ref[u], preferred_element_type=F32
            ).astype(BF)
            turned = grad_turned_ref[rows, :].T.astype(BF)
            product = jnp.dot(turned, values_ref[rows, :], preferred_element_type=F32)
            parts = [jnp.zeros((BLOCK, BLOCK), F32)] + [None] * (2 * reach + 1)
            for i in range(blocks):
                back = blocks - 1 - i
                for j in range(max(0, back - reach), min(blocks, back + reach + 1)):
                    here = (
                        slice(i * BLOCK, (i + 1) * BLOCK),
                        slice(j * BLOCK, (j + 1) * BLOCK),
                    )
                    block = product[here] * mask_turned_ref[here]
                    d = j - back + reach + 1
                    parts[d] = block if parts[d] is None else parts[d] + block
            aligned = pltpu.roll(jnp.concatenate(parts, axis=1), 0, 1, stride=1, stride_axis=0)
            grad_taps_ref[pl.ds(f, 1), :] = jnp.sum(aligned, axis=0, keepdims=True)
        return carry

    lax.fori_loop(0, filters // unroll, some, 0)


def conv_backward(segments, cond, base_turned, shift_turned, values, grad, unroll=4):
    filters, length = base_turned.shape[0], segments.shape[0]
    channels = values.shape[0] // filters
    reach = SENTENCE // BLOCK
    width = (2 * reach + 2) * BLOCK
    unroll = next(u for u in range(unroll, 0, -1) if filters % u == 0)
    vmem = pl.BlockSpec(memory_space=pltpu.VMEM)
    flops = 2 * values.shape[0] * length * length
    grad_values, grad_taps = pl.pallas_call(
        functools.partial(conv_backward_kernel, unroll, channels, reach),
        out_shape=(
            jax.ShapeDtypeStruct(values.shape, BF),
            jax.ShapeDtypeStruct((filters, width), F32),
        ),
        in_specs=[vmem] * 8,
        out_specs=(vmem, vmem),
        scratch_shapes=[
            pltpu.VMEM((length, length), BF),
            pltpu.VMEM((length, length), F32),
            pltpu.VMEM(base_turned.shape, F32),
            pltpu.VMEM((unroll, length, length), BF),
            pltpu.VMEM(values.shape, F32),
        ],
        compiler_params=pltpu.CompilerParams(vmem_limit_bytes=48 << 20),
        cost_estimate=pl.CostEstimate(
            flops=flops * 32, bytes_accessed=values.size * 6, transcendentals=0
        ),
        name="conv_backward",
    )(
        segments[:, None],
        segments[::-1][:, None],
        segments[None, :],
        cond[:, None],
        base_turned,
        shift_turned,
        values,
        grad,
    )
    lags = jnp.roll(grad_taps, -(BLOCK - 1), axis=1)[:, ::-1]
    start = length + (reach + 1) * BLOCK - (width - 1)
    full = jnp.pad(lags, ((0, 0), (start, 2 * length - start - width + 1)))
    return grad_values, full[:, : 2 * length]


def swap(value, axis, mask):
    return lax.ppermute(value, axis, [(i, i ^ mask) for i in range(lax.axis_size(axis))])


def bits_of(count):
    return [1 << b for b in range(count.bit_length() - 1)]


def gather_dp(block):
    bits = bits_of(lax.axis_size("dp"))
    half = block.shape[1] // 2
    found = []
    for part, order in ((block[:, :half], bits), (block[:, half:], bits[::-1])):
        held, masks = part[None], [0]
        for bit in order:
            held = jnp.concatenate([held, swap(held, "dp", bit)], axis=0)
            masks = masks + [m | bit for m in masks]
        found.append({m: held[i] for i, m in enumerate(masks)})
    return [jnp.concatenate([f[m] for f in found], axis=1) for m in range(lax.axis_size("dp"))]


def natural(pieces, me):
    held = jnp.stack(pieces)
    return jnp.concatenate(
        [lax.dynamic_index_in_dim(held, j ^ me, 0, keepdims=False) for j in range(len(pieces))],
        axis=1,
    )


def scatter_dp(pieces):
    bits = bits_of(lax.axis_size("dp"))
    half = pieces[0].shape[1] // 2
    done = []
    for part, order in ((slice(None, half), bits[::-1]), (slice(half, None), bits)):
        held = {m: p[:, part] for m, p in enumerate(pieces)}
        for bit in order:
            stay = [m for m in held if not m & bit]
            got = swap(jnp.stack([held[m | bit] for m in stay]), "dp", bit)
            held = {m: held[m] + got[i] for i, m in enumerate(stay)}
        done.append(held[0])
    return jnp.concatenate(done, axis=1)


def everywhere(value):
    for bit in bits_of(lax.axis_size("mp")):
        value = value + swap(value, "mp", bit)
    for bit in bits_of(lax.axis_size("dp")):
        value = value + swap(value, "dp", bit)
    return value


def statistics(value):
    centred = value - jnp.mean(value, axis=-1, keepdims=True)
    scale = lax.rsqrt(jnp.mean(centred * centred, axis=-1, keepdims=True) + epsilon)
    return centred * scale, scale


def normalize_back(normal, scale, gain, grad):
    scaled = grad * gain
    return scale * (
        scaled
        - jnp.mean(scaled, axis=-1, keepdims=True)
        - normal * jnp.mean(scaled * normal, axis=-1, keepdims=True)
    )


def mm(left, right, dims):
    return lax.dot_general(left, right, (dims, ((), ())), preferred_element_type=F32)


def body(
    tokens, segment_ids, gain_one, gain_two, value_weight, mixgate_weight, condition_weight,
    filter_base, filter_shift, mixout_weight, gate_weight, up_weight, down_weight, output_grad,
):
    dp_size, mp_size = lax.axis_size("dp"), lax.axis_size("mp")
    dp, mp = lax.axis_index("dp"), lax.axis_index("mp")
    core = mp & 1
    chips = mp_size // 2
    local, width = tokens.shape
    length = segment_ids.shape[1]
    whole_rows = local % length == 0
    total = 2 * local
    rows = total // length

    def pair(own, other):
        if whole_rows:
            return jnp.concatenate([own, other], axis=0)
        first = core == 0
        return jnp.concatenate([jnp.where(first, own, other), jnp.where(first, other, own)], axis=0)

    def mine(value):
        return value[:local] if whole_rows else lax.dynamic_slice_in_dim(value, core * local, local)

    def others(value):
        if whole_rows:
            return value[local:]
        return lax.dynamic_slice_in_dim(value, (1 - core) * local, local)

    def pair_sum(value):
        got = swap(value, "mp", 1)
        if whole_rows:
            got = jnp.concatenate([got[local:], got[:local]], axis=0)
        return value.astype(F32) + got.astype(F32)

    def pair_scatter(value):
        return mine(value) + swap(others(value).astype(BF), "mp", 1).astype(F32)

    block_c = value_weight.shape[1]
    block_g = condition_weight.shape[1]
    block_f = gate_weight.shape[1]
    taps = filter_base.shape[1]
    mixer_pack = jnp.stack([value_weight, mixgate_weight, mixout_weight.T])
    filter_pack = jnp.stack([filter_base.T, filter_shift.T])
    ffn_pack = jnp.stack([gate_weight, up_weight, down_weight.T])

    tokens_all = pair(tokens, swap(tokens, "mp", 1))
    grad_all = pair(output_grad, swap(output_grad, "mp", 1))
    if whole_rows:
        per = local // length
        seg_rows = jnp.concatenate(
            [
                lax.dynamic_slice_in_dim(segment_ids, mp * per, per),
                lax.dynamic_slice_in_dim(segment_ids, (mp ^ 1) * per, per),
            ]
        )
    else:
        seg_rows = lax.dynamic_slice_in_dim(segment_ids, (mp // 2) * rows, rows)

    def gather(block):
        found = [block] + [swap(block, "mp", 2 * k) for k in range(1, chips)]
        return [natural(gather_dp(b), dp) for b in found]

    mixer = jnp.concatenate(gather(mixer_pack), axis=2)
    small = jnp.concatenate(gather(jnp.pad(condition_weight, ((0, 0), (0, 0)))[None]), axis=2)[0]
    filters = jnp.concatenate(gather(filter_pack), axis=2)
    ffn = gather(ffn_pack)
    value_full, mixgate_full, mixout_full = mixer
    base, shift = jnp.swapaxes(filters, 1, 2)
    base_turned = jnp.roll(base[:, ::-1], 1, axis=1)
    shift_turned = jnp.roll(shift[:, ::-1], 1, axis=1)

    xf = tokens_all.astype(F32)
    normal_one, scale_one = statistics(xf)
    normed_one = (normal_one * gain_one).astype(BF)
    values = mm(value_full, normed_one, ((0,), (1,))).astype(BF)
    gates = mm(mixgate_full, normed_one, ((0,), (1,)))
    summary = jnp.mean(normed_one.astype(F32).reshape(rows, length, width), axis=1)
    condition = small.astype(F32)
    cond = jnp.tanh(jnp.dot(summary, condition, precision=highest))
    cuts = [slice(r * length, (r + 1) * length) for r in range(rows)]
    conv = jnp.concatenate(
        [conv_forward(seg_rows[r], cond[r], base, shift, values[:, cuts[r]]) for r in range(rows)],
        axis=1,
    )
    mixed = (conv * gates).astype(BF)
    branch = pair_sum(mm(mixed, mixout_full, ((0,), (1,))).astype(BF))
    middle = xf + branch
    normal_two, scale_two = statistics(middle)
    normed_two = (normal_two * gain_two).astype(BF)

    feed = jnp.zeros((total, width), F32)
    grad_two = jnp.zeros((total, width), F32)
    ffn_grads = []
    for k in range(chips):
        gate_full, up_full, down_full = ffn[k]
        gate_pre = mm(normed_two, gate_full, ((1,), (0,)))
        up_pre = mm(normed_two, up_full, ((1,), (0,)))
        grad_hidden = mm(grad_all, down_full, ((1,), (0,)))
        sigmoid = jax.nn.sigmoid(gate_pre)
        silu = gate_pre * sigmoid
        hidden = (silu * up_pre).astype(BF)
        grad_gate = (grad_hidden * up_pre * (sigmoid + silu * (1.0 - sigmoid))).astype(BF)
        grad_up = (grad_hidden * silu).astype(BF)
        feed = feed + mm(hidden, down_full, ((1,), (1,)))
        grad_two = (
            grad_two + mm(grad_gate, gate_full, ((1,), (1,))) + mm(grad_up, up_full, ((1,), (1,)))
        )
        ffn_grads.append(
            jnp.stack(
                [
                    mm(normed_two, grad_gate, ((0,), (0,))).astype(BF),
                    mm(normed_two, grad_up, ((0,), (0,))).astype(BF),
                    mm(grad_all, hidden, ((0,), (0,))).astype(BF),
                ]
            )
        )

    def scatter(grads):
        sums = None
        for k, grad in enumerate(grads):
            size = grad.shape[1] // dp_size
            pieces = [
                lax.dynamic_slice_in_dim(grad, (dp ^ m) * size, size, axis=1)
                for m in range(dp_size)
            ]
            part = scatter_dp(pieces)
            part = part if k == 0 else swap(part, "mp", 2 * k)
            sums = part.astype(F32) if sums is None else sums + part.astype(F32)
        return sums

    gate_sum, up_sum, down_sum = scatter(ffn_grads)
    output = (mine(middle) + pair_scatter(feed)).astype(BF)

    grad_normed_two = pair_sum(grad_two.astype(BF))
    gain_two_part = jnp.sum(mine(grad_normed_two * normal_two), axis=0)
    grad_middle = grad_all.astype(F32) + normalize_back(
        normal_two, scale_two, gain_two, grad_normed_two
    )
    grad_branch = grad_middle.astype(BF)

    mixout_grad = mm(grad_branch, mixed, ((0,), (1,)))
    grad_mixed = mm(mixout_full, grad_branch, ((0,), (1,)))
    grad_conv = (grad_mixed * gates).astype(BF)
    grad_gates = (grad_mixed * conv).astype(BF)
    backs = [
        conv_backward(
            seg_rows[r], cond[r], base_turned, shift_turned, values[:, cuts[r]],
            grad_conv[:, cuts[r]],
        )
        for r in range(rows)
    ]
    grad_values = jnp.concatenate([b[0] for b in backs], axis=1)
    grad_taps = jnp.stack([b[1] for b in backs])
    base_grad = jnp.sum(grad_taps, axis=0)
    shift_grad = jnp.sum(grad_taps * cond[:, :, None], axis=0)
    grad_cond = jnp.sum(grad_taps * shift.astype(F32)[None], axis=2) * (1.0 - cond * cond)
    condition_grad = mm(summary, grad_cond, ((0,), (0,)))
    grad_summary = jnp.dot(grad_cond, condition.T, precision=highest) / length
    value_grad = mm(normed_one, grad_values, ((0,), (1,)))
    mixgate_grad = mm(normed_one, grad_gates, ((0,), (1,)))
    grad_one = mm(grad_values, value_full, ((0,), (1,))) + mm(
        grad_gates, mixgate_full, ((0,), (1,))
    )
    grad_one = (grad_one.reshape(rows, length, width) + grad_summary[:, None, :]).reshape(
        total, width
    )
    grad_normed_one = pair_scatter(grad_one)
    input_grad = (
        mine(grad_middle)
        + normalize_back(mine(normal_one), mine(scale_one), gain_one, grad_normed_one)
    ).astype(BF)
    gain_one_part = jnp.sum(grad_normed_one * mine(normal_one), axis=0)
    gain_one_grad, gain_two_grad = everywhere(jnp.stack([gain_one_part, gain_two_part]))

    def split(grad, size):
        return [grad[..., k * size : (k + 1) * size].astype(BF) for k in range(chips)]

    value_sum, mixgate_sum, mixout_sum = scatter(
        split(jnp.stack([value_grad, mixgate_grad, mixout_grad]), block_c)
    )
    condition_sum = scatter(split(condition_grad[None], block_g))[0]
    base_sum, shift_sum = scatter(
        split(jnp.swapaxes(jnp.stack([base_grad, shift_grad]), 1, 2), block_g)
    )
    return (
        output, input_grad, gain_one_grad, gain_two_grad, value_sum, mixgate_sum, condition_sum,
        base_sum.T, shift_sum.T, mixout_sum.T, gate_sum, up_sum, down_sum.T,
    )


def hold(count):
    return [pl.BlockSpec(memory_space=pltpu.VMEM)] * count


def shaped(*shape, dtype=BF):
    return jax.ShapeDtypeStruct(shape, dtype)


def kernel_call(body, name, outs, scratch, args, flops, transcendentals=0, scalars=0, limit=16):
    held = sum(a.size * a.dtype.itemsize for a in tuple(args) + tuple(outs))
    smem = [pl.BlockSpec(memory_space=pltpu.SMEM)] * scalars
    return pl.pallas_call(
        body,
        out_shape=tuple(outs),
        in_specs=smem + hold(len(args) - scalars),
        out_specs=tuple(hold(len(outs))),
        scratch_shapes=scratch,
        compiler_params=pltpu.CompilerParams(vmem_limit_bytes=limit << 20),
        cost_estimate=pl.CostEstimate(
            flops=int(flops), bytes_accessed=int(held), transcendentals=transcendentals
        ),
        name=name,
    )(*args)


def nn(left, right):
    return lax.dot_general(left, right, (((1,), (0,)), ((), ())), preferred_element_type=F32)


def nt(left, right):
    return lax.dot_general(left, right, (((1,), (1,)), ((), ())), preferred_element_type=F32)


def turned_over(value):
    return value.astype(F32).T


def fold(value):
    rows = value.shape[0] // 2
    return jnp.concatenate([value[:rows], value[rows:]], axis=1)


def pack_kernel(
    value_ref, mixgate_ref, condition_ref, base_ref, shift_ref, mixout_ref, gate_ref, up_ref,
    down_ref, mixer_ref, ffn_ref,
):
    depth, block_c = value_ref.shape
    block_g = condition_ref.shape[0]
    span = base_ref.shape[1] // 128
    spare = 128 - block_c
    mixgate = mixgate_ref[...].astype(F32)
    mixout = turned_over(mixout_ref[...])
    first = jnp.concatenate([value_ref[...].astype(F32), mixgate[:, :spare]], axis=1)
    second = jnp.concatenate([mixgate[:, spare:], mixout[:, : 2 * spare]], axis=1)
    condition = jnp.concatenate(
        [condition_ref[...].astype(F32), jnp.zeros((spare - block_g, depth), F32)], axis=0
    )
    third = jnp.concatenate([mixout[:, 2 * spare :], condition.T], axis=1)
    half = mixer_ref.shape[1]
    cut = half - depth
    mixer_ref[0, :depth, :] = first.astype(BF)
    mixer_ref[0, depth:, :] = second[:cut].astype(BF)
    mixer_ref[1, : depth - cut, :] = second[cut:].astype(BF)
    start = depth - cut + depth // 2
    mixer_ref[1, depth - cut : start, :] = fold(third).astype(BF)
    blank = jnp.zeros((16 - span * block_g, 128), F32)
    for ref in (base_ref, shift_ref):
        pieces = [ref[:, h * 128 : (h + 1) * 128].astype(F32) for h in range(span)] + [blank]
        mixer_ref[1, start : start + 16, :] = jnp.concatenate(pieces, axis=0).astype(BF)
        start += 16
    part = ffn_ref.shape[2]
    for h in range(2):
        cut = slice(h * part, (h + 1) * part)
        ffn_ref[h, 0] = gate_ref[cut, :]
        ffn_ref[h, 1] = up_ref[cut, :]
        ffn_ref[h, 2] = down_ref[cut, :]


def norm_rows(value, gain):
    centred = value - jnp.mean(value, axis=-1, keepdims=True)
    scale = lax.rsqrt(jnp.mean(centred * centred, axis=-1, keepdims=True) + epsilon)
    normal = centred * scale
    return normal, scale, normal * gain


def column_of(row):
    return jnp.broadcast_to(row.astype(F32), (8, row.shape[1])).T[:, :1]


def mixer_forward_kernel(
    sizes, dp_ref, row_ref, own_ref, other_ref, gain_ref, p0_ref, p1_ref, p2_ref,
    p3a_ref, p3b_ref, branch_ref, values_0, values_1, gates_0, gates_1, conv_0, conv_1,
    weights_ref, mixout_ref, condition_ref, taps_0, taps_1, shift_out_ref, cond_ref, summary_ref,
    one_ref, two_ref, three_ref, base_ref, mask_ref, band_ref, mixed_ref,
):
    depth, block_c, block_g, chips, span, unroll, channels, reach, half = sizes
    length = own_ref.shape[0]
    values_refs, gates_refs = (values_0, values_1), (gates_0, gates_1)
    conv_refs, taps_refs = (conv_0, conv_1), (taps_0, taps_1)
    dp = dp_ref[0]
    pieces = ((p0_ref, None), (p1_ref, None), (p2_ref, None), (p3a_ref, p3b_ref))
    side = chips * block_c
    spare, cut = 128 - block_c, half - depth
    filters = chips * block_g

    for k in range(chips):
        for m, (first, second) in enumerate(pieces):
            low = first.at[0, k] if second is None else first.at[k]
            high = first.at[1, k] if second is None else second.at[k]
            j = dp ^ m
            at = pl.multiple_of(j * depth, depth)
            one_ref[pl.ds(at, depth), :] = low[:depth, :]
            two_ref[pl.ds(at, cut), :] = low[depth:, :]
            two_ref[pl.ds(pl.multiple_of(at + cut, cut), depth - cut), :] = high[: depth - cut, :]
            start = depth - cut + depth // 2
            folded = high[depth - cut : start, :]
            three_ref[pl.ds(at, depth // 2), :] = folded
            three_ref[pl.ds(pl.multiple_of(at + depth // 2, depth // 2), depth // 2), :] = (
                jnp.concatenate([folded[:, 64:], folded[:, :64]], axis=1)
            )
            for ref in (base_ref, shift_out_ref):
                piece = high[start : start + 16, :].astype(F32)
                start += 16
                for h in range(span):
                    lane = pl.multiple_of((j * span + h) * 128, 128)
                    ref[k * block_g : (k + 1) * block_g, pl.ds(lane, 128)] = piece[
                        h * block_g : (h + 1) * block_g
                    ]
        here, there = k * block_c, side + k * block_c
        turned = turned_over(one_ref[...]).astype(BF)
        weights_ref[here : here + block_c, :] = turned[:block_c]
        weights_ref[there : there + spare, :] = turned[block_c:]
        turned = turned_over(two_ref[...]).astype(BF)
        weights_ref[there + spare : there + block_c, :] = turned[: block_c - spare]
        mixout_ref[here : here + 2 * spare, :] = turned[block_c - spare :]
        turned = turned_over(three_ref[...]).astype(BF)
        mixout_ref[here + 2 * spare : here + block_c, :] = turned[:spare]
        condition_ref[k * block_g : (k + 1) * block_g, :] = turned[spare : 2 * spare].astype(F32)[
            :block_g
        ]

    band_ref[...] = jnp.zeros_like(band_ref)
    for r, ref in enumerate((own_ref, other_ref)):
        _, _, normed = norm_rows(ref[...].astype(F32), gain_ref[...])
        normed = normed.astype(BF)
        summary = jnp.mean(normed.astype(F32), axis=0, keepdims=True)
        summary_ref[r : r + 1, :] = summary
        cond = jnp.tanh(jnp.sum(condition_ref[...] * summary, axis=1, keepdims=True))
        cond_ref[r] = jnp.broadcast_to(cond, cond_ref.shape[1:])
        taps_refs[r][...] = base_ref[...] + cond * shift_out_ref[...]
        values_refs[r][...] = nt(weights_ref[:side, :], normed).astype(BF)
        gates_refs[r][...] = nt(weights_ref[side:, :], normed).astype(BF)
        ids = row_ref[r : r + 1, :]
        mask_ref[...] = (column_of(ids) == ids.astype(F32)).astype(BF)

        def some(step, carry, r=r):
            for u in range(unroll):
                f = step * unroll + u
                build_band(taps_refs[r][pl.ds(f, 1), :], mask_ref, band_ref.at[u], length, reach)
                at = pl.ds(pl.multiple_of(f * channels, channels), channels)
                conv = nn(values_refs[r][at, :], band_ref[u])
                conv_refs[r][at, :] = conv.astype(BF)
                mixed_ref[at, :] = (conv * gates_refs[r][at, :].astype(F32)).astype(BF)
            return carry

        lax.fori_loop(0, filters // unroll, some, 0)
        branch_ref[r * length : (r + 1) * length, :] = nn(
            mixed_ref[...].T, mixout_ref[...]
        ).astype(BF)


def norm_two_kernel(
    own_ref, other_ref, branch_ref, got_ref, gain_ref, normed_ref, normed_turned_ref,
):
    local = own_ref.shape[0]
    for h, ref in enumerate((own_ref, other_ref)):
        here, there = slice(h * local, (h + 1) * local), slice((1 - h) * local, (2 - h) * local)
        middle = (
            ref[...].astype(F32) + branch_ref[here, :].astype(F32) + got_ref[there, :].astype(F32)
        )
        _, _, normed = norm_rows(middle, gain_ref[...])
        normed = normed.astype(BF)
        normed_ref[here, :] = normed
        normed_turned_ref[:, here] = normed.T


def turn_kernel(own_ref, other_ref, turned_ref):
    local = own_ref.shape[0]
    turned_ref[:, :local] = own_ref[...].T
    turned_ref[:, local:] = other_ref[...].T


def ffn_kernel(
    carried, kept, apart, dp_ref, normed_ref, normed_turned_ref, grad_own_ref, grad_other_ref,
    grad_turned_ref, p0_ref, p1_ref, p2_ref, p3a_ref, p3b_ref, *refs,
):
    before, refs = refs[: 3 * carried], refs[3 * carried :]
    pieces_count = 8 if apart else 6
    kept_refs, refs = refs[: pieces_count * kept], refs[pieces_count * kept :]
    feed_own_ref, feed_other_ref, back_ref, g0a, g0b, g1a, g2b = refs[:7]
    moving, refs = refs[7 : 3 + pieces_count], refs[3 + pieces_count :]
    two_ref, down_ref, hidden_ref, act_ref, two_grad_ref, down_grad_ref = refs
    local = grad_own_ref.shape[0]
    _, _, part, block = g0a.shape
    dp = dp_ref[0]
    pieces = ((p0_ref, None), (p1_ref, None), (p2_ref, None), (p3a_ref, p3b_ref))
    if apart:
        g1b, g2a, g3a, g3b = moving
    else:
        gx, gy = moving
        g1b, g2a, g3a, g3b = gx.at[0], gy.at[0], gy.at[1], gx.at[1]
    outs = ((g0a, g0b), (g1a, g1b), (g2a, g2b), (g3a, g3b))
    for m, (one, two) in enumerate(pieces):
        for h in range(2):
            source = one.at[h, 0] if two is None else (one, two)[h].at[0]
            at = pl.ds(pl.multiple_of((dp ^ m) * (2 * part) + h * part, part), part)
            two_ref[at, :block] = source[0]
            two_ref[at, block:] = source[1]
            down_ref[at, :] = source[2]
    for t, (grad_ref, feed_ref) in enumerate(
        ((grad_own_ref, feed_own_ref), (grad_other_ref, feed_other_ref))
    ):
        here = slice(t * local, (t + 1) * local)
        both = nn(normed_ref[here, :], two_ref[...])
        gate_pre, up_pre = both[:, :block], both[:, block:]
        grad_hidden = nn(grad_ref[...], down_ref[...])
        sigmoid = 1.0 / (1.0 + jnp.exp(-gate_pre))
        silu = gate_pre * sigmoid
        hidden = (silu * up_pre).astype(BF)
        hidden_ref[here, :] = hidden
        act_ref[here, :block] = (
            grad_hidden * up_pre * (sigmoid + silu * (1.0 - sigmoid))
        ).astype(BF)
        act_ref[here, block:] = (grad_hidden * silu).astype(BF)
        feed = nt(hidden, down_ref[...])
        back = nt(act_ref[here, :], two_ref[...])
        if carried:
            feed = feed + before[t][...]
            back = back + before[2][here, :]
        feed_ref[...] = feed.astype(feed_ref.dtype)
        back_ref[here, :] = back.astype(back_ref.dtype)
    two_grad_ref[...] = nn(normed_turned_ref[...], act_ref[...]).astype(BF)
    down_grad_ref[...] = nn(grad_turned_ref[...], hidden_ref[...]).astype(BF)
    if kept:
        for source, target in zip(kept_refs, (g0a, g0b, g1a, g2b) + tuple(moving)):
            if len(target.shape) == 4:
                target[0] = source[0]
            else:
                target[:, 0] = source[:, 0]
    for m, pair in enumerate(outs):
        for h in range(2):
            at = pl.ds(pl.multiple_of((dp ^ m) * (2 * part) + h * part, part), part)
            pair[h][int(kept), 0] = two_grad_ref[at, :block]
            pair[h][int(kept), 1] = two_grad_ref[at, block:]
            pair[h][int(kept), 2] = down_grad_ref[at, :]


def ffn_call(fixed, group, before=(), kept=(), last=False, apart=False):
    total, width = fixed[1].shape
    local = fixed[3].shape[0]
    _, _, _, part, block = group[0].shape
    count, kind = 1 + bool(kept), BF if last else F32
    outs = [
        shaped(local, width, dtype=kind), shaped(local, width, dtype=kind),
        shaped(total, width, dtype=kind),
    ]
    if apart:
        outs += [shaped(count, 3, part, block)] * 8
    else:
        outs += [shaped(count, 3, part, block)] * 4 + [shaped(2, count, 3, part, block)] * 2
    return kernel_call(
        functools.partial(ffn_kernel, bool(before), bool(kept), apart), "feed_forward", outs,
        [
            pltpu.VMEM((width, 2 * block), BF), pltpu.VMEM((width, block), BF),
            pltpu.VMEM((total, block), BF), pltpu.VMEM((total, 2 * block), BF),
            pltpu.VMEM((width, 2 * block), BF), pltpu.VMEM((width, block), BF),
        ],
        fixed + tuple(group) + tuple(before) + tuple(kept),
        18 * total * width * block, transcendentals=total * block, scalars=1,
    )


def mixout_back_kernel(
    own_ref, other_ref, branch_ref, got_ref, back_ref, back_got_ref, grad_own_ref, grad_other_ref,
    gain_ref, weights_ref, gates_0, gates_1, conv_0, conv_1, middle_ref, mixout_ref, grad_conv_0,
    grad_conv_1, grad_gates_0, grad_gates_1, gain_grad_ref,
):
    local = own_ref.shape[0]
    mixout = None
    for h, (ref, grad_ref, gates_ref, conv_ref, grad_conv_ref, grad_gates_ref) in enumerate(
        (
            (own_ref, grad_own_ref, gates_0, conv_0, grad_conv_0, grad_gates_0),
            (other_ref, grad_other_ref, gates_1, conv_1, grad_conv_1, grad_gates_1),
        )
    ):
        here, there = slice(h * local, (h + 1) * local), slice((1 - h) * local, (2 - h) * local)
        middle = (
            ref[...].astype(F32) + branch_ref[here, :].astype(F32) + got_ref[there, :].astype(F32)
        )
        normal, scale, _ = norm_rows(middle, gain_ref[...])
        grad = back_ref[here, :].astype(F32) + back_got_ref[there, :].astype(F32)
        grad_middle = grad_ref[...].astype(F32) + normalize_back(
            normal, scale, gain_ref[...], grad
        )
        if h == 0:
            gain_grad_ref[...] = jnp.sum(grad * normal, axis=0, keepdims=True)
            middle_ref[...] = grad_middle
        rounded = grad_middle.astype(BF)
        grad_mixed = nt(weights_ref[...], rounded)
        gates, conv = gates_ref[...].astype(F32), conv_ref[...].astype(F32)
        grad_conv_ref[...] = (grad_mixed * gates).astype(BF)
        grad_gates_ref[...] = (grad_mixed * conv).astype(BF)
        part = nn((gates * conv).astype(BF), rounded)
        mixout = part if h == 0 else mixout + part
    mixout_ref[...] = mixout.astype(BF)


def conv_back_kernel(
    unroll, channels, reach, r, row_ref, taps_ref, values_ref, grad_ref, grad_values_ref,
    grad_taps_ref, mask_ref, mask_turned_ref, band_ref, grad_turned_ref,
):
    length = row_ref.shape[1]
    filters = taps_ref.shape[0]
    blocks = length // BLOCK
    ids = row_ref[r : r + 1, :]
    mask_ref[...] = (column_of(ids) == ids.astype(F32)).astype(BF)
    band_ref[...] = jnp.zeros_like(band_ref)
    turn = (
        lax.broadcasted_iota(jnp.int32, (length, length), 0)
        + lax.broadcasted_iota(jnp.int32, (length, length), 1)
        == length - 1
    ).astype(BF)
    grad_turned_ref[...] = nn(grad_ref[...], turn)
    mask_turned_ref[...] = nn(turn, mask_ref[...])

    def some(step, carry):
        for u in range(unroll):
            f = step * unroll + u
            build_band(taps_ref[pl.ds(f, 1), :], mask_ref, band_ref.at[u], length, reach)
            rows = pl.ds(pl.multiple_of(f * channels, channels), channels)
            grad_values_ref[rows, :] = nt(grad_ref[rows, :], band_ref[u]).astype(BF)
            turned = grad_turned_ref[rows, :].T.astype(BF)
            product = nn(turned, values_ref[rows, :])
            parts = [jnp.zeros((BLOCK, BLOCK), F32)] + [None] * (2 * reach + 1)
            for i in range(blocks):
                back = blocks - 1 - i
                for j in range(max(0, back - reach), min(blocks, back + reach + 1)):
                    here = (
                        slice(i * BLOCK, (i + 1) * BLOCK),
                        slice(j * BLOCK, (j + 1) * BLOCK),
                    )
                    block = product[here] * mask_turned_ref[here]
                    d = j - back + reach + 1
                    parts[d] = block if parts[d] is None else parts[d] + block
            aligned = pltpu.roll(jnp.concatenate(parts, axis=1), 0, 1, stride=1, stride_axis=0)
            grad_taps_ref[pl.ds(f, 1), :] = jnp.sum(aligned, axis=0, keepdims=True)
        return carry

    lax.fori_loop(0, filters // unroll, some, 0)


def mixer_back_kernel(
    sizes, dp_ref, own_ref, other_ref, gain_ref, gain_two_ref, gates_0, gates_1, mixout_ref,
    weights_ref, condition_ref, shift_ref, cond_ref, summary_ref, values_0, values_1, taps_0,
    taps_1, back_own_ref, back_other_ref, g0a_ref, g0b_ref, g1a_ref, g2b_ref, gx_ref, gy_ref,
    one_ref, two_ref, three_ref, filter_ref,
):
    depth, block_c, block_g, chips, span, unroll, channels, reach, half = sizes
    length = own_ref.shape[0]
    side = chips * block_c
    filters = chips * block_g
    width = taps_0.shape[1]
    taps = shift_ref.shape[1]
    spare, cut = 128 - block_c, half - depth
    dp = dp_ref[0]
    lane = lax.broadcasted_iota(jnp.int32, (width, taps), 0)
    tap = lax.broadcasted_iota(jnp.int32, (width, taps), 1)
    reachable = (tap > taps // 2 - (reach + 1) * BLOCK) & (tap < taps // 2 + (reach + 1) * BLOCK)
    spot = taps - 1 - tap
    spot = jnp.where(spot >= width, spot - width, spot)
    place = ((lane == spot) & reachable).astype(BF)
    shift_there = nt(shift_ref[...].astype(BF), place)
    base_grad = shift_grad = condition_grad = value_grad = gate_grad = gain_grad = None
    for r, (ref, values_ref, gates_ref, taps_ref, back_ref) in enumerate(
        (
            (own_ref, values_0, gates_0, taps_0, back_own_ref),
            (other_ref, values_1, gates_1, taps_1, back_other_ref),
        )
    ):
        normal, _, normed = norm_rows(ref[...].astype(F32), gain_ref[...])
        normed = normed.astype(BF)
        grad_taps = taps_ref[...]
        cond = cond_ref[r, :, :1]
        summary = summary_ref[r : r + 1, :]
        grad_cond = jnp.sum(grad_taps * shift_there, axis=1, keepdims=True) * (1.0 - cond * cond)
        grad_summary = jnp.sum(grad_cond * condition_ref[...], axis=0, keepdims=True) / length
        values, gates = values_ref[...], gates_ref[...]
        back = nn(values.T, weights_ref[:side, :]) + nn(gates.T, weights_ref[side:, :])
        back = back + grad_summary
        back_ref[...] = back.astype(BF)
        parts = (
            grad_taps, cond * grad_taps, grad_cond * summary, nn(values, normed),
            nn(gates, normed), jnp.sum(back * normal, axis=0, keepdims=True),
        )
        if r > 0:
            parts = tuple(
                p + q
                for p, q in zip(
                    (base_grad, shift_grad, condition_grad, value_grad, gate_grad, gain_grad), parts
                )
            )
        base_grad, shift_grad, condition_grad, value_grad, gate_grad, gain_grad = parts
    filter_ref[0] = nn(base_grad.astype(BF), place)
    filter_ref[1] = nn(shift_grad.astype(BF), place)
    gain_rows = jnp.concatenate(
        [
            vector[:, h * 128 : (h + 1) * 128]
            for vector in (gain_grad, gain_two_ref[...])
            for h in range(vector.shape[1] // 128)
        ],
        axis=0,
    )
    gain_rows = jnp.concatenate(
        [gain_rows, jnp.zeros((16 - gain_rows.shape[0], 128), F32)], axis=0
    ).astype(BF)
    outs = (
        (g0a_ref, g0b_ref), (g1a_ref, gx_ref.at[0]), (gy_ref.at[0], g2b_ref),
        (gy_ref.at[1], gx_ref.at[1]),
    )
    empty = jnp.zeros((128 - spare - block_g, value_grad.shape[1]), F32)
    blank = jnp.zeros((16 - span * block_g, 128), F32)
    for k in range(chips):
        at = k * block_c
        own = slice(k * block_g, (k + 1) * block_g)
        mixout = mixout_ref[at : at + block_c, :].astype(F32)
        value, gate = value_grad[at : at + block_c], gate_grad[at : at + block_c]
        one_ref[...] = jnp.concatenate([value, gate[:spare]], axis=0).T.astype(BF)
        two_ref[...] = jnp.concatenate([gate[spare:], mixout[: 2 * spare]], axis=0).T.astype(BF)
        third = jnp.concatenate(
            [mixout[2 * spare :], condition_grad[own], empty], axis=0
        ).T
        for j in range(third.shape[0] // depth):
            three_ref[j * (depth // 2) : (j + 1) * (depth // 2), :] = fold(
                third[j * depth : (j + 1) * depth, :64]
            ).astype(BF)
        for m, (low, high) in enumerate(outs):
            j = dp ^ m
            at = pl.multiple_of(j * depth, depth)
            low[k, :depth, :] = one_ref[pl.ds(at, depth), :]
            low[k, depth:, :] = two_ref[pl.ds(at, cut), :]
            high[k, : depth - cut, :] = two_ref[
                pl.ds(pl.multiple_of(at + cut, cut), depth - cut), :
            ]
            start = depth - cut + depth // 2
            high[k, depth - cut : start, :] = three_ref[
                pl.ds(pl.multiple_of(j * (depth // 2), depth // 2), depth // 2), :
            ]
            for n in range(2):
                parts = [
                    filter_ref[n, own, pl.ds(pl.multiple_of((j * span + h) * 128, 128), 128)]
                    for h in range(span)
                ] + [blank]
                high[k, start : start + 16, :] = jnp.concatenate(parts, axis=0).astype(BF)
                start += 16
            high[k, start:, :] = gain_rows


def unpack_kernel(
    half, span, p0_ref, p1_ref, p2_ref, p3_ref, value_ref, mixgate_ref, condition_ref, base_ref,
    shift_ref, mixout_ref, gains_ref,
):
    depth, block_c = value_ref.shape
    block_g = condition_ref.shape[0]
    spare, cut = 128 - block_c, half - depth
    total = p0_ref[...].astype(F32) + p1_ref[...].astype(F32)
    total = total + p2_ref[...].astype(F32) + p3_ref[...].astype(F32)
    first, second = total[:depth], total[depth : 2 * depth]
    start = 2 * depth + depth // 2
    folded = total[2 * depth : start]
    third = jnp.concatenate([folded[:, :64], folded[:, 64:]], axis=0)
    value_ref[...] = first[:, :block_c]
    mixgate_ref[...] = jnp.concatenate([first[:, block_c:], second[:, : block_c - spare]], axis=1)
    mixout_ref[...] = jnp.concatenate(
        [second[:, block_c - spare :], third[:, :spare]], axis=1
    ).T
    condition_ref[...] = third[:, spare:].T[:block_g]
    for ref in (base_ref, shift_ref):
        for h in range(span):
            ref[:, h * 128 : (h + 1) * 128] = total[start + h * block_g : start + (h + 1) * block_g]
        start += 16
    rows = gains_ref.shape[1] // 128
    for g in range(2):
        for h in range(rows):
            at = start + g * rows + h
            gains_ref[g : g + 1, h * 128 : (h + 1) * 128] = total[at : at + 1]


def norm_one_back_kernel(
    own_ref, back_ref, got_ref, middle_ref, gain_ref, grad_ref
):
    normal, scale, _ = norm_rows(own_ref[...].astype(F32), gain_ref[...])
    grad = back_ref[...].astype(F32) + got_ref[...].astype(F32)
    grad_ref[...] = (
        middle_ref[...] + normalize_back(normal, scale, gain_ref[...], grad)
    ).astype(BF)


def stage(*values):
    return lax.optimization_barrier(values)


def sides(column):
    return swap(column, "dp", 1), swap(column, "dp", 2)


def corners(along_x, along_y):
    return swap(along_x[0], "dp", 2), swap(along_y[1], "dp", 1)


def added(*terms):
    return sum(t.astype(F32) for t in terms).astype(BF)


class Scatter:
    def __init__(self, pieces):
        self.g0a, self.g0b, self.g1a, self.g2b, self.gx, self.gy = pieces

    def start(self):
        self.ex, self.ey = swap(self.gx, "dp", 1), swap(self.gy, "dp", 2)

    def middle(self):
        self.f1a = swap(added(self.g1a, self.ey[1]), "dp", 1)
        self.f2b = swap(added(self.g2b, self.ex[1]), "dp", 2)

    def end(self):
        f1a, f2b = self.f1a, self.f2b
        return [
            jnp.concatenate(
                [added(self.g0a[k], f1a[k], self.ey[0][k]), added(self.g0b[k], self.ex[0][k], f2b[k])],
                axis=-2,
            )
            for k in range(self.g0a.shape[0])
        ]


def fast_body(
    tokens, segment_ids, gain_one, gain_two, value_weight, mixgate_weight, condition_weight,
    filter_base, filter_shift, mixout_weight, gate_weight, up_weight, down_weight, output_grad,
):
    dp, mp = lax.axis_index("dp"), lax.axis_index("mp")
    chips = lax.axis_size("mp") // 2
    length, width = tokens.shape
    rows, total = 2, 2 * length
    depth, block_c = value_weight.shape
    block_g, taps = filter_base.shape
    block_f = gate_weight.shape[1]
    channels = block_c // block_g
    reach = SENTENCE // BLOCK
    side, filters = chips * block_c, chips * block_g
    half = 4 * depth // 3
    part = depth // 2
    span = taps // 128
    sizes = (depth, block_c, block_g, chips, span, 4, channels, reach, half)

    other, other_grad = swap(tokens, "mp", 1), swap(output_grad, "mp", 1)
    mixer_pack, ffn_pack = kernel_call(
        pack_kernel, "pack_weights",
        [shaped(2, half, 128), shaped(2, 3, part, block_f)], [],
        (
            value_weight, mixgate_weight, condition_weight.T, filter_base, filter_shift,
            mixout_weight, gate_weight, up_weight, down_weight.T,
        ),
        1e6, limit=60,
    )
    mixer_pack, ffn_pack, other, other_grad = stage(mixer_pack, ffn_pack, other, other_grad)

    mixer_line = [mixer_pack] + [swap(mixer_pack, "mp", 2 * k) for k in range(1, chips)]
    dp_one = dp[None].astype(jnp.int32)
    gains = (gain_one[None, :], gain_two[None, :])
    row_ids = [lax.dynamic_slice_in_dim(segment_ids, mp ^ r, 1) for r in range(rows)]
    two_rows = jnp.concatenate(row_ids)
    (grad_turned,) = kernel_call(
        turn_kernel, "turn_gradient", [shaped(width, total)], [], (output_grad, other_grad), 1e6
    )
    own_column = ffn_pack[:, None]
    mixer_line, own_sides, small, ffn_pack, grad_turned = stage(
        mixer_line, sides(own_column), (dp_one, gains, two_rows), ffn_pack, grad_turned
    )
    dp_one, (gain_first, gain_second), two_rows = small
    mixer_column = jnp.stack(mixer_line, axis=1)
    mixer_sides = sides(mixer_column)
    second_pack, first_pack = swap(ffn_pack, "mp", 4), swap(ffn_pack, "mp", 2)
    mixer_sides, own_sides = stage(mixer_sides, own_sides)
    mixer_corners = corners(*mixer_sides)
    mixer_corners, second_pack, first_pack, own_sides = stage(
        mixer_corners, second_pack, first_pack, own_sides
    )
    second_column = second_pack[:, None]
    second_sides = sides(second_column)
    own_corners = corners(*own_sides)
    third_pack = swap(second_pack, "mp", 2)
    (
        branch, values_0, values_1, gates_0, gates_1, conv_0, conv_1, weights, mixout, condition,
        taps_0, taps_1, shift, cond, summary,
    ) = kernel_call(
        functools.partial(mixer_forward_kernel, sizes), "mixer_forward",
        [shaped(total, width)] + [shaped(side, length)] * 6
        + [
            shaped(2 * side, width), shaped(side, width), shaped(filters, width, dtype=F32),
            shaped(filters, 2 * length, dtype=F32), shaped(filters, 2 * length, dtype=F32),
            shaped(filters, 2 * length, dtype=F32), shaped(rows, filters, 128, dtype=F32),
            shaped(rows, width, dtype=F32),
        ],
        [
            pltpu.VMEM((width, 128), BF), pltpu.VMEM((width, 128), BF),
            pltpu.VMEM((width, 128), BF), pltpu.VMEM((filters, 2 * length), F32),
            pltpu.VMEM((length, length), BF), pltpu.VMEM((sizes[5], length, length), BF),
            pltpu.VMEM((side, length), BF),
        ],
        (dp_one, two_rows, tokens, other, gain_first, mixer_column)
        + tuple(mixer_sides) + tuple(mixer_corners),
        14e9, scalars=1,
    )
    branch, second_sides, own_corners, third_pack = stage(
        branch, second_sides, own_corners, third_pack
    )
    values, gates, conv = (values_0, values_1), (gates_0, gates_1), (conv_0, conv_1)
    branch_got = swap(branch, "mp", 1)
    first_column, third_column = first_pack[:, None], third_pack[:, None]
    second_corners = corners(*second_sides)
    branch_got, second_corners, third_column = stage(branch_got, second_corners, third_column)
    third_sides = sides(third_column)
    normed_two, normed_turned = kernel_call(
        norm_two_kernel, "norm_two", [shaped(total, width), shaped(width, total)], [],
        (tokens, other, branch, branch_got, gain_second),
        1e9,
    )
    fixed = (dp_one, normed_two, normed_turned, output_grad, other_grad, grad_turned)
    own = ffn_call(fixed, (own_column, *own_sides, *own_corners))
    own, third_sides, first_column = stage(own, third_sides, first_column)
    third_corners = corners(*third_sides)
    first_sides = sides(first_column)
    far = ffn_call(
        fixed, (second_column, *second_sides, *second_corners), own[:3], apart=True
    )
    far, third_corners, first_sides = stage(far, third_corners, first_sides)
    first_corners = corners(*first_sides)
    far = ffn_call(
        fixed, (third_column, *third_sides, *third_corners), far[:3], far[3:], apart=True
    )
    far, first_corners = stage(far, first_corners)
    g0a, g0b, g1a, g2b, g1b, g2a, g3a, g3b = far[3:]
    f1b, f2a = swap(g1b, "dp", 1), swap(g2a, "dp", 2)
    second = ffn_call(
        fixed, (first_column, *first_sides, *first_corners), far[:3], own[3:], last=True
    )
    second, f1b, f2a, g3a, g3b = stage(second, f1b, f2a, g3a, g3b)
    feed, feed_other, back = second[:3]
    e1, e2 = swap(g3a, "dp", 2), swap(g3b, "dp", 1)
    back_got = swap(back, "mp", 1)
    grad_middle, mixout_grad, grad_conv_0, grad_conv_1, grad_gates_0, grad_gates_1, gain_two_part = (
        kernel_call(
            mixout_back_kernel, "mixout_back",
            [shaped(length, width, dtype=F32), shaped(side, width)]
            + [shaped(side, length)] * 4 + [shaped(1, width, dtype=F32)],
            [],
            (
                tokens, other, branch, branch_got, back, back_got, output_grad, other_grad,
                gain_second, mixout,
            ) + gates + conv,
            4 * total * width * side,
        )
    )
    grad_conv_0, grad_conv_1, e1, e2, later = stage(grad_conv_0, grad_conv_1, e1, e2, second[3:])
    far_sums, near_sums = Scatter((g0a, g0b, g1a, g2b, (f1b, e2), (f2a, e1))), Scatter(later)
    far_sums.ex, far_sums.ey = far_sums.gx, far_sums.gy
    far_sums.middle()
    near_sums.start()

    def conv_back(r, row_taps, grad_conv):
        return kernel_call(
            functools.partial(conv_back_kernel, 4, channels, reach, r), "conv_back",
            [shaped(side, length), shaped(filters, (2 * reach + 2) * BLOCK, dtype=F32)],
            [
                pltpu.VMEM((length, length), BF), pltpu.VMEM((length, length), F32),
                pltpu.VMEM((4, length, length), BF), pltpu.VMEM((side, length), F32),
            ],
            (two_rows, row_taps, values[r], grad_conv),
            8e9,
        )

    grad_values_0, grad_taps_0 = conv_back(0, taps_0, grad_conv_0)
    grad_taps_0, grad_conv_1, far_sums.f1a, far_sums.f2b = stage(
        grad_taps_0, grad_conv_1, far_sums.f1a, far_sums.f2b
    )
    feed_got = swap(feed_other, "mp", 1)
    second_sum, third_sum = far_sums.end()
    third_got = swap(third_sum, "mp", 2)
    grad_values_1, grad_taps_1 = conv_back(1, taps_1, grad_conv_1)
    grad_values_1, grad_taps_1, third_got = stage(grad_values_1, grad_taps_1, third_got)
    second_halves = [
        swap(added(second_sum[:, p], third_got[:, p]), "mp", 4)
        for p in (slice(0, part), slice(part, depth))
    ]
    results = kernel_call(
        functools.partial(mixer_back_kernel, sizes), "mixer_back",
        [shaped(length, width), shaped(length, width)]
        + [
            shaped(chips, half, 128), shaped(chips, half + 16, 128), shaped(chips, half, 128),
            shaped(chips, half + 16, 128), shaped(2, chips, half + 16, 128),
            shaped(2, chips, half, 128),
        ],
        [
            pltpu.VMEM((width, 128), BF), pltpu.VMEM((width, 128), BF),
            pltpu.VMEM((width, 128), BF), pltpu.VMEM((2, filters, 2 * length), F32),
        ],
        (
            dp_one, tokens, other, gain_first, gain_two_part, grad_gates_0, grad_gates_1,
            mixout_grad, weights, condition, shift, cond, summary, grad_values_0, grad_values_1,
            grad_taps_0, grad_taps_1,
        ),
        8 * total * width * side, scalars=1,
    )
    results, near_sums.ex, near_sums.ey, second_halves[0] = stage(
        results, near_sums.ex, near_sums.ey, second_halves[0]
    )
    near_sums.middle()
    back_own, back_other, mixer_grads = results[0], results[1], Scatter(results[2:])
    mixer_grads.start()
    got_one = swap(back_other, "mp", 1)
    got_one, back_own = stage(got_one, back_own)
    input_grad = kernel_call(
        norm_one_back_kernel, "norm_one_back",
        [shaped(length, width)], [],
        (tokens, back_own, got_one, grad_middle, gain_first),
        1e9,
    )[0]
    (
        input_grad, mixer_grads.ex, mixer_grads.ey, near_sums.f1a, near_sums.f2b, second_halves[1],
    ) = stage(
        input_grad, mixer_grads.ex, mixer_grads.ey, near_sums.f1a, near_sums.f2b, second_halves[1]
    )
    mixer_grads.middle()
    own_sum, first_sum = near_sums.end()
    first_got = swap(first_sum, "mp", 2)
    mixer_grads.f1a, mixer_grads.f2b, first_got, feed_got = stage(
        mixer_grads.f1a, mixer_grads.f2b, first_got, feed_got
    )
    ffn_terms = (own_sum, first_got, jnp.concatenate(second_halves, axis=1))
    mixer_terms = mixer_grads.end()
    mixer_terms = [mixer_terms[0]] + [swap(mixer_terms[k], "mp", 2 * k) for k in range(1, chips)]
    gate_sum, up_sum, down_sum = sum(t.astype(F32) for t in ffn_terms)
    output = (
        tokens.astype(F32) + branch[:length].astype(F32) + branch_got[length:].astype(F32)
        + feed.astype(F32) + feed_got.astype(F32)
    ).astype(BF)
    value_sum, mixgate_sum, condition_sum, base_sum, shift_sum, mixout_sum, gain_sums = kernel_call(
        functools.partial(unpack_kernel, half, span), "unpack",
        [
            shaped(depth, block_c, dtype=F32), shaped(depth, block_c, dtype=F32),
            shaped(block_g, depth, dtype=F32), shaped(block_g, taps, dtype=F32),
            shaped(block_g, taps, dtype=F32), shaped(block_c, depth, dtype=F32),
            shaped(2, width, dtype=F32),
        ],
        [], tuple(mixer_terms), 1e6,
    )
    gain_sums = gain_sums + swap(gain_sums, "mp", 1)
    return (
        output, input_grad, gain_sums[0], gain_sums[1], value_sum, mixgate_sum, condition_sum.T,
        base_sum, shift_sum, mixout_sum, gate_sum, up_sum, down_sum.T,
    )


def choose(tokens, segment_ids, gain_one, gain_two, value_weight, mixgate_weight, condition_weight,
           filter_base, filter_shift, mixout_weight, gate_weight, up_weight, down_weight,
           output_grad):
    fits = (
        lax.axis_size("dp") == 4
        and lax.axis_size("mp") == 8
        and tokens.shape[0] == segment_ids.shape[1] == 512
        and value_weight.shape == (192, 96)
        and filter_base.shape == (6, 256)
        and gate_weight.shape == (192, 384)
    )
    return (fast_body if fits else body)(
        tokens, segment_ids, gain_one, gain_two, value_weight, mixgate_weight, condition_weight,
        filter_base, filter_shift, mixout_weight, gate_weight, up_weight, down_weight, output_grad,
    )


def solution(mesh):
    sides = P(("dp", "mp"), None)
    columns, rows = P("dp", "mp"), P("mp", "dp")
    in_specs = (
        sides, P("dp", None), P(), P(), columns, columns, columns, rows, rows, rows, columns,
        columns, rows, sides,
    )
    out_specs = (
        sides, sides, P(), P(), columns, columns, columns, rows, rows, rows, columns, columns, rows,
    )
    return jax.shard_map(choose, mesh=mesh, in_specs=in_specs, out_specs=out_specs, check_vma=False)
```

```python
import functools

import jax
import jax.numpy as jnp
from jax import lax
from jax.experimental import pallas as pl
from jax.experimental.pallas import tpu as pltpu
from jax.sharding import PartitionSpec as P

epsilon = 1e-05
highest = lax.Precision.HIGHEST
BF = jnp.bfloat16
F32 = jnp.float32
BLOCK = 128
SENTENCE = 256


def build_band(taps_row, mask_ref, band_ref, length, reach):
    blocks = length // BLOCK
    low = length - (reach + 1) * BLOCK
    width = (2 * reach + 2) * BLOCK
    spread = jnp.broadcast_to(taps_row[:, low : low + width], (BLOCK, width))
    shifted = pltpu.roll(spread, 0, 1, stride=1, stride_axis=0).astype(BF)
    for i in range(blocks):
        first, last = max(0, i - reach), min(blocks, i + reach + 1)
        rows = slice(i * BLOCK, (i + 1) * BLOCK)
        columns = slice(first * BLOCK, last * BLOCK)
        offset = (first - i + reach + 1) * BLOCK
        band_ref[rows, columns] = (
            shifted[:, offset : offset + (last - first) * BLOCK] * mask_ref[rows, columns]
        )


def conv_forward_kernel(
    unroll, channels, reach, column_ref, row_ref, cond_ref, base_ref, shift_ref, values_ref,
    conv_ref, mask_ref, taps_ref, band_ref,
):
    length = row_ref.shape[1]
    filters = base_ref.shape[0]
    mask_ref[...] = (column_ref[...] == row_ref[...]).astype(BF)
    taps_ref[...] = base_ref[...].astype(F32) + cond_ref[...] * shift_ref[...].astype(F32)
    band_ref[...] = jnp.zeros_like(band_ref)

    def some(step, carry):
        for u in range(unroll):
            f = step * unroll + u
            build_band(taps_ref[pl.ds(f, 1), :], mask_ref, band_ref.at[u], length, reach)
            rows = pl.ds(pl.multiple_of(f * channels, channels), channels)
            conv_ref[rows, :] = jnp.dot(
                values_ref[rows, :], band_ref[u], preferred_element_type=F32
            )
        return carry

    lax.fori_loop(0, filters // unroll, some, 0)


def conv_forward(segments, cond, base, shift, values, unroll=8):
    filters, length = base.shape[0], segments.shape[0]
    channels = values.shape[0] // filters
    unroll = next(u for u in range(unroll, 0, -1) if filters % u == 0)
    vmem = pl.BlockSpec(memory_space=pltpu.VMEM)
    flops = 2 * values.shape[0] * length * length
    return pl.pallas_call(
        functools.partial(conv_forward_kernel, unroll, channels, SENTENCE // BLOCK),
        out_shape=jax.ShapeDtypeStruct(values.shape, F32),
        in_specs=[vmem] * 6,
        out_specs=vmem,
        scratch_shapes=[
            pltpu.VMEM((length, length), BF),
            pltpu.VMEM(base.shape, F32),
            pltpu.VMEM((unroll, length, length), BF),
        ],
        compiler_params=pltpu.CompilerParams(vmem_limit_bytes=40 << 20),
        cost_estimate=pl.CostEstimate(
            flops=flops * 16, bytes_accessed=values.size * 6, transcendentals=0
        ),
        name="conv_forward",
    )(segments[:, None], segments[None, :], cond[:, None], base, shift, values)


def conv_backward_kernel(
    unroll, channels, reach, column_ref, turned_ref, row_ref, cond_ref, base_ref, shift_ref,
    values_ref, grad_ref, grad_values_ref, grad_taps_ref, mask_ref, mask_turned_ref, taps_ref,
    band_ref, grad_turned_ref,
):
    length = row_ref.shape[1]
    filters = base_ref.shape[0]
    blocks = length // BLOCK
    mask_ref[...] = (column_ref[...] == row_ref[...]).astype(BF)
    mask_turned_ref[...] = (turned_ref[...] == row_ref[...]).astype(F32)
    taps_ref[...] = base_ref[...].astype(F32) + cond_ref[...] * shift_ref[...].astype(F32)
    band_ref[...] = jnp.zeros_like(band_ref)
    turn = (
        lax.broadcasted_iota(jnp.int32, (length, length), 0)
        + lax.broadcasted_iota(jnp.int32, (length, length), 1)
        == length - 1
    ).astype(BF)
    grad_turned_ref[...] = jnp.dot(grad_ref[...], turn, preferred_element_type=F32)

    def some(step, carry):
        for u in range(unroll):
            f = step * unroll + u
            build_band(taps_ref[pl.ds(f, 1), :], mask_ref, band_ref.at[u], length, reach)
            rows = pl.ds(pl.multiple_of(f * channels, channels), channels)
            grad_values_ref[rows, :] = jnp.dot(
                grad_ref[rows, :], band_ref[u], preferred_element_type=F32
            ).astype(BF)
            turned = grad_turned_ref[rows, :].T.astype(BF)
            product = jnp.dot(turned, values_ref[rows, :], preferred_element_type=F32)
            parts = [jnp.zeros((BLOCK, BLOCK), F32)] + [None] * (2 * reach + 1)
            for i in range(blocks):
                back = blocks - 1 - i
                for j in range(max(0, back - reach), min(blocks, back + reach + 1)):
                    here = (
                        slice(i * BLOCK, (i + 1) * BLOCK),
                        slice(j * BLOCK, (j + 1) * BLOCK),
                    )
                    block = product[here] * mask_turned_ref[here]
                    d = j - back + reach + 1
                    parts[d] = block if parts[d] is None else parts[d] + block
            aligned = pltpu.roll(jnp.concatenate(parts, axis=1), 0, 1, stride=1, stride_axis=0)
            grad_taps_ref[pl.ds(f, 1), :] = jnp.sum(aligned, axis=0, keepdims=True)
        return carry

    lax.fori_loop(0, filters // unroll, some, 0)


def conv_backward(segments, cond, base_turned, shift_turned, values, grad, unroll=4):
    filters, length = base_turned.shape[0], segments.shape[0]
    channels = values.shape[0] // filters
    reach = SENTENCE // BLOCK
    width = (2 * reach + 2) * BLOCK
    unroll = next(u for u in range(unroll, 0, -1) if filters % u == 0)
    vmem = pl.BlockSpec(memory_space=pltpu.VMEM)
    flops = 2 * values.shape[0] * length * length
    grad_values, grad_taps = pl.pallas_call(
        functools.partial(conv_backward_kernel, unroll, channels, reach),
        out_shape=(
            jax.ShapeDtypeStruct(values.shape, BF),
            jax.ShapeDtypeStruct((filters, width), F32),
        ),
        in_specs=[vmem] * 8,
        out_specs=(vmem, vmem),
        scratch_shapes=[
            pltpu.VMEM((length, length), BF),
            pltpu.VMEM((length, length), F32),
            pltpu.VMEM(base_turned.shape, F32),
            pltpu.VMEM((unroll, length, length), BF),
            pltpu.VMEM(values.shape, F32),
        ],
        compiler_params=pltpu.CompilerParams(vmem_limit_bytes=48 << 20),
        cost_estimate=pl.CostEstimate(
            flops=flops * 32, bytes_accessed=values.size * 6, transcendentals=0
        ),
        name="conv_backward",
    )(
        segments[:, None],
        segments[::-1][:, None],
        segments[None, :],
        cond[:, None],
        base_turned,
        shift_turned,
        values,
        grad,
    )
    lags = jnp.roll(grad_taps, -(BLOCK - 1), axis=1)[:, ::-1]
    start = length + (reach + 1) * BLOCK - (width - 1)
    full = jnp.pad(lags, ((0, 0), (start, 2 * length - start - width + 1)))
    return grad_values, full[:, : 2 * length]


def swap(value, axis, mask):
    return lax.ppermute(value, axis, [(i, i ^ mask) for i in range(lax.axis_size(axis))])


def bits_of(count):
    return [1 << b for b in range(count.bit_length() - 1)]


def gather_dp(block):
    bits = bits_of(lax.axis_size("dp"))
    half = block.shape[1] // 2
    found = []
    for part, order in ((block[:, :half], bits), (block[:, half:], bits[::-1])):
        held, masks = part[None], [0]
        for bit in order:
            held = jnp.concatenate([held, swap(held, "dp", bit)], axis=0)
            masks = masks + [m | bit for m in masks]
        found.append({m: held[i] for i, m in enumerate(masks)})
    return [jnp.concatenate([f[m] for f in found], axis=1) for m in range(lax.axis_size("dp"))]


def natural(pieces, me):
    held = jnp.stack(pieces)
    return jnp.concatenate(
        [lax.dynamic_index_in_dim(held, j ^ me, 0, keepdims=False) for j in range(len(pieces))],
        axis=1,
    )


def scatter_dp(pieces):
    bits = bits_of(lax.axis_size("dp"))
    half = pieces[0].shape[1] // 2
    done = []
    for part, order in ((slice(None, half), bits[::-1]), (slice(half, None), bits)):
        held = {m: p[:, part] for m, p in enumerate(pieces)}
        for bit in order:
            stay = [m for m in held if not m & bit]
            got = swap(jnp.stack([held[m | bit] for m in stay]), "dp", bit)
            held = {m: held[m] + got[i] for i, m in enumerate(stay)}
        done.append(held[0])
    return jnp.concatenate(done, axis=1)


def everywhere(value):
    for bit in bits_of(lax.axis_size("mp")):
        value = value + swap(value, "mp", bit)
    for bit in bits_of(lax.axis_size("dp")):
        value = value + swap(value, "dp", bit)
    return value


def statistics(value):
    centred = value - jnp.mean(value, axis=-1, keepdims=True)
    scale = lax.rsqrt(jnp.mean(centred * centred, axis=-1, keepdims=True) + epsilon)
    return centred * scale, scale


def normalize_back(normal, scale, gain, grad):
    scaled = grad * gain
    return scale * (
        scaled
        - jnp.mean(scaled, axis=-1, keepdims=True)
        - normal * jnp.mean(scaled * normal, axis=-1, keepdims=True)
    )


def mm(left, right, dims):
    return lax.dot_general(left, right, (dims, ((), ())), preferred_element_type=F32)


def body(
    tokens, segment_ids, gain_one, gain_two, value_weight, mixgate_weight, condition_weight,
    filter_base, filter_shift, mixout_weight, gate_weight, up_weight, down_weight, output_grad,
):
    dp_size, mp_size = lax.axis_size("dp"), lax.axis_size("mp")
    dp, mp = lax.axis_index("dp"), lax.axis_index("mp")
    core = mp & 1
    chips = mp_size // 2
    local, width = tokens.shape
    length = segment_ids.shape[1]
    whole_rows = local % length == 0
    total = 2 * local
    rows = total // length

    def pair(own, other):
        if whole_rows:
            return jnp.concatenate([own, other], axis=0)
        first = core == 0
        return jnp.concatenate([jnp.where(first, own, other), jnp.where(first, other, own)], axis=0)

    def mine(value):
        return value[:local] if whole_rows else lax.dynamic_slice_in_dim(value, core * local, local)

    def others(value):
        if whole_rows:
            return value[local:]
        return lax.dynamic_slice_in_dim(value, (1 - core) * local, local)

    def pair_sum(value):
        got = swap(value, "mp", 1)
        if whole_rows:
            got = jnp.concatenate([got[local:], got[:local]], axis=0)
        return value.astype(F32) + got.astype(F32)

    def pair_scatter(value):
        return mine(value) + swap(others(value).astype(BF), "mp", 1).astype(F32)

    block_c = value_weight.shape[1]
    block_g = condition_weight.shape[1]
    block_f = gate_weight.shape[1]
    taps = filter_base.shape[1]
    mixer_pack = jnp.stack([value_weight, mixgate_weight, mixout_weight.T])
    filter_pack = jnp.stack([filter_base.T, filter_shift.T])
    ffn_pack = jnp.stack([gate_weight, up_weight, down_weight.T])

    tokens_all = pair(tokens, swap(tokens, "mp", 1))
    grad_all = pair(output_grad, swap(output_grad, "mp", 1))
    if whole_rows:
        per = local // length
        seg_rows = jnp.concatenate(
            [
                lax.dynamic_slice_in_dim(segment_ids, mp * per, per),
                lax.dynamic_slice_in_dim(segment_ids, (mp ^ 1) * per, per),
            ]
        )
    else:
        seg_rows = lax.dynamic_slice_in_dim(segment_ids, (mp // 2) * rows, rows)

    def gather(block):
        found = [block] + [swap(block, "mp", 2 * k) for k in range(1, chips)]
        return [natural(gather_dp(b), dp) for b in found]

    mixer = jnp.concatenate(gather(mixer_pack), axis=2)
    small = jnp.concatenate(gather(jnp.pad(condition_weight, ((0, 0), (0, 0)))[None]), axis=2)[0]
    filters = jnp.concatenate(gather(filter_pack), axis=2)
    ffn = gather(ffn_pack)
    value_full, mixgate_full, mixout_full = mixer
    base, shift = jnp.swapaxes(filters, 1, 2)
    base_turned = jnp.roll(base[:, ::-1], 1, axis=1)
    shift_turned = jnp.roll(shift[:, ::-1], 1, axis=1)

    xf = tokens_all.astype(F32)
    normal_one, scale_one = statistics(xf)
    normed_one = (normal_one * gain_one).astype(BF)
    values = mm(value_full, normed_one, ((0,), (1,))).astype(BF)
    gates = mm(mixgate_full, normed_one, ((0,), (1,)))
    summary = jnp.mean(normed_one.astype(F32).reshape(rows, length, width), axis=1)
    condition = small.astype(F32)
    cond = jnp.tanh(jnp.dot(summary, condition, precision=highest))
    cuts = [slice(r * length, (r + 1) * length) for r in range(rows)]
    conv = jnp.concatenate(
        [conv_forward(seg_rows[r], cond[r], base, shift, values[:, cuts[r]]) for r in range(rows)],
        axis=1,
    )
    mixed = (conv * gates).astype(BF)
    branch = pair_sum(mm(mixed, mixout_full, ((0,), (1,))).astype(BF))
    middle = xf + branch
    normal_two, scale_two = statistics(middle)
    normed_two = (normal_two * gain_two).astype(BF)

    feed = jnp.zeros((total, width), F32)
    grad_two = jnp.zeros((total, width), F32)
    ffn_grads = []
    for k in range(chips):
        gate_full, up_full, down_full = ffn[k]
        gate_pre = mm(normed_two, gate_full, ((1,), (0,)))
        up_pre = mm(normed_two, up_full, ((1,), (0,)))
        grad_hidden = mm(grad_all, down_full, ((1,), (0,)))
        sigmoid = jax.nn.sigmoid(gate_pre)
        silu = gate_pre * sigmoid
        hidden = (silu * up_pre).astype(BF)
        grad_gate = (grad_hidden * up_pre * (sigmoid + silu * (1.0 - sigmoid))).astype(BF)
        grad_up = (grad_hidden * silu).astype(BF)
        feed = feed + mm(hidden, down_full, ((1,), (1,)))
        grad_two = (
            grad_two + mm(grad_gate, gate_full, ((1,), (1,))) + mm(grad_up, up_full, ((1,), (1,)))
        )
        ffn_grads.append(
            jnp.stack(
                [
                    mm(normed_two, grad_gate, ((0,), (0,))).astype(BF),
                    mm(normed_two, grad_up, ((0,), (0,))).astype(BF),
                    mm(grad_all, hidden, ((0,), (0,))).astype(BF),
                ]
            )
        )

    def scatter(grads):
        sums = None
        for k, grad in enumerate(grads):
            size = grad.shape[1] // dp_size
            pieces = [
                lax.dynamic_slice_in_dim(grad, (dp ^ m) * size, size, axis=1)
                for m in range(dp_size)
            ]
            part = scatter_dp(pieces)
            part = part if k == 0 else swap(part, "mp", 2 * k)
            sums = part.astype(F32) if sums is None else sums + part.astype(F32)
        return sums

    gate_sum, up_sum, down_sum = scatter(ffn_grads)
    output = (mine(middle) + pair_scatter(feed)).astype(BF)

    grad_normed_two = pair_sum(grad_two.astype(BF))
    gain_two_part = jnp.sum(mine(grad_normed_two * normal_two), axis=0)
    grad_middle = grad_all.astype(F32) + normalize_back(
        normal_two, scale_two, gain_two, grad_normed_two
    )
    grad_branch = grad_middle.astype(BF)

    mixout_grad = mm(grad_branch, mixed, ((0,), (1,)))
    grad_mixed = mm(mixout_full, grad_branch, ((0,), (1,)))
    grad_conv = (grad_mixed * gates).astype(BF)
    grad_gates = (grad_mixed * conv).astype(BF)
    backs = [
        conv_backward(
            seg_rows[r], cond[r], base_turned, shift_turned, values[:, cuts[r]],
            grad_conv[:, cuts[r]],
        )
        for r in range(rows)
    ]
    grad_values = jnp.concatenate([b[0] for b in backs], axis=1)
    grad_taps = jnp.stack([b[1] for b in backs])
    base_grad = jnp.sum(grad_taps, axis=0)
    shift_grad = jnp.sum(grad_taps * cond[:, :, None], axis=0)
    grad_cond = jnp.sum(grad_taps * shift.astype(F32)[None], axis=2) * (1.0 - cond * cond)
    condition_grad = mm(summary, grad_cond, ((0,), (0,)))
    grad_summary = jnp.dot(grad_cond, condition.T, precision=highest) / length
    value_grad = mm(normed_one, grad_values, ((0,), (1,)))
    mixgate_grad = mm(normed_one, grad_gates, ((0,), (1,)))
    grad_one = mm(grad_values, value_full, ((0,), (1,))) + mm(
        grad_gates, mixgate_full, ((0,), (1,))
    )
    grad_one = (grad_one.reshape(rows, length, width) + grad_summary[:, None, :]).reshape(
        total, width
    )
    grad_normed_one = pair_scatter(grad_one)
    input_grad = (
        mine(grad_middle)
        + normalize_back(mine(normal_one), mine(scale_one), gain_one, grad_normed_one)
    ).astype(BF)
    gain_one_part = jnp.sum(grad_normed_one * mine(normal_one), axis=0)
    gain_one_grad, gain_two_grad = everywhere(jnp.stack([gain_one_part, gain_two_part]))

    def split(grad, size):
        return [grad[..., k * size : (k + 1) * size].astype(BF) for k in range(chips)]

    value_sum, mixgate_sum, mixout_sum = scatter(
        split(jnp.stack([value_grad, mixgate_grad, mixout_grad]), block_c)
    )
    condition_sum = scatter(split(condition_grad[None], block_g))[0]
    base_sum, shift_sum = scatter(
        split(jnp.swapaxes(jnp.stack([base_grad, shift_grad]), 1, 2), block_g)
    )
    return (
        output, input_grad, gain_one_grad, gain_two_grad, value_sum, mixgate_sum, condition_sum,
        base_sum.T, shift_sum.T, mixout_sum.T, gate_sum, up_sum, down_sum.T,
    )


def hold(count):
    return [pl.BlockSpec(memory_space=pltpu.VMEM)] * count


def shaped(*shape, dtype=BF):
    return jax.ShapeDtypeStruct(shape, dtype)


def kernel_call(body, name, outs, scratch, args, flops, transcendentals=0, scalars=0, limit=16):
    held = sum(a.size * a.dtype.itemsize for a in tuple(args) + tuple(outs))
    smem = [pl.BlockSpec(memory_space=pltpu.SMEM)] * scalars
    return pl.pallas_call(
        body,
        out_shape=tuple(outs),
        in_specs=smem + hold(len(args) - scalars),
        out_specs=tuple(hold(len(outs))),
        scratch_shapes=scratch,
        compiler_params=pltpu.CompilerParams(vmem_limit_bytes=limit << 20),
        cost_estimate=pl.CostEstimate(
            flops=int(flops), bytes_accessed=int(held), transcendentals=transcendentals
        ),
        name=name,
    )(*args)


def nn(left, right):
    return lax.dot_general(left, right, (((1,), (0,)), ((), ())), preferred_element_type=F32)


def nt(left, right):
    return lax.dot_general(left, right, (((1,), (1,)), ((), ())), preferred_element_type=F32)


def turned_over(value):
    return value.astype(F32).T


def fold(value):
    rows = value.shape[0] // 2
    return jnp.concatenate([value[:rows], value[rows:]], axis=1)


def pack_kernel(
    value_ref, mixgate_ref, condition_ref, base_ref, shift_ref, mixout_ref, gate_ref, up_ref,
    down_ref, mixer_ref, ffn_ref,
):
    depth, block_c = value_ref.shape
    block_g = condition_ref.shape[0]
    span = base_ref.shape[1] // 128
    spare = 128 - block_c
    mixgate = mixgate_ref[...].astype(F32)
    mixout = turned_over(mixout_ref[...])
    first = jnp.concatenate([value_ref[...].astype(F32), mixgate[:, :spare]], axis=1)
    second = jnp.concatenate([mixgate[:, spare:], mixout[:, : 2 * spare]], axis=1)
    condition = jnp.concatenate(
        [condition_ref[...].astype(F32), jnp.zeros((spare - block_g, depth), F32)], axis=0
    )
    third = jnp.concatenate([mixout[:, 2 * spare :], condition.T], axis=1)
    half = mixer_ref.shape[1]
    cut = half - depth
    mixer_ref[0, :depth, :] = first.astype(BF)
    mixer_ref[0, depth:, :] = second[:cut].astype(BF)
    mixer_ref[1, : depth - cut, :] = second[cut:].astype(BF)
    start = depth - cut + depth // 2
    mixer_ref[1, depth - cut : start, :] = fold(third).astype(BF)
    blank = jnp.zeros((16 - span * block_g, 128), F32)
    for ref in (base_ref, shift_ref):
        pieces = [ref[:, h * 128 : (h + 1) * 128].astype(F32) for h in range(span)] + [blank]
        mixer_ref[1, start : start + 16, :] = jnp.concatenate(pieces, axis=0).astype(BF)
        start += 16
    part = ffn_ref.shape[2]
    for h in range(2):
        cut = slice(h * part, (h + 1) * part)
        ffn_ref[h, 0] = gate_ref[cut, :]
        ffn_ref[h, 1] = up_ref[cut, :]
        ffn_ref[h, 2] = down_ref[cut, :]


def norm_rows(value, gain):
    centred = value - jnp.mean(value, axis=-1, keepdims=True)
    scale = lax.rsqrt(jnp.mean(centred * centred, axis=-1, keepdims=True) + epsilon)
    normal = centred * scale
    return normal, scale, normal * gain


def column_of(row):
    return jnp.broadcast_to(row.astype(F32), (8, row.shape[1])).T[:, :1]


def mixer_forward_kernel(
    sizes, dp_ref, row_ref, own_ref, other_ref, gain_ref, p0_ref, p1_ref, p2_ref,
    p3a_ref, p3b_ref, branch_ref, values_0, values_1, gates_0, gates_1, conv_0, conv_1,
    weights_ref, mixout_ref, condition_ref, taps_0, taps_1, shift_out_ref, cond_ref, summary_ref,
    one_ref, two_ref, three_ref, base_ref, mask_ref, band_ref, mixed_ref,
):
    depth, block_c, block_g, chips, span, unroll, channels, reach, half = sizes
    length = own_ref.shape[0]
    values_refs, gates_refs = (values_0, values_1), (gates_0, gates_1)
    conv_refs, taps_refs = (conv_0, conv_1), (taps_0, taps_1)
    dp = dp_ref[0]
    pieces = ((p0_ref, None), (p1_ref, None), (p2_ref, None), (p3a_ref, p3b_ref))
    side = chips * block_c
    spare, cut = 128 - block_c, half - depth
    filters = chips * block_g

    for k in range(chips):
        for m, (first, second) in enumerate(pieces):
            low = first.at[0, k] if second is None else first.at[k]
            high = first.at[1, k] if second is None else second.at[k]
            j = dp ^ m
            at = pl.multiple_of(j * depth, depth)
            one_ref[pl.ds(at, depth), :] = low[:depth, :]
            two_ref[pl.ds(at, cut), :] = low[depth:, :]
            two_ref[pl.ds(pl.multiple_of(at + cut, cut), depth - cut), :] = high[: depth - cut, :]
            start = depth - cut + depth // 2
            folded = high[depth - cut : start, :]
            three_ref[pl.ds(at, depth // 2), :] = folded
            three_ref[pl.ds(pl.multiple_of(at + depth // 2, depth // 2), depth // 2), :] = (
                jnp.concatenate([folded[:, 64:], folded[:, :64]], axis=1)
            )
            for ref in (base_ref, shift_out_ref):
                piece = high[start : start + 16, :].astype(F32)
                start += 16
                for h in range(span):
                    lane = pl.multiple_of((j * span + h) * 128, 128)
                    ref[k * block_g : (k + 1) * block_g, pl.ds(lane, 128)] = piece[
                        h * block_g : (h + 1) * block_g
                    ]
        here, there = k * block_c, side + k * block_c
        turned = turned_over(one_ref[...]).astype(BF)
        weights_ref[here : here + block_c, :] = turned[:block_c]
        weights_ref[there : there + spare, :] = turned[block_c:]
        turned = turned_over(two_ref[...]).astype(BF)
        weights_ref[there + spare : there + block_c, :] = turned[: block_c - spare]
        mixout_ref[here : here + 2 * spare, :] = turned[block_c - spare :]
        turned = turned_over(three_ref[...]).astype(BF)
        mixout_ref[here + 2 * spare : here + block_c, :] = turned[:spare]
        condition_ref[k * block_g : (k + 1) * block_g, :] = turned[spare : 2 * spare].astype(F32)[
            :block_g
        ]

    band_ref[...] = jnp.zeros_like(band_ref)
    for r, ref in enumerate((own_ref, other_ref)):
        _, _, normed = norm_rows(ref[...].astype(F32), gain_ref[...])
        normed = normed.astype(BF)
        summary = jnp.mean(normed.astype(F32), axis=0, keepdims=True)
        summary_ref[r : r + 1, :] = summary
        cond = jnp.tanh(jnp.sum(condition_ref[...] * summary, axis=1, keepdims=True))
        cond_ref[r] = jnp.broadcast_to(cond, cond_ref.shape[1:])
        taps_refs[r][...] = base_ref[...] + cond * shift_out_ref[...]
        values_refs[r][...] = nt(weights_ref[:side, :], normed).astype(BF)
        gates_refs[r][...] = nt(weights_ref[side:, :], normed).astype(BF)
        ids = row_ref[r : r + 1, :]
        mask_ref[...] = (column_of(ids) == ids.astype(F32)).astype(BF)

        def some(step, carry, r=r):
            for u in range(unroll):
                f = step * unroll + u
                build_band(taps_refs[r][pl.ds(f, 1), :], mask_ref, band_ref.at[u], length, reach)
                at = pl.ds(pl.multiple_of(f * channels, channels), channels)
                conv = nn(values_refs[r][at, :], band_ref[u])
                conv_refs[r][at, :] = conv.astype(BF)
                mixed_ref[at, :] = (conv * gates_refs[r][at, :].astype(F32)).astype(BF)
            return carry

        lax.fori_loop(0, filters // unroll, some, 0)
        branch_ref[r * length : (r + 1) * length, :] = nn(
            mixed_ref[...].T, mixout_ref[...]
        ).astype(BF)


def norm_two_kernel(
    own_ref, other_ref, branch_ref, got_ref, gain_ref, normed_ref, normed_turned_ref,
):
    local = own_ref.shape[0]
    for h, ref in enumerate((own_ref, other_ref)):
        here, there = slice(h * local, (h + 1) * local), slice((1 - h) * local, (2 - h) * local)
        middle = (
            ref[...].astype(F32) + branch_ref[here, :].astype(F32) + got_ref[there, :].astype(F32)
        )
        _, _, normed = norm_rows(middle, gain_ref[...])
        normed = normed.astype(BF)
        normed_ref[here, :] = normed
        normed_turned_ref[:, here] = normed.T


def turn_kernel(own_ref, other_ref, turned_ref):
    local = own_ref.shape[0]
    turned_ref[:, :local] = own_ref[...].T
    turned_ref[:, local:] = other_ref[...].T


def ffn_kernel(
    carried, kept, apart, dp_ref, normed_ref, normed_turned_ref, grad_own_ref, grad_other_ref,
    grad_turned_ref, p0_ref, p1_ref, p2_ref, p3a_ref, p3b_ref, *refs,
):
    before, refs = refs[: 3 * carried], refs[3 * carried :]
    pieces_count = 8 if apart else 6
    kept_refs, refs = refs[: pieces_count * kept], refs[pieces_count * kept :]
    feed_own_ref, feed_other_ref, back_ref, g0a, g0b, g1a, g2b = refs[:7]
    moving, refs = refs[7 : 3 + pieces_count], refs[3 + pieces_count :]
    two_ref, down_ref, hidden_ref, act_ref, two_grad_ref, down_grad_ref = refs
    local = grad_own_ref.shape[0]
    _, _, part, block = g0a.shape
    dp = dp_ref[0]
    pieces = ((p0_ref, None), (p1_ref, None), (p2_ref, None), (p3a_ref, p3b_ref))
    if apart:
        g1b, g2a, g3a, g3b = moving
    else:
        gx, gy = moving
        g1b, g2a, g3a, g3b = gx.at[0], gy.at[0], gy.at[1], gx.at[1]
    outs = ((g0a, g0b), (g1a, g1b), (g2a, g2b), (g3a, g3b))
    for m, (one, two) in enumerate(pieces):
        for h in range(2):
            source = one.at[h, 0] if two is None else (one, two)[h].at[0]
            at = pl.ds(pl.multiple_of((dp ^ m) * (2 * part) + h * part, part), part)
            two_ref[at, :block] = source[0]
            two_ref[at, block:] = source[1]
            down_ref[at, :] = source[2]
    for t, (grad_ref, feed_ref) in enumerate(
        ((grad_own_ref, feed_own_ref), (grad_other_ref, feed_other_ref))
    ):
        here = slice(t * local, (t + 1) * local)
        both = nn(normed_ref[here, :], two_ref[...])
        gate_pre, up_pre = both[:, :block], both[:, block:]
        grad_hidden = nn(grad_ref[...], down_ref[...])
        sigmoid = 1.0 / (1.0 + jnp.exp(-gate_pre))
        silu = gate_pre * sigmoid
        hidden = (silu * up_pre).astype(BF)
        hidden_ref[here, :] = hidden
        act_ref[here, :block] = (
            grad_hidden * up_pre * (sigmoid + silu * (1.0 - sigmoid))
        ).astype(BF)
        act_ref[here, block:] = (grad_hidden * silu).astype(BF)
        feed = nt(hidden, down_ref[...])
        back = nt(act_ref[here, :], two_ref[...])
        if carried:
            feed = feed + before[t][...]
            back = back + before[2][here, :]
        feed_ref[...] = feed.astype(feed_ref.dtype)
        back_ref[here, :] = back.astype(back_ref.dtype)
    two_grad_ref[...] = nn(normed_turned_ref[...], act_ref[...]).astype(BF)
    down_grad_ref[...] = nn(grad_turned_ref[...], hidden_ref[...]).astype(BF)
    if kept:
        for source, target in zip(kept_refs, (g0a, g0b, g1a, g2b) + tuple(moving)):
            if len(target.shape) == 4:
                target[0] = source[0]
            else:
                target[:, 0] = source[:, 0]
    for m, pair in enumerate(outs):
        for h in range(2):
            at = pl.ds(pl.multiple_of((dp ^ m) * (2 * part) + h * part, part), part)
            pair[h][int(kept), 0] = two_grad_ref[at, :block]
            pair[h][int(kept), 1] = two_grad_ref[at, block:]
            pair[h][int(kept), 2] = down_grad_ref[at, :]


def ffn_call(fixed, group, before=(), kept=(), last=False, apart=False):
    total, width = fixed[1].shape
    local = fixed[3].shape[0]
    _, _, _, part, block = group[0].shape
    count, kind = 1 + bool(kept), BF if last else F32
    outs = [
        shaped(local, width, dtype=kind), shaped(local, width, dtype=kind),
        shaped(total, width, dtype=kind),
    ]
    if apart:
        outs += [shaped(count, 3, part, block)] * 8
    else:
        outs += [shaped(count, 3, part, block)] * 4 + [shaped(2, count, 3, part, block)] * 2
    return kernel_call(
        functools.partial(ffn_kernel, bool(before), bool(kept), apart), "feed_forward", outs,
        [
            pltpu.VMEM((width, 2 * block), BF), pltpu.VMEM((width, block), BF),
            pltpu.VMEM((total, block), BF), pltpu.VMEM((total, 2 * block), BF),
            pltpu.VMEM((width, 2 * block), BF), pltpu.VMEM((width, block), BF),
        ],
        fixed + tuple(group) + tuple(before) + tuple(kept),
        18 * total * width * block, transcendentals=total * block, scalars=1,
    )


def mixout_back_kernel(
    own_ref, other_ref, branch_ref, got_ref, back_ref, back_got_ref, grad_own_ref, grad_other_ref,
    gain_ref, weights_ref, gates_0, gates_1, conv_0, conv_1, middle_ref, mixout_ref, grad_conv_0,
    grad_conv_1, grad_gates_0, grad_gates_1, gain_grad_ref,
):
    local = own_ref.shape[0]
    mixout = None
    for h, (ref, grad_ref, gates_ref, conv_ref, grad_conv_ref, grad_gates_ref) in enumerate(
        (
            (own_ref, grad_own_ref, gates_0, conv_0, grad_conv_0, grad_gates_0),
            (other_ref, grad_other_ref, gates_1, conv_1, grad_conv_1, grad_gates_1),
        )
    ):
        here, there = slice(h * local, (h + 1) * local), slice((1 - h) * local, (2 - h) * local)
        middle = (
            ref[...].astype(F32) + branch_ref[here, :].astype(F32) + got_ref[there, :].astype(F32)
        )
        normal, scale, _ = norm_rows(middle, gain_ref[...])
        grad = back_ref[here, :].astype(F32) + back_got_ref[there, :].astype(F32)
        grad_middle = grad_ref[...].astype(F32) + normalize_back(
            normal, scale, gain_ref[...], grad
        )
        if h == 0:
            gain_grad_ref[...] = jnp.sum(grad * normal, axis=0, keepdims=True)
            middle_ref[...] = grad_middle
        rounded = grad_middle.astype(BF)
        grad_mixed = nt(weights_ref[...], rounded)
        gates, conv = gates_ref[...].astype(F32), conv_ref[...].astype(F32)
        grad_conv_ref[...] = (grad_mixed * gates).astype(BF)
        grad_gates_ref[...] = (grad_mixed * conv).astype(BF)
        part = nn((gates * conv).astype(BF), rounded)
        mixout = part if h == 0 else mixout + part
    mixout_ref[...] = mixout.astype(BF)


def conv_back_kernel(
    unroll, channels, reach, r, row_ref, taps_ref, values_ref, grad_ref, grad_values_ref,
    grad_taps_ref, mask_ref, mask_turned_ref, band_ref, grad_turned_ref,
):
    length = row_ref.shape[1]
    filters = taps_ref.shape[0]
    blocks = length // BLOCK
    ids = row_ref[r : r + 1, :]
    mask_ref[...] = (column_of(ids) == ids.astype(F32)).astype(BF)
    band_ref[...] = jnp.zeros_like(band_ref)
    turn = (
        lax.broadcasted_iota(jnp.int32, (length, length), 0)
        + lax.broadcasted_iota(jnp.int32, (length, length), 1)
        == length - 1
    ).astype(BF)
    grad_turned_ref[...] = nn(grad_ref[...], turn)
    mask_turned_ref[...] = nn(turn, mask_ref[...])

    def some(step, carry):
        for u in range(unroll):
            f = step * unroll + u
            build_band(taps_ref[pl.ds(f, 1), :], mask_ref, band_ref.at[u], length, reach)
            rows = pl.ds(pl.multiple_of(f * channels, channels), channels)
            grad_values_ref[rows, :] = nt(grad_ref[rows, :], band_ref[u]).astype(BF)
            turned = grad_turned_ref[rows, :].T.astype(BF)
            product = nn(turned, values_ref[rows, :])
            parts = [jnp.zeros((BLOCK, BLOCK), F32)] + [None] * (2 * reach + 1)
            for i in range(blocks):
                back = blocks - 1 - i
                for j in range(max(0, back - reach), min(blocks, back + reach + 1)):
                    here = (
                        slice(i * BLOCK, (i + 1) * BLOCK),
                        slice(j * BLOCK, (j + 1) * BLOCK),
                    )
                    block = product[here] * mask_turned_ref[here]
                    d = j - back + reach + 1
                    parts[d] = block if parts[d] is None else parts[d] + block
            aligned = pltpu.roll(jnp.concatenate(parts, axis=1), 0, 1, stride=1, stride_axis=0)
            grad_taps_ref[pl.ds(f, 1), :] = jnp.sum(aligned, axis=0, keepdims=True)
        return carry

    lax.fori_loop(0, filters // unroll, some, 0)


def mixer_back_kernel(
    sizes, dp_ref, own_ref, other_ref, gain_ref, gain_two_ref, gates_0, gates_1, mixout_ref,
    weights_ref, condition_ref, shift_ref, cond_ref, summary_ref, values_0, values_1, taps_0,
    taps_1, back_own_ref, back_other_ref, g0a_ref, g0b_ref, g1a_ref, g2b_ref, gx_ref, gy_ref,
    one_ref, two_ref, three_ref, filter_ref,
):
    depth, block_c, block_g, chips, span, unroll, channels, reach, half = sizes
    length = own_ref.shape[0]
    side = chips * block_c
    filters = chips * block_g
    width = taps_0.shape[1]
    taps = shift_ref.shape[1]
    spare, cut = 128 - block_c, half - depth
    dp = dp_ref[0]
    lane = lax.broadcasted_iota(jnp.int32, (width, taps), 0)
    tap = lax.broadcasted_iota(jnp.int32, (width, taps), 1)
    reachable = (tap > taps // 2 - (reach + 1) * BLOCK) & (tap < taps // 2 + (reach + 1) * BLOCK)
    spot = taps - 1 - tap
    spot = jnp.where(spot >= width, spot - width, spot)
    place = ((lane == spot) & reachable).astype(BF)
    shift_there = nt(shift_ref[...].astype(BF), place)
    base_grad = shift_grad = condition_grad = value_grad = gate_grad = gain_grad = None
    for r, (ref, values_ref, gates_ref, taps_ref, back_ref) in enumerate(
        (
            (own_ref, values_0, gates_0, taps_0, back_own_ref),
            (other_ref, values_1, gates_1, taps_1, back_other_ref),
        )
    ):
        normal, _, normed = norm_rows(ref[...].astype(F32), gain_ref[...])
        normed = normed.astype(BF)
        grad_taps = taps_ref[...]
        cond = cond_ref[r, :, :1]
        summary = summary_ref[r : r + 1, :]
        grad_cond = jnp.sum(grad_taps * shift_there, axis=1, keepdims=True) * (1.0 - cond * cond)
        grad_summary = jnp.sum(grad_cond * condition_ref[...], axis=0, keepdims=True) / length
        values, gates = values_ref[...], gates_ref[...]
        back = nn(values.T, weights_ref[:side, :]) + nn(gates.T, weights_ref[side:, :])
        back = back + grad_summary
        back_ref[...] = back.astype(BF)
        parts = (
            grad_taps, cond * grad_taps, grad_cond * summary, nn(values, normed),
            nn(gates, normed), jnp.sum(back * normal, axis=0, keepdims=True),
        )
        if r > 0:
            parts = tuple(
                p + q
                for p, q in zip(
                    (base_grad, shift_grad, condition_grad, value_grad, gate_grad, gain_grad), parts
                )
            )
        base_grad, shift_grad, condition_grad, value_grad, gate_grad, gain_grad = parts
    filter_ref[0] = nn(base_grad.astype(BF), place)
    filter_ref[1] = nn(shift_grad.astype(BF), place)
    gain_rows = jnp.concatenate(
        [
            vector[:, h * 128 : (h + 1) * 128]
            for vector in (gain_grad, gain_two_ref[...])
            for h in range(vector.shape[1] // 128)
        ],
        axis=0,
    )
    gain_rows = jnp.concatenate(
        [gain_rows, jnp.zeros((16 - gain_rows.shape[0], 128), F32)], axis=0
    ).astype(BF)
    outs = (
        (g0a_ref, g0b_ref), (g1a_ref, gx_ref.at[0]), (gy_ref.at[0], g2b_ref),
        (gy_ref.at[1], gx_ref.at[1]),
    )
    empty = jnp.zeros((128 - spare - block_g, value_grad.shape[1]), F32)
    blank = jnp.zeros((16 - span * block_g, 128), F32)
    for k in range(chips):
        at = k * block_c
        own = slice(k * block_g, (k + 1) * block_g)
        mixout = mixout_ref[at : at + block_c, :].astype(F32)
        value, gate = value_grad[at : at + block_c], gate_grad[at : at + block_c]
        one_ref[...] = jnp.concatenate([value, gate[:spare]], axis=0).T.astype(BF)
        two_ref[...] = jnp.concatenate([gate[spare:], mixout[: 2 * spare]], axis=0).T.astype(BF)
        third = jnp.concatenate(
            [mixout[2 * spare :], condition_grad[own], empty], axis=0
        ).T
        for j in range(third.shape[0] // depth):
            three_ref[j * (depth // 2) : (j + 1) * (depth // 2), :] = fold(
                third[j * depth : (j + 1) * depth, :64]
            ).astype(BF)
        for m, (low, high) in enumerate(outs):
            j = dp ^ m
            at = pl.multiple_of(j * depth, depth)
            low[k, :depth, :] = one_ref[pl.ds(at, depth), :]
            low[k, depth:, :] = two_ref[pl.ds(at, cut), :]
            high[k, : depth - cut, :] = two_ref[
                pl.ds(pl.multiple_of(at + cut, cut), depth - cut), :
            ]
            start = depth - cut + depth // 2
            high[k, depth - cut : start, :] = three_ref[
                pl.ds(pl.multiple_of(j * (depth // 2), depth // 2), depth // 2), :
            ]
            for n in range(2):
                parts = [
                    filter_ref[n, own, pl.ds(pl.multiple_of((j * span + h) * 128, 128), 128)]
                    for h in range(span)
                ] + [blank]
                high[k, start : start + 16, :] = jnp.concatenate(parts, axis=0).astype(BF)
                start += 16
            high[k, start:, :] = gain_rows


def unpack_kernel(
    half, span, p0_ref, p1_ref, p2_ref, p3_ref, value_ref, mixgate_ref, condition_ref, base_ref,
    shift_ref, mixout_ref, gains_ref,
):
    depth, block_c = value_ref.shape
    block_g = condition_ref.shape[0]
    spare, cut = 128 - block_c, half - depth
    total = p0_ref[...].astype(F32) + p1_ref[...].astype(F32)
    total = total + p2_ref[...].astype(F32) + p3_ref[...].astype(F32)
    first, second = total[:depth], total[depth : 2 * depth]
    start = 2 * depth + depth // 2
    folded = total[2 * depth : start]
    third = jnp.concatenate([folded[:, :64], folded[:, 64:]], axis=0)
    value_ref[...] = first[:, :block_c]
    mixgate_ref[...] = jnp.concatenate([first[:, block_c:], second[:, : block_c - spare]], axis=1)
    mixout_ref[...] = jnp.concatenate(
        [second[:, block_c - spare :], third[:, :spare]], axis=1
    ).T
    condition_ref[...] = third[:, spare:].T[:block_g]
    for ref in (base_ref, shift_ref):
        for h in range(span):
            ref[:, h * 128 : (h + 1) * 128] = total[start + h * block_g : start + (h + 1) * block_g]
        start += 16
    rows = gains_ref.shape[1] // 128
    for g in range(2):
        for h in range(rows):
            at = start + g * rows + h
            gains_ref[g : g + 1, h * 128 : (h + 1) * 128] = total[at : at + 1]


def norm_one_back_kernel(
    own_ref, back_ref, got_ref, middle_ref, gain_ref, grad_ref
):
    normal, scale, _ = norm_rows(own_ref[...].astype(F32), gain_ref[...])
    grad = back_ref[...].astype(F32) + got_ref[...].astype(F32)
    grad_ref[...] = (
        middle_ref[...] + normalize_back(normal, scale, gain_ref[...], grad)
    ).astype(BF)


def stage(*values):
    return lax.optimization_barrier(values)


def sides(column):
    return swap(column, "dp", 1), swap(column, "dp", 2)


def corners(along_x, along_y):
    return swap(along_x[0], "dp", 2), swap(along_y[1], "dp", 1)


def added(*terms):
    return sum(t.astype(F32) for t in terms).astype(BF)


class Scatter:
    def __init__(self, pieces):
        self.g0a, self.g0b, self.g1a, self.g2b, self.gx, self.gy = pieces

    def start(self):
        self.ex, self.ey = swap(self.gx, "dp", 1), swap(self.gy, "dp", 2)

    def middle(self):
        self.f1a = swap(added(self.g1a, self.ey[1]), "dp", 1)
        self.f2b = swap(added(self.g2b, self.ex[1]), "dp", 2)

    def end(self):
        f1a, f2b = self.f1a, self.f2b
        return [
            jnp.concatenate(
                [added(self.g0a[k], f1a[k], self.ey[0][k]), added(self.g0b[k], self.ex[0][k], f2b[k])],
                axis=-2,
            )
            for k in range(self.g0a.shape[0])
        ]


def fast_body(
    tokens, segment_ids, gain_one, gain_two, value_weight, mixgate_weight, condition_weight,
    filter_base, filter_shift, mixout_weight, gate_weight, up_weight, down_weight, output_grad,
):
    dp, mp = lax.axis_index("dp"), lax.axis_index("mp")
    chips = lax.axis_size("mp") // 2
    length, width = tokens.shape
    rows, total = 2, 2 * length
    depth, block_c = value_weight.shape
    block_g, taps = filter_base.shape
    block_f = gate_weight.shape[1]
    channels = block_c // block_g
    reach = SENTENCE // BLOCK
    side, filters = chips * block_c, chips * block_g
    half = 4 * depth // 3
    part = depth // 2
    span = taps // 128
    sizes = (depth, block_c, block_g, chips, span, 4, channels, reach, half)

    other, other_grad = swap(tokens, "mp", 1), swap(output_grad, "mp", 1)
    mixer_pack, ffn_pack = kernel_call(
        pack_kernel, "pack_weights",
        [shaped(2, half, 128), shaped(2, 3, part, block_f)], [],
        (
            value_weight, mixgate_weight, condition_weight.T, filter_base, filter_shift,
            mixout_weight, gate_weight, up_weight, down_weight.T,
        ),
        1e6, limit=60,
    )
    mixer_pack, ffn_pack, other, other_grad = stage(mixer_pack, ffn_pack, other, other_grad)

    mixer_line = [mixer_pack] + [swap(mixer_pack, "mp", 2 * k) for k in range(1, chips)]
    dp_one = dp[None].astype(jnp.int32)
    gains = (gain_one[None, :], gain_two[None, :])
    row_ids = [lax.dynamic_slice_in_dim(segment_ids, mp ^ r, 1) for r in range(rows)]
    two_rows = jnp.concatenate(row_ids)
    (grad_turned,) = kernel_call(
        turn_kernel, "turn_gradient", [shaped(width, total)], [], (output_grad, other_grad), 1e6
    )
    own_column = ffn_pack[:, None]
    mixer_line, own_sides, small, ffn_pack, grad_turned = stage(
        mixer_line, sides(own_column), (dp_one, gains, two_rows), ffn_pack, grad_turned
    )
    dp_one, (gain_first, gain_second), two_rows = small
    mixer_column = jnp.stack(mixer_line, axis=1)
    mixer_sides = sides(mixer_column)
    second_pack, first_pack = swap(ffn_pack, "mp", 4), swap(ffn_pack, "mp", 2)
    mixer_sides, own_sides = stage(mixer_sides, own_sides)
    mixer_corners = corners(*mixer_sides)
    mixer_corners, second_pack, first_pack, own_sides = stage(
        mixer_corners, second_pack, first_pack, own_sides
    )
    second_column = second_pack[:, None]
    second_sides = sides(second_column)
    own_corners = corners(*own_sides)
    third_pack = swap(second_pack, "mp", 2)
    (
        branch, values_0, values_1, gates_0, gates_1, conv_0, conv_1, weights, mixout, condition,
        taps_0, taps_1, shift, cond, summary,
    ) = kernel_call(
        functools.partial(mixer_forward_kernel, sizes), "mixer_forward",
        [shaped(total, width)] + [shaped(side, length)] * 6
        + [
            shaped(2 * side, width), shaped(side, width), shaped(filters, width, dtype=F32),
            shaped(filters, 2 * length, dtype=F32), shaped(filters, 2 * length, dtype=F32),
            shaped(filters, 2 * length, dtype=F32), shaped(rows, filters, 128, dtype=F32),
            shaped(rows, width, dtype=F32),
        ],
        [
            pltpu.VMEM((width, 128), BF), pltpu.VMEM((width, 128), BF),
            pltpu.VMEM((width, 128), BF), pltpu.VMEM((filters, 2 * length), F32),
            pltpu.VMEM((length, length), BF), pltpu.VMEM((sizes[5], length, length), BF),
            pltpu.VMEM((side, length), BF),
        ],
        (dp_one, two_rows, tokens, other, gain_first, mixer_column)
        + tuple(mixer_sides) + tuple(mixer_corners),
        14e9, scalars=1,
    )
    branch, second_sides, own_corners, third_pack = stage(
        branch, second_sides, own_corners, third_pack
    )
    values, gates, conv = (values_0, values_1), (gates_0, gates_1), (conv_0, conv_1)
    branch_got = swap(branch, "mp", 1)
    first_column, third_column = first_pack[:, None], third_pack[:, None]
    second_corners = corners(*second_sides)
    branch_got, second_corners, third_column = stage(branch_got, second_corners, third_column)
    third_sides = sides(third_column)
    normed_two, normed_turned = kernel_call(
        norm_two_kernel, "norm_two", [shaped(total, width), shaped(width, total)], [],
        (tokens, other, branch, branch_got, gain_second),
        1e9,
    )
    fixed = (dp_one, normed_two, normed_turned, output_grad, other_grad, grad_turned)
    first_x = swap(own_sides[0], "mp", 2)
    run = ffn_call(fixed, (second_column, *second_sides, *second_corners))
    run, third_sides, first_x, own_y = stage(run, third_sides, first_x, own_sides[1])
    second_scatter = Scatter(run[3:])
    third_corners = corners(*third_sides)
    second_scatter.start()
    first_y = swap(own_y, "mp", 2)
    run = ffn_call(fixed, (own_column, *own_sides, *own_corners), run[:3], apart=True)
    run, third_corners, first_y, far_corners, second_scatter.ex, second_scatter.ey = stage(
        run, third_corners, first_y, own_corners, second_scatter.ex, second_scatter.ey
    )
    own_pieces = run[3:]
    second_scatter.middle()
    first_corners = [swap(c, "mp", 2) for c in far_corners]
    run = ffn_call(fixed, (third_column, *third_sides, *third_corners), run[:3])
    run, first_corners, second_scatter.f1a, second_scatter.f2b = stage(
        run, first_corners, second_scatter.f1a, second_scatter.f2b
    )
    third_scatter = Scatter(run[3:])
    third_scatter.start()
    run = ffn_call(
        fixed, (first_column, first_x, first_y, *first_corners), run[:3], own_pieces, last=True,
        apart=True,
    )
    run, third_scatter.ex, third_scatter.ey = stage(run, third_scatter.ex, third_scatter.ey)
    (second_sum,) = second_scatter.end()
    feed, feed_other, back = run[:3]
    third_scatter.middle()
    back_got = swap(back, "mp", 1)
    grad_middle, mixout_grad, grad_conv_0, grad_conv_1, grad_gates_0, grad_gates_1, gain_two_part = (
        kernel_call(
            mixout_back_kernel, "mixout_back",
            [shaped(length, width, dtype=F32), shaped(side, width)]
            + [shaped(side, length)] * 4 + [shaped(1, width, dtype=F32)],
            [],
            (
                tokens, other, branch, branch_got, back, back_got, output_grad, other_grad,
                gain_second, mixout,
            ) + gates + conv,
            4 * total * width * side,
        )
    )
    grad_conv_0, grad_conv_1, third_scatter.f1a, third_scatter.f2b, near = stage(
        grad_conv_0, grad_conv_1, third_scatter.f1a, third_scatter.f2b, run[3:]
    )
    (third_sum,) = third_scatter.end()
    third_got = swap(third_sum, "mp", 2)
    g0a, g0b, g1a, g2b, g1b, g2a, g3a, g3b = near
    f1b, f2a = swap(g1b, "dp", 1), swap(g2a, "dp", 2)

    def conv_back(r, row_taps, grad_conv):
        return kernel_call(
            functools.partial(conv_back_kernel, 4, channels, reach, r), "conv_back",
            [shaped(side, length), shaped(filters, (2 * reach + 2) * BLOCK, dtype=F32)],
            [
                pltpu.VMEM((length, length), BF), pltpu.VMEM((length, length), F32),
                pltpu.VMEM((4, length, length), BF), pltpu.VMEM((side, length), F32),
            ],
            (two_rows, row_taps, values[r], grad_conv),
            8e9,
        )

    grad_values_0, grad_taps_0 = conv_back(0, taps_0, grad_conv_0)
    grad_taps_0, grad_conv_1, third_got, f1b, f2a, g3a, g3b = stage(
        grad_taps_0, grad_conv_1, third_got, f1b, f2a, g3a, g3b
    )
    e1, e2 = swap(g3a, "dp", 2), swap(g3b, "dp", 1)
    cut = slice(0, part), slice(part, depth)
    second_low = swap(added(second_sum[:, cut[0]], third_got[:, cut[0]]), "mp", 4)
    grad_values_1, grad_taps_1 = conv_back(1, taps_1, grad_conv_1)
    grad_values_1, grad_taps_1, e1, e2, second_low, second_rest = stage(
        grad_values_1, grad_taps_1, e1, e2, second_low, (second_sum[:, cut[1]], third_got[:, cut[1]])
    )
    near_sums = Scatter((g0a, g0b, g1a, g2b, (f1b, e2), (f2a, e1)))
    near_sums.ex, near_sums.ey = near_sums.gx, near_sums.gy
    near_sums.middle()
    second_high = swap(added(*second_rest), "mp", 4)
    feed_got = swap(feed_other, "mp", 1)
    results = kernel_call(
        functools.partial(mixer_back_kernel, sizes), "mixer_back",
        [shaped(length, width), shaped(length, width)]
        + [
            shaped(chips, half, 128), shaped(chips, half + 16, 128), shaped(chips, half, 128),
            shaped(chips, half + 16, 128), shaped(2, chips, half + 16, 128),
            shaped(2, chips, half, 128),
        ],
        [
            pltpu.VMEM((width, 128), BF), pltpu.VMEM((width, 128), BF),
            pltpu.VMEM((width, 128), BF), pltpu.VMEM((2, filters, 2 * length), F32),
        ],
        (
            dp_one, tokens, other, gain_first, gain_two_part, grad_gates_0, grad_gates_1,
            mixout_grad, weights, condition, shift, cond, summary, grad_values_0, grad_values_1,
            grad_taps_0, grad_taps_1,
        ),
        8 * total * width * side, scalars=1,
    )
    results, near_sums.f1a, near_sums.f2b, second_high = stage(
        results, near_sums.f1a, near_sums.f2b, second_high
    )
    mixer_grads = Scatter(results[2:])
    mixer_grads.start()
    got_one = swap(results[1], "mp", 1)
    own_sum, first_sum = near_sums.end()
    first_got = swap(first_sum, "mp", 2)
    got_one, back_own = stage(got_one, results[0])
    input_grad = kernel_call(
        norm_one_back_kernel, "norm_one_back",
        [shaped(length, width)], [],
        (tokens, back_own, got_one, grad_middle, gain_first),
        1e9,
    )[0]
    input_grad, mixer_grads.ex, mixer_grads.ey, first_got = stage(
        input_grad, mixer_grads.ex, mixer_grads.ey, first_got
    )
    mixer_grads.middle()
    mixer_grads.f1a, mixer_grads.f2b, feed_got = stage(
        mixer_grads.f1a, mixer_grads.f2b, feed_got
    )
    ffn_terms = (own_sum, first_got, jnp.concatenate([second_low, second_high], axis=1))
    mixer_terms = mixer_grads.end()
    mixer_terms = [mixer_terms[0]] + [swap(mixer_terms[k], "mp", 2 * k) for k in range(1, chips)]
    gate_sum, up_sum, down_sum = sum(t.astype(F32) for t in ffn_terms)
    output = (
        tokens.astype(F32) + branch[:length].astype(F32) + branch_got[length:].astype(F32)
        + feed.astype(F32) + feed_got.astype(F32)
    ).astype(BF)
    value_sum, mixgate_sum, condition_sum, base_sum, shift_sum, mixout_sum, gain_sums = kernel_call(
        functools.partial(unpack_kernel, half, span), "unpack",
        [
            shaped(depth, block_c, dtype=F32), shaped(depth, block_c, dtype=F32),
            shaped(block_g, depth, dtype=F32), shaped(block_g, taps, dtype=F32),
            shaped(block_g, taps, dtype=F32), shaped(block_c, depth, dtype=F32),
            shaped(2, width, dtype=F32),
        ],
        [], tuple(mixer_terms), 1e6,
    )
    gain_sums = gain_sums + swap(gain_sums, "mp", 1)
    return (
        output, input_grad, gain_sums[0], gain_sums[1], value_sum, mixgate_sum, condition_sum.T,
        base_sum, shift_sum, mixout_sum, gate_sum, up_sum, down_sum.T,
    )


def choose(tokens, segment_ids, gain_one, gain_two, value_weight, mixgate_weight, condition_weight,
           filter_base, filter_shift, mixout_weight, gate_weight, up_weight, down_weight,
           output_grad):
    fits = (
        lax.axis_size("dp") == 4
        and lax.axis_size("mp") == 8
        and tokens.shape[0] == segment_ids.shape[1] == 512
        and value_weight.shape == (192, 96)
        and filter_base.shape == (6, 256)
        and gate_weight.shape == (192, 384)
    )
    return (fast_body if fits else body)(
        tokens, segment_ids, gain_one, gain_two, value_weight, mixgate_weight, condition_weight,
        filter_base, filter_shift, mixout_weight, gate_weight, up_weight, down_weight, output_grad,
    )


def solution(mesh):
    sides = P(("dp", "mp"), None)
    columns, rows = P("dp", "mp"), P("mp", "dp")
    in_specs = (
        sides, P("dp", None), P(), P(), columns, columns, columns, rows, rows, rows, columns,
        columns, rows, sides,
    )
    out_specs = (
        sides, sides, P(), P(), columns, columns, columns, rows, rows, rows, columns, columns, rows,
    )
    return jax.shard_map(choose, mesh=mesh, in_specs=in_specs, out_specs=out_specs, check_vma=False)
```

```python
import functools

import jax
import jax.numpy as jnp
from jax import lax
from jax.experimental import pallas as pl
from jax.experimental.pallas import tpu as pltpu
from jax.sharding import PartitionSpec as P

epsilon = 1e-05
highest = lax.Precision.HIGHEST
BF = jnp.bfloat16
F32 = jnp.float32
BLOCK = 128
SENTENCE = 256


def build_band(taps_row, mask_ref, band_ref, length, reach):
    blocks = length // BLOCK
    low = length - (reach + 1) * BLOCK
    width = (2 * reach + 2) * BLOCK
    spread = jnp.broadcast_to(taps_row[:, low : low + width], (BLOCK, width))
    shifted = pltpu.roll(spread, 0, 1, stride=1, stride_axis=0).astype(BF)
    for i in range(blocks):
        first, last = max(0, i - reach), min(blocks, i + reach + 1)
        rows = slice(i * BLOCK, (i + 1) * BLOCK)
        columns = slice(first * BLOCK, last * BLOCK)
        offset = (first - i + reach + 1) * BLOCK
        band_ref[rows, columns] = (
            shifted[:, offset : offset + (last - first) * BLOCK] * mask_ref[rows, columns]
        )


def conv_forward_kernel(
    unroll, channels, reach, column_ref, row_ref, cond_ref, base_ref, shift_ref, values_ref,
    conv_ref, mask_ref, taps_ref, band_ref,
):
    length = row_ref.shape[1]
    filters = base_ref.shape[0]
    mask_ref[...] = (column_ref[...] == row_ref[...]).astype(BF)
    taps_ref[...] = base_ref[...].astype(F32) + cond_ref[...] * shift_ref[...].astype(F32)
    band_ref[...] = jnp.zeros_like(band_ref)

    def some(step, carry):
        for u in range(unroll):
            f = step * unroll + u
            build_band(taps_ref[pl.ds(f, 1), :], mask_ref, band_ref.at[u], length, reach)
            rows = pl.ds(pl.multiple_of(f * channels, channels), channels)
            conv_ref[rows, :] = jnp.dot(
                values_ref[rows, :], band_ref[u], preferred_element_type=F32
            )
        return carry

    lax.fori_loop(0, filters // unroll, some, 0)


def conv_forward(segments, cond, base, shift, values, unroll=8):
    filters, length = base.shape[0], segments.shape[0]
    channels = values.shape[0] // filters
    unroll = next(u for u in range(unroll, 0, -1) if filters % u == 0)
    vmem = pl.BlockSpec(memory_space=pltpu.VMEM)
    flops = 2 * values.shape[0] * length * length
    return pl.pallas_call(
        functools.partial(conv_forward_kernel, unroll, channels, SENTENCE // BLOCK),
        out_shape=jax.ShapeDtypeStruct(values.shape, F32),
        in_specs=[vmem] * 6,
        out_specs=vmem,
        scratch_shapes=[
            pltpu.VMEM((length, length), BF),
            pltpu.VMEM(base.shape, F32),
            pltpu.VMEM((unroll, length, length), BF),
        ],
        compiler_params=pltpu.CompilerParams(vmem_limit_bytes=40 << 20),
        cost_estimate=pl.CostEstimate(
            flops=flops * 16, bytes_accessed=values.size * 6, transcendentals=0
        ),
        name="conv_forward",
    )(segments[:, None], segments[None, :], cond[:, None], base, shift, values)


def conv_backward_kernel(
    unroll, channels, reach, column_ref, turned_ref, row_ref, cond_ref, base_ref, shift_ref,
    values_ref, grad_ref, grad_values_ref, grad_taps_ref, mask_ref, mask_turned_ref, taps_ref,
    band_ref, grad_turned_ref,
):
    length = row_ref.shape[1]
    filters = base_ref.shape[0]
    blocks = length // BLOCK
    mask_ref[...] = (column_ref[...] == row_ref[...]).astype(BF)
    mask_turned_ref[...] = (turned_ref[...] == row_ref[...]).astype(F32)
    taps_ref[...] = base_ref[...].astype(F32) + cond_ref[...] * shift_ref[...].astype(F32)
    band_ref[...] = jnp.zeros_like(band_ref)
    turn = (
        lax.broadcasted_iota(jnp.int32, (length, length), 0)
        + lax.broadcasted_iota(jnp.int32, (length, length), 1)
        == length - 1
    ).astype(BF)
    grad_turned_ref[...] = jnp.dot(grad_ref[...], turn, preferred_element_type=F32)

    def some(step, carry):
        for u in range(unroll):
            f = step * unroll + u
            build_band(taps_ref[pl.ds(f, 1), :], mask_ref, band_ref.at[u], length, reach)
            rows = pl.ds(pl.multiple_of(f * channels, channels), channels)
            grad_values_ref[rows, :] = jnp.dot(
                grad_ref[rows, :], band_ref[u], preferred_element_type=F32
            ).astype(BF)
            turned = grad_turned_ref[rows, :].T.astype(BF)
            product = jnp.dot(turned, values_ref[rows, :], preferred_element_type=F32)
            parts = [jnp.zeros((BLOCK, BLOCK), F32)] + [None] * (2 * reach + 1)
            for i in range(blocks):
                back = blocks - 1 - i
                for j in range(max(0, back - reach), min(blocks, back + reach + 1)):
                    here = (
                        slice(i * BLOCK, (i + 1) * BLOCK),
                        slice(j * BLOCK, (j + 1) * BLOCK),
                    )
                    block = product[here] * mask_turned_ref[here]
                    d = j - back + reach + 1
                    parts[d] = block if parts[d] is None else parts[d] + block
            aligned = pltpu.roll(jnp.concatenate(parts, axis=1), 0, 1, stride=1, stride_axis=0)
            grad_taps_ref[pl.ds(f, 1), :] = jnp.sum(aligned, axis=0, keepdims=True)
        return carry

    lax.fori_loop(0, filters // unroll, some, 0)


def conv_backward(segments, cond, base_turned, shift_turned, values, grad, unroll=4):
    filters, length = base_turned.shape[0], segments.shape[0]
    channels = values.shape[0] // filters
    reach = SENTENCE // BLOCK
    width = (2 * reach + 2) * BLOCK
    unroll = next(u for u in range(unroll, 0, -1) if filters % u == 0)
    vmem = pl.BlockSpec(memory_space=pltpu.VMEM)
    flops = 2 * values.shape[0] * length * length
    grad_values, grad_taps = pl.pallas_call(
        functools.partial(conv_backward_kernel, unroll, channels, reach),
        out_shape=(
            jax.ShapeDtypeStruct(values.shape, BF),
            jax.ShapeDtypeStruct((filters, width), F32),
        ),
        in_specs=[vmem] * 8,
        out_specs=(vmem, vmem),
        scratch_shapes=[
            pltpu.VMEM((length, length), BF),
            pltpu.VMEM((length, length), F32),
            pltpu.VMEM(base_turned.shape, F32),
            pltpu.VMEM((unroll, length, length), BF),
            pltpu.VMEM(values.shape, F32),
        ],
        compiler_params=pltpu.CompilerParams(vmem_limit_bytes=48 << 20),
        cost_estimate=pl.CostEstimate(
            flops=flops * 32, bytes_accessed=values.size * 6, transcendentals=0
        ),
        name="conv_backward",
    )(
        segments[:, None],
        segments[::-1][:, None],
        segments[None, :],
        cond[:, None],
        base_turned,
        shift_turned,
        values,
        grad,
    )
    lags = jnp.roll(grad_taps, -(BLOCK - 1), axis=1)[:, ::-1]
    start = length + (reach + 1) * BLOCK - (width - 1)
    full = jnp.pad(lags, ((0, 0), (start, 2 * length - start - width + 1)))
    return grad_values, full[:, : 2 * length]


def swap(value, axis, mask):
    return lax.ppermute(value, axis, [(i, i ^ mask) for i in range(lax.axis_size(axis))])


def bits_of(count):
    return [1 << b for b in range(count.bit_length() - 1)]


def gather_dp(block):
    bits = bits_of(lax.axis_size("dp"))
    half = block.shape[1] // 2
    found = []
    for part, order in ((block[:, :half], bits), (block[:, half:], bits[::-1])):
        held, masks = part[None], [0]
        for bit in order:
            held = jnp.concatenate([held, swap(held, "dp", bit)], axis=0)
            masks = masks + [m | bit for m in masks]
        found.append({m: held[i] for i, m in enumerate(masks)})
    return [jnp.concatenate([f[m] for f in found], axis=1) for m in range(lax.axis_size("dp"))]


def natural(pieces, me):
    held = jnp.stack(pieces)
    return jnp.concatenate(
        [lax.dynamic_index_in_dim(held, j ^ me, 0, keepdims=False) for j in range(len(pieces))],
        axis=1,
    )


def scatter_dp(pieces):
    bits = bits_of(lax.axis_size("dp"))
    half = pieces[0].shape[1] // 2
    done = []
    for part, order in ((slice(None, half), bits[::-1]), (slice(half, None), bits)):
        held = {m: p[:, part] for m, p in enumerate(pieces)}
        for bit in order:
            stay = [m for m in held if not m & bit]
            got = swap(jnp.stack([held[m | bit] for m in stay]), "dp", bit)
            held = {m: held[m] + got[i] for i, m in enumerate(stay)}
        done.append(held[0])
    return jnp.concatenate(done, axis=1)


def everywhere(value):
    for bit in bits_of(lax.axis_size("mp")):
        value = value + swap(value, "mp", bit)
    for bit in bits_of(lax.axis_size("dp")):
        value = value + swap(value, "dp", bit)
    return value


def statistics(value):
    centred = value - jnp.mean(value, axis=-1, keepdims=True)
    scale = lax.rsqrt(jnp.mean(centred * centred, axis=-1, keepdims=True) + epsilon)
    return centred * scale, scale


def normalize_back(normal, scale, gain, grad):
    scaled = grad * gain
    return scale * (
        scaled
        - jnp.mean(scaled, axis=-1, keepdims=True)
        - normal * jnp.mean(scaled * normal, axis=-1, keepdims=True)
    )


def mm(left, right, dims):
    return lax.dot_general(left, right, (dims, ((), ())), preferred_element_type=F32)


def body(
    tokens, segment_ids, gain_one, gain_two, value_weight, mixgate_weight, condition_weight,
    filter_base, filter_shift, mixout_weight, gate_weight, up_weight, down_weight, output_grad,
):
    dp_size, mp_size = lax.axis_size("dp"), lax.axis_size("mp")
    dp, mp = lax.axis_index("dp"), lax.axis_index("mp")
    core = mp & 1
    chips = mp_size // 2
    local, width = tokens.shape
    length = segment_ids.shape[1]
    whole_rows = local % length == 0
    total = 2 * local
    rows = total // length

    def pair(own, other):
        if whole_rows:
            return jnp.concatenate([own, other], axis=0)
        first = core == 0
        return jnp.concatenate([jnp.where(first, own, other), jnp.where(first, other, own)], axis=0)

    def mine(value):
        return value[:local] if whole_rows else lax.dynamic_slice_in_dim(value, core * local, local)

    def others(value):
        if whole_rows:
            return value[local:]
        return lax.dynamic_slice_in_dim(value, (1 - core) * local, local)

    def pair_sum(value):
        got = swap(value, "mp", 1)
        if whole_rows:
            got = jnp.concatenate([got[local:], got[:local]], axis=0)
        return value.astype(F32) + got.astype(F32)

    def pair_scatter(value):
        return mine(value) + swap(others(value).astype(BF), "mp", 1).astype(F32)

    block_c = value_weight.shape[1]
    block_g = condition_weight.shape[1]
    block_f = gate_weight.shape[1]
    taps = filter_base.shape[1]
    mixer_pack = jnp.stack([value_weight, mixgate_weight, mixout_weight.T])
    filter_pack = jnp.stack([filter_base.T, filter_shift.T])
    ffn_pack = jnp.stack([gate_weight, up_weight, down_weight.T])

    tokens_all = pair(tokens, swap(tokens, "mp", 1))
    grad_all = pair(output_grad, swap(output_grad, "mp", 1))
    if whole_rows:
        per = local // length
        seg_rows = jnp.concatenate(
            [
                lax.dynamic_slice_in_dim(segment_ids, mp * per, per),
                lax.dynamic_slice_in_dim(segment_ids, (mp ^ 1) * per, per),
            ]
        )
    else:
        seg_rows = lax.dynamic_slice_in_dim(segment_ids, (mp // 2) * rows, rows)

    def gather(block):
        found = [block] + [swap(block, "mp", 2 * k) for k in range(1, chips)]
        return [natural(gather_dp(b), dp) for b in found]

    mixer = jnp.concatenate(gather(mixer_pack), axis=2)
    small = jnp.concatenate(gather(jnp.pad(condition_weight, ((0, 0), (0, 0)))[None]), axis=2)[0]
    filters = jnp.concatenate(gather(filter_pack), axis=2)
    ffn = gather(ffn_pack)
    value_full, mixgate_full, mixout_full = mixer
    base, shift = jnp.swapaxes(filters, 1, 2)
    base_turned = jnp.roll(base[:, ::-1], 1, axis=1)
    shift_turned = jnp.roll(shift[:, ::-1], 1, axis=1)

    xf = tokens_all.astype(F32)
    normal_one, scale_one = statistics(xf)
    normed_one = (normal_one * gain_one).astype(BF)
    values = mm(value_full, normed_one, ((0,), (1,))).astype(BF)
    gates = mm(mixgate_full, normed_one, ((0,), (1,)))
    summary = jnp.mean(normed_one.astype(F32).reshape(rows, length, width), axis=1)
    condition = small.astype(F32)
    cond = jnp.tanh(jnp.dot(summary, condition, precision=highest))
    cuts = [slice(r * length, (r + 1) * length) for r in range(rows)]
    conv = jnp.concatenate(
        [conv_forward(seg_rows[r], cond[r], base, shift, values[:, cuts[r]]) for r in range(rows)],
        axis=1,
    )
    mixed = (conv * gates).astype(BF)
    branch = pair_sum(mm(mixed, mixout_full, ((0,), (1,))).astype(BF))
    middle = xf + branch
    normal_two, scale_two = statistics(middle)
    normed_two = (normal_two * gain_two).astype(BF)

    feed = jnp.zeros((total, width), F32)
    grad_two = jnp.zeros((total, width), F32)
    ffn_grads = []
    for k in range(chips):
        gate_full, up_full, down_full = ffn[k]
        gate_pre = mm(normed_two, gate_full, ((1,), (0,)))
        up_pre = mm(normed_two, up_full, ((1,), (0,)))
        grad_hidden = mm(grad_all, down_full, ((1,), (0,)))
        sigmoid = jax.nn.sigmoid(gate_pre)
        silu = gate_pre * sigmoid
        hidden = (silu * up_pre).astype(BF)
        grad_gate = (grad_hidden * up_pre * (sigmoid + silu * (1.0 - sigmoid))).astype(BF)
        grad_up = (grad_hidden * silu).astype(BF)
        feed = feed + mm(hidden, down_full, ((1,), (1,)))
        grad_two = (
            grad_two + mm(grad_gate, gate_full, ((1,), (1,))) + mm(grad_up, up_full, ((1,), (1,)))
        )
        ffn_grads.append(
            jnp.stack(
                [
                    mm(normed_two, grad_gate, ((0,), (0,))).astype(BF),
                    mm(normed_two, grad_up, ((0,), (0,))).astype(BF),
                    mm(grad_all, hidden, ((0,), (0,))).astype(BF),
                ]
            )
        )

    def scatter(grads):
        sums = None
        for k, grad in enumerate(grads):
            size = grad.shape[1] // dp_size
            pieces = [
                lax.dynamic_slice_in_dim(grad, (dp ^ m) * size, size, axis=1)
                for m in range(dp_size)
            ]
            part = scatter_dp(pieces)
            part = part if k == 0 else swap(part, "mp", 2 * k)
            sums = part.astype(F32) if sums is None else sums + part.astype(F32)
        return sums

    gate_sum, up_sum, down_sum = scatter(ffn_grads)
    output = (mine(middle) + pair_scatter(feed)).astype(BF)

    grad_normed_two = pair_sum(grad_two.astype(BF))
    gain_two_part = jnp.sum(mine(grad_normed_two * normal_two), axis=0)
    grad_middle = grad_all.astype(F32) + normalize_back(
        normal_two, scale_two, gain_two, grad_normed_two
    )
    grad_branch = grad_middle.astype(BF)

    mixout_grad = mm(grad_branch, mixed, ((0,), (1,)))
    grad_mixed = mm(mixout_full, grad_branch, ((0,), (1,)))
    grad_conv = (grad_mixed * gates).astype(BF)
    grad_gates = (grad_mixed * conv).astype(BF)
    backs = [
        conv_backward(
            seg_rows[r], cond[r], base_turned, shift_turned, values[:, cuts[r]],
            grad_conv[:, cuts[r]],
        )
        for r in range(rows)
    ]
    grad_values = jnp.concatenate([b[0] for b in backs], axis=1)
    grad_taps = jnp.stack([b[1] for b in backs])
    base_grad = jnp.sum(grad_taps, axis=0)
    shift_grad = jnp.sum(grad_taps * cond[:, :, None], axis=0)
    grad_cond = jnp.sum(grad_taps * shift.astype(F32)[None], axis=2) * (1.0 - cond * cond)
    condition_grad = mm(summary, grad_cond, ((0,), (0,)))
    grad_summary = jnp.dot(grad_cond, condition.T, precision=highest) / length
    value_grad = mm(normed_one, grad_values, ((0,), (1,)))
    mixgate_grad = mm(normed_one, grad_gates, ((0,), (1,)))
    grad_one = mm(grad_values, value_full, ((0,), (1,))) + mm(
        grad_gates, mixgate_full, ((0,), (1,))
    )
    grad_one = (grad_one.reshape(rows, length, width) + grad_summary[:, None, :]).reshape(
        total, width
    )
    grad_normed_one = pair_scatter(grad_one)
    input_grad = (
        mine(grad_middle)
        + normalize_back(mine(normal_one), mine(scale_one), gain_one, grad_normed_one)
    ).astype(BF)
    gain_one_part = jnp.sum(grad_normed_one * mine(normal_one), axis=0)
    gain_one_grad, gain_two_grad = everywhere(jnp.stack([gain_one_part, gain_two_part]))

    def split(grad, size):
        return [grad[..., k * size : (k + 1) * size].astype(BF) for k in range(chips)]

    value_sum, mixgate_sum, mixout_sum = scatter(
        split(jnp.stack([value_grad, mixgate_grad, mixout_grad]), block_c)
    )
    condition_sum = scatter(split(condition_grad[None], block_g))[0]
    base_sum, shift_sum = scatter(
        split(jnp.swapaxes(jnp.stack([base_grad, shift_grad]), 1, 2), block_g)
    )
    return (
        output, input_grad, gain_one_grad, gain_two_grad, value_sum, mixgate_sum, condition_sum,
        base_sum.T, shift_sum.T, mixout_sum.T, gate_sum, up_sum, down_sum.T,
    )


def hold(count):
    return [pl.BlockSpec(memory_space=pltpu.VMEM)] * count


def shaped(*shape, dtype=BF):
    return jax.ShapeDtypeStruct(shape, dtype)


def kernel_call(body, name, outs, scratch, args, flops, transcendentals=0, scalars=0, limit=16):
    held = sum(a.size * a.dtype.itemsize for a in tuple(args) + tuple(outs))
    smem = [pl.BlockSpec(memory_space=pltpu.SMEM)] * scalars
    return pl.pallas_call(
        body,
        out_shape=tuple(outs),
        in_specs=smem + hold(len(args) - scalars),
        out_specs=tuple(hold(len(outs))),
        scratch_shapes=scratch,
        compiler_params=pltpu.CompilerParams(vmem_limit_bytes=limit << 20),
        cost_estimate=pl.CostEstimate(
            flops=int(flops), bytes_accessed=int(held), transcendentals=transcendentals
        ),
        name=name,
    )(*args)


def nn(left, right):
    return lax.dot_general(left, right, (((1,), (0,)), ((), ())), preferred_element_type=F32)


def nt(left, right):
    return lax.dot_general(left, right, (((1,), (1,)), ((), ())), preferred_element_type=F32)


def turned_over(value):
    return value.astype(F32).T


def fold(value):
    rows = value.shape[0] // 2
    return jnp.concatenate([value[:rows], value[rows:]], axis=1)


def pack_kernel(
    value_ref, mixgate_ref, condition_ref, base_ref, shift_ref, mixout_ref, gate_ref, up_ref,
    down_ref, mixer_ref, ffn_ref,
):
    depth, block_c = value_ref.shape
    block_g = condition_ref.shape[0]
    span = base_ref.shape[1] // 128
    spare = 128 - block_c
    mixgate = mixgate_ref[...].astype(F32)
    mixout = turned_over(mixout_ref[...])
    first = jnp.concatenate([value_ref[...].astype(F32), mixgate[:, :spare]], axis=1)
    second = jnp.concatenate([mixgate[:, spare:], mixout[:, : 2 * spare]], axis=1)
    condition = jnp.concatenate(
        [condition_ref[...].astype(F32), jnp.zeros((spare - block_g, depth), F32)], axis=0
    )
    third = jnp.concatenate([mixout[:, 2 * spare :], condition.T], axis=1)
    half = mixer_ref.shape[1]
    cut = half - depth
    mixer_ref[0, :depth, :] = first.astype(BF)
    mixer_ref[0, depth:, :] = second[:cut].astype(BF)
    mixer_ref[1, : depth - cut, :] = second[cut:].astype(BF)
    start = depth - cut + depth // 2
    mixer_ref[1, depth - cut : start, :] = fold(third).astype(BF)
    blank = jnp.zeros((16 - span * block_g, 128), F32)
    for ref in (base_ref, shift_ref):
        pieces = [ref[:, h * 128 : (h + 1) * 128].astype(F32) for h in range(span)] + [blank]
        mixer_ref[1, start : start + 16, :] = jnp.concatenate(pieces, axis=0).astype(BF)
        start += 16
    part = ffn_ref.shape[2]
    for h in range(2):
        cut = slice(h * part, (h + 1) * part)
        ffn_ref[h, 0] = gate_ref[cut, :]
        ffn_ref[h, 1] = up_ref[cut, :]
        ffn_ref[h, 2] = down_ref[cut, :]


def norm_rows(value, gain):
    centred = value - jnp.mean(value, axis=-1, keepdims=True)
    scale = lax.rsqrt(jnp.mean(centred * centred, axis=-1, keepdims=True) + epsilon)
    normal = centred * scale
    return normal, scale, normal * gain


def column_of(row):
    return jnp.broadcast_to(row.astype(F32), (8, row.shape[1])).T[:, :1]


def mixer_forward_kernel(
    sizes, dp_ref, row_ref, own_ref, other_ref, gain_ref, p0_ref, p1_ref, p2_ref,
    p3a_ref, p3b_ref, branch_ref, values_0, values_1, gates_0, gates_1, conv_0, conv_1,
    weights_ref, mixout_ref, condition_ref, taps_0, taps_1, shift_out_ref, cond_ref, summary_ref,
    one_ref, two_ref, three_ref, base_ref, mask_ref, band_ref, mixed_ref,
):
    depth, block_c, block_g, chips, span, unroll, channels, reach, half = sizes
    length = own_ref.shape[0]
    values_refs, gates_refs = (values_0, values_1), (gates_0, gates_1)
    conv_refs, taps_refs = (conv_0, conv_1), (taps_0, taps_1)
    dp = dp_ref[0]
    pieces = ((p0_ref, None), (p1_ref, None), (p2_ref, None), (p3a_ref, p3b_ref))
    side = chips * block_c
    spare, cut = 128 - block_c, half - depth
    filters = chips * block_g

    for k in range(chips):
        for m, (first, second) in enumerate(pieces):
            low = first.at[0, k] if second is None else first.at[k]
            high = first.at[1, k] if second is None else second.at[k]
            j = dp ^ m
            at = pl.multiple_of(j * depth, depth)
            one_ref[pl.ds(at, depth), :] = low[:depth, :]
            two_ref[pl.ds(at, cut), :] = low[depth:, :]
            two_ref[pl.ds(pl.multiple_of(at + cut, cut), depth - cut), :] = high[: depth - cut, :]
            start = depth - cut + depth // 2
            folded = high[depth - cut : start, :]
            three_ref[pl.ds(at, depth // 2), :] = folded
            three_ref[pl.ds(pl.multiple_of(at + depth // 2, depth // 2), depth // 2), :] = (
                jnp.concatenate([folded[:, 64:], folded[:, :64]], axis=1)
            )
            for ref in (base_ref, shift_out_ref):
                piece = high[start : start + 16, :].astype(F32)
                start += 16
                for h in range(span):
                    lane = pl.multiple_of((j * span + h) * 128, 128)
                    ref[k * block_g : (k + 1) * block_g, pl.ds(lane, 128)] = piece[
                        h * block_g : (h + 1) * block_g
                    ]
        here, there = k * block_c, side + k * block_c
        turned = turned_over(one_ref[...]).astype(BF)
        weights_ref[here : here + block_c, :] = turned[:block_c]
        weights_ref[there : there + spare, :] = turned[block_c:]
        turned = turned_over(two_ref[...]).astype(BF)
        weights_ref[there + spare : there + block_c, :] = turned[: block_c - spare]
        mixout_ref[here : here + 2 * spare, :] = turned[block_c - spare :]
        turned = turned_over(three_ref[...]).astype(BF)
        mixout_ref[here + 2 * spare : here + block_c, :] = turned[:spare]
        condition_ref[k * block_g : (k + 1) * block_g, :] = turned[spare : 2 * spare].astype(F32)[
            :block_g
        ]

    band_ref[...] = jnp.zeros_like(band_ref)
    for r, ref in enumerate((own_ref, other_ref)):
        _, _, normed = norm_rows(ref[...].astype(F32), gain_ref[...])
        normed = normed.astype(BF)
        summary = jnp.mean(normed.astype(F32), axis=0, keepdims=True)
        summary_ref[r : r + 1, :] = summary
        cond = jnp.tanh(jnp.sum(condition_ref[...] * summary, axis=1, keepdims=True))
        cond_ref[r] = jnp.broadcast_to(cond, cond_ref.shape[1:])
        taps_refs[r][...] = base_ref[...] + cond * shift_out_ref[...]
        values_refs[r][...] = nt(weights_ref[:side, :], normed).astype(BF)
        gates_refs[r][...] = nt(weights_ref[side:, :], normed).astype(BF)
        ids = row_ref[r : r + 1, :]
        mask_ref[...] = (column_of(ids) == ids.astype(F32)).astype(BF)

        def some(step, carry, r=r):
            for u in range(unroll):
                f = step * unroll + u
                build_band(taps_refs[r][pl.ds(f, 1), :], mask_ref, band_ref.at[u], length, reach)
                at = pl.ds(pl.multiple_of(f * channels, channels), channels)
                conv = nn(values_refs[r][at, :], band_ref[u])
                conv_refs[r][at, :] = conv.astype(BF)
                mixed_ref[at, :] = (conv * gates_refs[r][at, :].astype(F32)).astype(BF)
            return carry

        lax.fori_loop(0, filters // unroll, some, 0)
        branch_ref[r * length : (r + 1) * length, :] = nn(
            mixed_ref[...].T, mixout_ref[...]
        ).astype(BF)


def norm_two_kernel(
    own_ref, other_ref, branch_ref, got_ref, gain_ref, normed_ref, normed_turned_ref,
):
    local = own_ref.shape[0]
    for h, ref in enumerate((own_ref, other_ref)):
        here, there = slice(h * local, (h + 1) * local), slice((1 - h) * local, (2 - h) * local)
        middle = (
            ref[...].astype(F32) + branch_ref[here, :].astype(F32) + got_ref[there, :].astype(F32)
        )
        _, _, normed = norm_rows(middle, gain_ref[...])
        normed = normed.astype(BF)
        normed_ref[here, :] = normed
        normed_turned_ref[:, here] = normed.T


def turn_kernel(own_ref, other_ref, turned_ref):
    local = own_ref.shape[0]
    turned_ref[:, :local] = own_ref[...].T
    turned_ref[:, local:] = other_ref[...].T


def ffn_kernel(
    carried, kept, apart, dp_ref, normed_ref, normed_turned_ref, grad_own_ref, grad_other_ref,
    grad_turned_ref, p0_ref, p1_ref, p2_ref, p3a_ref, p3b_ref, *refs,
):
    before, refs = refs[: 3 * carried], refs[3 * carried :]
    pieces_count = 8 if apart else 6
    kept_refs, refs = refs[: pieces_count * kept], refs[pieces_count * kept :]
    feed_own_ref, feed_other_ref, back_ref, g0a, g0b, g1a, g2b = refs[:7]
    moving, refs = refs[7 : 3 + pieces_count], refs[3 + pieces_count :]
    two_ref, down_ref, hidden_ref, act_ref, two_grad_ref, down_grad_ref = refs
    local = grad_own_ref.shape[0]
    _, _, part, block = g0a.shape
    dp = dp_ref[0]
    pieces = ((p0_ref, None), (p1_ref, None), (p2_ref, None), (p3a_ref, p3b_ref))
    if apart:
        g1b, g2a, g3a, g3b = moving
    else:
        gx, gy = moving
        g1b, g2a, g3a, g3b = gx.at[0], gy.at[0], gy.at[1], gx.at[1]
    outs = ((g0a, g0b), (g1a, g1b), (g2a, g2b), (g3a, g3b))
    for m, (one, two) in enumerate(pieces):
        for h in range(2):
            source = one.at[h, 0] if two is None else (one, two)[h].at[0]
            at = pl.ds(pl.multiple_of((dp ^ m) * (2 * part) + h * part, part), part)
            two_ref[at, :block] = source[0]
            two_ref[at, block:] = source[1]
            down_ref[at, :] = source[2]
    for t, (grad_ref, feed_ref) in enumerate(
        ((grad_own_ref, feed_own_ref), (grad_other_ref, feed_other_ref))
    ):
        here = slice(t * local, (t + 1) * local)
        both = nn(normed_ref[here, :], two_ref[...])
        gate_pre, up_pre = both[:, :block], both[:, block:]
        grad_hidden = nn(grad_ref[...], down_ref[...])
        sigmoid = 1.0 / (1.0 + jnp.exp(-gate_pre))
        silu = gate_pre * sigmoid
        hidden = (silu * up_pre).astype(BF)
        hidden_ref[here, :] = hidden
        act_ref[here, :block] = (
            grad_hidden * up_pre * (sigmoid + silu * (1.0 - sigmoid))
        ).astype(BF)
        act_ref[here, block:] = (grad_hidden * silu).astype(BF)
        feed = nt(hidden, down_ref[...])
        back = nt(act_ref[here, :], two_ref[...])
        if carried:
            feed = feed + before[t][...]
            back = back + before[2][here, :]
        feed_ref[...] = feed.astype(feed_ref.dtype)
        back_ref[here, :] = back.astype(back_ref.dtype)
    two_grad_ref[...] = nn(normed_turned_ref[...], act_ref[...]).astype(BF)
    down_grad_ref[...] = nn(grad_turned_ref[...], hidden_ref[...]).astype(BF)
    if kept:
        for source, target in zip(kept_refs, (g0a, g0b, g1a, g2b) + tuple(moving)):
            if len(target.shape) == 4:
                target[0] = source[0]
            else:
                target[:, 0] = source[:, 0]
    for m, pair in enumerate(outs):
        for h in range(2):
            at = pl.ds(pl.multiple_of((dp ^ m) * (2 * part) + h * part, part), part)
            pair[h][int(kept), 0] = two_grad_ref[at, :block]
            pair[h][int(kept), 1] = two_grad_ref[at, block:]
            pair[h][int(kept), 2] = down_grad_ref[at, :]


def ffn_call(fixed, group, before=(), kept=(), last=False, apart=False):
    total, width = fixed[1].shape
    local = fixed[3].shape[0]
    _, _, _, part, block = group[0].shape
    count, kind = 1 + bool(kept), BF if last else F32
    outs = [
        shaped(local, width, dtype=kind), shaped(local, width, dtype=kind),
        shaped(total, width, dtype=kind),
    ]
    if apart:
        outs += [shaped(count, 3, part, block)] * 8
    else:
        outs += [shaped(count, 3, part, block)] * 4 + [shaped(2, count, 3, part, block)] * 2
    return kernel_call(
        functools.partial(ffn_kernel, bool(before), bool(kept), apart), "feed_forward", outs,
        [
            pltpu.VMEM((width, 2 * block), BF), pltpu.VMEM((width, block), BF),
            pltpu.VMEM((total, block), BF), pltpu.VMEM((total, 2 * block), BF),
            pltpu.VMEM((width, 2 * block), BF), pltpu.VMEM((width, block), BF),
        ],
        fixed + tuple(group) + tuple(before) + tuple(kept),
        18 * total * width * block, transcendentals=total * block, scalars=1,
    )


def mixout_back_kernel(
    own_ref, other_ref, branch_ref, got_ref, back_ref, back_got_ref, grad_own_ref, grad_other_ref,
    gain_ref, weights_ref, gates_0, gates_1, conv_0, conv_1, middle_ref, mixout_ref, grad_conv_0,
    grad_conv_1, grad_gates_0, grad_gates_1, gain_grad_ref,
):
    local = own_ref.shape[0]
    mixout = None
    for h, (ref, grad_ref, gates_ref, conv_ref, grad_conv_ref, grad_gates_ref) in enumerate(
        (
            (own_ref, grad_own_ref, gates_0, conv_0, grad_conv_0, grad_gates_0),
            (other_ref, grad_other_ref, gates_1, conv_1, grad_conv_1, grad_gates_1),
        )
    ):
        here, there = slice(h * local, (h + 1) * local), slice((1 - h) * local, (2 - h) * local)
        middle = (
            ref[...].astype(F32) + branch_ref[here, :].astype(F32) + got_ref[there, :].astype(F32)
        )
        normal, scale, _ = norm_rows(middle, gain_ref[...])
        grad = back_ref[here, :].astype(F32) + back_got_ref[there, :].astype(F32)
        grad_middle = grad_ref[...].astype(F32) + normalize_back(
            normal, scale, gain_ref[...], grad
        )
        if h == 0:
            gain_grad_ref[...] = jnp.sum(grad * normal, axis=0, keepdims=True)
            middle_ref[...] = grad_middle
        rounded = grad_middle.astype(BF)
        grad_mixed = nt(weights_ref[...], rounded)
        gates, conv = gates_ref[...].astype(F32), conv_ref[...].astype(F32)
        grad_conv_ref[...] = (grad_mixed * gates).astype(BF)
        grad_gates_ref[...] = (grad_mixed * conv).astype(BF)
        part = nn((gates * conv).astype(BF), rounded)
        mixout = part if h == 0 else mixout + part
    mixout_ref[...] = mixout.astype(BF)


def conv_back_kernel(
    unroll, channels, reach, row_ref, taps_0, taps_1, values_0, values_1, grad_0, grad_1,
    grad_values_0, grad_values_1, grad_taps_0, grad_taps_1, *scratch,
):
    for r, refs in enumerate(
        (
            (taps_0, values_0, grad_0, grad_values_0, grad_taps_0),
            (taps_1, values_1, grad_1, grad_values_1, grad_taps_1),
        )
    ):
        conv_back_row(unroll, channels, reach, r, row_ref, *refs, *scratch)


def conv_back_row(
    unroll, channels, reach, r, row_ref, taps_ref, values_ref, grad_ref, grad_values_ref,
    grad_taps_ref, mask_ref, mask_turned_ref, band_ref, grad_turned_ref,
):
    length = row_ref.shape[1]
    filters = taps_ref.shape[0]
    blocks = length // BLOCK
    ids = row_ref[r : r + 1, :]
    mask_ref[...] = (column_of(ids) == ids.astype(F32)).astype(BF)
    band_ref[...] = jnp.zeros_like(band_ref)
    turn = (
        lax.broadcasted_iota(jnp.int32, (length, length), 0)
        + lax.broadcasted_iota(jnp.int32, (length, length), 1)
        == length - 1
    ).astype(BF)
    grad_turned_ref[...] = nn(grad_ref[...], turn)
    mask_turned_ref[...] = nn(turn, mask_ref[...])

    def some(step, carry):
        for u in range(unroll):
            f = step * unroll + u
            build_band(taps_ref[pl.ds(f, 1), :], mask_ref, band_ref.at[u], length, reach)
            rows = pl.ds(pl.multiple_of(f * channels, channels), channels)
            grad_values_ref[rows, :] = nt(grad_ref[rows, :], band_ref[u]).astype(BF)
            turned = grad_turned_ref[rows, :].T.astype(BF)
            product = nn(turned, values_ref[rows, :])
            parts = [jnp.zeros((BLOCK, BLOCK), F32)] + [None] * (2 * reach + 1)
            for i in range(blocks):
                back = blocks - 1 - i
                for j in range(max(0, back - reach), min(blocks, back + reach + 1)):
                    here = (
                        slice(i * BLOCK, (i + 1) * BLOCK),
                        slice(j * BLOCK, (j + 1) * BLOCK),
                    )
                    block = product[here] * mask_turned_ref[here]
                    d = j - back + reach + 1
                    parts[d] = block if parts[d] is None else parts[d] + block
            aligned = pltpu.roll(jnp.concatenate(parts, axis=1), 0, 1, stride=1, stride_axis=0)
            grad_taps_ref[pl.ds(f, 1), :] = jnp.sum(aligned, axis=0, keepdims=True)
        return carry

    lax.fori_loop(0, filters // unroll, some, 0)


def mixer_back_kernel(
    sizes, dp_ref, own_ref, other_ref, gain_ref, gain_two_ref, gates_0, gates_1, mixout_ref,
    weights_ref, condition_ref, shift_ref, cond_ref, summary_ref, values_0, values_1, taps_0,
    taps_1, back_own_ref, back_other_ref, g0a_ref, g0b_ref, g1a_ref, g2b_ref, gx_ref, gy_ref,
    one_ref, two_ref, three_ref, filter_ref,
):
    depth, block_c, block_g, chips, span, unroll, channels, reach, half = sizes
    length = own_ref.shape[0]
    side = chips * block_c
    filters = chips * block_g
    width = taps_0.shape[1]
    taps = shift_ref.shape[1]
    spare, cut = 128 - block_c, half - depth
    dp = dp_ref[0]
    lane = lax.broadcasted_iota(jnp.int32, (width, taps), 0)
    tap = lax.broadcasted_iota(jnp.int32, (width, taps), 1)
    reachable = (tap > taps // 2 - (reach + 1) * BLOCK) & (tap < taps // 2 + (reach + 1) * BLOCK)
    spot = taps - 1 - tap
    spot = jnp.where(spot >= width, spot - width, spot)
    place = ((lane == spot) & reachable).astype(BF)
    shift_there = nt(shift_ref[...].astype(BF), place)
    base_grad = shift_grad = condition_grad = value_grad = gate_grad = gain_grad = None
    for r, (ref, values_ref, gates_ref, taps_ref, back_ref) in enumerate(
        (
            (own_ref, values_0, gates_0, taps_0, back_own_ref),
            (other_ref, values_1, gates_1, taps_1, back_other_ref),
        )
    ):
        normal, _, normed = norm_rows(ref[...].astype(F32), gain_ref[...])
        normed = normed.astype(BF)
        grad_taps = taps_ref[...]
        cond = cond_ref[r, :, :1]
        summary = summary_ref[r : r + 1, :]
        grad_cond = jnp.sum(grad_taps * shift_there, axis=1, keepdims=True) * (1.0 - cond * cond)
        grad_summary = jnp.sum(grad_cond * condition_ref[...], axis=0, keepdims=True) / length
        values, gates = values_ref[...], gates_ref[...]
        back = nn(values.T, weights_ref[:side, :]) + nn(gates.T, weights_ref[side:, :])
        back = back + grad_summary
        back_ref[...] = back.astype(BF)
        parts = (
            grad_taps, cond * grad_taps, grad_cond * summary, nn(values, normed),
            nn(gates, normed), jnp.sum(back * normal, axis=0, keepdims=True),
        )
        if r > 0:
            parts = tuple(
                p + q
                for p, q in zip(
                    (base_grad, shift_grad, condition_grad, value_grad, gate_grad, gain_grad), parts
                )
            )
        base_grad, shift_grad, condition_grad, value_grad, gate_grad, gain_grad = parts
    filter_ref[0] = nn(base_grad.astype(BF), place)
    filter_ref[1] = nn(shift_grad.astype(BF), place)
    gain_rows = jnp.concatenate(
        [
            vector[:, h * 128 : (h + 1) * 128]
            for vector in (gain_grad, gain_two_ref[...])
            for h in range(vector.shape[1] // 128)
        ],
        axis=0,
    )
    gain_rows = jnp.concatenate(
        [gain_rows, jnp.zeros((16 - gain_rows.shape[0], 128), F32)], axis=0
    ).astype(BF)
    outs = (
        (g0a_ref, g0b_ref), (g1a_ref, gx_ref.at[0]), (gy_ref.at[0], g2b_ref),
        (gy_ref.at[1], gx_ref.at[1]),
    )
    empty = jnp.zeros((128 - spare - block_g, value_grad.shape[1]), F32)
    blank = jnp.zeros((16 - span * block_g, 128), F32)
    for k in range(chips):
        at = k * block_c
        own = slice(k * block_g, (k + 1) * block_g)
        mixout = mixout_ref[at : at + block_c, :].astype(F32)
        value, gate = value_grad[at : at + block_c], gate_grad[at : at + block_c]
        one_ref[...] = jnp.concatenate([value, gate[:spare]], axis=0).T.astype(BF)
        two_ref[...] = jnp.concatenate([gate[spare:], mixout[: 2 * spare]], axis=0).T.astype(BF)
        third = jnp.concatenate(
            [mixout[2 * spare :], condition_grad[own], empty], axis=0
        ).T
        for j in range(third.shape[0] // depth):
            three_ref[j * (depth // 2) : (j + 1) * (depth // 2), :] = fold(
                third[j * depth : (j + 1) * depth, :64]
            ).astype(BF)
        for m, (low, high) in enumerate(outs):
            j = dp ^ m
            at = pl.multiple_of(j * depth, depth)
            low[k, :depth, :] = one_ref[pl.ds(at, depth), :]
            low[k, depth:, :] = two_ref[pl.ds(at, cut), :]
            high[k, : depth - cut, :] = two_ref[
                pl.ds(pl.multiple_of(at + cut, cut), depth - cut), :
            ]
            start = depth - cut + depth // 2
            high[k, depth - cut : start, :] = three_ref[
                pl.ds(pl.multiple_of(j * (depth // 2), depth // 2), depth // 2), :
            ]
            for n in range(2):
                parts = [
                    filter_ref[n, own, pl.ds(pl.multiple_of((j * span + h) * 128, 128), 128)]
                    for h in range(span)
                ] + [blank]
                high[k, start : start + 16, :] = jnp.concatenate(parts, axis=0).astype(BF)
                start += 16
            high[k, start:, :] = gain_rows


def unpack_kernel(
    half, span, p0_ref, p1_ref, p2_ref, p3_ref, value_ref, mixgate_ref, condition_ref, base_ref,
    shift_ref, mixout_ref, gains_ref,
):
    depth, block_c = value_ref.shape
    block_g = condition_ref.shape[0]
    spare, cut = 128 - block_c, half - depth
    total = p0_ref[...].astype(F32) + p1_ref[...].astype(F32)
    total = total + p2_ref[...].astype(F32) + p3_ref[...].astype(F32)
    first, second = total[:depth], total[depth : 2 * depth]
    start = 2 * depth + depth // 2
    folded = total[2 * depth : start]
    third = jnp.concatenate([folded[:, :64], folded[:, 64:]], axis=0)
    value_ref[...] = first[:, :block_c]
    mixgate_ref[...] = jnp.concatenate([first[:, block_c:], second[:, : block_c - spare]], axis=1)
    mixout_ref[...] = jnp.concatenate(
        [second[:, block_c - spare :], third[:, :spare]], axis=1
    ).T
    condition_ref[...] = third[:, spare:].T[:block_g]
    for ref in (base_ref, shift_ref):
        for h in range(span):
            ref[:, h * 128 : (h + 1) * 128] = total[start + h * block_g : start + (h + 1) * block_g]
        start += 16
    rows = gains_ref.shape[1] // 128
    for g in range(2):
        for h in range(rows):
            at = start + g * rows + h
            gains_ref[g : g + 1, h * 128 : (h + 1) * 128] = total[at : at + 1]


def norm_one_back_kernel(
    own_ref, back_ref, got_ref, middle_ref, gain_ref, grad_ref
):
    normal, scale, _ = norm_rows(own_ref[...].astype(F32), gain_ref[...])
    grad = back_ref[...].astype(F32) + got_ref[...].astype(F32)
    grad_ref[...] = (
        middle_ref[...] + normalize_back(normal, scale, gain_ref[...], grad)
    ).astype(BF)


def stage(*values):
    return lax.optimization_barrier(values)


def sides(column):
    return swap(column, "dp", 1), swap(column, "dp", 2)


def corners(along_x, along_y):
    return swap(along_x[0], "dp", 2), swap(along_y[1], "dp", 1)


def added(*terms):
    return sum(t.astype(F32) for t in terms).astype(BF)


class Scatter:
    def __init__(self, pieces):
        self.g0a, self.g0b, self.g1a, self.g2b, self.gx, self.gy = pieces

    def start(self):
        self.ex, self.ey = swap(self.gx, "dp", 1), swap(self.gy, "dp", 2)

    def middle(self):
        self.f1a = swap(added(self.g1a, self.ey[1]), "dp", 1)
        self.f2b = swap(added(self.g2b, self.ex[1]), "dp", 2)

    def end(self):
        f1a, f2b = self.f1a, self.f2b
        return [
            jnp.concatenate(
                [added(self.g0a[k], f1a[k], self.ey[0][k]), added(self.g0b[k], self.ex[0][k], f2b[k])],
                axis=-2,
            )
            for k in range(self.g0a.shape[0])
        ]


def fast_body(
    tokens, segment_ids, gain_one, gain_two, value_weight, mixgate_weight, condition_weight,
    filter_base, filter_shift, mixout_weight, gate_weight, up_weight, down_weight, output_grad,
):
    dp, mp = lax.axis_index("dp"), lax.axis_index("mp")
    chips = lax.axis_size("mp") // 2
    length, width = tokens.shape
    rows, total = 2, 2 * length
    depth, block_c = value_weight.shape
    block_g, taps = filter_base.shape
    block_f = gate_weight.shape[1]
    channels = block_c // block_g
    reach = SENTENCE // BLOCK
    side, filters = chips * block_c, chips * block_g
    half = 4 * depth // 3
    part = depth // 2
    span = taps // 128
    sizes = (depth, block_c, block_g, chips, span, 8, channels, reach, half)

    other, other_grad = swap(tokens, "mp", 1), swap(output_grad, "mp", 1)
    mixer_pack, ffn_pack = kernel_call(
        pack_kernel, "pack_weights",
        [shaped(2, half, 128), shaped(2, 3, part, block_f)], [],
        (
            value_weight, mixgate_weight, condition_weight.T, filter_base, filter_shift,
            mixout_weight, gate_weight, up_weight, down_weight.T,
        ),
        1e6, limit=60,
    )
    mixer_pack, ffn_pack, other, other_grad = stage(mixer_pack, ffn_pack, other, other_grad)

    mixer_line = [mixer_pack] + [swap(mixer_pack, "mp", 2 * k) for k in range(1, chips)]
    dp_one = dp[None].astype(jnp.int32)
    gains = (gain_one[None, :], gain_two[None, :])
    row_ids = [lax.dynamic_slice_in_dim(segment_ids, mp ^ r, 1) for r in range(rows)]
    two_rows = jnp.concatenate(row_ids)
    (grad_turned,) = kernel_call(
        turn_kernel, "turn_gradient", [shaped(width, total)], [], (output_grad, other_grad), 1e6
    )
    own_column = ffn_pack[:, None]
    mixer_line, own_sides, small, ffn_pack, grad_turned = stage(
        mixer_line, sides(own_column), (dp_one, gains, two_rows), ffn_pack, grad_turned
    )
    dp_one, (gain_first, gain_second), two_rows = small
    mixer_column = jnp.stack(mixer_line, axis=1)
    mixer_sides = sides(mixer_column)
    second_pack, first_pack = swap(ffn_pack, "mp", 4), swap(ffn_pack, "mp", 2)
    mixer_sides, own_sides = stage(mixer_sides, own_sides)
    mixer_corners = corners(*mixer_sides)
    mixer_corners, second_pack, first_pack, own_sides = stage(
        mixer_corners, second_pack, first_pack, own_sides
    )
    second_column = second_pack[:, None]
    second_sides = sides(second_column)
    own_corners = corners(*own_sides)
    third_pack = swap(second_pack, "mp", 2)
    (
        branch, values_0, values_1, gates_0, gates_1, conv_0, conv_1, weights, mixout, condition,
        taps_0, taps_1, shift, cond, summary,
    ) = kernel_call(
        functools.partial(mixer_forward_kernel, sizes), "mixer_forward",
        [shaped(total, width)] + [shaped(side, length)] * 6
        + [
            shaped(2 * side, width), shaped(side, width), shaped(filters, width, dtype=F32),
            shaped(filters, 2 * length, dtype=F32), shaped(filters, 2 * length, dtype=F32),
            shaped(filters, 2 * length, dtype=F32), shaped(rows, filters, 128, dtype=F32),
            shaped(rows, width, dtype=F32),
        ],
        [
            pltpu.VMEM((width, 128), BF), pltpu.VMEM((width, 128), BF),
            pltpu.VMEM((width, 128), BF), pltpu.VMEM((filters, 2 * length), F32),
            pltpu.VMEM((length, length), BF), pltpu.VMEM((sizes[5], length, length), BF),
            pltpu.VMEM((side, length), BF),
        ],
        (dp_one, two_rows, tokens, other, gain_first, mixer_column)
        + tuple(mixer_sides) + tuple(mixer_corners),
        14e9, scalars=1,
    )
    branch, second_sides, own_corners, third_pack = stage(
        branch, second_sides, own_corners, third_pack
    )
    values, gates, conv = (values_0, values_1), (gates_0, gates_1), (conv_0, conv_1)
    branch_got = swap(branch, "mp", 1)
    first_column, third_column = first_pack[:, None], third_pack[:, None]
    second_corners = corners(*second_sides)
    branch_got, second_corners, third_column = stage(branch_got, second_corners, third_column)
    third_sides = sides(third_column)
    normed_two, normed_turned = kernel_call(
        norm_two_kernel, "norm_two", [shaped(total, width), shaped(width, total)], [],
        (tokens, other, branch, branch_got, gain_second),
        1e9,
    )
    fixed = (dp_one, normed_two, normed_turned, output_grad, other_grad, grad_turned)
    first_x = swap(own_sides[0], "mp", 2)
    run = ffn_call(fixed, (second_column, *second_sides, *second_corners))
    run, third_sides, first_x, own_y = stage(run, third_sides, first_x, own_sides[1])
    second_scatter = Scatter(run[3:])
    third_corners = corners(*third_sides)
    second_scatter.start()
    first_y = swap(own_y, "mp", 2)
    run = ffn_call(fixed, (own_column, *own_sides, *own_corners), run[:3])
    run, third_corners, first_y, far_corners, second_scatter.ex, second_scatter.ey = stage(
        run, third_corners, first_y, own_corners, second_scatter.ex, second_scatter.ey
    )
    own_pieces = run[3:]
    second_scatter.middle()
    first_corners = [swap(c, "mp", 2) for c in far_corners]
    run = ffn_call(fixed, (third_column, *third_sides, *third_corners), run[:3])
    run, first_corners, second_scatter.f1a, second_scatter.f2b = stage(
        run, first_corners, second_scatter.f1a, second_scatter.f2b
    )
    third_scatter = Scatter(run[3:])
    third_scatter.start()
    run = ffn_call(
        fixed, (first_column, first_x, first_y, *first_corners), run[:3], own_pieces, last=True
    )
    run, third_scatter.ex, third_scatter.ey = stage(run, third_scatter.ex, third_scatter.ey)
    (second_sum,) = second_scatter.end()
    feed, feed_other, back = run[:3]
    third_scatter.middle()
    back_got = swap(back, "mp", 1)
    grad_middle, mixout_grad, grad_conv_0, grad_conv_1, grad_gates_0, grad_gates_1, gain_two_part = (
        kernel_call(
            mixout_back_kernel, "mixout_back",
            [shaped(length, width, dtype=F32), shaped(side, width)]
            + [shaped(side, length)] * 4 + [shaped(1, width, dtype=F32)],
            [],
            (
                tokens, other, branch, branch_got, back, back_got, output_grad, other_grad,
                gain_second, mixout,
            ) + gates + conv,
            4 * total * width * side,
        )
    )
    grad_conv_0, grad_conv_1, third_scatter.f1a, third_scatter.f2b, near = stage(
        grad_conv_0, grad_conv_1, third_scatter.f1a, third_scatter.f2b, run[3:]
    )
    near_sums = Scatter(near)
    near_sums.start()
    (third_sum,) = third_scatter.end()
    third_got = swap(third_sum, "mp", 2)
    grad_values_0, grad_values_1, grad_taps_0, grad_taps_1 = kernel_call(
        functools.partial(conv_back_kernel, 8, channels, reach), "conv_back",
        [shaped(side, length)] * 2 + [shaped(filters, (2 * reach + 2) * BLOCK, dtype=F32)] * 2,
        [
            pltpu.VMEM((length, length), BF), pltpu.VMEM((length, length), F32),
            pltpu.VMEM((8, length, length), BF), pltpu.VMEM((side, length), F32),
        ],
        (two_rows, taps_0, taps_1, *values, grad_conv_0, grad_conv_1),
        16e9,
    )
    grad_values_1, grad_taps_1, near_sums.ex, near_sums.ey, third_got = stage(
        grad_values_1, grad_taps_1, near_sums.ex, near_sums.ey, third_got
    )
    near_sums.middle()
    cut = slice(0, part), slice(part, depth)
    second_low = swap(added(second_sum[:, cut[0]], third_got[:, cut[0]]), "mp", 4)
    second_rest = second_sum[:, cut[1]], third_got[:, cut[1]]
    feed_got = swap(feed_other, "mp", 1)
    results = kernel_call(
        functools.partial(mixer_back_kernel, sizes), "mixer_back",
        [shaped(length, width), shaped(length, width)]
        + [
            shaped(chips, half, 128), shaped(chips, half + 16, 128), shaped(chips, half, 128),
            shaped(chips, half + 16, 128), shaped(2, chips, half + 16, 128),
            shaped(2, chips, half, 128),
        ],
        [
            pltpu.VMEM((width, 128), BF), pltpu.VMEM((width, 128), BF),
            pltpu.VMEM((width, 128), BF), pltpu.VMEM((2, filters, 2 * length), F32),
        ],
        (
            dp_one, tokens, other, gain_first, gain_two_part, grad_gates_0, grad_gates_1,
            mixout_grad, weights, condition, shift, cond, summary, grad_values_0, grad_values_1,
            grad_taps_0, grad_taps_1,
        ),
        8 * total * width * side, scalars=1,
    )
    results, near_sums.f1a, near_sums.f2b, second_low, second_rest = stage(
        results, near_sums.f1a, near_sums.f2b, second_low, second_rest
    )
    second_high = swap(added(*second_rest), "mp", 4)
    mixer_grads = Scatter(results[2:])
    mixer_grads.start()
    got_one = swap(results[1], "mp", 1)
    own_sum, first_sum = near_sums.end()
    first_got = swap(first_sum, "mp", 2)
    got_one, back_own = stage(got_one, results[0])
    input_grad = kernel_call(
        norm_one_back_kernel, "norm_one_back",
        [shaped(length, width)], [],
        (tokens, back_own, got_one, grad_middle, gain_first),
        1e9,
    )[0]
    input_grad, mixer_grads.ex, mixer_grads.ey, second_high = stage(
        input_grad, mixer_grads.ex, mixer_grads.ey, second_high
    )
    mixer_grads.middle()
    mixer_grads.f1a, mixer_grads.f2b, feed_got, first_got = stage(
        mixer_grads.f1a, mixer_grads.f2b, feed_got, first_got
    )
    ffn_terms = (own_sum, first_got, jnp.concatenate([second_low, second_high], axis=1))
    mixer_terms = mixer_grads.end()
    mixer_terms = [mixer_terms[0]] + [swap(mixer_terms[k], "mp", 2 * k) for k in range(1, chips)]
    gate_sum, up_sum, down_sum = sum(t.astype(F32) for t in ffn_terms)
    output = (
        tokens.astype(F32) + branch[:length].astype(F32) + branch_got[length:].astype(F32)
        + feed.astype(F32) + feed_got.astype(F32)
    ).astype(BF)
    value_sum, mixgate_sum, condition_sum, base_sum, shift_sum, mixout_sum, gain_sums = kernel_call(
        functools.partial(unpack_kernel, half, span), "unpack",
        [
            shaped(depth, block_c, dtype=F32), shaped(depth, block_c, dtype=F32),
            shaped(block_g, depth, dtype=F32), shaped(block_g, taps, dtype=F32),
            shaped(block_g, taps, dtype=F32), shaped(block_c, depth, dtype=F32),
            shaped(2, width, dtype=F32),
        ],
        [], tuple(mixer_terms), 1e6,
    )
    gain_sums = gain_sums + swap(gain_sums, "mp", 1)
    return (
        output, input_grad, gain_sums[0], gain_sums[1], value_sum, mixgate_sum, condition_sum.T,
        base_sum, shift_sum, mixout_sum, gate_sum, up_sum, down_sum.T,
    )


def choose(tokens, segment_ids, gain_one, gain_two, value_weight, mixgate_weight, condition_weight,
           filter_base, filter_shift, mixout_weight, gate_weight, up_weight, down_weight,
           output_grad):
    fits = (
        lax.axis_size("dp") == 4
        and lax.axis_size("mp") == 8
        and tokens.shape[0] == segment_ids.shape[1] == 512
        and value_weight.shape == (192, 96)
        and filter_base.shape == (6, 256)
        and gate_weight.shape == (192, 384)
    )
    return (fast_body if fits else body)(
        tokens, segment_ids, gain_one, gain_two, value_weight, mixgate_weight, condition_weight,
        filter_base, filter_shift, mixout_weight, gate_weight, up_weight, down_weight, output_grad,
    )


def solution(mesh):
    sides = P(("dp", "mp"), None)
    columns, rows = P("dp", "mp"), P("mp", "dp")
    in_specs = (
        sides, P("dp", None), P(), P(), columns, columns, columns, rows, rows, rows, columns,
        columns, rows, sides,
    )
    out_specs = (
        sides, sides, P(), P(), columns, columns, columns, rows, rows, rows, columns, columns, rows,
    )
    return jax.shard_map(choose, mesh=mesh, in_specs=in_specs, out_specs=out_specs, check_vma=False)
```

```python
import functools

import jax
import jax.numpy as jnp
from jax import lax
from jax.experimental import pallas as pl
from jax.experimental.pallas import tpu as pltpu
from jax.sharding import PartitionSpec as P

epsilon = 1e-05
highest = lax.Precision.HIGHEST
BF = jnp.bfloat16
F32 = jnp.float32
BLOCK = 128
SENTENCE = 256


def build_band(taps_row, mask_ref, band_ref, length, reach):
    blocks = length // BLOCK
    low = length - (reach + 1) * BLOCK
    width = (2 * reach + 2) * BLOCK
    spread = jnp.broadcast_to(taps_row[:, low : low + width], (BLOCK, width))
    shifted = pltpu.roll(spread, 0, 1, stride=1, stride_axis=0).astype(BF)
    for i in range(blocks):
        first, last = max(0, i - reach), min(blocks, i + reach + 1)
        rows = slice(i * BLOCK, (i + 1) * BLOCK)
        columns = slice(first * BLOCK, last * BLOCK)
        offset = (first - i + reach + 1) * BLOCK
        band_ref[rows, columns] = (
            shifted[:, offset : offset + (last - first) * BLOCK] * mask_ref[rows, columns]
        )


def conv_forward_kernel(
    unroll, channels, reach, column_ref, row_ref, cond_ref, base_ref, shift_ref, values_ref,
    conv_ref, mask_ref, taps_ref, band_ref,
):
    length = row_ref.shape[1]
    filters = base_ref.shape[0]
    mask_ref[...] = (column_ref[...] == row_ref[...]).astype(BF)
    taps_ref[...] = base_ref[...].astype(F32) + cond_ref[...] * shift_ref[...].astype(F32)
    band_ref[...] = jnp.zeros_like(band_ref)

    def some(step, carry):
        for u in range(unroll):
            f = step * unroll + u
            build_band(taps_ref[pl.ds(f, 1), :], mask_ref, band_ref.at[u], length, reach)
            rows = pl.ds(pl.multiple_of(f * channels, channels), channels)
            conv_ref[rows, :] = jnp.dot(
                values_ref[rows, :], band_ref[u], preferred_element_type=F32
            )
        return carry

    lax.fori_loop(0, filters // unroll, some, 0)


def conv_forward(segments, cond, base, shift, values, unroll=8):
    filters, length = base.shape[0], segments.shape[0]
    channels = values.shape[0] // filters
    unroll = next(u for u in range(unroll, 0, -1) if filters % u == 0)
    vmem = pl.BlockSpec(memory_space=pltpu.VMEM)
    flops = 2 * values.shape[0] * length * length
    return pl.pallas_call(
        functools.partial(conv_forward_kernel, unroll, channels, SENTENCE // BLOCK),
        out_shape=jax.ShapeDtypeStruct(values.shape, F32),
        in_specs=[vmem] * 6,
        out_specs=vmem,
        scratch_shapes=[
            pltpu.VMEM((length, length), BF),
            pltpu.VMEM(base.shape, F32),
            pltpu.VMEM((unroll, length, length), BF),
        ],
        compiler_params=pltpu.CompilerParams(vmem_limit_bytes=40 << 20),
        cost_estimate=pl.CostEstimate(
            flops=flops * 16, bytes_accessed=values.size * 6, transcendentals=0
        ),
        name="conv_forward",
    )(segments[:, None], segments[None, :], cond[:, None], base, shift, values)


def conv_backward_kernel(
    unroll, channels, reach, column_ref, turned_ref, row_ref, cond_ref, base_ref, shift_ref,
    values_ref, grad_ref, grad_values_ref, grad_taps_ref, mask_ref, mask_turned_ref, taps_ref,
    band_ref, grad_turned_ref,
):
    length = row_ref.shape[1]
    filters = base_ref.shape[0]
    blocks = length // BLOCK
    mask_ref[...] = (column_ref[...] == row_ref[...]).astype(BF)
    mask_turned_ref[...] = (turned_ref[...] == row_ref[...]).astype(F32)
    taps_ref[...] = base_ref[...].astype(F32) + cond_ref[...] * shift_ref[...].astype(F32)
    band_ref[...] = jnp.zeros_like(band_ref)
    turn = (
        lax.broadcasted_iota(jnp.int32, (length, length), 0)
        + lax.broadcasted_iota(jnp.int32, (length, length), 1)
        == length - 1
    ).astype(BF)
    grad_turned_ref[...] = jnp.dot(grad_ref[...], turn, preferred_element_type=F32)

    def some(step, carry):
        for u in range(unroll):
            f = step * unroll + u
            build_band(taps_ref[pl.ds(f, 1), :], mask_ref, band_ref.at[u], length, reach)
            rows = pl.ds(pl.multiple_of(f * channels, channels), channels)
            grad_values_ref[rows, :] = jnp.dot(
                grad_ref[rows, :], band_ref[u], preferred_element_type=F32
            ).astype(BF)
            turned = grad_turned_ref[rows, :].T.astype(BF)
            product = jnp.dot(turned, values_ref[rows, :], preferred_element_type=F32)
            parts = [jnp.zeros((BLOCK, BLOCK), F32)] + [None] * (2 * reach + 1)
            for i in range(blocks):
                back = blocks - 1 - i
                for j in range(max(0, back - reach), min(blocks, back + reach + 1)):
                    here = (
                        slice(i * BLOCK, (i + 1) * BLOCK),
                        slice(j * BLOCK, (j + 1) * BLOCK),
                    )
                    block = product[here] * mask_turned_ref[here]
                    d = j - back + reach + 1
                    parts[d] = block if parts[d] is None else parts[d] + block
            aligned = pltpu.roll(jnp.concatenate(parts, axis=1), 0, 1, stride=1, stride_axis=0)
            grad_taps_ref[pl.ds(f, 1), :] = jnp.sum(aligned, axis=0, keepdims=True)
        return carry

    lax.fori_loop(0, filters // unroll, some, 0)


def conv_backward(segments, cond, base_turned, shift_turned, values, grad, unroll=4):
    filters, length = base_turned.shape[0], segments.shape[0]
    channels = values.shape[0] // filters
    reach = SENTENCE // BLOCK
    width = (2 * reach + 2) * BLOCK
    unroll = next(u for u in range(unroll, 0, -1) if filters % u == 0)
    vmem = pl.BlockSpec(memory_space=pltpu.VMEM)
    flops = 2 * values.shape[0] * length * length
    grad_values, grad_taps = pl.pallas_call(
        functools.partial(conv_backward_kernel, unroll, channels, reach),
        out_shape=(
            jax.ShapeDtypeStruct(values.shape, BF),
            jax.ShapeDtypeStruct((filters, width), F32),
        ),
        in_specs=[vmem] * 8,
        out_specs=(vmem, vmem),
        scratch_shapes=[
            pltpu.VMEM((length, length), BF),
            pltpu.VMEM((length, length), F32),
            pltpu.VMEM(base_turned.shape, F32),
            pltpu.VMEM((unroll, length, length), BF),
            pltpu.VMEM(values.shape, F32),
        ],
        compiler_params=pltpu.CompilerParams(vmem_limit_bytes=48 << 20),
        cost_estimate=pl.CostEstimate(
            flops=flops * 32, bytes_accessed=values.size * 6, transcendentals=0
        ),
        name="conv_backward",
    )(
        segments[:, None],
        segments[::-1][:, None],
        segments[None, :],
        cond[:, None],
        base_turned,
        shift_turned,
        values,
        grad,
    )
    lags = jnp.roll(grad_taps, -(BLOCK - 1), axis=1)[:, ::-1]
    start = length + (reach + 1) * BLOCK - (width - 1)
    full = jnp.pad(lags, ((0, 0), (start, 2 * length - start - width + 1)))
    return grad_values, full[:, : 2 * length]


def swap(value, axis, mask):
    return lax.ppermute(value, axis, [(i, i ^ mask) for i in range(lax.axis_size(axis))])


def bits_of(count):
    return [1 << b for b in range(count.bit_length() - 1)]


def gather_dp(block):
    bits = bits_of(lax.axis_size("dp"))
    half = block.shape[1] // 2
    found = []
    for part, order in ((block[:, :half], bits), (block[:, half:], bits[::-1])):
        held, masks = part[None], [0]
        for bit in order:
            held = jnp.concatenate([held, swap(held, "dp", bit)], axis=0)
            masks = masks + [m | bit for m in masks]
        found.append({m: held[i] for i, m in enumerate(masks)})
    return [jnp.concatenate([f[m] for f in found], axis=1) for m in range(lax.axis_size("dp"))]


def natural(pieces, me):
    held = jnp.stack(pieces)
    return jnp.concatenate(
        [lax.dynamic_index_in_dim(held, j ^ me, 0, keepdims=False) for j in range(len(pieces))],
        axis=1,
    )


def scatter_dp(pieces):
    bits = bits_of(lax.axis_size("dp"))
    half = pieces[0].shape[1] // 2
    done = []
    for part, order in ((slice(None, half), bits[::-1]), (slice(half, None), bits)):
        held = {m: p[:, part] for m, p in enumerate(pieces)}
        for bit in order:
            stay = [m for m in held if not m & bit]
            got = swap(jnp.stack([held[m | bit] for m in stay]), "dp", bit)
            held = {m: held[m] + got[i] for i, m in enumerate(stay)}
        done.append(held[0])
    return jnp.concatenate(done, axis=1)


def everywhere(value):
    for bit in bits_of(lax.axis_size("mp")):
        value = value + swap(value, "mp", bit)
    for bit in bits_of(lax.axis_size("dp")):
        value = value + swap(value, "dp", bit)
    return value


def statistics(value):
    centred = value - jnp.mean(value, axis=-1, keepdims=True)
    scale = lax.rsqrt(jnp.mean(centred * centred, axis=-1, keepdims=True) + epsilon)
    return centred * scale, scale


def normalize_back(normal, scale, gain, grad):
    scaled = grad * gain
    return scale * (
        scaled
        - jnp.mean(scaled, axis=-1, keepdims=True)
        - normal * jnp.mean(scaled * normal, axis=-1, keepdims=True)
    )


def mm(left, right, dims):
    return lax.dot_general(left, right, (dims, ((), ())), preferred_element_type=F32)


def body(
    tokens, segment_ids, gain_one, gain_two, value_weight, mixgate_weight, condition_weight,
    filter_base, filter_shift, mixout_weight, gate_weight, up_weight, down_weight, output_grad,
):
    dp_size, mp_size = lax.axis_size("dp"), lax.axis_size("mp")
    dp, mp = lax.axis_index("dp"), lax.axis_index("mp")
    core = mp & 1
    chips = mp_size // 2
    local, width = tokens.shape
    length = segment_ids.shape[1]
    whole_rows = local % length == 0
    total = 2 * local
    rows = total // length

    def pair(own, other):
        if whole_rows:
            return jnp.concatenate([own, other], axis=0)
        first = core == 0
        return jnp.concatenate([jnp.where(first, own, other), jnp.where(first, other, own)], axis=0)

    def mine(value):
        return value[:local] if whole_rows else lax.dynamic_slice_in_dim(value, core * local, local)

    def others(value):
        if whole_rows:
            return value[local:]
        return lax.dynamic_slice_in_dim(value, (1 - core) * local, local)

    def pair_sum(value):
        got = swap(value, "mp", 1)
        if whole_rows:
            got = jnp.concatenate([got[local:], got[:local]], axis=0)
        return value.astype(F32) + got.astype(F32)

    def pair_scatter(value):
        return mine(value) + swap(others(value).astype(BF), "mp", 1).astype(F32)

    block_c = value_weight.shape[1]
    block_g = condition_weight.shape[1]
    block_f = gate_weight.shape[1]
    taps = filter_base.shape[1]
    mixer_pack = jnp.stack([value_weight, mixgate_weight, mixout_weight.T])
    filter_pack = jnp.stack([filter_base.T, filter_shift.T])
    ffn_pack = jnp.stack([gate_weight, up_weight, down_weight.T])

    tokens_all = pair(tokens, swap(tokens, "mp", 1))
    grad_all = pair(output_grad, swap(output_grad, "mp", 1))
    if whole_rows:
        per = local // length
        seg_rows = jnp.concatenate(
            [
                lax.dynamic_slice_in_dim(segment_ids, mp * per, per),
                lax.dynamic_slice_in_dim(segment_ids, (mp ^ 1) * per, per),
            ]
        )
    else:
        seg_rows = lax.dynamic_slice_in_dim(segment_ids, (mp // 2) * rows, rows)

    def gather(block):
        found = [block] + [swap(block, "mp", 2 * k) for k in range(1, chips)]
        return [natural(gather_dp(b), dp) for b in found]

    mixer = jnp.concatenate(gather(mixer_pack), axis=2)
    small = jnp.concatenate(gather(jnp.pad(condition_weight, ((0, 0), (0, 0)))[None]), axis=2)[0]
    filters = jnp.concatenate(gather(filter_pack), axis=2)
    ffn = gather(ffn_pack)
    value_full, mixgate_full, mixout_full = mixer
    base, shift = jnp.swapaxes(filters, 1, 2)
    base_turned = jnp.roll(base[:, ::-1], 1, axis=1)
    shift_turned = jnp.roll(shift[:, ::-1], 1, axis=1)

    xf = tokens_all.astype(F32)
    normal_one, scale_one = statistics(xf)
    normed_one = (normal_one * gain_one).astype(BF)
    values = mm(value_full, normed_one, ((0,), (1,))).astype(BF)
    gates = mm(mixgate_full, normed_one, ((0,), (1,)))
    summary = jnp.mean(normed_one.astype(F32).reshape(rows, length, width), axis=1)
    condition = small.astype(F32)
    cond = jnp.tanh(jnp.dot(summary, condition, precision=highest))
    cuts = [slice(r * length, (r + 1) * length) for r in range(rows)]
    conv = jnp.concatenate(
        [conv_forward(seg_rows[r], cond[r], base, shift, values[:, cuts[r]]) for r in range(rows)],
        axis=1,
    )
    mixed = (conv * gates).astype(BF)
    branch = pair_sum(mm(mixed, mixout_full, ((0,), (1,))).astype(BF))
    middle = xf + branch
    normal_two, scale_two = statistics(middle)
    normed_two = (normal_two * gain_two).astype(BF)

    feed = jnp.zeros((total, width), F32)
    grad_two = jnp.zeros((total, width), F32)
    ffn_grads = []
    for k in range(chips):
        gate_full, up_full, down_full = ffn[k]
        gate_pre = mm(normed_two, gate_full, ((1,), (0,)))
        up_pre = mm(normed_two, up_full, ((1,), (0,)))
        grad_hidden = mm(grad_all, down_full, ((1,), (0,)))
        sigmoid = jax.nn.sigmoid(gate_pre)
        silu = gate_pre * sigmoid
        hidden = (silu * up_pre).astype(BF)
        grad_gate = (grad_hidden * up_pre * (sigmoid + silu * (1.0 - sigmoid))).astype(BF)
        grad_up = (grad_hidden * silu).astype(BF)
        feed = feed + mm(hidden, down_full, ((1,), (1,)))
        grad_two = (
            grad_two + mm(grad_gate, gate_full, ((1,), (1,))) + mm(grad_up, up_full, ((1,), (1,)))
        )
        ffn_grads.append(
            jnp.stack(
                [
                    mm(normed_two, grad_gate, ((0,), (0,))).astype(BF),
                    mm(normed_two, grad_up, ((0,), (0,))).astype(BF),
                    mm(grad_all, hidden, ((0,), (0,))).astype(BF),
                ]
            )
        )

    def scatter(grads):
        sums = None
        for k, grad in enumerate(grads):
            size = grad.shape[1] // dp_size
            pieces = [
                lax.dynamic_slice_in_dim(grad, (dp ^ m) * size, size, axis=1)
                for m in range(dp_size)
            ]
            part = scatter_dp(pieces)
            part = part if k == 0 else swap(part, "mp", 2 * k)
            sums = part.astype(F32) if sums is None else sums + part.astype(F32)
        return sums

    gate_sum, up_sum, down_sum = scatter(ffn_grads)
    output = (mine(middle) + pair_scatter(feed)).astype(BF)

    grad_normed_two = pair_sum(grad_two.astype(BF))
    gain_two_part = jnp.sum(mine(grad_normed_two * normal_two), axis=0)
    grad_middle = grad_all.astype(F32) + normalize_back(
        normal_two, scale_two, gain_two, grad_normed_two
    )
    grad_branch = grad_middle.astype(BF)

    mixout_grad = mm(grad_branch, mixed, ((0,), (1,)))
    grad_mixed = mm(mixout_full, grad_branch, ((0,), (1,)))
    grad_conv = (grad_mixed * gates).astype(BF)
    grad_gates = (grad_mixed * conv).astype(BF)
    backs = [
        conv_backward(
            seg_rows[r], cond[r], base_turned, shift_turned, values[:, cuts[r]],
            grad_conv[:, cuts[r]],
        )
        for r in range(rows)
    ]
    grad_values = jnp.concatenate([b[0] for b in backs], axis=1)
    grad_taps = jnp.stack([b[1] for b in backs])
    base_grad = jnp.sum(grad_taps, axis=0)
    shift_grad = jnp.sum(grad_taps * cond[:, :, None], axis=0)
    grad_cond = jnp.sum(grad_taps * shift.astype(F32)[None], axis=2) * (1.0 - cond * cond)
    condition_grad = mm(summary, grad_cond, ((0,), (0,)))
    grad_summary = jnp.dot(grad_cond, condition.T, precision=highest) / length
    value_grad = mm(normed_one, grad_values, ((0,), (1,)))
    mixgate_grad = mm(normed_one, grad_gates, ((0,), (1,)))
    grad_one = mm(grad_values, value_full, ((0,), (1,))) + mm(
        grad_gates, mixgate_full, ((0,), (1,))
    )
    grad_one = (grad_one.reshape(rows, length, width) + grad_summary[:, None, :]).reshape(
        total, width
    )
    grad_normed_one = pair_scatter(grad_one)
    input_grad = (
        mine(grad_middle)
        + normalize_back(mine(normal_one), mine(scale_one), gain_one, grad_normed_one)
    ).astype(BF)
    gain_one_part = jnp.sum(grad_normed_one * mine(normal_one), axis=0)
    gain_one_grad, gain_two_grad = everywhere(jnp.stack([gain_one_part, gain_two_part]))

    def split(grad, size):
        return [grad[..., k * size : (k + 1) * size].astype(BF) for k in range(chips)]

    value_sum, mixgate_sum, mixout_sum = scatter(
        split(jnp.stack([value_grad, mixgate_grad, mixout_grad]), block_c)
    )
    condition_sum = scatter(split(condition_grad[None], block_g))[0]
    base_sum, shift_sum = scatter(
        split(jnp.swapaxes(jnp.stack([base_grad, shift_grad]), 1, 2), block_g)
    )
    return (
        output, input_grad, gain_one_grad, gain_two_grad, value_sum, mixgate_sum, condition_sum,
        base_sum.T, shift_sum.T, mixout_sum.T, gate_sum, up_sum, down_sum.T,
    )


def hold(count):
    return [pl.BlockSpec(memory_space=pltpu.VMEM)] * count


def shaped(*shape, dtype=BF):
    return jax.ShapeDtypeStruct(shape, dtype)


def kernel_call(body, name, outs, scratch, args, flops, transcendentals=0, scalars=0, limit=16):
    held = sum(a.size * a.dtype.itemsize for a in tuple(args) + tuple(outs))
    smem = [pl.BlockSpec(memory_space=pltpu.SMEM)] * scalars
    return pl.pallas_call(
        body,
        out_shape=tuple(outs),
        in_specs=smem + hold(len(args) - scalars),
        out_specs=tuple(hold(len(outs))),
        scratch_shapes=scratch,
        compiler_params=pltpu.CompilerParams(vmem_limit_bytes=limit << 20),
        cost_estimate=pl.CostEstimate(
            flops=int(flops), bytes_accessed=int(held), transcendentals=transcendentals
        ),
        name=name,
    )(*args)


def nn(left, right):
    return lax.dot_general(left, right, (((1,), (0,)), ((), ())), preferred_element_type=F32)


def nt(left, right):
    return lax.dot_general(left, right, (((1,), (1,)), ((), ())), preferred_element_type=F32)


def turned_over(value):
    return value.astype(F32).T


def fold(value):
    rows = value.shape[0] // 2
    return jnp.concatenate([value[:rows], value[rows:]], axis=1)


def pack_kernel(
    value_ref, mixgate_ref, condition_ref, base_ref, shift_ref, mixout_ref, gate_ref, up_ref,
    down_ref, mixer_ref, ffn_ref,
):
    depth, block_c = value_ref.shape
    block_g = condition_ref.shape[0]
    span = base_ref.shape[1] // 128
    spare = 128 - block_c
    mixgate = mixgate_ref[...].astype(F32)
    mixout = turned_over(mixout_ref[...])
    first = jnp.concatenate([value_ref[...].astype(F32), mixgate[:, :spare]], axis=1)
    second = jnp.concatenate([mixgate[:, spare:], mixout[:, : 2 * spare]], axis=1)
    condition = jnp.concatenate(
        [condition_ref[...].astype(F32), jnp.zeros((spare - block_g, depth), F32)], axis=0
    )
    third = jnp.concatenate([mixout[:, 2 * spare :], condition.T], axis=1)
    half = mixer_ref.shape[1]
    cut = half - depth
    mixer_ref[0, :depth, :] = first.astype(BF)
    mixer_ref[0, depth:, :] = second[:cut].astype(BF)
    mixer_ref[1, : depth - cut, :] = second[cut:].astype(BF)
    start = depth - cut + depth // 2
    mixer_ref[1, depth - cut : start, :] = fold(third).astype(BF)
    blank = jnp.zeros((16 - span * block_g, 128), F32)
    for ref in (base_ref, shift_ref):
        pieces = [ref[:, h * 128 : (h + 1) * 128].astype(F32) for h in range(span)] + [blank]
        mixer_ref[1, start : start + 16, :] = jnp.concatenate(pieces, axis=0).astype(BF)
        start += 16
    part = ffn_ref.shape[2]
    for h in range(2):
        cut = slice(h * part, (h + 1) * part)
        ffn_ref[h, 0] = gate_ref[cut, :]
        ffn_ref[h, 1] = up_ref[cut, :]
        ffn_ref[h, 2] = down_ref[cut, :]


def norm_rows(value, gain):
    centred = value - jnp.mean(value, axis=-1, keepdims=True)
    scale = lax.rsqrt(jnp.mean(centred * centred, axis=-1, keepdims=True) + epsilon)
    normal = centred * scale
    return normal, scale, normal * gain


def column_of(row):
    return jnp.broadcast_to(row.astype(F32), (8, row.shape[1])).T[:, :1]


def mixer_forward_kernel(
    sizes, dp_ref, row_ref, own_ref, other_ref, gain_ref, p0_ref, p1_ref, p2_ref,
    p3a_ref, p3b_ref, branch_ref, values_0, values_1, gates_0, gates_1, conv_0, conv_1,
    weights_ref, mixout_ref, condition_ref, taps_0, taps_1, shift_out_ref, cond_ref, summary_ref,
    one_ref, two_ref, three_ref, base_ref, mask_ref, band_ref, mixed_ref,
):
    depth, block_c, block_g, chips, span, unroll, channels, reach, half = sizes
    length = own_ref.shape[0]
    values_refs, gates_refs = (values_0, values_1), (gates_0, gates_1)
    conv_refs, taps_refs = (conv_0, conv_1), (taps_0, taps_1)
    dp = dp_ref[0]
    pieces = ((p0_ref, None), (p1_ref, None), (p2_ref, None), (p3a_ref, p3b_ref))
    side = chips * block_c
    spare, cut = 128 - block_c, half - depth
    filters = chips * block_g

    for k in range(chips):
        for m, (first, second) in enumerate(pieces):
            low = first.at[0, k] if second is None else first.at[k]
            high = first.at[1, k] if second is None else second.at[k]
            j = dp ^ m
            at = pl.multiple_of(j * depth, depth)
            one_ref[pl.ds(at, depth), :] = low[:depth, :]
            two_ref[pl.ds(at, cut), :] = low[depth:, :]
            two_ref[pl.ds(pl.multiple_of(at + cut, cut), depth - cut), :] = high[: depth - cut, :]
            start = depth - cut + depth // 2
            folded = high[depth - cut : start, :]
            three_ref[pl.ds(at, depth // 2), :] = folded
            three_ref[pl.ds(pl.multiple_of(at + depth // 2, depth // 2), depth // 2), :] = (
                jnp.concatenate([folded[:, 64:], folded[:, :64]], axis=1)
            )
            for ref in (base_ref, shift_out_ref):
                piece = high[start : start + 16, :].astype(F32)
                start += 16
                for h in range(span):
                    lane = pl.multiple_of((j * span + h) * 128, 128)
                    ref[k * block_g : (k + 1) * block_g, pl.ds(lane, 128)] = piece[
                        h * block_g : (h + 1) * block_g
                    ]
        here, there = k * block_c, side + k * block_c
        turned = turned_over(one_ref[...]).astype(BF)
        weights_ref[here : here + block_c, :] = turned[:block_c]
        weights_ref[there : there + spare, :] = turned[block_c:]
        turned = turned_over(two_ref[...]).astype(BF)
        weights_ref[there + spare : there + block_c, :] = turned[: block_c - spare]
        mixout_ref[here : here + 2 * spare, :] = turned[block_c - spare :]
        turned = turned_over(three_ref[...]).astype(BF)
        mixout_ref[here + 2 * spare : here + block_c, :] = turned[:spare]
        condition_ref[k * block_g : (k + 1) * block_g, :] = turned[spare : 2 * spare].astype(F32)[
            :block_g
        ]

    band_ref[...] = jnp.zeros_like(band_ref)
    for r, ref in enumerate((own_ref, other_ref)):
        _, _, normed = norm_rows(ref[...].astype(F32), gain_ref[...])
        normed = normed.astype(BF)
        summary = jnp.mean(normed.astype(F32), axis=0, keepdims=True)
        summary_ref[r : r + 1, :] = summary
        cond = jnp.tanh(jnp.sum(condition_ref[...] * summary, axis=1, keepdims=True))
        cond_ref[r] = jnp.broadcast_to(cond, cond_ref.shape[1:])
        taps_refs[r][...] = base_ref[...] + cond * shift_out_ref[...]
        values_refs[r][...] = nt(weights_ref[:side, :], normed).astype(BF)
        gates_refs[r][...] = nt(weights_ref[side:, :], normed).astype(BF)
        ids = row_ref[r : r + 1, :]
        mask_ref[...] = (column_of(ids) == ids.astype(F32)).astype(BF)

        def some(step, carry, r=r):
            for u in range(unroll):
                f = step * unroll + u
                build_band(taps_refs[r][pl.ds(f, 1), :], mask_ref, band_ref.at[u], length, reach)
                at = pl.ds(pl.multiple_of(f * channels, channels), channels)
                conv = nn(values_refs[r][at, :], band_ref[u])
                conv_refs[r][at, :] = conv.astype(BF)
                mixed_ref[at, :] = (conv * gates_refs[r][at, :].astype(F32)).astype(BF)
            return carry

        lax.fori_loop(0, filters // unroll, some, 0)
        branch_ref[r * length : (r + 1) * length, :] = nn(
            mixed_ref[...].T, mixout_ref[...]
        ).astype(BF)


def norm_two_kernel(
    own_ref, other_ref, branch_ref, got_ref, gain_ref, normed_ref, normed_turned_ref,
):
    local = own_ref.shape[0]
    for h, ref in enumerate((own_ref, other_ref)):
        here, there = slice(h * local, (h + 1) * local), slice((1 - h) * local, (2 - h) * local)
        middle = (
            ref[...].astype(F32) + branch_ref[here, :].astype(F32) + got_ref[there, :].astype(F32)
        )
        _, _, normed = norm_rows(middle, gain_ref[...])
        normed = normed.astype(BF)
        normed_ref[here, :] = normed
        normed_turned_ref[:, here] = normed.T


def turn_kernel(own_ref, other_ref, turned_ref):
    local = own_ref.shape[0]
    turned_ref[:, :local] = own_ref[...].T
    turned_ref[:, local:] = other_ref[...].T


def ffn_kernel(
    carried, kept, apart, dp_ref, normed_ref, normed_turned_ref, grad_own_ref, grad_other_ref,
    grad_turned_ref, p0_ref, p1_ref, p2_ref, p3a_ref, p3b_ref, *refs,
):
    before, refs = refs[: 3 * carried], refs[3 * carried :]
    pieces_count = 8 if apart else 6
    kept_refs, refs = refs[: pieces_count * kept], refs[pieces_count * kept :]
    feed_own_ref, feed_other_ref, back_ref, g0a, g0b, g1a, g2b = refs[:7]
    moving, refs = refs[7 : 3 + pieces_count], refs[3 + pieces_count :]
    two_ref, down_ref, hidden_ref, act_ref, two_grad_ref, down_grad_ref = refs
    local = grad_own_ref.shape[0]
    _, _, part, block = g0a.shape
    dp = dp_ref[0]
    pieces = ((p0_ref, None), (p1_ref, None), (p2_ref, None), (p3a_ref, p3b_ref))
    if apart:
        g1b, g2a, g3a, g3b = moving
    else:
        gx, gy = moving
        g1b, g2a, g3a, g3b = gx.at[0], gy.at[0], gy.at[1], gx.at[1]
    outs = ((g0a, g0b), (g1a, g1b), (g2a, g2b), (g3a, g3b))
    for m, (one, two) in enumerate(pieces):
        for h in range(2):
            source = one.at[h, 0] if two is None else (one, two)[h].at[0]
            at = pl.ds(pl.multiple_of((dp ^ m) * (2 * part) + h * part, part), part)
            two_ref[at, :block] = source[0]
            two_ref[at, block:] = source[1]
            down_ref[at, :] = source[2]
    for t, (grad_ref, feed_ref) in enumerate(
        ((grad_own_ref, feed_own_ref), (grad_other_ref, feed_other_ref))
    ):
        here = slice(t * local, (t + 1) * local)
        both = nn(normed_ref[here, :], two_ref[...])
        gate_pre, up_pre = both[:, :block], both[:, block:]
        grad_hidden = nn(grad_ref[...], down_ref[...])
        sigmoid = 1.0 / (1.0 + jnp.exp(-gate_pre))
        silu = gate_pre * sigmoid
        hidden = (silu * up_pre).astype(BF)
        hidden_ref[here, :] = hidden
        act_ref[here, :block] = (
            grad_hidden * up_pre * (sigmoid + silu * (1.0 - sigmoid))
        ).astype(BF)
        act_ref[here, block:] = (grad_hidden * silu).astype(BF)
        feed = nt(hidden, down_ref[...])
        back = nt(act_ref[here, :], two_ref[...])
        if carried:
            feed = feed + before[t][...]
            back = back + before[2][here, :]
        feed_ref[...] = feed.astype(feed_ref.dtype)
        back_ref[here, :] = back.astype(back_ref.dtype)
    two_grad_ref[...] = nn(normed_turned_ref[...], act_ref[...]).astype(BF)
    down_grad_ref[...] = nn(grad_turned_ref[...], hidden_ref[...]).astype(BF)
    if kept:
        for source, target in zip(kept_refs, (g0a, g0b, g1a, g2b) + tuple(moving)):
            if len(target.shape) == 4:
                target[0] = source[0]
            else:
                target[:, 0] = source[:, 0]
    for m, pair in enumerate(outs):
        for h in range(2):
            at = pl.ds(pl.multiple_of((dp ^ m) * (2 * part) + h * part, part), part)
            pair[h][int(kept), 0] = two_grad_ref[at, :block]
            pair[h][int(kept), 1] = two_grad_ref[at, block:]
            pair[h][int(kept), 2] = down_grad_ref[at, :]


def ffn_call(fixed, group, before=(), kept=(), last=False, apart=False):
    total, width = fixed[1].shape
    local = fixed[3].shape[0]
    _, _, _, part, block = group[0].shape
    count, kind = 1 + bool(kept), BF if last else F32
    outs = [
        shaped(local, width, dtype=kind), shaped(local, width, dtype=kind),
        shaped(total, width, dtype=kind),
    ]
    if apart:
        outs += [shaped(count, 3, part, block)] * 8
    else:
        outs += [shaped(count, 3, part, block)] * 4 + [shaped(2, count, 3, part, block)] * 2
    return kernel_call(
        functools.partial(ffn_kernel, bool(before), bool(kept), apart), "feed_forward", outs,
        [
            pltpu.VMEM((width, 2 * block), BF), pltpu.VMEM((width, block), BF),
            pltpu.VMEM((total, block), BF), pltpu.VMEM((total, 2 * block), BF),
            pltpu.VMEM((width, 2 * block), BF), pltpu.VMEM((width, block), BF),
        ],
        fixed + tuple(group) + tuple(before) + tuple(kept),
        18 * total * width * block, transcendentals=total * block, scalars=1,
    )


def mixout_back_kernel(
    own_ref, other_ref, branch_ref, got_ref, back_ref, back_got_ref, grad_own_ref, grad_other_ref,
    gain_ref, weights_ref, gates_0, gates_1, conv_0, conv_1, middle_ref, mixout_ref, grad_conv_0,
    grad_conv_1, grad_gates_0, grad_gates_1, gain_grad_ref,
):
    local = own_ref.shape[0]
    mixout = None
    for h, (ref, grad_ref, gates_ref, conv_ref, grad_conv_ref, grad_gates_ref) in enumerate(
        (
            (own_ref, grad_own_ref, gates_0, conv_0, grad_conv_0, grad_gates_0),
            (other_ref, grad_other_ref, gates_1, conv_1, grad_conv_1, grad_gates_1),
        )
    ):
        here, there = slice(h * local, (h + 1) * local), slice((1 - h) * local, (2 - h) * local)
        middle = (
            ref[...].astype(F32) + branch_ref[here, :].astype(F32) + got_ref[there, :].astype(F32)
        )
        normal, scale, _ = norm_rows(middle, gain_ref[...])
        grad = back_ref[here, :].astype(F32) + back_got_ref[there, :].astype(F32)
        grad_middle = grad_ref[...].astype(F32) + normalize_back(
            normal, scale, gain_ref[...], grad
        )
        if h == 0:
            gain_grad_ref[...] = jnp.sum(grad * normal, axis=0, keepdims=True)
            middle_ref[...] = grad_middle
        rounded = grad_middle.astype(BF)
        grad_mixed = nt(weights_ref[...], rounded)
        gates, conv = gates_ref[...].astype(F32), conv_ref[...].astype(F32)
        grad_conv_ref[...] = (grad_mixed * gates).astype(BF)
        grad_gates_ref[...] = (grad_mixed * conv).astype(BF)
        part = nn((gates * conv).astype(BF), rounded)
        mixout = part if h == 0 else mixout + part
    mixout_ref[...] = mixout.astype(BF)


def conv_back_kernel(
    unroll, channels, reach, row_ref, taps_0, taps_1, values_0, values_1, grad_0, grad_1,
    grad_values_0, grad_values_1, grad_taps_0, grad_taps_1, *scratch,
):
    for r, refs in enumerate(
        (
            (taps_0, values_0, grad_0, grad_values_0, grad_taps_0),
            (taps_1, values_1, grad_1, grad_values_1, grad_taps_1),
        )
    ):
        conv_back_row(unroll, channels, reach, r, row_ref, *refs, *scratch)


def conv_back_row(
    unroll, channels, reach, r, row_ref, taps_ref, values_ref, grad_ref, grad_values_ref,
    grad_taps_ref, mask_ref, mask_turned_ref, band_ref, grad_turned_ref,
):
    length = row_ref.shape[1]
    filters = taps_ref.shape[0]
    blocks = length // BLOCK
    ids = row_ref[r : r + 1, :]
    mask_ref[...] = (column_of(ids) == ids.astype(F32)).astype(BF)
    band_ref[...] = jnp.zeros_like(band_ref)
    turn = (
        lax.broadcasted_iota(jnp.int32, (length, length), 0)
        + lax.broadcasted_iota(jnp.int32, (length, length), 1)
        == length - 1
    ).astype(BF)
    grad_turned_ref[...] = nn(grad_ref[...], turn)
    mask_turned_ref[...] = nn(turn, mask_ref[...])

    def some(step, carry):
        for u in range(unroll):
            f = step * unroll + u
            build_band(taps_ref[pl.ds(f, 1), :], mask_ref, band_ref.at[u], length, reach)
            rows = pl.ds(pl.multiple_of(f * channels, channels), channels)
            grad_values_ref[rows, :] = nt(grad_ref[rows, :], band_ref[u]).astype(BF)
            turned = grad_turned_ref[rows, :].T.astype(BF)
            product = nn(turned, values_ref[rows, :])
            parts = [jnp.zeros((BLOCK, BLOCK), F32)] + [None] * (2 * reach + 1)
            for i in range(blocks):
                back = blocks - 1 - i
                for j in range(max(0, back - reach), min(blocks, back + reach + 1)):
                    here = (
                        slice(i * BLOCK, (i + 1) * BLOCK),
                        slice(j * BLOCK, (j + 1) * BLOCK),
                    )
                    block = product[here] * mask_turned_ref[here]
                    d = j - back + reach + 1
                    parts[d] = block if parts[d] is None else parts[d] + block
            aligned = pltpu.roll(jnp.concatenate(parts, axis=1), 0, 1, stride=1, stride_axis=0)
            grad_taps_ref[pl.ds(f, 1), :] = jnp.sum(aligned, axis=0, keepdims=True)
        return carry

    lax.fori_loop(0, filters // unroll, some, 0)


def mixer_back_kernel(
    sizes, dp_ref, own_ref, other_ref, gain_ref, gain_two_ref, gates_0, gates_1, mixout_ref,
    weights_ref, condition_ref, shift_ref, cond_ref, summary_ref, values_0, values_1, taps_0,
    taps_1, back_own_ref, back_other_ref, g0a_ref, g0b_ref, g1a_ref, g2b_ref, gx_ref, gy_ref,
    one_ref, two_ref, three_ref, filter_ref,
):
    depth, block_c, block_g, chips, span, unroll, channels, reach, half = sizes
    length = own_ref.shape[0]
    side = chips * block_c
    filters = chips * block_g
    width = taps_0.shape[1]
    taps = shift_ref.shape[1]
    spare, cut = 128 - block_c, half - depth
    dp = dp_ref[0]
    lane = lax.broadcasted_iota(jnp.int32, (width, taps), 0)
    tap = lax.broadcasted_iota(jnp.int32, (width, taps), 1)
    reachable = (tap > taps // 2 - (reach + 1) * BLOCK) & (tap < taps // 2 + (reach + 1) * BLOCK)
    spot = taps - 1 - tap
    spot = jnp.where(spot >= width, spot - width, spot)
    place = ((lane == spot) & reachable).astype(BF)
    shift_there = nt(shift_ref[...].astype(BF), place)
    base_grad = shift_grad = condition_grad = value_grad = gate_grad = gain_grad = None
    for r, (ref, values_ref, gates_ref, taps_ref, back_ref) in enumerate(
        (
            (own_ref, values_0, gates_0, taps_0, back_own_ref),
            (other_ref, values_1, gates_1, taps_1, back_other_ref),
        )
    ):
        normal, _, normed = norm_rows(ref[...].astype(F32), gain_ref[...])
        normed = normed.astype(BF)
        grad_taps = taps_ref[...]
        cond = cond_ref[r, :, :1]
        summary = summary_ref[r : r + 1, :]
        grad_cond = jnp.sum(grad_taps * shift_there, axis=1, keepdims=True) * (1.0 - cond * cond)
        grad_summary = jnp.sum(grad_cond * condition_ref[...], axis=0, keepdims=True) / length
        values, gates = values_ref[...], gates_ref[...]
        back = nn(values.T, weights_ref[:side, :]) + nn(gates.T, weights_ref[side:, :])
        back = back + grad_summary
        back_ref[...] = back.astype(BF)
        parts = (
            grad_taps, cond * grad_taps, grad_cond * summary, nn(values, normed),
            nn(gates, normed), jnp.sum(back * normal, axis=0, keepdims=True),
        )
        if r > 0:
            parts = tuple(
                p + q
                for p, q in zip(
                    (base_grad, shift_grad, condition_grad, value_grad, gate_grad, gain_grad), parts
                )
            )
        base_grad, shift_grad, condition_grad, value_grad, gate_grad, gain_grad = parts
    filter_ref[0] = nn(base_grad.astype(BF), place)
    filter_ref[1] = nn(shift_grad.astype(BF), place)
    gain_rows = jnp.concatenate(
        [
            vector[:, h * 128 : (h + 1) * 128]
            for vector in (gain_grad, gain_two_ref[...])
            for h in range(vector.shape[1] // 128)
        ],
        axis=0,
    )
    gain_rows = jnp.concatenate(
        [gain_rows, jnp.zeros((16 - gain_rows.shape[0], 128), F32)], axis=0
    ).astype(BF)
    outs = (
        (g0a_ref, g0b_ref), (g1a_ref, gx_ref.at[0]), (gy_ref.at[0], g2b_ref),
        (gy_ref.at[1], gx_ref.at[1]),
    )
    empty = jnp.zeros((128 - spare - block_g, value_grad.shape[1]), F32)
    blank = jnp.zeros((16 - span * block_g, 128), F32)
    for k in range(chips):
        at = k * block_c
        own = slice(k * block_g, (k + 1) * block_g)
        mixout = mixout_ref[at : at + block_c, :].astype(F32)
        value, gate = value_grad[at : at + block_c], gate_grad[at : at + block_c]
        one_ref[...] = jnp.concatenate([value, gate[:spare]], axis=0).T.astype(BF)
        two_ref[...] = jnp.concatenate([gate[spare:], mixout[: 2 * spare]], axis=0).T.astype(BF)
        third = jnp.concatenate(
            [mixout[2 * spare :], condition_grad[own], empty], axis=0
        ).T
        for j in range(third.shape[0] // depth):
            three_ref[j * (depth // 2) : (j + 1) * (depth // 2), :] = fold(
                third[j * depth : (j + 1) * depth, :64]
            ).astype(BF)
        for m, (low, high) in enumerate(outs):
            j = dp ^ m
            at = pl.multiple_of(j * depth, depth)
            low[k, :depth, :] = one_ref[pl.ds(at, depth), :]
            low[k, depth:, :] = two_ref[pl.ds(at, cut), :]
            high[k, : depth - cut, :] = two_ref[
                pl.ds(pl.multiple_of(at + cut, cut), depth - cut), :
            ]
            start = depth - cut + depth // 2
            high[k, depth - cut : start, :] = three_ref[
                pl.ds(pl.multiple_of(j * (depth // 2), depth // 2), depth // 2), :
            ]
            for n in range(2):
                parts = [
                    filter_ref[n, own, pl.ds(pl.multiple_of((j * span + h) * 128, 128), 128)]
                    for h in range(span)
                ] + [blank]
                high[k, start : start + 16, :] = jnp.concatenate(parts, axis=0).astype(BF)
                start += 16
            high[k, start:, :] = gain_rows


def unpack_kernel(
    half, span, p0_ref, p1_ref, p2_ref, p3_ref, value_ref, mixgate_ref, condition_ref, base_ref,
    shift_ref, mixout_ref, gains_ref,
):
    depth, block_c = value_ref.shape
    block_g = condition_ref.shape[0]
    spare, cut = 128 - block_c, half - depth
    total = p0_ref[...].astype(F32) + p1_ref[...].astype(F32)
    total = total + p2_ref[...].astype(F32) + p3_ref[...].astype(F32)
    first, second = total[:depth], total[depth : 2 * depth]
    start = 2 * depth + depth // 2
    folded = total[2 * depth : start]
    third = jnp.concatenate([folded[:, :64], folded[:, 64:]], axis=0)
    value_ref[...] = first[:, :block_c]
    mixgate_ref[...] = jnp.concatenate([first[:, block_c:], second[:, : block_c - spare]], axis=1)
    mixout_ref[...] = jnp.concatenate(
        [second[:, block_c - spare :], third[:, :spare]], axis=1
    ).T
    condition_ref[...] = third[:, spare:].T[:block_g]
    for ref in (base_ref, shift_ref):
        for h in range(span):
            ref[:, h * 128 : (h + 1) * 128] = total[start + h * block_g : start + (h + 1) * block_g]
        start += 16
    rows = gains_ref.shape[1] // 128
    for g in range(2):
        for h in range(rows):
            at = start + g * rows + h
            gains_ref[g : g + 1, h * 128 : (h + 1) * 128] = total[at : at + 1]


def norm_one_back_kernel(
    own_ref, back_ref, got_ref, middle_ref, gain_ref, grad_ref
):
    normal, scale, _ = norm_rows(own_ref[...].astype(F32), gain_ref[...])
    grad = back_ref[...].astype(F32) + got_ref[...].astype(F32)
    grad_ref[...] = (
        middle_ref[...] + normalize_back(normal, scale, gain_ref[...], grad)
    ).astype(BF)


def stage(*values):
    return lax.optimization_barrier(values)


def sides(column):
    return swap(column, "dp", 1), swap(column, "dp", 2)


def corners(along_x, along_y):
    return swap(along_x[0], "dp", 2), swap(along_y[1], "dp", 1)


def added(*terms):
    return sum(t.astype(F32) for t in terms).astype(BF)


class Scatter:
    def __init__(self, pieces):
        self.g0a, self.g0b, self.g1a, self.g2b, self.gx, self.gy = pieces

    def start(self):
        self.ex, self.ey = swap(self.gx, "dp", 1), swap(self.gy, "dp", 2)

    def middle(self):
        self.f1a = swap(added(self.g1a, self.ey[1]), "dp", 1)
        self.f2b = swap(added(self.g2b, self.ex[1]), "dp", 2)

    def end(self):
        f1a, f2b = self.f1a, self.f2b
        return [
            jnp.concatenate(
                [added(self.g0a[k], f1a[k], self.ey[0][k]), added(self.g0b[k], self.ex[0][k], f2b[k])],
                axis=-2,
            )
            for k in range(self.g0a.shape[0])
        ]


def fast_body(
    tokens, segment_ids, gain_one, gain_two, value_weight, mixgate_weight, condition_weight,
    filter_base, filter_shift, mixout_weight, gate_weight, up_weight, down_weight, output_grad,
):
    dp, mp = lax.axis_index("dp"), lax.axis_index("mp")
    chips = lax.axis_size("mp") // 2
    length, width = tokens.shape
    rows, total = 2, 2 * length
    depth, block_c = value_weight.shape
    block_g, taps = filter_base.shape
    block_f = gate_weight.shape[1]
    channels = block_c // block_g
    reach = SENTENCE // BLOCK
    side, filters = chips * block_c, chips * block_g
    half = 4 * depth // 3
    part = depth // 2
    span = taps // 128
    sizes = (depth, block_c, block_g, chips, span, 8, channels, reach, half)

    other, other_grad = swap(tokens, "mp", 1), swap(output_grad, "mp", 1)
    mixer_pack, ffn_pack = kernel_call(
        pack_kernel, "pack_weights",
        [shaped(2, half, 128), shaped(2, 3, part, block_f)], [],
        (
            value_weight, mixgate_weight, condition_weight.T, filter_base, filter_shift,
            mixout_weight, gate_weight, up_weight, down_weight.T,
        ),
        1e6, limit=60,
    )
    mixer_pack, ffn_pack, other_grad = stage(mixer_pack, ffn_pack, other_grad)

    mixer_line = [mixer_pack] + [swap(mixer_pack, "mp", 2 * k) for k in range(1, chips)]
    dp_one = dp[None].astype(jnp.int32)
    gains = (gain_one[None, :], gain_two[None, :])
    row_ids = [lax.dynamic_slice_in_dim(segment_ids, mp ^ r, 1) for r in range(rows)]
    two_rows = jnp.concatenate(row_ids)
    (grad_turned,) = kernel_call(
        turn_kernel, "turn_gradient", [shaped(width, total)], [], (output_grad, other_grad), 1e6
    )
    own_column = ffn_pack[:, None]
    mixer_line, own_sides, small, ffn_pack, grad_turned, other = stage(
        mixer_line, sides(own_column), (dp_one, gains, two_rows), ffn_pack, grad_turned, other
    )
    dp_one, (gain_first, gain_second), two_rows = small
    mixer_column = jnp.stack(mixer_line, axis=1)
    mixer_sides = sides(mixer_column)
    second_pack, first_pack = swap(ffn_pack, "mp", 4), swap(ffn_pack, "mp", 2)
    mixer_sides, own_sides = stage(mixer_sides, own_sides)
    mixer_corners = corners(*mixer_sides)
    mixer_corners, second_pack, first_pack, own_sides = stage(
        mixer_corners, second_pack, first_pack, own_sides
    )
    second_column = second_pack[:, None]
    second_sides = sides(second_column)
    own_corners = corners(*own_sides)
    third_pack = swap(second_pack, "mp", 2)
    (
        branch, values_0, values_1, gates_0, gates_1, conv_0, conv_1, weights, mixout, condition,
        taps_0, taps_1, shift, cond, summary,
    ) = kernel_call(
        functools.partial(mixer_forward_kernel, sizes), "mixer_forward",
        [shaped(total, width)] + [shaped(side, length)] * 6
        + [
            shaped(2 * side, width), shaped(side, width), shaped(filters, width, dtype=F32),
            shaped(filters, 2 * length, dtype=F32), shaped(filters, 2 * length, dtype=F32),
            shaped(filters, 2 * length, dtype=F32), shaped(rows, filters, 128, dtype=F32),
            shaped(rows, width, dtype=F32),
        ],
        [
            pltpu.VMEM((width, 128), BF), pltpu.VMEM((width, 128), BF),
            pltpu.VMEM((width, 128), BF), pltpu.VMEM((filters, 2 * length), F32),
            pltpu.VMEM((length, length), BF), pltpu.VMEM((sizes[5], length, length), BF),
            pltpu.VMEM((side, length), BF),
        ],
        (dp_one, two_rows, tokens, other, gain_first, mixer_column)
        + tuple(mixer_sides) + tuple(mixer_corners),
        14e9, scalars=1,
    )
    branch, second_sides, own_corners, third_pack = stage(
        branch, second_sides, own_corners, third_pack
    )
    values, gates, conv = (values_0, values_1), (gates_0, gates_1), (conv_0, conv_1)
    branch_got = swap(branch, "mp", 1)
    first_column, third_column = first_pack[:, None], third_pack[:, None]
    second_corners = corners(*second_sides)
    normed_two, normed_turned = kernel_call(
        norm_two_kernel, "norm_two", [shaped(total, width), shaped(width, total)], [],
        (tokens, other, branch, branch_got, gain_second),
        1e9,
    )
    normed_two, normed_turned, second_corners, third_column = stage(
        normed_two, normed_turned, second_corners, third_column
    )
    third_sides = sides(third_column)

    fixed = (dp_one, normed_two, normed_turned, output_grad, other_grad, grad_turned)
    first_x = swap(own_sides[0], "mp", 2)
    run = ffn_call(fixed, (second_column, *second_sides, *second_corners))
    run, third_sides, first_x, own_y = stage(run, third_sides, first_x, own_sides[1])
    second_scatter = Scatter(run[3:])
    third_corners = corners(*third_sides)
    second_scatter.start()
    first_y = swap(own_y, "mp", 2)
    run = ffn_call(fixed, (own_column, *own_sides, *own_corners), run[:3])
    run, third_corners, first_y, far_corners, second_scatter.ex, second_scatter.ey = stage(
        run, third_corners, first_y, own_corners, second_scatter.ex, second_scatter.ey
    )
    own_pieces = run[3:]
    second_scatter.middle()
    first_corners = [swap(c, "mp", 2) for c in far_corners]
    run = ffn_call(fixed, (third_column, *third_sides, *third_corners), run[:3])
    run, first_corners, second_scatter.f1a, second_scatter.f2b = stage(
        run, first_corners, second_scatter.f1a, second_scatter.f2b
    )
    third_scatter = Scatter(run[3:])
    third_scatter.start()
    run = ffn_call(
        fixed, (first_column, first_x, first_y, *first_corners), run[:3], own_pieces, last=True
    )
    run, third_scatter.ex, third_scatter.ey = stage(run, third_scatter.ex, third_scatter.ey)
    (second_sum,) = second_scatter.end()
    feed, feed_other, back = run[:3]
    third_scatter.middle()
    back_got = swap(back, "mp", 1)
    grad_middle, mixout_grad, grad_conv_0, grad_conv_1, grad_gates_0, grad_gates_1, gain_two_part = (
        kernel_call(
            mixout_back_kernel, "mixout_back",
            [shaped(length, width, dtype=F32), shaped(side, width)]
            + [shaped(side, length)] * 4 + [shaped(1, width, dtype=F32)],
            [],
            (
                tokens, other, branch, branch_got, back, back_got, output_grad, other_grad,
                gain_second, mixout,
            ) + gates + conv,
            4 * total * width * side,
        )
    )
    grad_conv_0, grad_conv_1, third_scatter.f1a, third_scatter.f2b, near = stage(
        grad_conv_0, grad_conv_1, third_scatter.f1a, third_scatter.f2b, run[3:]
    )
    near_sums = Scatter(near)
    near_sums.start()
    (third_sum,) = third_scatter.end()
    third_got = swap(third_sum, "mp", 2)
    grad_values_0, grad_values_1, grad_taps_0, grad_taps_1 = kernel_call(
        functools.partial(conv_back_kernel, 8, channels, reach), "conv_back",
        [shaped(side, length)] * 2 + [shaped(filters, (2 * reach + 2) * BLOCK, dtype=F32)] * 2,
        [
            pltpu.VMEM((length, length), BF), pltpu.VMEM((length, length), F32),
            pltpu.VMEM((8, length, length), BF), pltpu.VMEM((side, length), F32),
        ],
        (two_rows, taps_0, taps_1, *values, grad_conv_0, grad_conv_1),
        16e9,
    )
    grad_values_1, grad_taps_1, near_sums.ex, near_sums.ey, third_got = stage(
        grad_values_1, grad_taps_1, near_sums.ex, near_sums.ey, third_got
    )
    near_sums.middle()
    cut = slice(0, part), slice(part, depth)
    second_low = swap(added(second_sum[:, cut[0]], third_got[:, cut[0]]), "mp", 4)
    second_rest = second_sum[:, cut[1]], third_got[:, cut[1]]
    feed_got = swap(feed_other, "mp", 1)
    results = kernel_call(
        functools.partial(mixer_back_kernel, sizes), "mixer_back",
        [shaped(length, width), shaped(length, width)]
        + [
            shaped(chips, half, 128), shaped(chips, half + 16, 128), shaped(chips, half, 128),
            shaped(chips, half + 16, 128), shaped(2, chips, half + 16, 128),
            shaped(2, chips, half, 128),
        ],
        [
            pltpu.VMEM((width, 128), BF), pltpu.VMEM((width, 128), BF),
            pltpu.VMEM((width, 128), BF), pltpu.VMEM((2, filters, 2 * length), F32),
        ],
        (
            dp_one, tokens, other, gain_first, gain_two_part, grad_gates_0, grad_gates_1,
            mixout_grad, weights, condition, shift, cond, summary, grad_values_0, grad_values_1,
            grad_taps_0, grad_taps_1,
        ),
        8 * total * width * side, scalars=1,
    )
    results, near_sums.f1a, near_sums.f2b, second_low, second_rest = stage(
        results, near_sums.f1a, near_sums.f2b, second_low, second_rest
    )
    second_high = swap(added(*second_rest), "mp", 4)
    mixer_grads = Scatter(results[2:])
    mixer_grads.start()
    got_one = swap(results[1], "mp", 1)
    own_sum, first_sum = near_sums.end()
    first_got = swap(first_sum, "mp", 2)
    got_one, back_own = stage(got_one, results[0])
    input_grad = kernel_call(
        norm_one_back_kernel, "norm_one_back",
        [shaped(length, width)], [],
        (tokens, back_own, got_one, grad_middle, gain_first),
        1e9,
    )[0]
    input_grad, mixer_grads.ex, mixer_grads.ey, second_high = stage(
        input_grad, mixer_grads.ex, mixer_grads.ey, second_high
    )
    mixer_grads.middle()
    mixer_grads.f1a, mixer_grads.f2b, feed_got, first_got = stage(
        mixer_grads.f1a, mixer_grads.f2b, feed_got, first_got
    )
    ffn_terms = (own_sum, first_got, jnp.concatenate([second_low, second_high], axis=1))
    mixer_terms = mixer_grads.end()
    mixer_terms = [mixer_terms[0]] + [swap(mixer_terms[k], "mp", 2 * k) for k in range(1, chips)]
    gate_sum, up_sum, down_sum = sum(t.astype(F32) for t in ffn_terms)
    output = (
        tokens.astype(F32) + branch[:length].astype(F32) + branch_got[length:].astype(F32)
        + feed.astype(F32) + feed_got.astype(F32)
    ).astype(BF)
    value_sum, mixgate_sum, condition_sum, base_sum, shift_sum, mixout_sum, gain_sums = kernel_call(
        functools.partial(unpack_kernel, half, span), "unpack",
        [
            shaped(depth, block_c, dtype=F32), shaped(depth, block_c, dtype=F32),
            shaped(block_g, depth, dtype=F32), shaped(block_g, taps, dtype=F32),
            shaped(block_g, taps, dtype=F32), shaped(block_c, depth, dtype=F32),
            shaped(2, width, dtype=F32),
        ],
        [], tuple(mixer_terms), 1e6,
    )
    gain_sums = gain_sums + swap(gain_sums, "mp", 1)
    return (
        output, input_grad, gain_sums[0], gain_sums[1], value_sum, mixgate_sum, condition_sum.T,
        base_sum, shift_sum, mixout_sum, gate_sum, up_sum, down_sum.T,
    )


def choose(tokens, segment_ids, gain_one, gain_two, value_weight, mixgate_weight, condition_weight,
           filter_base, filter_shift, mixout_weight, gate_weight, up_weight, down_weight,
           output_grad):
    fits = (
        lax.axis_size("dp") == 4
        and lax.axis_size("mp") == 8
        and tokens.shape[0] == segment_ids.shape[1] == 512
        and value_weight.shape == (192, 96)
        and filter_base.shape == (6, 256)
        and gate_weight.shape == (192, 384)
    )
    return (fast_body if fits else body)(
        tokens, segment_ids, gain_one, gain_two, value_weight, mixgate_weight, condition_weight,
        filter_base, filter_shift, mixout_weight, gate_weight, up_weight, down_weight, output_grad,
    )


def solution(mesh):
    sides = P(("dp", "mp"), None)
    columns, rows = P("dp", "mp"), P("mp", "dp")
    in_specs = (
        sides, P("dp", None), P(), P(), columns, columns, columns, rows, rows, rows, columns,
        columns, rows, sides,
    )
    out_specs = (
        sides, sides, P(), P(), columns, columns, columns, rows, rows, rows, columns, columns, rows,
    )
    return jax.shard_map(choose, mesh=mesh, in_specs=in_specs, out_specs=out_specs, check_vma=False)
```
